32 devices in a mesh: dp: 8 (over y, x, core), tensor: 4 (over z).
Axes of the slice: x: 2, y: 2, z: 4, core: 2. Of those that a mesh axis runs over, the one named last changes fastest.
Arguments:
- tokens: bfloat16 [16, 1024, 1024], P('dp', 'tensor'), may hold values from -6 to 6
- segments: int32 [16, 1024], P('dp'), may hold values from 0 to 3, as said below
- qkv_weight: bfloat16 [3, 1024, 1024], P(None, None, 'tensor'), may hold values from -0.1875 to 0.1875
- qkv_bias: float32 [3, 1024], P(None, 'tensor'), may hold values from -1.5 to 1.5
- out_weight: bfloat16 [1024, 1024], P('tensor'), may hold values from -0.75 to 0.75
- out_bias: float32 [1024], replicated, may hold values from -1.5 to 1.5
- gain_one: float32 [1024], replicated, may hold values from 0.5 to 1.5
- shift_one: float32 [1024], replicated, may hold values from -1.5 to 1.5
- up_weight: bfloat16 [1024, 4096], P(None, 'tensor'), may hold values from -0.1875 to 0.1875
- up_bias: float32 [4096], P('tensor'), may hold values from -1.5 to 1.5
- down_weight: bfloat16 [4096, 1024], P('tensor'), may hold values from -0.1875 to 0.1875
- down_bias: float32 [1024], replicated, may hold values from -1.5 to 1.5
- gain_two: float32 [1024], replicated, may hold values from 0.5 to 1.5
- shift_two: float32 [1024], replicated, may hold values from -1.5 to 1.5
- proj_weight: bfloat16 [1024, 288], replicated, may hold values from -0.1875 to 0.1875
- out_grad: bfloat16 [16, 1024, 1024], P('dp', 'tensor'), may hold values from -6 to 6
- embed_grad: bfloat16 [16, 1024, 288], P('dp', 'tensor'), may hold values from -6 to 6
Outputs:
- layer_out: bfloat16 [16, 1024, 1024], P('dp', 'tensor')
- embeddings: bfloat16 [16, 1024, 288], P('dp', 'tensor')
- tokens_grad: float32 [16, 1024, 1024], P('dp', 'tensor')
- qkv_weight_grad: float32 [3, 1024, 1024], P(None, None, 'tensor')
- qkv_bias_grad: float32 [3, 1024], P(None, 'tensor')
- out_weight_grad: float32 [1024, 1024], P('tensor')
- out_bias_grad: float32 [1024], replicated
- gain_one_grad: float32 [1024], replicated
- shift_one_grad: float32 [1024], replicated
- up_weight_grad: float32 [1024, 4096], P(None, 'tensor')
- up_bias_grad: float32 [4096], P('tensor')
- down_weight_grad: float32 [4096, 1024], P('tensor')
- down_bias_grad: float32 [1024], replicated
- gain_two_grad: float32 [1024], replicated
- shift_two_grad: float32 [1024], replicated
- proj_weight_grad: float32 [1024, 288], replicated
The draws below stay inside these ranges and needn't reach their ends.
Inputs may be any that keep to these rules, and one draw needn't show every extreme that they name: `segments`: segment numbers never fall along a sequence; every sequence holds 4 documents, each of at least 200 tokens, and in every sequence some document has exactly 200.
All inputs are finite; a program needn't handle non-finite values.
Results may differ from the reference program's by a relative error of at most 0.018.
Values may be sent and summed in bfloat16 or wider, within the bound.
A program may use at most 192 MiB of HBM per device.

```python
import math
import jax
import jax.numpy as jnp
from jax import lax

D = 1024
HEADS = 16
HEAD_DIM = 64
FF = 4096
SEQ_LEN = 1024
DOCS = 4
DOC_LEAST = 200
PROJ = 288
SEQS = 16


def one_packing(key):
    spare = SEQ_LEN - DOCS * DOC_LEAST
    cut_key, pick_key = jax.random.split(key)
    cuts = jnp.sort(jax.random.randint(cut_key, (DOCS - 2,), 0, spare + 1).astype(jnp.int32))
    bounds = jnp.concatenate([jnp.zeros((1,), jnp.int32), cuts, jnp.full((1,), spare, jnp.int32)])
    extras = bounds[1:] - bounds[:-1]
    chosen = jax.random.randint(pick_key, (), 0, DOCS).astype(jnp.int32)
    doc_index = jnp.arange(DOCS, dtype=jnp.int32)
    lower_index = jnp.clip(doc_index, 0, DOCS - 2)
    upper_index = jnp.clip(doc_index - 1, 0, DOCS - 2)
    extra_all = jnp.where(doc_index < chosen, extras[lower_index], jnp.where(doc_index == chosen, 0, extras[upper_index]))
    lengths = DOC_LEAST + extra_all
    ends = jnp.cumsum(lengths).astype(jnp.int32)
    token_index = jnp.arange(SEQ_LEN, dtype=jnp.int32)
    return jnp.sum((token_index[:, None] >= ends[None, :-1]).astype(jnp.int32), axis=1).astype(jnp.int32)


def draw_segments(key, part):
    row_keys = jax.random.split(jax.random.fold_in(key, 11), SEQS)
    return jax.vmap(one_packing)(row_keys)


def block_levels(own_key, extent, shards, least, high):
    level = 1.0
    for dim, blocks in shards:
        steps = jax.random.uniform(jax.random.fold_in(jax.random.fold_in(own_key, 6), dim), (blocks,), jnp.float32, least / len(shards), high / len(shards))
        level = level * jnp.repeat(jnp.exp(steps), extent[dim] // blocks).reshape((-1,) + (1,) * (len(extent) - 1 - dim))
    return level


def gaussian(rng, shape, scale, most, cuts=(), kind=jnp.bfloat16):
    values = jax.random.normal(rng, shape, jnp.float32) * scale
    if len(cuts) > 0:
        values = block_levels(rng, shape, cuts, -0.22, 0.18) * values
    return jnp.clip(values, min=-most, max=most).astype(kind)


def setup_inputs(seed: int = 0) -> dict:
    splits = jax.random.split(jax.random.key(seed), 18)
    return {
        "tokens": gaussian(splits[0], (SEQS, SEQ_LEN, D), 1.0, 6.0, ((0, 8), (1, 4))),
        "segments": draw_segments(jax.random.fold_in(splits[17], 71), 0),
        "qkv_weight": gaussian(splits[2], (3, D, D), D ** -0.5, 0.1875, ((2, 4),)),
        "qkv_bias": gaussian(splits[3], (3, D), 0.3, 1.5, ((1, 4),), jnp.float32),
        "out_weight": gaussian(splits[4], (D, D), (D // 16) ** -0.5, 0.75, ((0, 4),)),
        "out_bias": gaussian(splits[5], (D,), 0.3, 1.5, (), jnp.float32),
        "gain_one": jnp.clip(1.0 + 0.1 * jax.random.normal(splits[6], (D,), jnp.float32), 0.5, 1.5),
        "shift_one": gaussian(splits[7], (D,), 0.3, 1.5, (), jnp.float32),
        "up_weight": gaussian(splits[8], (D, FF), D ** -0.5, 0.1875, ((1, 4),)),
        "up_bias": gaussian(splits[9], (FF,), 0.3, 1.5, ((0, 4),), jnp.float32),
        "down_weight": gaussian(splits[10], (FF, D), (FF // 4) ** -0.5, 0.1875, ((0, 4),)),
        "down_bias": gaussian(splits[11], (D,), 0.3, 1.5, (), jnp.float32),
        "gain_two": jnp.clip(1.0 + 0.1 * jax.random.normal(splits[12], (D,), jnp.float32), 0.5, 1.5),
        "shift_two": gaussian(splits[13], (D,), 0.3, 1.5, (), jnp.float32),
        "proj_weight": gaussian(splits[14], (D, PROJ), D ** -0.5, 0.1875),
        "out_grad": gaussian(splits[15], (SEQS, SEQ_LEN, D), 1.0, 6.0, ((0, 8), (1, 4))),
        "embed_grad": gaussian(splits[16], (SEQS, SEQ_LEN, PROJ), 1.0, 6.0, ((0, 8), (1, 4))),
    }


@jax.custom_vjp
def low(v):
    return lax.optimization_barrier(v.astype(jnp.bfloat16)).astype(jnp.float32)

@jax.custom_vjp
def low_back(v):
    return v

def low_keep(v):
    return (low(v), None)

def low_pass(kept, grad):
    return (grad,)

def back_keep(v):
    return (v, None)

def back_low(kept, grad):
    return (low(grad),)
low.defvjp(low_keep, low_pass)
low_back.defvjp(back_keep, back_low)
eps = 1e-05

def matmul(left, right):
    return jnp.dot(left, right, precision=lax.Precision.HIGHEST, preferred_element_type=jnp.float32)

def doc_positions(segment_rows):
    length = segment_rows.shape[-1]
    row_index = jnp.broadcast_to(jnp.arange(length, dtype=jnp.int32), segment_rows.shape)
    change = jnp.concatenate([jnp.ones(segment_rows.shape[:-1] + (1,), jnp.bool_), segment_rows[..., 1:] != segment_rows[..., :-1]], axis=-1)
    doc_start = lax.cummax(jnp.where(change, row_index, jnp.zeros_like(row_index)), axis=segment_rows.ndim - 1)
    return row_index - doc_start

def rotary_tables(positions, head_dim):
    half_dim = head_dim // 2
    exponent = jnp.arange(half_dim, dtype=jnp.float32) * (2.0 / head_dim)
    frequency = jnp.exp(-exponent * math.log(10000.0))
    angles = positions.astype(jnp.float32)[..., None] * frequency
    angles = jnp.concatenate([angles, angles], axis=-1)
    return (jnp.cos(angles), jnp.sin(angles))

def rotate(field, cosine, sine):
    half_dim = field.shape[-1] // 2
    rotated = jnp.concatenate([-field[..., half_dim:], field[..., :half_dim]], axis=-1)
    return field * cosine + rotated * sine

def layer_norm(field, gain, shift):
    row_mean = lax.optimization_barrier(jnp.mean(field, axis=-1, keepdims=True))
    centred = field - row_mean
    variance = lax.optimization_barrier(jnp.mean(centred * centred, axis=-1, keepdims=True))
    return centred * lax.rsqrt(variance + eps) * gain + shift

def forward(params, tokens, segment_row):
    qkv_weight, qkv_bias, out_weight, out_bias, gain_one, shift_one, up_weight, up_bias, down_weight, down_bias, gain_two, shift_two, proj_weight = params
    length = tokens.shape[0]
    positions = doc_positions(segment_row[None])[0]
    cosine, sine = rotary_tables(positions, HEAD_DIM)

    def split_heads(field):
        return field.reshape(length, HEADS, HEAD_DIM).transpose(1, 0, 2)
    queries = split_heads(low_back(matmul(tokens, qkv_weight[0]) + qkv_bias[0]))
    keys = split_heads(low_back(matmul(tokens, qkv_weight[1]) + qkv_bias[1]))
    values_low = split_heads(low(low_back(matmul(tokens, qkv_weight[2]) + qkv_bias[2])))
    queries = low(rotate(queries, cosine, sine) * HEAD_DIM ** (-0.5))
    keys = low(rotate(keys, cosine, sine))
    same_doc = segment_row[:, None] == segment_row[None, :]
    scores = jnp.einsum('hqd,hkd->hqk', queries, keys, precision=lax.Precision.HIGHEST)
    scores = low_back(jnp.where(same_doc[None], scores, -1000000000.0))
    row_peak = lax.optimization_barrier(jnp.max(scores, axis=-1, keepdims=True))
    shifted = jnp.exp(scores - row_peak)
    probs = shifted / lax.optimization_barrier(jnp.sum(shifted, axis=-1, keepdims=True))
    mixed = jnp.einsum('hqk,hkd->hqd', low(probs), values_low, precision=lax.Precision.HIGHEST)
    mixed = low(low_back(mixed.transpose(1, 0, 2).reshape(length, HEADS * HEAD_DIM)))
    attn_part = low_back(matmul(mixed, out_weight) + out_bias)
    normed = layer_norm(tokens + attn_part, gain_one, shift_one)
    hidden = low_back(matmul(low(normed), up_weight) + up_bias)
    active = low(jax.nn.gelu(hidden, approximate=False))
    ffn_part = low_back(matmul(active, down_weight) + down_bias)
    result = layer_norm(normed + ffn_part, gain_two, shift_two)
    embedded = matmul(low(result), proj_weight)
    return (result, embedded)

def reference(tokens, segments, qkv_weight, qkv_bias, out_weight, out_bias, gain_one, shift_one, up_weight, up_bias, down_weight, down_bias, gain_two, shift_two, proj_weight, out_grad, embed_grad):
    params = tuple((p.astype(jnp.float32) for p in (qkv_weight, qkv_bias, out_weight, out_bias, gain_one, shift_one, up_weight, up_bias, down_weight, down_bias, gain_two, shift_two, proj_weight)))

    def one_seq(running, per_seq):
        tok_row, seg_row, dy_row, de_row = per_seq

        def forward_one(prm, inputs):
            return forward(prm, inputs, seg_row)
        (result, embedded), pull_back = jax.vjp(forward_one, params, tok_row.astype(jnp.float32))
        param_grads, input_grad = pull_back((dy_row.astype(jnp.float32), de_row.astype(jnp.float32)))
        running = jax.tree.map(lambda acc, add: acc + add, running, param_grads)
        return (running, (result.astype(jnp.bfloat16), embedded.astype(jnp.bfloat16), input_grad))
    empty_grads = tuple((jnp.zeros_like(p) for p in params))
    summed, (layer_out, embeddings, tokens_grad) = lax.scan(one_seq, empty_grads, (tokens, segments, out_grad, embed_grad))
    return (layer_out, embeddings, tokens_grad, summed[0], summed[1], summed[2], summed[3], summed[4], summed[5], summed[6], summed[7], summed[8], summed[9], summed[10], summed[11], summed[12])
```

```python
import math

import jax
import jax.numpy as jnp
from jax import lax
from jax.sharding import Mesh
from jax.sharding import PartitionSpec as P

HEAD_DIM = 64
eps = 1e-05
DP = ("xb", "x", "yb", "y", "core")
CELL = ("x", "y", "core")
ALL = DP + ("z",)
f32 = jnp.float32
bf16 = jnp.bfloat16


def doc_positions(segment_rows):
    length = segment_rows.shape[-1]
    row_index = jnp.broadcast_to(jnp.arange(length, dtype=jnp.int32), segment_rows.shape)
    change = jnp.concatenate(
        [
            jnp.ones(segment_rows.shape[:-1] + (1,), jnp.bool_),
            segment_rows[..., 1:] != segment_rows[..., :-1],
        ],
        axis=-1,
    )
    doc_start = lax.cummax(
        jnp.where(change, row_index, jnp.zeros_like(row_index)), axis=segment_rows.ndim - 1
    )
    return row_index - doc_start


def rotary_tables(positions, head_dim):
    half_dim = head_dim // 2
    exponent = jnp.arange(half_dim, dtype=f32) * (2.0 / head_dim)
    frequency = jnp.exp(-exponent * math.log(10000.0))
    angles = positions.astype(f32)[..., None] * frequency
    angles = jnp.concatenate([angles, angles], axis=-1)
    return (jnp.cos(angles), jnp.sin(angles))


def rotate(field, cosine, sine):
    half_dim = field.shape[-1] // 2
    rotated = jnp.concatenate([-field[..., half_dim:], field[..., :half_dim]], axis=-1)
    return field * cosine + rotated * sine


def rotate_back(field, cosine, sine):
    half_dim = field.shape[-1] // 2
    rotated = jnp.concatenate([-field[..., half_dim:], field[..., :half_dim]], axis=-1)
    return field * cosine - rotated * sine


def norm_forward(field, gain, shift):
    row_mean = jnp.mean(field, axis=-1, keepdims=True)
    centred = field - row_mean
    variance = jnp.mean(centred * centred, axis=-1, keepdims=True)
    inv_std = lax.rsqrt(variance + eps)
    scaled = centred * inv_std
    return (scaled * gain + shift, scaled, inv_std)


def norm_backward(upstream, scaled, inv_std, gain):
    grad_scaled = upstream * gain
    grad_input = inv_std * (
        grad_scaled
        - jnp.mean(grad_scaled, axis=-1, keepdims=True)
        - scaled * jnp.mean(grad_scaled * scaled, axis=-1, keepdims=True)
    )
    return (grad_input, jnp.sum(upstream * scaled, axis=0), jnp.sum(upstream, axis=0))


def masked_scores(queries, keys, seg_row):
    scores = jnp.einsum("hqd,hkd->hqk", queries, keys, preferred_element_type=f32)
    same_doc = seg_row[:, None] == seg_row[None, :]
    return jnp.where(same_doc[None], scores, -1000000000.0)


def attend(inputs):
    queries, keys, values_low, seg_row = inputs
    scores = masked_scores(queries, keys, seg_row)
    row_peak = jnp.max(scores, axis=-1, keepdims=True)
    shifted = jnp.exp(scores - row_peak)
    row_total = jnp.sum(shifted, axis=-1, keepdims=True)
    probs = (shifted / row_total).astype(bf16)
    mixed_heads = jnp.einsum("hqk,hkd->hqd", probs, values_low, preferred_element_type=f32)
    return (mixed_heads, row_peak + jnp.log(row_total))


def attend_back(inputs):
    queries, keys, values_low, seg_row, log_total, grad_mixed = inputs
    scores = masked_scores(queries, keys, seg_row)
    probs = jnp.exp(scores - log_total)
    grad_values = jnp.einsum("hqk,hqd->hkd", probs.astype(bf16), grad_mixed, preferred_element_type=f32)
    grad_probs = jnp.einsum("hqd,hkd->hqk", grad_mixed, values_low, preferred_element_type=f32)
    row_inner = jnp.sum(probs * grad_probs, axis=-1, keepdims=True)
    grad_scores = (probs * (grad_probs - row_inner)).astype(bf16)
    grad_queries = jnp.einsum("hqk,hkd->hqd", grad_scores, keys, preferred_element_type=f32)
    grad_keys = jnp.einsum("hqk,hqd->hkd", grad_scores, queries, preferred_element_type=f32)
    return (grad_queries, grad_keys, grad_values)


def piece_of(shard):
    rows = shard.shape[0] // 8
    return lax.dynamic_slice_in_dim(shard, lax.axis_index(CELL) * rows, rows, 0)


def gather_all(shard, zsize):
    whole = lax.all_gather(piece_of(shard), ("z",) + CELL, axis=0, tiled=True)
    return whole.reshape((zsize,) + shard.shape)


def reduce_all(partial):
    rows = partial.shape[0] * partial.shape[1]
    piece = lax.psum_scatter(
        partial.reshape(rows, partial.shape[2]), ("z",) + CELL, scatter_dimension=0, tiled=True
    )
    return lax.all_gather(piece, CELL, axis=0, tiled=True)


def per_device(blocks, tokens, segments, qkv_weight, qkv_bias, out_weight, out_bias, gain_one, shift_one,
               up_weight, up_bias, down_weight, down_bias, gain_two, shift_two, proj_weight, out_grad, embed_grad):
    groups, local_rows, model_width = tokens.shape
    length = segments.shape[1]
    zsize = length // local_rows
    heads_here = qkv_weight.shape[2] // HEAD_DIM
    head_cols = qkv_weight.shape[2]
    units_here = up_weight.shape[1]
    rows = groups * local_rows
    zi = lax.axis_index("z")
    q_scale = HEAD_DIM ** (-0.5)
    cosine, sine = rotary_tables(doc_positions(segments), HEAD_DIM)
    cosine = cosine[:, None]
    sine = sine[:, None]

    def split_heads(field):
        return field.reshape(groups, length, heads_here, HEAD_DIM).transpose(0, 2, 1, 3)

    def join_heads(field):
        return field.transpose(0, 2, 1, 3).reshape(groups, length, head_cols)

    whole_tokens = lax.all_gather(tokens, "z", axis=1, tiled=True)
    out_all = gather_all(out_weight, zsize).reshape(model_width, model_width)
    up_all = gather_all(up_weight, zsize)
    down_all = gather_all(down_weight, zsize)
    full_up_bias = lax.all_gather(up_bias, "z", axis=0, tiled=False)

    projected = jnp.einsum("gld,cde->cgle", whole_tokens, qkv_weight, preferred_element_type=f32)
    projected = projected + qkv_bias[:, None, None, :]
    queries = (rotate(split_heads(projected[0]), cosine, sine) * q_scale).astype(bf16)
    keys = rotate(split_heads(projected[1]), cosine, sine).astype(bf16)
    values_low = split_heads(projected[2]).astype(bf16)
    got = [attend((queries[g], keys[g], values_low[g], segments[g])) for g in range(groups)]
    log_total = [g[1] for g in got]
    mixed = join_heads(jnp.stack([g[0] for g in got])).astype(bf16)
    mixed = lax.all_to_all(mixed, "z", split_axis=1, concat_axis=2, tiled=True).reshape(rows, model_width)

    first_sum = tokens.reshape(rows, model_width).astype(f32) + (
        jnp.dot(mixed, out_all, preferred_element_type=f32) + out_bias
    )
    normed, scaled_one, inv_one = norm_forward(first_sum, gain_one, shift_one)
    normed_low = normed.astype(bf16)
    hidden = jnp.einsum("nd,zdf->znf", normed_low, up_all, preferred_element_type=f32)
    hidden = hidden + full_up_bias[:, None, :]
    active, gelu_pull = jax.vjp(lambda field: jax.nn.gelu(field, approximate=False), hidden)
    active = active.astype(bf16)
    ffn = jnp.einsum("znf,zfd->nd", active, down_all, preferred_element_type=f32)
    second_sum = normed + (ffn + down_bias)
    result, scaled_two, inv_two = norm_forward(second_sum, gain_two, shift_two)
    result_low = result.astype(bf16)
    embedded = jnp.dot(result_low, proj_weight, preferred_element_type=f32).astype(bf16)
    embed_rows = embed_grad.reshape(rows, -1)
    grad_result = out_grad.reshape(rows, model_width).astype(f32) + jnp.einsum(
        "np,dp->nd", embed_rows, proj_weight, preferred_element_type=f32
    )
    proj_grad = jnp.einsum("nd,np->dp", result_low, embed_rows, preferred_element_type=f32)
    grad_second, gain_two_grad, shift_two_grad = norm_backward(grad_result, scaled_two, inv_two, gain_two)
    second_low = grad_second.astype(bf16)
    down_bias_grad = jnp.sum(second_low.astype(f32), axis=0)
    down_grad = jnp.einsum("znf,nd->zfd", active, second_low, preferred_element_type=f32).astype(bf16)
    grad_active = jnp.einsum("nd,zfd->znf", second_low, down_all, preferred_element_type=f32)
    grad_hidden = gelu_pull(grad_active)[0].astype(bf16)
    up_bias_grad = jnp.sum(grad_hidden.astype(f32), axis=1)
    up_grad = jnp.einsum("nd,znf->zdf", normed_low, grad_hidden, preferred_element_type=f32).astype(bf16)
    grad_normed = grad_second + jnp.einsum("znf,zdf->nd", grad_hidden, up_all, preferred_element_type=f32)
    grad_first, gain_one_grad, shift_one_grad = norm_backward(grad_normed, scaled_one, inv_one, gain_one)
    first_low = grad_first.astype(bf16)
    out_bias_grad = jnp.sum(first_low.astype(f32), axis=0)
    out_grad_w = jnp.einsum("nh,nd->hd", mixed, first_low, preferred_element_type=f32).astype(bf16)
    grad_mixed = jnp.einsum("nd,hd->nh", first_low, out_all, preferred_element_type=f32).astype(bf16)
    grad_mixed = grad_mixed.reshape(groups, local_rows, model_width)
    grad_mixed = lax.all_to_all(grad_mixed, "z", split_axis=2, concat_axis=1, tiled=True)
    grad_mixed = split_heads(grad_mixed)
    back = [
        attend_back((queries[g], keys[g], values_low[g], segments[g], log_total[g], grad_mixed[g]))
        for g in range(groups)
    ]
    grad_queries = rotate_back(jnp.stack([b[0] for b in back]) * q_scale, cosine, sine)
    grad_keys = rotate_back(jnp.stack([b[1] for b in back]), cosine, sine)
    grad_values = jnp.stack([b[2] for b in back])
    grad_qkv = jnp.stack(
        [join_heads(grad_queries), join_heads(grad_keys), join_heads(grad_values)]
    ).astype(bf16)
    qkv_bias_grad = jnp.sum(grad_qkv.astype(f32), axis=(1, 2))
    qkv_weight_grad = jnp.einsum("gld,cgle->cde", whole_tokens, grad_qkv, preferred_element_type=f32)
    input_back = jnp.einsum("cgle,cde->gld", grad_qkv, qkv_weight, preferred_element_type=f32).astype(bf16)
    input_back = lax.psum_scatter(input_back, "z", scatter_dimension=1, tiled=True)
    tokens_grad = grad_first.reshape(groups, local_rows, model_width) + input_back.astype(f32)

    qkv_weight_grad = lax.psum(qkv_weight_grad.astype(bf16), DP).astype(f32)
    down_grad = reduce_all(down_grad)
    up_grad = reduce_all(up_grad)
    out_grad_w = reduce_all(out_grad_w.reshape(zsize, head_cols, model_width))
    if blocks > 1:
        down_grad, up_grad, out_grad_w = lax.psum((down_grad, up_grad, out_grad_w), ("xb", "yb"))
    small = jnp.concatenate(
        [
            out_bias_grad, gain_one_grad, shift_one_grad, down_bias_grad, gain_two_grad, shift_two_grad,
            up_bias_grad.reshape(-1),
            lax.dynamic_update_slice(
                jnp.zeros((zsize, 3 * head_cols), f32), qkv_bias_grad.reshape(1, -1), (zi, 0)
            ).reshape(-1),
        ]
    )
    small = lax.psum(small, ALL)
    proj_grad = lax.psum(proj_grad, ALL)
    base = 6 * model_width
    vec = [small[i * model_width:(i + 1) * model_width] for i in range(6)]
    up_bias_grad = lax.dynamic_slice(small, (base + zi * units_here,), (units_here,))
    qkv_bias_grad = lax.dynamic_slice(
        small, (base + zsize * units_here + zi * 3 * head_cols,), (3 * head_cols,)
    ).reshape(3, head_cols)
    shape3 = (groups, local_rows, model_width)
    return (
        result_low.reshape(shape3),
        embedded.reshape(groups, local_rows, -1),
        tokens_grad,
        qkv_weight_grad,
        qkv_bias_grad,
        out_grad_w.astype(f32),
        vec[0], vec[1], vec[2],
        up_grad.astype(f32),
        up_bias_grad,
        down_grad.astype(f32),
        vec[3], vec[4], vec[5],
        proj_grad,
    )


def solution(mesh):
    dp_size, zsize = mesh.shape["dp"], mesh.shape["tensor"]
    side = math.isqrt(dp_size // 2) // 2
    cut = Mesh(mesh.devices.reshape(side, 2, side, 2, 2, zsize), DP + ("z",))
    rows3 = P(DP, "z", None)
    in_specs = (
        rows3, P(DP, None), P(None, None, "z"), P(None, "z"), P("z", None), P(), P(), P(),
        P(None, "z"), P("z"), P("z", None), P(), P(), P(), P(), rows3, rows3,
    )
    out_specs = (
        rows3, rows3, rows3, P(None, None, "z"), P(None, "z"), P("z", None), P(), P(), P(),
        P(None, "z"), P("z"), P("z", None), P(), P(), P(), P(),
    )

    def run(*args):
        return per_device(side * side, *args)

    return jax.shard_map(run, mesh=cut, in_specs=in_specs, out_specs=out_specs, check_vma=False)
```

```python
import functools
import math

import jax
import jax.numpy as jnp
from jax import lax
from jax.experimental import pallas as pl
from jax.experimental.pallas import tpu as pltpu
from jax.sharding import Mesh
from jax.sharding import PartitionSpec as P

HEAD_DIM = 64
eps = 1e-05
DP = ("xb", "x", "yb", "y", "core")
CELL = ("x", "y", "core")
ALL = DP + ("z",)
f32 = jnp.float32
bf16 = jnp.bfloat16


def doc_positions(segment_rows):
    length = segment_rows.shape[-1]
    row_index = jnp.broadcast_to(jnp.arange(length, dtype=jnp.int32), segment_rows.shape)
    change = jnp.concatenate(
        [
            jnp.ones(segment_rows.shape[:-1] + (1,), jnp.bool_),
            segment_rows[..., 1:] != segment_rows[..., :-1],
        ],
        axis=-1,
    )
    doc_start = lax.cummax(
        jnp.where(change, row_index, jnp.zeros_like(row_index)), axis=segment_rows.ndim - 1
    )
    return row_index - doc_start


def rotary_tables(positions, head_dim):
    half_dim = head_dim // 2
    exponent = jnp.arange(half_dim, dtype=f32) * (2.0 / head_dim)
    frequency = jnp.exp(-exponent * math.log(10000.0))
    angles = positions.astype(f32)[..., None] * frequency
    angles = jnp.concatenate([angles, angles], axis=-1)
    return (jnp.cos(angles), jnp.sin(angles))


def rotate(field, cosine, sine):
    half_dim = field.shape[-1] // 2
    rotated = jnp.concatenate([-field[..., half_dim:], field[..., :half_dim]], axis=-1)
    return field * cosine + rotated * sine


def rotate_back(field, cosine, sine):
    half_dim = field.shape[-1] // 2
    rotated = jnp.concatenate([-field[..., half_dim:], field[..., :half_dim]], axis=-1)
    return field * cosine - rotated * sine


def norm_forward(field, gain, shift):
    row_mean = jnp.mean(field, axis=-1, keepdims=True)
    centred = field - row_mean
    variance = jnp.mean(centred * centred, axis=-1, keepdims=True)
    inv_std = lax.rsqrt(variance + eps)
    scaled = centred * inv_std
    return (scaled * gain + shift, scaled, inv_std)


def norm_backward(upstream, scaled, inv_std, gain):
    grad_scaled = upstream * gain
    grad_input = inv_std * (
        grad_scaled
        - jnp.mean(grad_scaled, axis=-1, keepdims=True)
        - scaled * jnp.mean(grad_scaled * scaled, axis=-1, keepdims=True)
    )
    return (grad_input, jnp.sum(upstream * scaled, axis=0), jnp.sum(upstream, axis=0))


def masked_scores(queries, keys, seg_row):
    scores = jnp.einsum("hqd,hkd->hqk", queries, keys, preferred_element_type=f32)
    same_doc = seg_row[:, None] == seg_row[None, :]
    return jnp.where(same_doc[None], scores, -1000000000.0)


def attend(inputs):
    queries, keys, values_low, seg_row = inputs
    scores = masked_scores(queries, keys, seg_row)
    row_peak = jnp.max(scores, axis=-1, keepdims=True)
    shifted = jnp.exp(scores - row_peak)
    row_total = jnp.sum(shifted, axis=-1, keepdims=True)
    probs = (shifted / row_total).astype(bf16)
    mixed_heads = jnp.einsum("hqk,hkd->hqd", probs, values_low, preferred_element_type=f32)
    return (mixed_heads, row_peak + jnp.log(row_total))


def attend_back(inputs):
    queries, keys, values_low, seg_row, log_total, grad_mixed = inputs
    scores = masked_scores(queries, keys, seg_row)
    probs = jnp.exp(scores - log_total)
    grad_values = jnp.einsum("hqk,hqd->hkd", probs.astype(bf16), grad_mixed, preferred_element_type=f32)
    grad_probs = jnp.einsum("hqd,hkd->hqk", grad_mixed, values_low, preferred_element_type=f32)
    row_inner = jnp.sum(probs * grad_probs, axis=-1, keepdims=True)
    grad_scores = (probs * (grad_probs - row_inner)).astype(bf16)
    grad_queries = jnp.einsum("hqk,hkd->hqd", grad_scores, keys, preferred_element_type=f32)
    grad_keys = jnp.einsum("hqk,hqd->hkd", grad_scores, queries, preferred_element_type=f32)
    return (grad_queries, grad_keys, grad_values)


MESH_ID = pl.DeviceIdType.MESH
HBM = pl.BlockSpec(memory_space=pl.ANY)


def other(axis):
    return {axis: 1 - lax.axis_index(axis)}


def greet(zsize):
    z = lax.axis_index("z")
    barrier = pltpu.get_barrier_semaphore()
    for axis in CELL:
        pl.semaphore_signal(barrier, inc=1, device_id=other(axis), device_id_type=MESH_ID)

    @pl.when(z > 0)
    def _():
        pl.semaphore_signal(barrier, inc=1, device_id={"z": z - 1}, device_id_type=MESH_ID)

    @pl.when(z < zsize - 1)
    def _():
        pl.semaphore_signal(barrier, inc=1, device_id={"z": z + 1}, device_id_type=MESH_ID)

    peers = len(CELL) + jnp.where(z > 0, 1, 0) + jnp.where(z < zsize - 1, 1, 0)
    pl.semaphore_wait(barrier, peers)


def remote(src, dst, send_sem, recv_sem, device):
    return pltpu.make_async_remote_copy(
        src_ref=src, dst_ref=dst, send_sem=send_sem, recv_sem=recv_sem, device_id=device, device_id_type=MESH_ID
    )


ORDERS = {"xy": ("x", "y"), "yx": ("y", "x")}


def gather_kernel(zsize, orders, *refs):
    n = len(orders)
    tok, bias, shards = refs[0], refs[1], refs[2:2 + n]
    tok_all, bias_all, wholes = refs[2 + n], refs[3 + n], refs[4 + n:4 + 2 * n]
    local_sem, z_send, z_recv, p_send, p_recv = refs[4 + 2 * n:]
    z = lax.axis_index("z")
    c = lax.axis_index("core")
    place = [(lax.axis_index(o[0]), lax.axis_index(o[1])) for o in orders]

    local = []
    for k in range(n):
        local.append(pltpu.make_async_copy(shards[k], wholes[k].at[z], local_sem.at[k]))
    local.append(pltpu.make_async_copy(tok, tok_all.at[z], local_sem.at[n]))
    local.append(pltpu.make_async_copy(bias, bias_all.at[z], local_sem.at[n + 1]))
    for copy in local:
        copy.start()
    greet(zsize)

    def line(item, src, step, side):
        to = z + 1 if side == 0 else z - 1
        if item < n:
            f, s = place[item]
            own = shards[item].at[c, f, s]
            dst = wholes[item].at[src, c, f, s]
        else:
            own = (tok, bias)[item - n]
            dst = (tok_all, bias_all)[item - n].at[src]
        return remote(
            own if step == 0 else dst, dst, z_send.at[side, item, step], z_recv.at[side, item, step], {"z": to}
        )

    def exchange(k, src, stage, slot):
        f, s = place[k]
        whole = wholes[k]
        ref = (whole.at[src, c, f, s], whole.at[src, c, f], whole.at[src, c])[stage]
        axis = (orders[k][1], orders[k][0], "core")[stage]
        return remote(ref, ref, p_send.at[slot, k, stage], p_recv.at[slot, k, stage], other(axis))

    def valid_from(side, step):
        return z - step - 1 >= 0 if side == 0 else z + step + 1 < zsize

    def source(side, step):
        return z - step - 1 if side == 0 else z + step + 1

    def has_next(side):
        return z < zsize - 1 if side == 0 else z > 0

    for side in range(2):

        @pl.when(has_next(side))
        def _():
            for item in range(n):
                line(item, z, 0, side).start()

    def stage_on(stage, step):
        for side in range(2):

            @pl.when(valid_from(side, step))
            def _():
                src = source(side, step)
                slot = side * (zsize - 1) + step
                for k in range(n):
                    exchange(k, src, stage - 1, slot).wait_recv()
                    if stage < 3:
                        exchange(k, src, stage, slot).start()

    def arrive(items, step):
        for side in range(2):

            @pl.when(valid_from(side, step))
            def _():
                src = source(side, step)
                for item in items:
                    line(item, src, step, side).wait_recv()
                    if step + 1 < zsize - 1:

                        @pl.when(has_next(side))
                        def _():
                            line(item, src, step + 1, side).start()

                    if item < n:
                        exchange(item, src, 0, side * (zsize - 1) + step).start()

    for step in range(zsize - 1):
        arrive(range(n), step)
        if step == zsize - 2:
            for side in range(2):

                @pl.when(has_next(side))
                def _():
                    for item in range(n, n + 2):
                        line(item, z, 0, side).start()

        if step >= 1:
            stage_on(1, step - 1)
    for step in range(zsize - 1):
        if step == 0:
            stage_on(1, zsize - 2)
        stage_on(2, step)
        arrive(range(n, n + 2), step)
    for step in range(zsize - 1):
        stage_on(3, step)
    for copy in local:
        copy.wait()
    for side in range(2):

        @pl.when(has_next(side))
        def _():
            for item in range(n + 2):
                line(item, z, 0, side).wait_send()

        for step in range(zsize - 1):

            @pl.when(valid_from(side, step))
            def _():
                src = source(side, step)
                if step + 1 < zsize - 1:

                    @pl.when(has_next(side))
                    def _():
                        for item in range(n + 2):
                            line(item, src, step + 1, side).wait_send()

                for k in range(n):
                    for stage in range(3):
                        exchange(k, src, stage, side * (zsize - 1) + step).wait_send()


def gather_start(tokens, bias, weights, zsize):
    orders = [ORDERS[o] for o, _ in weights]
    shards = [w for _, w in weights]
    n = len(shards)
    stack = lambda a: jax.ShapeDtypeStruct((zsize,) + a.shape, a.dtype)
    return pl.pallas_call(
        functools.partial(gather_kernel, zsize, orders),
        out_shape=[stack(tokens), stack(bias)] + [stack(w) for w in shards],
        in_specs=[HBM] * (n + 2),
        out_specs=[HBM] * (n + 2),
        scratch_shapes=[
            pltpu.SemaphoreType.DMA((n + 2,)),
            pltpu.SemaphoreType.DMA((2, n + 2, zsize - 1)),
            pltpu.SemaphoreType.DMA((2, n + 2, zsize - 1)),
            pltpu.SemaphoreType.DMA((2 * (zsize - 1), n, 3)),
            pltpu.SemaphoreType.DMA((2 * (zsize - 1), n, 3)),
        ],
        compiler_params=pltpu.CompilerParams(collective_id=0, has_side_effects=True),
    )(tokens, bias, *shards)


def add_rows(dst, src):
    rows = dst.shape[0]
    step = min(rows, 32)

    def body(i, carry):
        at = pl.ds(pl.multiple_of(i * step, step), step)
        dst[at, :] = dst[at, :] + src[at, :]
        return carry

    lax.fori_loop(0, rows // step, body, 0)


def reduce_kernel(zsize, orders, *refs):
    n = len(orders)
    m = n - 2
    parts, back, small = refs[:n], refs[n], refs[n + 1]
    outs, back_out, small_out = refs[n + 2:2 * n + 2], refs[2 * n + 2], refs[2 * n + 3]
    pos = 2 * n + 4
    mine, got_c, got_1, got_2 = (refs[pos + i * n:pos + (i + 1) * n] for i in range(4))
    pos += 4 * n
    got_z = refs[pos:pos + m + 1]
    pos += m + 1
    back_mine, small_mine, small_got, small_line, small_total, part_line, part_total = refs[pos:pos + 7]
    (local_sem, send, recv, z_send, z_recv, s_send, s_recv, t_send, t_recv, g_send, g_recv, end_sem) = refs[pos + 7:]
    z = lax.axis_index("z")
    c = lax.axis_index("core")
    place = [(lax.axis_index(o[0]), lax.axis_index(o[1])) for o in orders]
    turn = []
    for i in range(zsize // 2):
        turn += [i, zsize - 1 - i]
    few = parts[m].shape[0]
    groups = [[(m, b) for b in range(few)] + [(m + 1, 0)]] + [[(k, b) for k in range(m)] for b in turn]
    steps = [kb for group in groups for kb in group]

    def load(k, b):
        return pltpu.make_async_copy(parts[k].at[b, c], mine[k].at[b], local_sem.at[k, b])

    def load_back(b):
        return pltpu.make_async_copy(back.at[b], back_mine.at[b], local_sem.at[n, b])

    load_small = pltpu.make_async_copy(small, small_mine.at[0], local_sem.at[n + 1, 0])

    def half(k, b, stage):
        f, s = place[k]
        if stage == 0:
            src, dst, axis = parts[k].at[b, 1 - c], got_c[k].at[b], "core"
        elif stage == 1:
            src, dst, axis = mine[k].at[b, 1 - f], got_1[k].at[b], orders[k][0]
        else:
            src, dst, axis = mine[k].at[b, f, 1 - s], got_2[k].at[b], orders[k][1]
        return remote(src, dst, send.at[stage, k, b], recv.at[stage, k, b], other(axis))

    def own(k, b):
        if k == m:
            return back_mine.at[b]
        f, s = place[k]
        return mine[k].at[b, f, s]

    def hop(k, b, side):
        to = z + 1 if side == 0 else z - 1
        at = b if side == 0 else jnp.where(b == z - 1, zsize, b)
        return remote(own(k, b), got_z[k].at[at], z_send.at[k, b], z_recv.at[k, at], {"z": to})

    def take(k, b, side):
        at = b if side == 0 else jnp.where(b == z, zsize, b)
        ref = got_z[k].at[at]
        sender = z - 1 if side == 0 else z + 1
        remote(own(k, b), ref, z_send.at[k, b], z_recv.at[k, at], {"z": sender}).wait_recv()
        add_rows(own(k, b), ref)

    def line_step(ks, b, hops):
        for side in range(2):
            here = z == hops if side == 0 else z == zsize - 1 - hops
            goes = jnp.logical_and(here, z < b) if side == 0 else jnp.logical_and(here, z > b)
            if hops:
                ends = jnp.logical_and(here, z == b)

                @pl.when(jnp.logical_or(goes, ends))
                def _():
                    for k in ks:
                        take(k, b, side)

            @pl.when(goes)
            def _():
                for k in ks:
                    hop(k, b, side).start()

    def small_swap(stage):
        return remote(
            small_mine.at[stage], small_got.at[stage], s_send.at[stage], s_recv.at[stage], other(CELL[stage])
        )

    def small_step(stage):
        small_swap(stage).wait_recv()
        small_mine[stage + 1] = small_mine[stage] + small_got[stage]
        if stage < 2:
            small_swap(stage + 1).start()

    last = len(CELL)
    last_part = own(m + 1, 0)

    def total_copy(item, way):
        line, total = ((small_line, small_total), (part_line, part_total))[item]
        src = (small_mine.at[last], last_part)[item] if way == 0 else total
        dst = line if way == 0 else total
        to = z + 1 if way == 0 else z - 1
        return remote(src, dst, t_send.at[item, way], t_recv.at[item, way], {"z": to})

    def total_step(tick):
        if 0 <= tick < zsize:

            @pl.when(z == tick)
            def _():
                if tick > 0:
                    for item in range(2):
                        total_copy(item, 0).wait_recv()
                    small_mine[last] = small_mine[last] + small_line[...]
                    add_rows(last_part, part_line)
                if tick < zsize - 1:
                    for item in range(2):
                        total_copy(item, 0).start()
                else:
                    small_total[...] = small_mine[last]
                    part_total[...] = last_part[...]

        back_tick = tick - (zsize - 1)
        if 0 <= back_tick < zsize:

            @pl.when(z == zsize - 1 - back_tick)
            def _():
                if back_tick > 0:
                    for item in range(2):
                        total_copy(item, 1).wait_recv()
                if back_tick < zsize - 1:
                    for item in range(2):
                        total_copy(item, 1).start()

    for b in turn:
        load_back(b).start()
    load_small.start()
    for k, b in steps:
        load(k, b).start()
    greet(zsize)
    for k, b in groups[0]:
        half(k, b, 0).start()
    for b in turn:
        load_back(b).wait()
    for b in turn:
        line_step([m], b, 0)
    load_small.wait()
    small_swap(0).start()
    for k, b in steps[len(groups[0]):]:
        half(k, b, 0).start()

    def stage_1(k, b):
        f, s = place[k]
        load(k, b).wait()
        half(k, b, 0).wait_recv()
        for i in range(2):
            add_rows(mine[k].at[b, 1 - f, i], got_c[k].at[b, 1 - f, i])
        half(k, b, 1).start()
        for i in range(2):
            add_rows(mine[k].at[b, f, i], got_c[k].at[b, f, i])

    def stage_2(k, b):
        f, s = place[k]
        half(k, b, 1).wait_recv()
        add_rows(mine[k].at[b, f, 1 - s], got_1[k].at[b, 1 - s])
        half(k, b, 2).start()
        add_rows(mine[k].at[b, f, s], got_1[k].at[b, s])

    def stage_3(k, b):
        f, s = place[k]
        half(k, b, 2).wait_recv()
        add_rows(mine[k].at[b, f, s], got_2[k].at[b])

    def result(k, b):
        return part_total if k == m + 1 else own(k, b) if k != m else mine[m].at[b, place[m][0], place[m][1]]

    def out_of(k, b):
        return outs[k].at[b] if k == m else outs[k]

    def put(k, b, slot):
        f, s = place[k]
        return pltpu.make_async_copy(result(k, b), out_of(k, b).at[c, f, s], end_sem.at[slot])

    def spread(k, b, stage, slot):
        f, s = place[k]
        out = out_of(k, b)
        dst = (out.at[c, f, s], out.at[c, f], out.at[c])[stage]
        src = result(k, b) if stage == 0 else dst
        axis = (orders[k][1], orders[k][0], "core")[stage]
        return remote(src, dst, g_send.at[slot, stage], g_recv.at[slot, stage], other(axis))

    first = [(m, b, b) for b in range(few)]
    rest = [(k, z, few + k) for k in range(m)] + [(m + 1, 0, few + m)]

    def spread_start(items):
        for k, b, slot in items:
            spread(k, b, 0, slot).start()
            put(k, b, slot).start()

    def spread_on(items, stage):
        for k, b, slot in items:
            if stage == 1:
                put(k, b, slot).wait()
            spread(k, b, stage - 1, slot).wait_recv()
            if stage < 3:
                spread(k, b, stage, slot).start()

    ks = list(range(m))
    small_tick = 3
    back_ticks = [2 + i + (1 if i > 1 else 0) for i in range(zsize)]
    for tick in range(len(groups) + zsize + 2):
        if tick < len(groups):
            for k, b in groups[tick]:
                stage_1(k, b)
        if 1 <= tick <= len(groups):
            for k, b in groups[tick - 1]:
                stage_2(k, b)
        if 2 <= tick <= len(groups) + 1:
            for k, b in groups[tick - 2]:
                stage_3(k, b)
        if 1 <= tick <= 3:
            small_step(tick - 1)
        for i in range(1, zsize):
            if tick == back_ticks[i - 1]:
                for b in turn:
                    line_step([m], b, i)
        for j, b in enumerate(turn):
            hops = tick - 3 - j
            if 0 <= hops < zsize:
                line_step(ks, b, hops)
        total_step(tick - small_tick)
        if tick == 4:
            spread_start(first)
        if 5 <= tick <= 7:
            spread_on(first, tick - 4)
    for tick in range(len(groups) + zsize + 2 - small_tick, 2 * zsize):
        total_step(tick)
    finish_back = pltpu.make_async_copy(back_mine.at[z], back_out, local_sem.at[n, 0])
    finish_back.start()
    finish_small = pltpu.make_async_copy(small_total, small_out, local_sem.at[n + 1, 0])
    finish_small.start()
    spread_start(rest)
    for stage in (1, 2, 3):
        spread_on(rest, stage)
    finish_back.wait()
    finish_small.wait()
    for b in range(zsize):

        @pl.when(z != b)
        def _():
            for k in range(m + 1):
                hop(k, b, 0).wait_send()

    for way in range(2):

        @pl.when(z < zsize - 1 if way == 0 else z > 0)
        def _():
            for item in range(2):
                total_copy(item, way).wait_send()

    for k, b in steps:
        for stage in range(3):
            half(k, b, stage).wait_send()
    for stage in range(3):
        small_swap(stage).wait_send()
    for k, b, slot in first + rest:
        for stage in range(3):
            spread(k, b, stage, slot).wait_send()


def reduce_end(parts, cell_part, all_part, back, small, zsize):
    orders = [ORDERS[o] for o, _ in parts + [cell_part, all_part]]
    arrays = [a for _, a in parts + [cell_part, all_part]]
    n = len(arrays)
    shapes = [a.shape for a in arrays]
    like = jax.ShapeDtypeStruct
    outs = [like(s if i == n - 2 else s[1:], bf16) for i, s in enumerate(shapes)]
    outs += [like(back.shape[1:], bf16), like(small.shape, f32)]
    scratch = [pltpu.VMEM((s[0],) + s[2:], bf16) for s in shapes]
    scratch += [pltpu.VMEM((s[0],) + s[2:], bf16) for s in shapes]
    scratch += [pltpu.VMEM((s[0],) + s[3:], bf16) for s in shapes]
    scratch += [pltpu.VMEM((s[0],) + s[4:], bf16) for s in shapes]
    scratch += [pltpu.VMEM((zsize + 1,) + s[4:], bf16) for s in shapes[:-2]]
    scratch += [pltpu.VMEM((zsize + 1,) + back.shape[1:], bf16), pltpu.VMEM(back.shape, bf16)]
    scratch += [pltpu.VMEM((4,) + small.shape, f32), pltpu.VMEM((3,) + small.shape, f32)]
    scratch += [pltpu.VMEM(small.shape, f32)] * 2 + [pltpu.VMEM(shapes[-1][4:], bf16)] * 2
    dma = pltpu.SemaphoreType.DMA
    most = max(zsize, shapes[-2][0])
    ends = n - 1 + shapes[-2][0]
    scratch += [
        dma((n + 2, most)), dma((3, n, most)), dma((3, n, most)), dma((n - 1, zsize)), dma((n - 1, zsize + 1)),
        dma((3,)), dma((3,)), dma((2, 2)), dma((2, 2)), dma((ends, 3)), dma((ends, 3)), dma((ends,)),
    ]
    return pl.pallas_call(
        functools.partial(reduce_kernel, zsize, orders),
        out_shape=outs,
        in_specs=[HBM] * (n + 2),
        out_specs=[HBM] * (n + 2),
        scratch_shapes=scratch,
        compiler_params=pltpu.CompilerParams(
            collective_id=1, has_side_effects=True, vmem_limit_bytes=60 * 1024 * 1024
        ),
    )(*arrays, back, small)


def per_device(blocks, tokens, segments, qkv_weight, qkv_bias, out_weight, out_bias, gain_one, shift_one,
               up_weight, up_bias, down_weight, down_bias, gain_two, shift_two, proj_weight, out_grad, embed_grad):
    groups, local_rows, model_width = tokens.shape
    length = segments.shape[1]
    zsize = length // local_rows
    heads_here = qkv_weight.shape[2] // HEAD_DIM
    head_cols = qkv_weight.shape[2]
    units_here = up_weight.shape[1]
    rows = groups * local_rows
    zi = lax.axis_index("z")
    q_scale = HEAD_DIM ** (-0.5)
    cosine, sine = rotary_tables(doc_positions(segments), HEAD_DIM)
    cosine = cosine[:, None]
    sine = sine[:, None]

    def split_heads(field):
        return field.reshape(groups, length, heads_here, HEAD_DIM).transpose(0, 2, 1, 3)

    def join_heads(field):
        return field.transpose(0, 2, 1, 3).reshape(groups, length, head_cols)

    def cut(array, rows_at):
        shape = array.shape
        return array.reshape(shape[:rows_at] + (2, 2, 2, shape[rows_at] // 8) + shape[rows_at + 1:])

    token_rows = tokens.reshape(rows, model_width)
    token_blocks, bias_blocks, out_all, up_all, down_all = gather_start(
        token_rows,
        up_bias.reshape(8, units_here // 8),
        [("xy", cut(out_weight, 0)), ("xy", cut(up_weight, 0)), ("yx", cut(down_weight, 0))],
        zsize,
    )
    whole_tokens = token_blocks.reshape(zsize, groups, local_rows, model_width).transpose(1, 0, 2, 3)
    whole_tokens = whole_tokens.reshape(groups, length, model_width)
    out_all = out_all.reshape(model_width, model_width)
    up_all = up_all.reshape(zsize, model_width, units_here)
    down_all = down_all.reshape(zsize, units_here, model_width)
    full_up_bias = bias_blocks.reshape(zsize, units_here)

    projected = jnp.einsum("gld,cde->cgle", whole_tokens, qkv_weight, preferred_element_type=f32)
    projected = projected + qkv_bias[:, None, None, :]
    queries = (rotate(split_heads(projected[0]), cosine, sine) * q_scale).astype(bf16)
    keys = rotate(split_heads(projected[1]), cosine, sine).astype(bf16)
    values_low = split_heads(projected[2]).astype(bf16)
    got = [attend((queries[g], keys[g], values_low[g], segments[g])) for g in range(groups)]
    log_total = [g[1] for g in got]
    mixed = join_heads(jnp.stack([g[0] for g in got])).astype(bf16)
    mixed = lax.all_to_all(mixed, "z", split_axis=1, concat_axis=2, tiled=True).reshape(rows, model_width)

    first_sum = tokens.reshape(rows, model_width).astype(f32) + (
        jnp.dot(mixed, out_all, preferred_element_type=f32) + out_bias
    )
    normed, scaled_one, inv_one = norm_forward(first_sum, gain_one, shift_one)
    normed_low = normed.astype(bf16)
    hidden = jnp.einsum("nd,zdf->znf", normed_low, up_all, preferred_element_type=f32)
    hidden = hidden + full_up_bias[:, None, :]
    active, gelu_pull = jax.vjp(lambda field: jax.nn.gelu(field, approximate=False), hidden)
    active = active.astype(bf16)
    ffn = jnp.einsum("znf,zfd->nd", active, down_all, preferred_element_type=f32)
    second_sum = normed + (ffn + down_bias)
    result, scaled_two, inv_two = norm_forward(second_sum, gain_two, shift_two)
    result_low = result.astype(bf16)
    embedded = jnp.dot(result_low, proj_weight, preferred_element_type=f32).astype(bf16)
    embed_rows = embed_grad.reshape(rows, -1)
    grad_result = out_grad.reshape(rows, model_width).astype(f32) + jnp.einsum(
        "np,dp->nd", embed_rows, proj_weight, preferred_element_type=f32
    )
    proj_grad = jnp.einsum("nd,np->dp", result_low, embed_rows, preferred_element_type=f32)
    grad_second, gain_two_grad, shift_two_grad = norm_backward(grad_result, scaled_two, inv_two, gain_two)
    second_low = grad_second.astype(bf16)
    down_bias_grad = jnp.sum(second_low.astype(f32), axis=0)
    down_grad = jnp.einsum("znf,nd->zfd", active, second_low, preferred_element_type=f32).astype(bf16)
    grad_active = jnp.einsum("nd,zfd->znf", second_low, down_all, preferred_element_type=f32)
    grad_hidden = gelu_pull(grad_active)[0].astype(bf16)
    up_bias_grad = jnp.sum(grad_hidden.astype(f32), axis=1)
    up_grad = jnp.einsum("nd,znf->zdf", normed_low, grad_hidden, preferred_element_type=f32).astype(bf16)
    grad_normed = grad_second + jnp.einsum("znf,zdf->nd", grad_hidden, up_all, preferred_element_type=f32)
    grad_first, gain_one_grad, shift_one_grad = norm_backward(grad_normed, scaled_one, inv_one, gain_one)
    first_low = grad_first.astype(bf16)
    out_bias_grad = jnp.sum(first_low.astype(f32), axis=0)
    out_grad_w = jnp.einsum("nh,nd->hd", mixed, first_low, preferred_element_type=f32).astype(bf16)
    grad_mixed = jnp.einsum("nd,hd->nh", first_low, out_all, preferred_element_type=f32).astype(bf16)
    grad_mixed = grad_mixed.reshape(groups, local_rows, model_width)
    grad_mixed = lax.all_to_all(grad_mixed, "z", split_axis=2, concat_axis=1, tiled=True)
    grad_mixed = split_heads(grad_mixed)
    back = [
        attend_back((queries[g], keys[g], values_low[g], segments[g], log_total[g], grad_mixed[g]))
        for g in range(groups)
    ]
    grad_queries = rotate_back(jnp.stack([b[0] for b in back]) * q_scale, cosine, sine)
    grad_keys = rotate_back(jnp.stack([b[1] for b in back]), cosine, sine)
    grad_values = jnp.stack([b[2] for b in back])
    grad_qkv = jnp.stack(
        [join_heads(grad_queries), join_heads(grad_keys), join_heads(grad_values)]
    ).astype(bf16)
    qkv_bias_grad = jnp.sum(grad_qkv.astype(f32), axis=(1, 2))
    qkv_weight_grad = jnp.einsum("gld,cgle->cde", whole_tokens, grad_qkv, preferred_element_type=f32)
    input_back = jnp.einsum("cgle,cde->gld", grad_qkv, qkv_weight, preferred_element_type=f32).astype(bf16)
    back = input_back.reshape(groups, zsize, local_rows, model_width).transpose(1, 0, 2, 3)
    small = jnp.concatenate(
        [
            out_bias_grad, gain_one_grad, shift_one_grad, down_bias_grad, gain_two_grad, shift_two_grad,
            up_bias_grad.reshape(-1),
            lax.dynamic_update_slice(
                jnp.zeros((zsize, 3 * head_cols), f32), qkv_bias_grad.reshape(1, -1), (zi, 0)
            ).reshape(-1),
        ]
    )
    proj_cols = proj_grad.shape[1]
    proj_grad = jnp.pad(proj_grad.astype(bf16), ((0, 0), (0, -proj_cols % 128)))
    out_grad_w, up_grad, down_grad, qkv_weight_grad, proj_grad, back, small = reduce_end(
        [
            ("xy", cut(out_grad_w.reshape(zsize, head_cols, model_width), 1)),
            ("xy", cut(up_grad, 1)),
            ("yx", cut(down_grad, 1)),
        ],
        ("yx", cut(qkv_weight_grad.astype(bf16), 1)),
        ("xy", cut(proj_grad[None], 1)),
        back.reshape(zsize, rows, model_width),
        small.reshape(8, -1),
        zsize,
    )
    tokens_grad = grad_first.reshape(groups, local_rows, model_width) + back.astype(f32).reshape(
        groups, local_rows, model_width
    )
    qkv_weight_grad = qkv_weight_grad.reshape(qkv_weight.shape)
    proj_grad = proj_grad.reshape(model_width, -1)[:, :proj_cols].astype(f32)
    out_grad_w = out_grad_w.reshape(out_weight.shape)
    up_grad = up_grad.reshape(up_weight.shape)
    down_grad = down_grad.reshape(down_weight.shape)
    if blocks > 1:
        down_grad, up_grad, out_grad_w, qkv_weight_grad = lax.psum(
            (down_grad, up_grad, out_grad_w, qkv_weight_grad), ("xb", "yb")
        )
        small, proj_grad = lax.psum((small, proj_grad), ("xb", "yb"))
    small = small.reshape(-1)
    base = 6 * model_width
    vec = [small[i * model_width:(i + 1) * model_width] for i in range(6)]
    up_bias_grad = lax.dynamic_slice(small, (base + zi * units_here,), (units_here,))
    qkv_bias_grad = lax.dynamic_slice(
        small, (base + zsize * units_here + zi * 3 * head_cols,), (3 * head_cols,)
    ).reshape(3, head_cols)
    shape3 = (groups, local_rows, model_width)
    return (
        result_low.reshape(shape3),
        embedded.reshape(groups, local_rows, -1),
        tokens_grad,
        qkv_weight_grad.astype(f32),
        qkv_bias_grad,
        out_grad_w.astype(f32),
        vec[0], vec[1], vec[2],
        up_grad.astype(f32),
        up_bias_grad,
        down_grad.astype(f32),
        vec[3], vec[4], vec[5],
        proj_grad,
    )


def solution(mesh):
    dp_size, zsize = mesh.shape["dp"], mesh.shape["tensor"]
    side = math.isqrt(dp_size // 2) // 2
    cut = Mesh(mesh.devices.reshape(side, 2, side, 2, 2, zsize), DP + ("z",))
    rows3 = P(DP, "z", None)
    in_specs = (
        rows3, P(DP, None), P(None, None, "z"), P(None, "z"), P("z", None), P(), P(), P(),
        P(None, "z"), P("z"), P("z", None), P(), P(), P(), P(), rows3, rows3,
    )
    out_specs = (
        rows3, rows3, rows3, P(None, None, "z"), P(None, "z"), P("z", None), P(), P(), P(),
        P(None, "z"), P("z"), P("z", None), P(), P(), P(), P(),
    )

    def run(*args):
        return per_device(side * side, *args)

    return jax.shard_map(run, mesh=cut, in_specs=in_specs, out_specs=out_specs, check_vma=False)
```

```python
import functools
import math

import jax
import jax.numpy as jnp
from jax import lax
from jax.experimental import pallas as pl
from jax.experimental.pallas import tpu as pltpu
from jax.sharding import Mesh
from jax.sharding import PartitionSpec as P

HEAD_DIM = 64
eps = 1e-05
DP = ("xb", "x", "yb", "y", "core")
CELL = ("x", "y", "core")
ALL = DP + ("z",)
f32 = jnp.float32
bf16 = jnp.bfloat16


def doc_positions(segment_rows):
    length = segment_rows.shape[-1]
    row_index = jnp.broadcast_to(jnp.arange(length, dtype=jnp.int32), segment_rows.shape)
    change = jnp.concatenate(
        [
            jnp.ones(segment_rows.shape[:-1] + (1,), jnp.bool_),
            segment_rows[..., 1:] != segment_rows[..., :-1],
        ],
        axis=-1,
    )
    doc_start = lax.cummax(
        jnp.where(change, row_index, jnp.zeros_like(row_index)), axis=segment_rows.ndim - 1
    )
    return row_index - doc_start


def rotary_tables(positions, head_dim):
    half_dim = head_dim // 2
    exponent = jnp.arange(half_dim, dtype=f32) * (2.0 / head_dim)
    frequency = jnp.exp(-exponent * math.log(10000.0))
    angles = positions.astype(f32)[..., None] * frequency
    angles = jnp.concatenate([angles, angles], axis=-1)
    return (jnp.cos(angles), jnp.sin(angles))


def norm_forward(field, gain, shift):
    row_mean = jnp.mean(field, axis=-1, keepdims=True)
    centred = field - row_mean
    variance = jnp.mean(centred * centred, axis=-1, keepdims=True)
    inv_std = lax.rsqrt(variance + eps)
    scaled = centred * inv_std
    return (scaled * gain + shift, scaled, inv_std)


def norm_backward(upstream, scaled, inv_std, gain):
    grad_scaled = upstream * gain
    grad_input = inv_std * (
        grad_scaled
        - jnp.mean(grad_scaled, axis=-1, keepdims=True)
        - scaled * jnp.mean(grad_scaled * scaled, axis=-1, keepdims=True)
    )
    return (grad_input, jnp.sum(upstream * scaled, axis=0), jnp.sum(upstream, axis=0))


BLOCK = 256


def turn_halves(field, sign_sine):
    lane = lax.broadcasted_iota(jnp.int32, field.shape, 1)
    half = HEAD_DIM // 2
    width = field.shape[1]
    swapped = jnp.where(lane % HEAD_DIM < half, pltpu.roll(field, width - half, 1), pltpu.roll(field, half, 1))
    return swapped * sign_sine


def scores_of(keys, queries):
    return lax.dot_general(keys, queries, (((1,), (1,)), ((), ())), preferred_element_type=f32)


def attend_kernel(group, lo_ref, hi_ref, tok_ref, w_ref, b_ref, cos_ref, sin_ref, seg_ref, mixed_ref, q_ref, k_ref, v_ref,
                  lse_ref, vt_ref, m_ref, l_ref, acc_ref):
    zsize, _, rows, _ = tok_ref.shape
    length = zsize * rows
    heads = q_ref.shape[1]
    pair = 2 * HEAD_DIM
    scale = HEAD_DIM ** (-0.5)

    def project(i, carry):
        at = pl.ds(pl.multiple_of(i * rows, rows), rows)
        x = tok_ref[i, 0]
        lane = lax.broadcasted_iota(jnp.int32, (rows, pair), 1)
        doc = seg_ref[0, at, :]
        same = lane - HEAD_DIM == doc
        low = lane < HEAD_DIM
        feature = lane < HEAD_DIM + 4
        extra_q = jnp.where(same, 1.0, 0.0)
        extra_k = jnp.where(jnp.logical_and(feature, jnp.logical_not(same)), -1e9, 0.0)
        cosine = cos_ref[0, at, :]
        sine = sin_ref[0, at, :]
        for c in range(3):
            field = jnp.dot(x, w_ref[c], preferred_element_type=f32) + b_ref[c:c + 1, :]
            for j in range(heads // 2):
                part = field[:, j * pair:(j + 1) * pair]
                if c < 2:
                    part = part * cosine + turn_halves(part, sine)
                if c == 0:
                    part = part * scale
                for h in range(2):
                    one = part if h == 0 else pltpu.roll(part, HEAD_DIM, 1)
                    head = 2 * j + h
                    if c == 0:
                        q_ref[0, head, at, :] = jnp.where(low, one, extra_q).astype(bf16)
                    elif c == 1:
                        k_ref[0, head, at, :] = jnp.where(low, one, extra_k).astype(bf16)
                    else:
                        one = jnp.where(low, one, 0.0)
                        v_ref[0, head, at, :] = one.astype(bf16)
                        vt_ref[head, :, at] = one.T[:HEAD_DIM].astype(bf16)
        return carry

    lax.fori_loop(0, zsize, project, 0)

    def query_block(i, carry):
        at = pl.ds(pl.multiple_of(i * BLOCK, BLOCK), BLOCK)
        m_ref[...] = jnp.full(m_ref.shape, -1e30, f32)
        l_ref[...] = jnp.zeros(l_ref.shape, f32)
        acc_ref[...] = jnp.zeros(acc_ref.shape, f32)

        def key_block(j, carry):
            keys_at = pl.ds(pl.multiple_of(j * BLOCK, BLOCK), BLOCK)
            for h in range(heads):
                st = scores_of(k_ref[0, h, keys_at, :], q_ref[0, h, at, :])
                peak = m_ref[h:h + 1, :]
                new = jnp.maximum(peak, jnp.max(st, axis=0, keepdims=True))
                p = jnp.exp(st - new)
                old = jnp.exp(peak - new)
                m_ref[h:h + 1, :] = new
                l_ref[h:h + 1, :] = l_ref[h:h + 1, :] * old + jnp.sum(p, axis=0, keepdims=True)
                acc_ref[h] = acc_ref[h] * old + jnp.dot(
                    vt_ref[h, :, keys_at], p.astype(bf16), preferred_element_type=f32
                )
            return carry

        lax.fori_loop(lo_ref[group, i], hi_ref[group, i], key_block, 0)
        out = [acc_ref[h] / l_ref[h:h + 1, :] for h in range(heads)]
        for j in range(heads // 2):
            both = jnp.concatenate([out[2 * j], out[2 * j + 1]], axis=0)
            mixed_ref[0, at, j * pair:(j + 1) * pair] = both.T.astype(bf16)
        lse_ref[0, :, at] = m_ref[...] + jnp.log(l_ref[...])
        return carry

    lax.fori_loop(0, length // BLOCK, query_block, 0)


def attend_forward(group, bounds, tokens, weight, bias, cosine, sine, docs):
    zsize, _, rows, width = tokens.shape
    length = zsize * rows
    cols = weight.shape[2]
    heads = cols // HEAD_DIM
    pair = 2 * HEAD_DIM
    whole = lambda shape: pl.BlockSpec(shape, lambda i, *_: (0,) * len(shape))
    of_group = lambda shape: pl.BlockSpec(shape, lambda i, *_: (group,) + (0,) * (len(shape) - 1))
    like = jax.ShapeDtypeStruct
    return pl.pallas_call(
        functools.partial(attend_kernel, group),
        grid_spec=pltpu.PrefetchScalarGridSpec(
            num_scalar_prefetch=2,
            grid=(1,),
            in_specs=[
                pl.BlockSpec((zsize, 1, rows, width), lambda i, *_: (0, group, 0, 0)),
                whole(weight.shape), whole(bias.shape),
                of_group((1, length, pair)), of_group((1, length, pair)), of_group((1, length, 1)),
            ],
            out_specs=[
                whole((1, length, cols)),
                whole((1, heads, length, pair)), whole((1, heads, length, pair)), whole((1, heads, length, pair)),
                whole((1, heads, length)),
            ],
            scratch_shapes=[
                pltpu.VMEM((heads, HEAD_DIM, length), bf16),
                pltpu.VMEM((heads, BLOCK), f32), pltpu.VMEM((heads, BLOCK), f32),
                pltpu.VMEM((heads, HEAD_DIM, BLOCK), f32),
            ],
        ),
        out_shape=[
            like((1, length, cols), bf16),
            like((1, heads, length, pair), bf16), like((1, heads, length, pair), bf16),
            like((1, heads, length, pair), bf16), like((1, heads, length), f32),
        ],
        compiler_params=pltpu.CompilerParams(vmem_limit_bytes=48 * 1024 * 1024),
        cost_estimate=pl.CostEstimate(
            flops=2 * length * width * 3 * cols + 4 * length * length * cols,
            bytes_accessed=2 * length * width + 6 * width * cols + 8 * length * cols,
            transcendentals=length * length * heads,
        ),
    )(*bounds, tokens, weight, bias, cosine, sine, docs)


def attend_back_kernel(group, lo_ref, hi_ref, q_ref, k_ref, v_ref, lse_ref, mixed_ref, do_ref, cos_ref, sin_ref,
                       grad_ref, sum_ref, dox_ref, kt_ref, delta_ref, dk_ref, dv_ref, dqt_ref):
    heads, length = q_ref.shape[1], q_ref.shape[2]
    pair = 2 * HEAD_DIM
    scale = HEAD_DIM ** (-0.5)
    blocks = length // BLOCK

    def prepare(i, carry):
        at = pl.ds(pl.multiple_of(i * BLOCK, BLOCK), BLOCK)
        low = lax.broadcasted_iota(jnp.int32, (BLOCK, pair), 1) < HEAD_DIM
        for j in range(heads // 2):
            upstream = do_ref[0, at, j * pair:(j + 1) * pair].astype(f32)
            product = (upstream * mixed_ref[0, at, j * pair:(j + 1) * pair].astype(f32)).T
            for h in range(2):
                head = 2 * j + h
                one = upstream if h == 0 else pltpu.roll(upstream, HEAD_DIM, 1)
                dox_ref[head, at, :] = jnp.where(low, one, 0.0).astype(bf16)
                delta_ref[head:head + 1, at] = jnp.sum(
                    product[h * HEAD_DIM:(h + 1) * HEAD_DIM], axis=0, keepdims=True
                )
                kt_ref[head, :, at] = k_ref[0, head, at, :].astype(f32).T[:HEAD_DIM].astype(bf16)
                dk_ref[head, at, :] = jnp.zeros((BLOCK, pair), f32)
                dv_ref[head, at, :] = jnp.zeros((BLOCK, pair), f32)
        return carry

    lax.fori_loop(0, blocks, prepare, 0)
    sum_ref[...] = jnp.zeros(sum_ref.shape, f32)

    def put(c, j, at, field):
        low = field.astype(bf16)
        grad_ref[c, 0, at, j * pair:(j + 1) * pair] = low
        cols = pl.ds(j * pair, pair)
        sum_ref[c:c + 1, cols] = sum_ref[c:c + 1, cols] + jnp.sum(low.astype(f32), axis=0, keepdims=True)

    def back(field, at):
        return field * cos_ref[0, at, :] - turn_halves(field, sin_ref[0, at, :])

    def query_block(i, carry):
        at = pl.ds(pl.multiple_of(i * BLOCK, BLOCK), BLOCK)
        dqt_ref[...] = jnp.zeros(dqt_ref.shape, f32)

        def key_block(j, carry):
            keys_at = pl.ds(pl.multiple_of(j * BLOCK, BLOCK), BLOCK)
            for h in range(heads):
                queries = q_ref[0, h, at, :]
                upstream = dox_ref[h, at, :]
                st = scores_of(k_ref[0, h, keys_at, :], queries)
                p = jnp.exp(st - lse_ref[0, h:h + 1, at])
                dp = scores_of(v_ref[0, h, keys_at, :], upstream)
                ds = (p * (dp - delta_ref[h:h + 1, at])).astype(bf16)
                dv_ref[h, keys_at, :] = dv_ref[h, keys_at, :] + jnp.dot(
                    p.astype(bf16), upstream, preferred_element_type=f32
                )
                dk_ref[h, keys_at, :] = dk_ref[h, keys_at, :] + jnp.dot(ds, queries, preferred_element_type=f32)
                dqt_ref[h] = dqt_ref[h] + jnp.dot(kt_ref[h, :, keys_at], ds, preferred_element_type=f32)
            return carry

        lax.fori_loop(lo_ref[group, i], hi_ref[group, i], key_block, 0)
        for j in range(heads // 2):
            both = jnp.concatenate([dqt_ref[2 * j], dqt_ref[2 * j + 1]], axis=0)
            put(0, j, at, back(both.T * scale, at))
        return carry

    lax.fori_loop(0, blocks, query_block, 0)

    def finish(i, carry):
        at = pl.ds(pl.multiple_of(i * BLOCK, BLOCK), BLOCK)
        low = lax.broadcasted_iota(jnp.int32, (BLOCK, pair), 1) < HEAD_DIM
        for j in range(heads // 2):
            field = jnp.where(low, dk_ref[2 * j, at, :], pltpu.roll(dk_ref[2 * j + 1, at, :], HEAD_DIM, 1))
            put(1, j, at, back(field, at))
            field = jnp.where(low, dv_ref[2 * j, at, :], pltpu.roll(dv_ref[2 * j + 1, at, :], HEAD_DIM, 1))
            put(2, j, at, field)
        return carry

    lax.fori_loop(0, blocks, finish, 0)


def attend_backward(group, bounds, kept, mixed, upstream, cosine, sine):
    queries, keys, values, lse = kept
    _, heads, length, pair = queries.shape
    cols = heads * HEAD_DIM
    whole = lambda shape: pl.BlockSpec(shape, lambda i, *_: (0,) * len(shape))
    of_group = lambda shape: pl.BlockSpec(shape, lambda i, *_: (group,) + (0,) * (len(shape) - 1))
    like = jax.ShapeDtypeStruct
    wide = (heads, length, pair)
    return pl.pallas_call(
        functools.partial(attend_back_kernel, group),
        grid_spec=pltpu.PrefetchScalarGridSpec(
            num_scalar_prefetch=2,
            grid=(1,),
            in_specs=[
                whole(queries.shape), whole(keys.shape), whole(values.shape), whole(lse.shape), whole(mixed.shape),
                of_group((1, length, cols)), of_group((1, length, pair)), of_group((1, length, pair)),
            ],
            out_specs=[whole((3, 1, length, cols)), whole((8, cols))],
            scratch_shapes=[
                pltpu.VMEM(wide, bf16), pltpu.VMEM((heads, HEAD_DIM, length), bf16), pltpu.VMEM((heads, length), f32),
                pltpu.VMEM(wide, f32), pltpu.VMEM(wide, f32), pltpu.VMEM((heads, HEAD_DIM, BLOCK), f32),
            ],
        ),
        out_shape=[like((3, 1, length, cols), bf16), like((8, cols), f32)],
        compiler_params=pltpu.CompilerParams(vmem_limit_bytes=48 * 1024 * 1024),
        cost_estimate=pl.CostEstimate(
            flops=10 * length * length * cols, bytes_accessed=24 * length * cols, transcendentals=length * length * heads
        ),
    )(*bounds, queries, keys, values, lse, mixed, upstream, cosine, sine)


MESH_ID = pl.DeviceIdType.MESH
HBM = pl.BlockSpec(memory_space=pl.ANY)


def other(axis):
    return {axis: 1 - lax.axis_index(axis)}


def greet(zsize):
    z = lax.axis_index("z")
    barrier = pltpu.get_barrier_semaphore()
    for axis in CELL:
        pl.semaphore_signal(barrier, inc=1, device_id=other(axis), device_id_type=MESH_ID)

    @pl.when(z > 0)
    def _():
        pl.semaphore_signal(barrier, inc=1, device_id={"z": z - 1}, device_id_type=MESH_ID)

    @pl.when(z < zsize - 1)
    def _():
        pl.semaphore_signal(barrier, inc=1, device_id={"z": z + 1}, device_id_type=MESH_ID)

    peers = len(CELL) + jnp.where(z > 0, 1, 0) + jnp.where(z < zsize - 1, 1, 0)
    pl.semaphore_wait(barrier, peers)


def remote(src, dst, send_sem, recv_sem, device):
    return pltpu.make_async_remote_copy(
        src_ref=src, dst_ref=dst, send_sem=send_sem, recv_sem=recv_sem, device_id=device, device_id_type=MESH_ID
    )


def swap_kernel(zsize, to_rows, *refs):
    sources, target = refs[:-4], refs[-4]
    held, local_sem, send, recv = refs[-3], refs[-2], refs[-1].at[0], refs[-1].at[1]
    groups = target.shape[0]
    rows, cols = (target.shape[1], target.shape[2] // zsize) if to_rows else (target.shape[1] // zsize, target.shape[2])
    z = lax.axis_index("z")

    def source(g, peer):
        if to_rows:
            return sources[g].at[0, pl.ds(pl.multiple_of(peer * rows, rows), rows), :]
        return sources[0].at[g, :, pl.ds(pl.multiple_of(peer * cols, cols), cols)]

    def place(g, peer):
        if to_rows:
            return target.at[g, :, pl.ds(pl.multiple_of(peer * cols, cols), cols)]
        return target.at[g, pl.ds(pl.multiple_of(peer * rows, rows), rows), :]

    def copy_to(g, step):
        peer = lax.rem(z + step, zsize)
        return remote(source(g, peer), place(g, z), send.at[step, g], recv.at[step, g], {"z": peer})

    def copy_from(g, step):
        peer = lax.rem(z + zsize - step, zsize)
        return remote(source(g, peer), place(g, peer), send.at[step, g], recv.at[step, g], {"z": peer})

    into = [pltpu.make_async_copy(source(g, z), held.at[g], local_sem.at[0, g]) for g in range(groups)]
    onward = [pltpu.make_async_copy(held.at[g], place(g, z), local_sem.at[1, g]) for g in range(groups)]
    for copy in into:
        copy.start()
    barrier = pltpu.get_barrier_semaphore()
    for step in range(1, zsize):
        peer = lax.rem(z + step, zsize)
        pl.semaphore_signal(barrier, inc=1, device_id={"z": peer}, device_id_type=MESH_ID)
    pl.semaphore_wait(barrier, zsize - 1)
    for g in range(groups):
        for step in range(1, zsize):
            copy_to(g, step).start()
    for g in range(groups):
        into[g].wait()
        onward[g].start()
    for g in range(groups):
        for step in range(1, zsize):
            copy_from(g, step).wait_recv()
        onward[g].wait()
    for g in range(groups):
        for step in range(1, zsize):
            copy_to(g, step).wait_send()


def swap(sources, zsize, to_rows):
    if to_rows:
        groups, rows, cols = len(sources), sources[0].shape[1] // zsize, sources[0].shape[2]
        shape = (groups, rows, zsize * cols)
    else:
        groups, rows, cols = sources[0].shape
        cols //= zsize
        shape = (groups, zsize * rows, cols)
    return pl.pallas_call(
        functools.partial(swap_kernel, zsize, to_rows),
        out_shape=jax.ShapeDtypeStruct(shape, bf16),
        in_specs=[HBM] * len(sources),
        out_specs=HBM,
        scratch_shapes=[
            pltpu.VMEM((groups, rows, cols), bf16),
            pltpu.SemaphoreType.DMA((2, groups)),
            pltpu.SemaphoreType.DMA((2, zsize, groups)),
        ],
        compiler_params=pltpu.CompilerParams(
            collective_id=2 if to_rows else 3, has_side_effects=True, vmem_limit_bytes=8 * 1024 * 1024
        ),
    )(*sources)


ORDERS = {"xy": ("x", "y"), "yx": ("y", "x")}


def gather_kernel(zsize, orders, *refs):
    n = len(orders)
    tok, bias, shards = refs[0], refs[1], refs[2:2 + n]
    tok_all, bias_all, wholes = refs[2 + n], refs[3 + n], refs[4 + n:4 + 2 * n]
    held = refs[4 + 2 * n:6 + 3 * n]
    local_sem, z_send, z_recv, p_send, p_recv = refs[6 + 3 * n:]
    z = lax.axis_index("z")
    c = lax.axis_index("core")
    place = [(lax.axis_index(o[0]), lax.axis_index(o[1])) for o in orders]

    sources = list(shards) + [tok, bias]
    targets = list(wholes) + [tok_all, bias_all]
    into = [pltpu.make_async_copy(sources[i], held[i], local_sem.at[0, i]) for i in range(n + 2)]
    local = [pltpu.make_async_copy(held[i], targets[i].at[z], local_sem.at[1, i]) for i in range(n + 2)]
    for copy in into:
        copy.start()
    greet(zsize)

    def line(item, src, step, side):
        to = z + 1 if side == 0 else z - 1
        if item < n:
            f, s = place[item]
            own = shards[item].at[c, f, s]
            dst = wholes[item].at[src, c, f, s]
        else:
            own = (tok, bias)[item - n]
            dst = (tok_all, bias_all)[item - n].at[src]
        return remote(
            own if step == 0 else dst, dst, z_send.at[side, item, step], z_recv.at[side, item, step], {"z": to}
        )

    def exchange(k, src, stage, slot):
        f, s = place[k]
        whole = wholes[k]
        ref = (whole.at[src, c, f, s], whole.at[src, c, f], whole.at[src, c])[stage]
        axis = (orders[k][1], orders[k][0], "core")[stage]
        return remote(ref, ref, p_send.at[slot, k, stage], p_recv.at[slot, k, stage], other(axis))

    def valid_from(side, step):
        return z - step - 1 >= 0 if side == 0 else z + step + 1 < zsize

    def source(side, step):
        return z - step - 1 if side == 0 else z + step + 1

    def has_next(side):
        return z < zsize - 1 if side == 0 else z > 0

    for side in range(2):

        @pl.when(has_next(side))
        def _():
            for item in range(n):
                line(item, z, 0, side).start()

    def stage_on(stage, step):
        for side in range(2):

            @pl.when(valid_from(side, step))
            def _():
                src = source(side, step)
                slot = side * (zsize - 1) + step
                for k in range(n):
                    exchange(k, src, stage - 1, slot).wait_recv()
                    if stage < 3:
                        exchange(k, src, stage, slot).start()

    def arrive(items, step):
        for side in range(2):

            @pl.when(valid_from(side, step))
            def _():
                src = source(side, step)
                for item in items:
                    line(item, src, step, side).wait_recv()
                    if step + 1 < zsize - 1:

                        @pl.when(has_next(side))
                        def _():
                            line(item, src, step + 1, side).start()

                    if item < n:
                        exchange(item, src, 0, side * (zsize - 1) + step).start()

    for copy, onward in zip(into, local):
        copy.wait()
        onward.start()
    for step in range(zsize - 1):
        arrive(range(n), step)
        if step == zsize - 2:
            for side in range(2):

                @pl.when(has_next(side))
                def _():
                    for item in range(n, n + 2):
                        line(item, z, 0, side).start()

        if step >= 1:
            stage_on(1, step - 1)
    for step in range(zsize - 1):
        if step == 0:
            stage_on(1, zsize - 2)
        stage_on(2, step)
        arrive(range(n, n + 2), step)
    for step in range(zsize - 1):
        stage_on(3, step)
    for copy in local:
        copy.wait()
    for side in range(2):

        @pl.when(has_next(side))
        def _():
            for item in range(n + 2):
                line(item, z, 0, side).wait_send()

        for step in range(zsize - 1):

            @pl.when(valid_from(side, step))
            def _():
                src = source(side, step)
                if step + 1 < zsize - 1:

                    @pl.when(has_next(side))
                    def _():
                        for item in range(n + 2):
                            line(item, src, step + 1, side).wait_send()

                for k in range(n):
                    for stage in range(3):
                        exchange(k, src, stage, side * (zsize - 1) + step).wait_send()


def gather_start(tokens, bias, weights, zsize):
    orders = [ORDERS[o] for o, _ in weights]
    shards = [w for _, w in weights]
    n = len(shards)
    stack = lambda a: jax.ShapeDtypeStruct((zsize,) + a.shape, a.dtype)
    return pl.pallas_call(
        functools.partial(gather_kernel, zsize, orders),
        out_shape=[stack(tokens), stack(bias)] + [stack(w) for w in shards],
        in_specs=[HBM] * (n + 2),
        out_specs=[HBM] * (n + 2),
        scratch_shapes=[pltpu.VMEM(a.shape, a.dtype) for a in shards + [tokens, bias]] + [
            pltpu.SemaphoreType.DMA((2, n + 2)),
            pltpu.SemaphoreType.DMA((2, n + 2, zsize - 1)),
            pltpu.SemaphoreType.DMA((2, n + 2, zsize - 1)),
            pltpu.SemaphoreType.DMA((2 * (zsize - 1), n, 3)),
            pltpu.SemaphoreType.DMA((2 * (zsize - 1), n, 3)),
        ],
        compiler_params=pltpu.CompilerParams(
            collective_id=0, has_side_effects=True, vmem_limit_bytes=32 * 1024 * 1024
        ),
    )(tokens, bias, *shards)


def add_rows(dst, src):
    rows = dst.shape[0]
    step = min(rows, 32)

    def body(i, carry):
        at = pl.ds(pl.multiple_of(i * step, step), step)
        dst[at, :] = dst[at, :] + src[at, :]
        return carry

    lax.fori_loop(0, rows // step, body, 0)


def reduce_kernel(zsize, orders, *refs):
    n = len(orders)
    m = n - 2
    parts, back, small = refs[:n], refs[n], refs[n + 1]
    outs, back_out, small_out = refs[n + 2:2 * n + 2], refs[2 * n + 2], refs[2 * n + 3]
    pos = 2 * n + 4
    mine, got_c, got_1, got_2 = (refs[pos + i * n:pos + (i + 1) * n] for i in range(4))
    pos += 4 * n
    got_z = refs[pos:pos + m + 1]
    pos += m + 1
    back_mine, small_mine, small_got, small_line, small_total, part_line, part_total = refs[pos:pos + 7]
    (local_sem, send, recv, z_send, z_recv, s_send, s_recv, t_send, t_recv, g_send, g_recv, end_sem) = refs[pos + 7:]
    z = lax.axis_index("z")
    c = lax.axis_index("core")
    place = [(lax.axis_index(o[0]), lax.axis_index(o[1])) for o in orders]
    turn = []
    for i in range(zsize // 2):
        turn += [i, zsize - 1 - i]
    few = parts[m].shape[0]
    groups = [[(m, b) for b in range(few)] + [(m + 1, 0)]] + [[(k, b) for k in range(m)] for b in turn]
    steps = [kb for group in groups for kb in group]

    def load(k, b):
        return pltpu.make_async_copy(parts[k].at[b, c], mine[k].at[b], local_sem.at[k, b])

    def load_back(b):
        return pltpu.make_async_copy(back.at[b], back_mine.at[b], local_sem.at[n, b])

    load_small = pltpu.make_async_copy(small, small_mine.at[0], local_sem.at[n + 1, 0])

    def half(k, b, stage):
        f, s = place[k]
        if stage == 0:
            src, dst, axis = parts[k].at[b, 1 - c], got_c[k].at[b], "core"
        elif stage == 1:
            src, dst, axis = mine[k].at[b, 1 - f], got_1[k].at[b], orders[k][0]
        else:
            src, dst, axis = mine[k].at[b, f, 1 - s], got_2[k].at[b], orders[k][1]
        return remote(src, dst, send.at[stage, k, b], recv.at[stage, k, b], other(axis))

    def own(k, b):
        if k == m:
            return back_mine.at[b]
        f, s = place[k]
        return mine[k].at[b, f, s]

    def hop(k, b, side):
        to = z + 1 if side == 0 else z - 1
        at = b if side == 0 else jnp.where(b == z - 1, zsize, b)
        return remote(own(k, b), got_z[k].at[at], z_send.at[k, b], z_recv.at[k, at], {"z": to})

    def take(k, b, side):
        at = b if side == 0 else jnp.where(b == z, zsize, b)
        ref = got_z[k].at[at]
        sender = z - 1 if side == 0 else z + 1
        remote(own(k, b), ref, z_send.at[k, b], z_recv.at[k, at], {"z": sender}).wait_recv()
        add_rows(own(k, b), ref)

    def line_step(ks, b, hops):
        for side in range(2):
            here = z == hops if side == 0 else z == zsize - 1 - hops
            goes = jnp.logical_and(here, z < b) if side == 0 else jnp.logical_and(here, z > b)
            if hops:
                ends = jnp.logical_and(here, z == b)

                @pl.when(jnp.logical_or(goes, ends))
                def _():
                    for k in ks:
                        take(k, b, side)

            @pl.when(goes)
            def _():
                for k in ks:
                    hop(k, b, side).start()

    def small_swap(stage):
        return remote(
            small_mine.at[stage], small_got.at[stage], s_send.at[stage], s_recv.at[stage], other(CELL[stage])
        )

    def small_step(stage):
        small_swap(stage).wait_recv()
        small_mine[stage + 1] = small_mine[stage] + small_got[stage]
        if stage < 2:
            small_swap(stage + 1).start()

    last = len(CELL)
    last_part = own(m + 1, 0)

    def total_copy(item, way):
        line, total = ((small_line, small_total), (part_line, part_total))[item]
        src = (small_mine.at[last], last_part)[item] if way == 0 else total
        dst = line if way == 0 else total
        to = z + 1 if way == 0 else z - 1
        return remote(src, dst, t_send.at[item, way], t_recv.at[item, way], {"z": to})

    def total_step(tick):
        if 0 <= tick < zsize:

            @pl.when(z == tick)
            def _():
                if tick > 0:
                    for item in range(2):
                        total_copy(item, 0).wait_recv()
                    small_mine[last] = small_mine[last] + small_line[...]
                    add_rows(last_part, part_line)
                if tick < zsize - 1:
                    for item in range(2):
                        total_copy(item, 0).start()
                else:
                    small_total[...] = small_mine[last]
                    part_total[...] = last_part[...]

        back_tick = tick - (zsize - 1)
        if 0 <= back_tick < zsize:

            @pl.when(z == zsize - 1 - back_tick)
            def _():
                if back_tick > 0:
                    for item in range(2):
                        total_copy(item, 1).wait_recv()
                if back_tick < zsize - 1:
                    for item in range(2):
                        total_copy(item, 1).start()

    for b in turn:
        load_back(b).start()
    load_small.start()
    for k, b in steps:
        load(k, b).start()
    greet(zsize)
    for k, b in groups[0]:
        half(k, b, 0).start()
    for b in turn:
        load_back(b).wait()
    for b in turn:
        line_step([m], b, 0)
    load_small.wait()
    small_swap(0).start()
    for k, b in steps[len(groups[0]):]:
        half(k, b, 0).start()

    def stage_1(k, b):
        f, s = place[k]
        load(k, b).wait()
        half(k, b, 0).wait_recv()
        for i in range(2):
            add_rows(mine[k].at[b, 1 - f, i], got_c[k].at[b, 1 - f, i])
        half(k, b, 1).start()
        for i in range(2):
            add_rows(mine[k].at[b, f, i], got_c[k].at[b, f, i])

    def stage_2(k, b):
        f, s = place[k]
        half(k, b, 1).wait_recv()
        add_rows(mine[k].at[b, f, 1 - s], got_1[k].at[b, 1 - s])
        half(k, b, 2).start()
        add_rows(mine[k].at[b, f, s], got_1[k].at[b, s])

    def stage_3(k, b):
        f, s = place[k]
        half(k, b, 2).wait_recv()
        add_rows(mine[k].at[b, f, s], got_2[k].at[b])

    def result(k, b):
        return part_total if k == m + 1 else own(k, b) if k != m else mine[m].at[b, place[m][0], place[m][1]]

    def out_of(k, b):
        return outs[k].at[b] if k == m else outs[k]

    def put(k, b, slot):
        f, s = place[k]
        return pltpu.make_async_copy(result(k, b), out_of(k, b).at[c, f, s], end_sem.at[slot])

    def spread(k, b, stage, slot):
        f, s = place[k]
        out = out_of(k, b)
        dst = (out.at[c, f, s], out.at[c, f], out.at[c])[stage]
        src = result(k, b) if stage == 0 else dst
        axis = (orders[k][1], orders[k][0], "core")[stage]
        return remote(src, dst, g_send.at[slot, stage], g_recv.at[slot, stage], other(axis))

    first = [(m, b, b) for b in range(few)]
    rest = [(k, z, few + k) for k in range(m)] + [(m + 1, 0, few + m)]

    def spread_start(items):
        for k, b, slot in items:
            spread(k, b, 0, slot).start()
            put(k, b, slot).start()

    def spread_on(items, stage):
        for k, b, slot in items:
            if stage == 1:
                put(k, b, slot).wait()
            spread(k, b, stage - 1, slot).wait_recv()
            if stage < 3:
                spread(k, b, stage, slot).start()

    ks = list(range(m))
    small_tick = 3
    back_ticks = [2 + i + (1 if i > 1 else 0) for i in range(zsize)]
    for tick in range(len(groups) + zsize + 2):
        if tick < len(groups):
            for k, b in groups[tick]:
                stage_1(k, b)
        if 1 <= tick <= len(groups):
            for k, b in groups[tick - 1]:
                stage_2(k, b)
        if 2 <= tick <= len(groups) + 1:
            for k, b in groups[tick - 2]:
                stage_3(k, b)
        if 1 <= tick <= 3:
            small_step(tick - 1)
        for i in range(1, zsize):
            if tick == back_ticks[i - 1]:
                for b in turn:
                    line_step([m], b, i)
        for j, b in enumerate(turn):
            hops = tick - 3 - j
            if 0 <= hops < zsize:
                line_step(ks, b, hops)
        total_step(tick - small_tick)
        if tick == 4:
            spread_start(first)
        if 5 <= tick <= 7:
            spread_on(first, tick - 4)
    for tick in range(len(groups) + zsize + 2 - small_tick, 2 * zsize):
        total_step(tick)
    finish_back = pltpu.make_async_copy(back_mine.at[z], back_out, local_sem.at[n, 0])
    finish_back.start()
    finish_small = pltpu.make_async_copy(small_total, small_out, local_sem.at[n + 1, 0])
    finish_small.start()
    spread_start(rest)
    for stage in (1, 2, 3):
        spread_on(rest, stage)
    finish_back.wait()
    finish_small.wait()
    for b in range(zsize):

        @pl.when(z != b)
        def _():
            for k in range(m + 1):
                hop(k, b, 0).wait_send()

    for way in range(2):

        @pl.when(z < zsize - 1 if way == 0 else z > 0)
        def _():
            for item in range(2):
                total_copy(item, way).wait_send()

    for k, b in steps:
        for stage in range(3):
            half(k, b, stage).wait_send()
    for stage in range(3):
        small_swap(stage).wait_send()
    for k, b, slot in first + rest:
        for stage in range(3):
            spread(k, b, stage, slot).wait_send()


def reduce_end(parts, cell_part, all_part, back, small, zsize):
    orders = [ORDERS[o] for o, _ in parts + [cell_part, all_part]]
    arrays = [a for _, a in parts + [cell_part, all_part]]
    n = len(arrays)
    shapes = [a.shape for a in arrays]
    like = jax.ShapeDtypeStruct
    outs = [like(s if i == n - 2 else s[1:], bf16) for i, s in enumerate(shapes)]
    outs += [like(back.shape[1:], bf16), like(small.shape, f32)]
    scratch = [pltpu.VMEM((s[0],) + s[2:], bf16) for s in shapes]
    scratch += [pltpu.VMEM((s[0],) + s[2:], bf16) for s in shapes]
    scratch += [pltpu.VMEM((s[0],) + s[3:], bf16) for s in shapes]
    scratch += [pltpu.VMEM((s[0],) + s[4:], bf16) for s in shapes]
    scratch += [pltpu.VMEM((zsize + 1,) + s[4:], bf16) for s in shapes[:-2]]
    scratch += [pltpu.VMEM((zsize + 1,) + back.shape[1:], bf16), pltpu.VMEM(back.shape, bf16)]
    scratch += [pltpu.VMEM((4,) + small.shape, f32), pltpu.VMEM((3,) + small.shape, f32)]
    scratch += [pltpu.VMEM(small.shape, f32)] * 2 + [pltpu.VMEM(shapes[-1][4:], bf16)] * 2
    dma = pltpu.SemaphoreType.DMA
    most = max(zsize, shapes[-2][0])
    ends = n - 1 + shapes[-2][0]
    scratch += [
        dma((n + 2, most)), dma((3, n, most)), dma((3, n, most)), dma((n - 1, zsize)), dma((n - 1, zsize + 1)),
        dma((3,)), dma((3,)), dma((2, 2)), dma((2, 2)), dma((ends, 3)), dma((ends, 3)), dma((ends,)),
    ]
    return pl.pallas_call(
        functools.partial(reduce_kernel, zsize, orders),
        out_shape=outs,
        in_specs=[HBM] * (n + 2),
        out_specs=[HBM] * (n + 2),
        scratch_shapes=scratch,
        compiler_params=pltpu.CompilerParams(
            collective_id=1, has_side_effects=True, vmem_limit_bytes=60 * 1024 * 1024
        ),
    )(*arrays, back, small)


def per_device(blocks, tokens, segments, qkv_weight, qkv_bias, out_weight, out_bias, gain_one, shift_one,
               up_weight, up_bias, down_weight, down_bias, gain_two, shift_two, proj_weight, out_grad, embed_grad):
    groups, local_rows, model_width = tokens.shape
    length = segments.shape[1]
    zsize = length // local_rows
    head_cols = qkv_weight.shape[2]
    units_here = up_weight.shape[1]
    rows = groups * local_rows
    zi = lax.axis_index("z")
    cosine, sine = rotary_tables(doc_positions(segments), HEAD_DIM)
    half = HEAD_DIM // 2
    signs = jnp.where(jnp.arange(2 * HEAD_DIM) % HEAD_DIM < half, -1.0, 1.0)
    cosine = jnp.concatenate([cosine, cosine], axis=-1)
    sine = jnp.concatenate([sine, sine], axis=-1) * signs
    firsts = segments[:, ::BLOCK]
    lasts = segments[:, BLOCK - 1::BLOCK]
    bounds = (
        jnp.sum(segments[:, None, :] < firsts[:, :, None], axis=2, dtype=jnp.int32) // BLOCK,
        (jnp.sum(segments[:, None, :] <= lasts[:, :, None], axis=2, dtype=jnp.int32) + BLOCK - 1) // BLOCK,
    )
    docs = segments[:, :, None]

    def cut(array, rows_at):
        shape = array.shape
        return array.reshape(shape[:rows_at] + (2, 2, 2, shape[rows_at] // 8) + shape[rows_at + 1:])

    token_rows = tokens.reshape(rows, model_width)
    token_blocks, bias_blocks, out_all, up_all, down_all = gather_start(
        token_rows,
        up_bias.reshape(8, units_here // 8),
        [("xy", cut(out_weight, 0)), ("xy", cut(up_weight, 0)), ("yx", cut(down_weight, 0))],
        zsize,
    )
    token_blocks = token_blocks.reshape(zsize, groups, local_rows, model_width)
    out_all = out_all.reshape(model_width, model_width)
    up_all = up_all.reshape(zsize, model_width, units_here)
    down_all = down_all.reshape(zsize, units_here, model_width)
    full_up_bias = bias_blocks.reshape(zsize, units_here)

    heads = [
        attend_forward(g, bounds, token_blocks, qkv_weight, qkv_bias, cosine, sine, docs) for g in range(groups)
    ]
    mixed = swap([h[0] for h in heads], zsize, True).reshape(rows, model_width)

    first_sum = tokens.reshape(rows, model_width).astype(f32) + (
        jnp.dot(mixed, out_all, preferred_element_type=f32) + out_bias
    )
    normed, scaled_one, inv_one = norm_forward(first_sum, gain_one, shift_one)
    normed_low = normed.astype(bf16)
    hidden = jnp.einsum("nd,zdf->znf", normed_low, up_all, preferred_element_type=f32)
    hidden = hidden + full_up_bias[:, None, :]
    active, gelu_pull = jax.vjp(lambda field: jax.nn.gelu(field, approximate=False), hidden)
    active = active.astype(bf16)
    ffn = jnp.einsum("znf,zfd->nd", active, down_all, preferred_element_type=f32)
    second_sum = normed + (ffn + down_bias)
    result, scaled_two, inv_two = norm_forward(second_sum, gain_two, shift_two)
    result_low = result.astype(bf16)
    embedded = jnp.dot(result_low, proj_weight, preferred_element_type=f32).astype(bf16)
    embed_rows = embed_grad.reshape(rows, -1)
    grad_result = out_grad.reshape(rows, model_width).astype(f32) + jnp.einsum(
        "np,dp->nd", embed_rows, proj_weight, preferred_element_type=f32
    )
    proj_grad = jnp.einsum("nd,np->dp", result_low, embed_rows, preferred_element_type=f32)
    grad_second, gain_two_grad, shift_two_grad = norm_backward(grad_result, scaled_two, inv_two, gain_two)
    second_low = grad_second.astype(bf16)
    down_bias_grad = jnp.sum(second_low.astype(f32), axis=0)
    down_grad = jnp.einsum("znf,nd->zfd", active, second_low, preferred_element_type=f32).astype(bf16)
    grad_active = jnp.einsum("nd,zfd->znf", second_low, down_all, preferred_element_type=f32)
    grad_hidden = gelu_pull(grad_active)[0].astype(bf16)
    up_bias_grad = jnp.sum(grad_hidden.astype(f32), axis=1)
    up_grad = jnp.einsum("nd,znf->zdf", normed_low, grad_hidden, preferred_element_type=f32).astype(bf16)
    grad_normed = grad_second + jnp.einsum("znf,zdf->nd", grad_hidden, up_all, preferred_element_type=f32)
    grad_first, gain_one_grad, shift_one_grad = norm_backward(grad_normed, scaled_one, inv_one, gain_one)
    first_low = grad_first.astype(bf16)
    out_bias_grad = jnp.sum(first_low.astype(f32), axis=0)
    out_grad_w = jnp.einsum("nh,nd->hd", mixed, first_low, preferred_element_type=f32).astype(bf16)
    grad_mixed = jnp.einsum("nd,hd->nh", first_low, out_all, preferred_element_type=f32).astype(bf16)
    grad_mixed = grad_mixed.reshape(groups, local_rows, model_width)
    upstream = swap([grad_mixed], zsize, False)
    back = [
        attend_backward(g, bounds, heads[g][1:], heads[g][0], upstream, cosine, sine) for g in range(groups)
    ]
    grad_qkv = jnp.concatenate([b[0] for b in back], axis=1)
    qkv_bias_grad = sum(b[1] for b in back)[:3]
    by_z = grad_qkv.reshape(3, groups, zsize, local_rows, head_cols)
    qkv_weight_grad = jnp.einsum("zgld,cgzle->cde", token_blocks, by_z, preferred_element_type=f32)
    input_back = jnp.einsum("cgzle,cde->zgld", by_z, qkv_weight, preferred_element_type=f32).astype(bf16)
    small = jnp.concatenate(
        [
            out_bias_grad, gain_one_grad, shift_one_grad, down_bias_grad, gain_two_grad, shift_two_grad,
            up_bias_grad.reshape(-1),
            lax.dynamic_update_slice(
                jnp.zeros((zsize, 3 * head_cols), f32), qkv_bias_grad.reshape(1, -1), (zi, 0)
            ).reshape(-1),
        ]
    )
    proj_cols = proj_grad.shape[1]
    proj_grad = jnp.pad(proj_grad.astype(bf16), ((0, 0), (0, -proj_cols % 128)))
    out_grad_w, up_grad, down_grad, qkv_weight_grad, proj_grad, back, small = reduce_end(
        [
            ("xy", cut(out_grad_w.reshape(zsize, head_cols, model_width), 1)),
            ("xy", cut(up_grad, 1)),
            ("yx", cut(down_grad, 1)),
        ],
        ("yx", cut(qkv_weight_grad.astype(bf16), 1)),
        ("xy", cut(proj_grad[None], 1)),
        input_back.reshape(zsize, rows, model_width),
        small.reshape(8, -1),
        zsize,
    )
    tokens_grad = grad_first.reshape(groups, local_rows, model_width) + back.astype(f32).reshape(
        groups, local_rows, model_width
    )
    qkv_weight_grad = qkv_weight_grad.reshape(qkv_weight.shape)
    proj_grad = proj_grad.reshape(model_width, -1)[:, :proj_cols].astype(f32)
    out_grad_w = out_grad_w.reshape(out_weight.shape)
    up_grad = up_grad.reshape(up_weight.shape)
    down_grad = down_grad.reshape(down_weight.shape)
    if blocks > 1:
        down_grad, up_grad, out_grad_w, qkv_weight_grad = lax.psum(
            (down_grad, up_grad, out_grad_w, qkv_weight_grad), ("xb", "yb")
        )
        small, proj_grad = lax.psum((small, proj_grad), ("xb", "yb"))
    small = small.reshape(-1)
    base = 6 * model_width
    vec = [small[i * model_width:(i + 1) * model_width] for i in range(6)]
    up_bias_grad = lax.dynamic_slice(small, (base + zi * units_here,), (units_here,))
    qkv_bias_grad = lax.dynamic_slice(
        small, (base + zsize * units_here + zi * 3 * head_cols,), (3 * head_cols,)
    ).reshape(3, head_cols)
    shape3 = (groups, local_rows, model_width)
    return (
        result_low.reshape(shape3),
        embedded.reshape(groups, local_rows, -1),
        tokens_grad,
        qkv_weight_grad.astype(f32),
        qkv_bias_grad,
        out_grad_w.astype(f32),
        vec[0], vec[1], vec[2],
        up_grad.astype(f32),
        up_bias_grad,
        down_grad.astype(f32),
        vec[3], vec[4], vec[5],
        proj_grad,
    )


def solution(mesh):
    dp_size, zsize = mesh.shape["dp"], mesh.shape["tensor"]
    side = math.isqrt(dp_size // 2) // 2
    cut = Mesh(mesh.devices.reshape(side, 2, side, 2, 2, zsize), DP + ("z",))
    rows3 = P(DP, "z", None)
    in_specs = (
        rows3, P(DP, None), P(None, None, "z"), P(None, "z"), P("z", None), P(), P(), P(),
        P(None, "z"), P("z"), P("z", None), P(), P(), P(), P(), rows3, rows3,
    )
    out_specs = (
        rows3, rows3, rows3, P(None, None, "z"), P(None, "z"), P("z", None), P(), P(), P(),
        P(None, "z"), P("z"), P("z", None), P(), P(), P(), P(),
    )

    def run(*args):
        return per_device(side * side, *args)

    return jax.shard_map(run, mesh=cut, in_specs=in_specs, out_specs=out_specs, check_vma=False)
```

```python
import functools
import math

import jax
import jax.numpy as jnp
from jax import lax
from jax.experimental import pallas as pl
from jax.experimental.pallas import tpu as pltpu
from jax.sharding import Mesh
from jax.sharding import PartitionSpec as P

HEAD_DIM = 64
eps = 1e-05
DP = ("xb", "x", "yb", "y", "core")
CELL = ("x", "y", "core")
ALL = DP + ("z",)
f32 = jnp.float32
bf16 = jnp.bfloat16


def doc_positions(segment_rows):
    length = segment_rows.shape[-1]
    row_index = jnp.broadcast_to(jnp.arange(length, dtype=jnp.int32), segment_rows.shape)
    change = jnp.concatenate(
        [
            jnp.ones(segment_rows.shape[:-1] + (1,), jnp.bool_),
            segment_rows[..., 1:] != segment_rows[..., :-1],
        ],
        axis=-1,
    )
    doc_start = lax.cummax(
        jnp.where(change, row_index, jnp.zeros_like(row_index)), axis=segment_rows.ndim - 1
    )
    return row_index - doc_start


def rotary_tables(positions, head_dim):
    half_dim = head_dim // 2
    exponent = jnp.arange(half_dim, dtype=f32) * (2.0 / head_dim)
    frequency = jnp.exp(-exponent * math.log(10000.0))
    angles = positions.astype(f32)[..., None] * frequency
    angles = jnp.concatenate([angles, angles], axis=-1)
    return (jnp.cos(angles), jnp.sin(angles))


def norm_forward(field, gain, shift):
    row_mean = jnp.mean(field, axis=-1, keepdims=True)
    centred = field - row_mean
    variance = jnp.mean(centred * centred, axis=-1, keepdims=True)
    inv_std = lax.rsqrt(variance + eps)
    scaled = centred * inv_std
    return (scaled * gain + shift, scaled, inv_std)


def norm_backward(upstream, scaled, inv_std, gain):
    grad_scaled = upstream * gain
    grad_input = inv_std * (
        grad_scaled
        - jnp.mean(grad_scaled, axis=-1, keepdims=True)
        - scaled * jnp.mean(grad_scaled * scaled, axis=-1, keepdims=True)
    )
    return (grad_input, jnp.sum(upstream * scaled, axis=0), jnp.sum(upstream, axis=0))


BLOCK = 256


def turn_halves(field, sign_sine):
    lane = lax.broadcasted_iota(jnp.int32, field.shape, 1)
    half = HEAD_DIM // 2
    width = field.shape[1]
    swapped = jnp.where(lane % HEAD_DIM < half, pltpu.roll(field, width - half, 1), pltpu.roll(field, half, 1))
    return swapped * sign_sine


def scores_of(keys, queries):
    return lax.dot_general(keys, queries, (((1,), (1,)), ((), ())), preferred_element_type=f32)


def attend_kernel(lo_ref, hi_ref, tok_ref, w_ref, b_ref, cos_ref, sin_ref, seg_ref, mixed_ref, q_ref, k_ref, v_ref,
                  lse_ref, vt_ref, m_ref, l_ref, acc_ref):
    group = pl.program_id(0)
    zsize, _, rows, _ = tok_ref.shape
    length = zsize * rows
    heads = q_ref.shape[1]
    pair = 2 * HEAD_DIM
    scale = HEAD_DIM ** (-0.5)

    def project(i, carry):
        at = pl.ds(pl.multiple_of(i * rows, rows), rows)
        x = tok_ref[i, 0]
        lane = lax.broadcasted_iota(jnp.int32, (rows, pair), 1)
        doc = seg_ref[0, at, :]
        same = lane - HEAD_DIM == doc
        low = lane < HEAD_DIM
        feature = lane < HEAD_DIM + 4
        extra_q = jnp.where(same, 1.0, 0.0)
        extra_k = jnp.where(jnp.logical_and(feature, jnp.logical_not(same)), -1e9, 0.0)
        cosine = cos_ref[0, at, :]
        sine = sin_ref[0, at, :]
        for c in range(3):
            field = jnp.dot(x, w_ref[c], preferred_element_type=f32) + b_ref[c:c + 1, :]
            for j in range(heads // 2):
                part = field[:, j * pair:(j + 1) * pair]
                if c < 2:
                    part = part * cosine + turn_halves(part, sine)
                if c == 0:
                    part = part * scale
                for h in range(2):
                    one = part if h == 0 else pltpu.roll(part, HEAD_DIM, 1)
                    head = 2 * j + h
                    if c == 0:
                        q_ref[0, head, at, :] = jnp.where(low, one, extra_q).astype(bf16)
                    elif c == 1:
                        k_ref[0, head, at, :] = jnp.where(low, one, extra_k).astype(bf16)
                    else:
                        one = jnp.where(low, one, 0.0)
                        v_ref[0, head, at, :] = one.astype(bf16)
                        vt_ref[head, :, at] = one.T[:HEAD_DIM].astype(bf16)
        return carry

    lax.fori_loop(0, zsize, project, 0)

    def query_block(i, carry):
        at = pl.ds(pl.multiple_of(i * BLOCK, BLOCK), BLOCK)
        m_ref[...] = jnp.full(m_ref.shape, -1e30, f32)
        l_ref[...] = jnp.zeros(l_ref.shape, f32)
        acc_ref[...] = jnp.zeros(acc_ref.shape, f32)

        def key_block(j, carry):
            keys_at = pl.ds(pl.multiple_of(j * BLOCK, BLOCK), BLOCK)
            for h in range(heads):
                st = scores_of(k_ref[0, h, keys_at, :], q_ref[0, h, at, :])
                peak = m_ref[h:h + 1, :]
                new = jnp.maximum(peak, jnp.max(st, axis=0, keepdims=True))
                p = jnp.exp(st - new)
                old = jnp.exp(peak - new)
                m_ref[h:h + 1, :] = new
                l_ref[h:h + 1, :] = l_ref[h:h + 1, :] * old + jnp.sum(p, axis=0, keepdims=True)
                acc_ref[h] = acc_ref[h] * old + jnp.dot(
                    vt_ref[h, :, keys_at], p.astype(bf16), preferred_element_type=f32
                )
            return carry

        lax.fori_loop(lo_ref[group, i], hi_ref[group, i], key_block, 0)
        out = [acc_ref[h] / l_ref[h:h + 1, :] for h in range(heads)]
        for j in range(heads // 2):
            both = jnp.concatenate([out[2 * j], out[2 * j + 1]], axis=0)
            mixed_ref[0, at, j * pair:(j + 1) * pair] = both.T.astype(bf16)
        lse_ref[0, :, at] = m_ref[...] + jnp.log(l_ref[...])
        return carry

    lax.fori_loop(0, length // BLOCK, query_block, 0)


def attend_forward(bounds, tokens, weight, bias, cosine, sine, docs):
    zsize, groups, rows, width = tokens.shape
    length = zsize * rows
    cols = weight.shape[2]
    heads = cols // HEAD_DIM
    pair = 2 * HEAD_DIM
    whole = lambda shape: pl.BlockSpec(shape, lambda i, *_: (0,) * len(shape))
    of_group = lambda shape: pl.BlockSpec(shape, lambda i, *_: (i,) + (0,) * (len(shape) - 1))
    like = jax.ShapeDtypeStruct
    return pl.pallas_call(
        attend_kernel,
        grid_spec=pltpu.PrefetchScalarGridSpec(
            num_scalar_prefetch=2,
            grid=(groups,),
            in_specs=[
                pl.BlockSpec((zsize, 1, rows, width), lambda i, *_: (0, i, 0, 0)),
                whole(weight.shape), whole(bias.shape),
                of_group((1, length, pair)), of_group((1, length, pair)), of_group((1, length, 1)),
            ],
            out_specs=[
                of_group((1, length, cols)),
                of_group((1, heads, length, pair)), of_group((1, heads, length, pair)), of_group((1, heads, length, pair)),
                of_group((1, heads, length)),
            ],
            scratch_shapes=[
                pltpu.VMEM((heads, HEAD_DIM, length), bf16),
                pltpu.VMEM((heads, BLOCK), f32), pltpu.VMEM((heads, BLOCK), f32),
                pltpu.VMEM((heads, HEAD_DIM, BLOCK), f32),
            ],
        ),
        out_shape=[
            like((groups, length, cols), bf16),
            like((groups, heads, length, pair), bf16), like((groups, heads, length, pair), bf16),
            like((groups, heads, length, pair), bf16), like((groups, heads, length), f32),
        ],
        compiler_params=pltpu.CompilerParams(vmem_limit_bytes=48 * 1024 * 1024),
        cost_estimate=pl.CostEstimate(
            flops=groups * (2 * length * width * 3 * cols + 4 * length * length * cols),
            bytes_accessed=2 * length * width + 6 * width * cols + 8 * length * cols,
            transcendentals=length * length * heads,
        ),
    )(*bounds, tokens, weight, bias, cosine, sine, docs)


def attend_back_kernel(lo_ref, hi_ref, q_ref, k_ref, v_ref, lse_ref, mixed_ref, do_ref, cos_ref, sin_ref,
                       grad_ref, sum_ref, dox_ref, kt_ref, delta_ref, dk_ref, dv_ref, dqt_ref):
    group = pl.program_id(0)
    heads, length = q_ref.shape[1], q_ref.shape[2]
    pair = 2 * HEAD_DIM
    scale = HEAD_DIM ** (-0.5)
    blocks = length // BLOCK

    def prepare(i, carry):
        at = pl.ds(pl.multiple_of(i * BLOCK, BLOCK), BLOCK)
        low = lax.broadcasted_iota(jnp.int32, (BLOCK, pair), 1) < HEAD_DIM
        for j in range(heads // 2):
            upstream = do_ref[0, at, j * pair:(j + 1) * pair].astype(f32)
            product = (upstream * mixed_ref[0, at, j * pair:(j + 1) * pair].astype(f32)).T
            for h in range(2):
                head = 2 * j + h
                one = upstream if h == 0 else pltpu.roll(upstream, HEAD_DIM, 1)
                dox_ref[head, at, :] = jnp.where(low, one, 0.0).astype(bf16)
                delta_ref[head:head + 1, at] = jnp.sum(
                    product[h * HEAD_DIM:(h + 1) * HEAD_DIM], axis=0, keepdims=True
                )
                kt_ref[head, :, at] = k_ref[0, head, at, :].astype(f32).T[:HEAD_DIM].astype(bf16)
                dk_ref[head, at, :] = jnp.zeros((BLOCK, pair), f32)
                dv_ref[head, at, :] = jnp.zeros((BLOCK, pair), f32)
        return carry

    lax.fori_loop(0, blocks, prepare, 0)
    @pl.when(group == 0)
    def _():
        sum_ref[...] = jnp.zeros(sum_ref.shape, f32)

    def put(c, j, at, field):
        low = field.astype(bf16)
        grad_ref[c, 0, at, j * pair:(j + 1) * pair] = low
        cols = pl.ds(j * pair, pair)
        sum_ref[c:c + 1, cols] = sum_ref[c:c + 1, cols] + jnp.sum(low.astype(f32), axis=0, keepdims=True)

    def back(field, at):
        return field * cos_ref[0, at, :] - turn_halves(field, sin_ref[0, at, :])

    def query_block(i, carry):
        at = pl.ds(pl.multiple_of(i * BLOCK, BLOCK), BLOCK)
        dqt_ref[...] = jnp.zeros(dqt_ref.shape, f32)

        def key_block(j, carry):
            keys_at = pl.ds(pl.multiple_of(j * BLOCK, BLOCK), BLOCK)
            for h in range(heads):
                queries = q_ref[0, h, at, :]
                upstream = dox_ref[h, at, :]
                st = scores_of(k_ref[0, h, keys_at, :], queries)
                p = jnp.exp(st - lse_ref[0, h:h + 1, at])
                dp = scores_of(v_ref[0, h, keys_at, :], upstream)
                ds = (p * (dp - delta_ref[h:h + 1, at])).astype(bf16)
                dv_ref[h, keys_at, :] = dv_ref[h, keys_at, :] + jnp.dot(
                    p.astype(bf16), upstream, preferred_element_type=f32
                )
                dk_ref[h, keys_at, :] = dk_ref[h, keys_at, :] + jnp.dot(ds, queries, preferred_element_type=f32)
                dqt_ref[h] = dqt_ref[h] + jnp.dot(kt_ref[h, :, keys_at], ds, preferred_element_type=f32)
            return carry

        lax.fori_loop(lo_ref[group, i], hi_ref[group, i], key_block, 0)
        for j in range(heads // 2):
            both = jnp.concatenate([dqt_ref[2 * j], dqt_ref[2 * j + 1]], axis=0)
            put(0, j, at, back(both.T * scale, at))
        return carry

    lax.fori_loop(0, blocks, query_block, 0)

    def finish(i, carry):
        at = pl.ds(pl.multiple_of(i * BLOCK, BLOCK), BLOCK)
        low = lax.broadcasted_iota(jnp.int32, (BLOCK, pair), 1) < HEAD_DIM
        for j in range(heads // 2):
            field = jnp.where(low, dk_ref[2 * j, at, :], pltpu.roll(dk_ref[2 * j + 1, at, :], HEAD_DIM, 1))
            put(1, j, at, back(field, at))
            field = jnp.where(low, dv_ref[2 * j, at, :], pltpu.roll(dv_ref[2 * j + 1, at, :], HEAD_DIM, 1))
            put(2, j, at, field)
        return carry

    lax.fori_loop(0, blocks, finish, 0)


def attend_backward(bounds, kept, mixed, upstream, cosine, sine):
    queries, keys, values, lse = kept
    groups, heads, length, pair = queries.shape
    cols = heads * HEAD_DIM
    whole = lambda shape: pl.BlockSpec(shape, lambda i, *_: (0,) * len(shape))
    of_group = lambda shape: pl.BlockSpec(shape, lambda i, *_: (i,) + (0,) * (len(shape) - 1))
    like = jax.ShapeDtypeStruct
    wide = (heads, length, pair)
    return pl.pallas_call(
        attend_back_kernel,
        grid_spec=pltpu.PrefetchScalarGridSpec(
            num_scalar_prefetch=2,
            grid=(groups,),
            in_specs=[of_group((1,) + wide)] * 3 + [
                of_group((1, heads, length)), of_group((1, length, cols)),
                of_group((1, length, cols)), of_group((1, length, pair)), of_group((1, length, pair)),
            ],
            out_specs=[
                pl.BlockSpec((3, 1, length, cols), lambda i, *_: (0, i, 0, 0)), whole((8, cols)),
            ],
            scratch_shapes=[
                pltpu.VMEM(wide, bf16), pltpu.VMEM((heads, HEAD_DIM, length), bf16), pltpu.VMEM((heads, length), f32),
                pltpu.VMEM(wide, f32), pltpu.VMEM(wide, f32), pltpu.VMEM((heads, HEAD_DIM, BLOCK), f32),
            ],
        ),
        out_shape=[like((3, groups, length, cols), bf16), like((8, cols), f32)],
        compiler_params=pltpu.CompilerParams(vmem_limit_bytes=48 * 1024 * 1024),
        cost_estimate=pl.CostEstimate(
            flops=groups * 10 * length * length * cols, bytes_accessed=24 * length * cols, transcendentals=length * length * heads
        ),
    )(*bounds, queries, keys, values, lse, mixed, upstream, cosine, sine)


MESH_ID = pl.DeviceIdType.MESH
HBM = pl.BlockSpec(memory_space=pl.ANY)


def other(axis):
    return {axis: 1 - lax.axis_index(axis)}


def greet(zsize):
    z = lax.axis_index("z")
    barrier = pltpu.get_barrier_semaphore()
    for axis in CELL:
        pl.semaphore_signal(barrier, inc=1, device_id=other(axis), device_id_type=MESH_ID)

    @pl.when(z > 0)
    def _():
        pl.semaphore_signal(barrier, inc=1, device_id={"z": z - 1}, device_id_type=MESH_ID)

    @pl.when(z < zsize - 1)
    def _():
        pl.semaphore_signal(barrier, inc=1, device_id={"z": z + 1}, device_id_type=MESH_ID)

    peers = len(CELL) + jnp.where(z > 0, 1, 0) + jnp.where(z < zsize - 1, 1, 0)
    pl.semaphore_wait(barrier, peers)


def remote(src, dst, send_sem, recv_sem, device):
    return pltpu.make_async_remote_copy(
        src_ref=src, dst_ref=dst, send_sem=send_sem, recv_sem=recv_sem, device_id=device, device_id_type=MESH_ID
    )


def swap_kernel(zsize, to_rows, origin, target, held, local_sem, send, recv):
    groups = target.shape[0]
    rows, cols = (target.shape[1], target.shape[2] // zsize) if to_rows else (target.shape[1] // zsize, target.shape[2])
    z = lax.axis_index("z")

    def source(g, peer):
        if to_rows:
            return origin.at[g, pl.ds(pl.multiple_of(peer * rows, rows), rows), :]
        return origin.at[g, :, pl.ds(pl.multiple_of(peer * cols, cols), cols)]

    def place(g, peer):
        if to_rows:
            return target.at[g, :, pl.ds(pl.multiple_of(peer * cols, cols), cols)]
        return target.at[g, pl.ds(pl.multiple_of(peer * rows, rows), rows), :]

    def copy_to(g, step):
        peer = lax.rem(z + step, zsize)
        return remote(source(g, peer), place(g, z), send.at[step, g], recv.at[step, g], {"z": peer})

    def copy_from(g, step):
        peer = lax.rem(z + zsize - step, zsize)
        return remote(source(g, peer), place(g, peer), send.at[step, g], recv.at[step, g], {"z": peer})

    into = [pltpu.make_async_copy(source(g, z), held.at[g], local_sem.at[0, g]) for g in range(groups)]
    onward = [pltpu.make_async_copy(held.at[g], place(g, z), local_sem.at[1, g]) for g in range(groups)]
    for copy in into:
        copy.start()
    barrier = pltpu.get_barrier_semaphore()
    for step in range(1, zsize):
        peer = lax.rem(z + step, zsize)
        pl.semaphore_signal(barrier, inc=1, device_id={"z": peer}, device_id_type=MESH_ID)
    pl.semaphore_wait(barrier, zsize - 1)
    for g in range(groups):
        for step in range(1, zsize):
            copy_to(g, step).start()
    for g in range(groups):
        into[g].wait()
        onward[g].start()
    for g in range(groups):
        for step in range(1, zsize):
            copy_from(g, step).wait_recv()
        onward[g].wait()
    for g in range(groups):
        for step in range(1, zsize):
            copy_to(g, step).wait_send()


def swap(array, zsize, to_rows):
    groups, rows, cols = array.shape
    if to_rows:
        rows //= zsize
        shape = (groups, rows, zsize * cols)
    else:
        cols //= zsize
        shape = (groups, zsize * rows, cols)
    return pl.pallas_call(
        functools.partial(swap_kernel, zsize, to_rows),
        out_shape=jax.ShapeDtypeStruct(shape, bf16),
        in_specs=[HBM],
        out_specs=HBM,
        scratch_shapes=[
            pltpu.VMEM((groups, rows, cols), bf16),
            pltpu.SemaphoreType.DMA((2, groups)),
            pltpu.SemaphoreType.DMA((zsize, groups)),
            pltpu.SemaphoreType.DMA((zsize, groups)),
        ],
        compiler_params=pltpu.CompilerParams(
            collective_id=2 if to_rows else 3, has_side_effects=True, vmem_limit_bytes=8 * 1024 * 1024
        ),
    )(array)


ORDERS = {"xy": ("x", "y"), "yx": ("y", "x")}


def gather_kernel(zsize, orders, *refs):
    n = len(orders)
    tok, bias, shards = refs[0], refs[1], refs[2:2 + n]
    tok_all, bias_all, wholes = refs[2 + n], refs[3 + n], refs[4 + n:4 + 2 * n]
    held = refs[4 + 2 * n:6 + 3 * n]
    local_sem, z_send, z_recv, p_send, p_recv = refs[6 + 3 * n:]
    z = lax.axis_index("z")
    c = lax.axis_index("core")
    place = [(lax.axis_index(o[0]), lax.axis_index(o[1])) for o in orders]

    sources = list(shards) + [tok, bias]
    targets = list(wholes) + [tok_all, bias_all]
    into = [pltpu.make_async_copy(sources[i], held[i], local_sem.at[0, i]) for i in range(n + 2)]
    local = [pltpu.make_async_copy(held[i], targets[i].at[z], local_sem.at[1, i]) for i in range(n + 2)]
    for copy in into:
        copy.start()
    greet(zsize)

    def line(item, src, step, side):
        to = z + 1 if side == 0 else z - 1
        if item < n:
            f, s = place[item]
            own = shards[item].at[c, f, s]
            dst = wholes[item].at[src, c, f, s]
        else:
            own = (tok, bias)[item - n]
            dst = (tok_all, bias_all)[item - n].at[src]
        return remote(
            own if step == 0 else dst, dst, z_send.at[side, item, step], z_recv.at[side, item, step], {"z": to}
        )

    def exchange(k, src, stage, slot):
        f, s = place[k]
        whole = wholes[k]
        ref = (whole.at[src, c, f, s], whole.at[src, c, f], whole.at[src, c])[stage]
        axis = (orders[k][1], orders[k][0], "core")[stage]
        return remote(ref, ref, p_send.at[slot, k, stage], p_recv.at[slot, k, stage], other(axis))

    def valid_from(side, step):
        return z - step - 1 >= 0 if side == 0 else z + step + 1 < zsize

    def source(side, step):
        return z - step - 1 if side == 0 else z + step + 1

    def has_next(side):
        return z < zsize - 1 if side == 0 else z > 0

    for side in range(2):

        @pl.when(has_next(side))
        def _():
            for item in range(n):
                line(item, z, 0, side).start()

    def stage_on(stage, step):
        for side in range(2):

            @pl.when(valid_from(side, step))
            def _():
                src = source(side, step)
                slot = side * (zsize - 1) + step
                for k in range(n):
                    exchange(k, src, stage - 1, slot).wait_recv()
                    if stage < 3:
                        exchange(k, src, stage, slot).start()

    def arrive(items, step):
        for side in range(2):

            @pl.when(valid_from(side, step))
            def _():
                src = source(side, step)
                for item in items:
                    line(item, src, step, side).wait_recv()
                    if step + 1 < zsize - 1:

                        @pl.when(has_next(side))
                        def _():
                            line(item, src, step + 1, side).start()

                    if item < n:
                        exchange(item, src, 0, side * (zsize - 1) + step).start()

    for copy, onward in zip(into, local):
        copy.wait()
        onward.start()
    for step in range(zsize - 1):
        arrive(range(n), step)
        if step == zsize - 2:
            for side in range(2):

                @pl.when(has_next(side))
                def _():
                    for item in range(n, n + 2):
                        line(item, z, 0, side).start()

        if step >= 1:
            stage_on(1, step - 1)
    for step in range(zsize - 1):
        if step == 0:
            stage_on(1, zsize - 2)
        stage_on(2, step)
        arrive(range(n, n + 2), step)
    for step in range(zsize - 1):
        stage_on(3, step)
    for copy in local:
        copy.wait()
    for side in range(2):

        @pl.when(has_next(side))
        def _():
            for item in range(n + 2):
                line(item, z, 0, side).wait_send()

        for step in range(zsize - 1):

            @pl.when(valid_from(side, step))
            def _():
                src = source(side, step)
                if step + 1 < zsize - 1:

                    @pl.when(has_next(side))
                    def _():
                        for item in range(n + 2):
                            line(item, src, step + 1, side).wait_send()

                for k in range(n):
                    for stage in range(3):
                        exchange(k, src, stage, side * (zsize - 1) + step).wait_send()


def gather_start(tokens, bias, weights, zsize):
    orders = [ORDERS[o] for o, _ in weights]
    shards = [w for _, w in weights]
    n = len(shards)
    stack = lambda a: jax.ShapeDtypeStruct((zsize,) + a.shape, a.dtype)
    return pl.pallas_call(
        functools.partial(gather_kernel, zsize, orders),
        out_shape=[stack(tokens), stack(bias)] + [stack(w) for w in shards],
        in_specs=[HBM] * (n + 2),
        out_specs=[HBM] * (n + 2),
        scratch_shapes=[pltpu.VMEM(a.shape, a.dtype) for a in shards + [tokens, bias]] + [
            pltpu.SemaphoreType.DMA((2, n + 2)),
            pltpu.SemaphoreType.DMA((2, n + 2, zsize - 1)),
            pltpu.SemaphoreType.DMA((2, n + 2, zsize - 1)),
            pltpu.SemaphoreType.DMA((2 * (zsize - 1), n, 3)),
            pltpu.SemaphoreType.DMA((2 * (zsize - 1), n, 3)),
        ],
        compiler_params=pltpu.CompilerParams(
            collective_id=0, has_side_effects=True, vmem_limit_bytes=32 * 1024 * 1024
        ),
    )(tokens, bias, *shards)


def add_rows(dst, src):
    rows = dst.shape[0]
    step = min(rows, 32)

    def body(i, carry):
        at = pl.ds(pl.multiple_of(i * step, step), step)
        dst[at, :] = dst[at, :] + src[at, :]
        return carry

    lax.fori_loop(0, rows // step, body, 0)


def reduce_kernel(zsize, orders, w, *refs):
    n = 3
    p = len(orders) - n
    items = n + p
    pieces, came, refs = refs[:p], refs[p:2 * p], refs[2 * p:]
    parts, backs, small = refs[:n], refs[n:n + w], refs[n + w]
    pos = n + w + 1
    piece_out, part_out, back_out = refs[pos:pos + p], refs[pos + p:pos + p + n], refs[pos + p + n:pos + p + n + w]
    small_out = refs[pos + p + n + w]
    outs = list(part_out) + list(piece_out)
    pos += p + n + w + 1
    mine = refs[pos:pos + items + w]
    pos += items + w
    got_c, got_1, got_2 = refs[pos:pos + n], refs[pos + n:pos + n + items], refs[pos + n + items:pos + n + 2 * items]
    pos += n + 2 * items
    lines = [0] + list(range(n, items + w))
    line_backs = list(range(items, items + w))
    got_z = dict(zip(lines, refs[pos:pos + len(lines)]))
    pos += len(lines)
    small_mine, small_got, small_line, small_total, part_line, part_total = refs[pos:pos + 6]
    (local_sem, send, recv, z_send, z_recv, s_send, s_recv, t_send, t_recv, g_send, g_recv, end_sem) = refs[pos + 6:]
    z = lax.axis_index("z")
    c = lax.axis_index("core")
    orders = orders[p:] + orders[:p]
    place = [(lax.axis_index(o[0]), lax.axis_index(o[1])) for o in orders]
    turn = []
    for i in range(zsize // 2):
        turn += [i, zsize - 1 - i]
    few = parts[1].shape[0]
    steps = [(1, b) for b in range(few)] + [(2, 0)] + [(0, b) for b in turn]

    def load(k, b):
        src = parts[k].at[b, c] if k < n else pieces[k - n].at[b] if k < items else backs[k - items].at[b]
        return pltpu.make_async_copy(src, mine[k].at[b], local_sem.at[k, b])

    def load_came(k, b):
        return pltpu.make_async_copy(came[k - n].at[b], got_1[k].at[b], local_sem.at[items + w + 1 + k - n, b])

    load_small = pltpu.make_async_copy(small, small_mine.at[0], local_sem.at[items + w, 0])

    def half(k, b, stage):
        f, s = place[k]
        if stage == 0:
            src, dst, axis = parts[k].at[b, 1 - c], got_c[k].at[b], "core"
        elif stage == 1:
            src, dst, axis = mine[k].at[b, 1 - f], got_1[k].at[b], orders[k][0]
        else:
            held = mine[k].at[b, f] if k < n else mine[k].at[b]
            src, dst, axis = held.at[1 - s], got_2[k].at[b], orders[k][1]
        return remote(src, dst, send.at[stage, k, b], recv.at[stage, k, b], other(axis))

    def own(k, b):
        if k >= items:
            return mine[k].at[b]
        f, s = place[k]
        return mine[k].at[b, s] if k >= n else mine[k].at[b, f, s]

    def hop(k, b, side):
        to = z + 1 if side == 0 else z - 1
        at = b if side == 0 else jnp.where(b == z - 1, zsize, b)
        return remote(own(k, b), got_z[k].at[at], z_send.at[k, b], z_recv.at[k, at], {"z": to})

    def take(k, b, side):
        at = b if side == 0 else jnp.where(b == z, zsize, b)
        ref = got_z[k].at[at]
        sender = z - 1 if side == 0 else z + 1
        remote(own(k, b), ref, z_send.at[k, b], z_recv.at[k, at], {"z": sender}).wait_recv()
        add_rows(own(k, b), ref)

    def line_start(ks, messages):
        for side in range(2):

            @pl.when(z == (0 if side == 0 else zsize - 1))
            def _():
                for i in messages:
                    for k in ks:
                        hop(k, zsize - 1 - i if side == 0 else i, side).start()

    def line_slot(ks, slot):
        for i in range(slot):
            for side in range(2):
                b = zsize - 1 - i if side == 0 else i

                @pl.when(z == (slot - i if side == 0 else zsize - 1 - slot + i))
                def _():
                    for k in ks:
                        take(k, b, side)

                        @pl.when(z < b if side == 0 else z > b)
                        def _():
                            hop(k, b, side).start()

    def small_swap(stage):
        return remote(
            small_mine.at[stage], small_got.at[stage], s_send.at[stage], s_recv.at[stage], other(CELL[stage])
        )

    def small_step(stage):
        small_swap(stage).wait_recv()
        small_mine[stage + 1] = small_mine[stage] + small_got[stage]
        if stage < 2:
            small_swap(stage + 1).start()

    last = len(CELL)
    last_part = own(2, 0)

    def total_copy(item, way):
        line, total = ((small_line, small_total), (part_line, part_total))[item]
        src = (small_mine.at[last], last_part)[item] if way == 0 else total
        dst = line if way == 0 else total
        to = z + 1 if way == 0 else z - 1
        return remote(src, dst, t_send.at[item, way], t_recv.at[item, way], {"z": to})

    def total_step(tick):
        if 0 <= tick < zsize:

            @pl.when(z == tick)
            def _():
                if tick > 0:
                    for item in range(2):
                        total_copy(item, 0).wait_recv()
                    small_mine[last] = small_mine[last] + small_line[...]
                    add_rows(last_part, part_line)
                if tick < zsize - 1:
                    for item in range(2):
                        total_copy(item, 0).start()
                else:
                    small_total[...] = small_mine[last]
                    part_total[...] = last_part[...]

        back_tick = tick - (zsize - 1)
        if 0 <= back_tick < zsize:

            @pl.when(z == zsize - 1 - back_tick)
            def _():
                if back_tick > 0:
                    for item in range(2):
                        total_copy(item, 1).wait_recv()
                if back_tick < zsize - 1:
                    for item in range(2):
                        total_copy(item, 1).start()

    line_pieces = list(range(n, items))
    piece_steps = [(k, b) for b in turn for k in line_pieces]
    for b in turn:
        for k in line_backs:
            load(k, b).start()
    for k, b in piece_steps:
        load(k, b).start()
        load_came(k, b).start()
    for k, b in steps:
        load(k, b).start()
    load_small.start()
    greet(zsize)
    for k, b in steps:
        half(k, b, 0).start()
    for b in turn:
        for k in line_backs:
            load(k, b).wait()
    line_start(line_backs, [0])
    load_small.wait()
    small_swap(0).start()

    def stage_1(k, b):
        f, s = place[k]
        load(k, b).wait()
        half(k, b, 0).wait_recv()
        for i in range(2):
            add_rows(mine[k].at[b, 1 - f, i], got_c[k].at[b, 1 - f, i])
        half(k, b, 1).start()
        for i in range(2):
            add_rows(mine[k].at[b, f, i], got_c[k].at[b, f, i])

    def stage_2(k, b):
        f, s = place[k]
        held = mine[k].at[b, f] if k < n else mine[k].at[b]
        if k < n:
            half(k, b, 1).wait_recv()
        else:
            load(k, b).wait()
            load_came(k, b).wait()
        add_rows(held.at[1 - s], got_1[k].at[b, 1 - s])
        half(k, b, 2).start()
        add_rows(held.at[s], got_1[k].at[b, s])

    def stage_3(k, b):
        half(k, b, 2).wait_recv()
        add_rows(own(k, b), got_2[k].at[b])

    def result(k, b):
        return part_total if k == 2 else own(k, b)

    def out_of(k, b):
        return outs[k].at[b] if k == 1 else outs[k]

    def put(k, b, slot):
        f, s = place[k]
        return pltpu.make_async_copy(result(k, b), out_of(k, b).at[c, f, s], end_sem.at[slot])

    def spread(k, b, stage, slot):
        f, s = place[k]
        out = out_of(k, b)
        dst = (out.at[c, f, s], out.at[c, f], out.at[c])[stage]
        src = result(k, b) if stage == 0 else dst
        axis = (orders[k][1], orders[k][0], "core")[stage]
        return remote(src, dst, g_send.at[slot, stage], g_recv.at[slot, stage], other(axis))

    spreads = [
        [(1, b, b) for b in range(few)],
        [(k, z, few + k - n) for k in line_pieces],
        [(0, z, few + p), (2, 0, few + p + 1)],
    ]

    def spread_step(group, stage):
        for k, b, slot in spreads[group]:
            if stage == 0:
                spread(k, b, 0, slot).start()
                put(k, b, slot).start()
                continue
            if stage == 1:
                put(k, b, slot).wait()
            spread(k, b, stage - 1, slot).wait_recv()
            if stage < 3:
                spread(k, b, stage, slot).start()

    def sent(ks):
        for b in range(zsize):

            @pl.when(z != b)
            def _():
                for k in ks:
                    hop(k, b, 0).wait_send()

    at_end = jnp.logical_or(z == 0, z == zsize - 1)
    for k, b in piece_steps:
        stage_2(k, b)
    for k, b in steps:
        stage_1(k, b)
    small_step(0)
    for k, b in piece_steps:
        stage_3(k, b)
    line_start(line_pieces, range(zsize - 1))
    for k, b in steps:
        stage_2(k, b)
    small_step(1)
    line_slot(line_backs, 1)
    for k, b in steps:
        stage_3(k, b)
    small_step(2)
    spread_step(0, 0)
    line_start([0], range(zsize - 1))
    total_step(0)

    @pl.when(at_end)
    def _():
        sent(line_pieces)

    line_start(line_backs, range(1, zsize - 1))
    ticks = list(range(1, 2 * zsize - 1))
    later = [(0, 1), (0, 2), (0, 3)]

    def fill(group_stages, count):
        for _ in range(count):
            if group_stages:
                spread_step(*group_stages.pop(0))

    for slot in range(1, zsize):
        line_slot(line_pieces, slot)
        total_step(ticks.pop(0))
        fill(later, 1)
        if slot >= 2:
            line_slot([0], slot - 1)
    fill(later, 3)
    spread_step(1, 0)
    later = [(1, 1), (1, 2), (1, 3)]
    total_step(ticks.pop(0))
    line_slot([0], zsize - 1)
    for slot in range(2, zsize - 1):
        line_slot(line_backs, slot)
        fill(later, 1)
    for tick in ticks:
        total_step(tick)
    spread_step(2, 0)
    fill(later, 1)
    spread_step(2, 1)
    fill(later, 1)
    spread_step(2, 2)
    fill(later, 3)
    line_slot(line_backs, zsize - 1)
    finish_back = [
        pltpu.make_async_copy(mine[k].at[z], back_out[k - items], local_sem.at[k, 0]) for k in line_backs
    ]
    for copy in finish_back:
        copy.start()
    finish_small = pltpu.make_async_copy(small_total, small_out, local_sem.at[items + w, 0])
    finish_small.start()
    spread_step(2, 3)
    for copy in finish_back:
        copy.wait()
    finish_small.wait()
    sent([0] + line_backs)

    @pl.when(jnp.logical_not(at_end))
    def _():
        sent(line_pieces)

    for way in range(2):

        @pl.when(z < zsize - 1 if way == 0 else z > 0)
        def _():
            for item in range(2):
                total_copy(item, way).wait_send()

    for k, b in steps:
        for stage in range(3):
            half(k, b, stage).wait_send()
    for k, b in piece_steps:
        half(k, b, 2).wait_send()
    for stage in range(3):
        small_swap(stage).wait_send()
    for group in spreads:
        for k, b, slot in group:
            for stage in range(3):
                spread(k, b, stage, slot).wait_send()


def reduce_end(pieces, parts, backs, small, zsize):
    orders = [ORDERS[o[0]] for o in pieces + parts]
    piece_arrays = [a for _, a, _ in pieces]
    came = [a for _, _, a in pieces]
    arrays = [a for _, a in parts]
    p, n, w = len(pieces), len(parts), len(backs)
    shapes = [a.shape for a in arrays]
    like = jax.ShapeDtypeStruct
    outs = [like((2, 2, 2) + a.shape[2:], bf16) for a in piece_arrays]
    outs += [like(s if i == 1 else s[1:], bf16) for i, s in enumerate(shapes)]
    outs += [like(a.shape[1:], bf16) for a in backs] + [like(small.shape, f32)]
    held = lambda shape: pltpu.VMEM(shape, bf16)
    scratch = [held((s[0],) + s[2:]) for s in shapes]
    scratch += [held(a.shape) for a in piece_arrays + backs]
    scratch += [held((s[0],) + s[2:]) for s in shapes]
    scratch += [held((s[0],) + s[3:]) for s in shapes] + [held(a.shape) for a in piece_arrays]
    scratch += [held((s[0],) + s[4:]) for s in shapes] + [held(a.shape[:1] + a.shape[2:]) for a in piece_arrays]
    scratch += [held((zsize + 1,) + shapes[0][4:])]
    scratch += [held((zsize + 1,) + a.shape[2:]) for a in piece_arrays] + [held((zsize + 1,) + a.shape[1:]) for a in backs]
    scratch += [pltpu.VMEM((4,) + small.shape, f32), pltpu.VMEM((3,) + small.shape, f32)]
    scratch += [pltpu.VMEM(small.shape, f32)] * 2 + [held(shapes[2][4:])] * 2
    dma = pltpu.SemaphoreType.DMA
    most = max(zsize, shapes[1][0])
    ends = shapes[1][0] + p + 2
    scratch += [
        dma((n + 2 * p + w + 1, most)), dma((3, n + p, most)), dma((3, n + p, most)),
        dma((n + p + w, zsize)), dma((n + p + w, zsize + 1)),
        dma((3,)), dma((3,)), dma((2, 2)), dma((2, 2)), dma((ends, 3)), dma((ends, 3)), dma((ends,)),
    ]
    return pl.pallas_call(
        functools.partial(reduce_kernel, zsize, orders, w),
        out_shape=outs,
        in_specs=[HBM] * (n + 2 * p + w + 1),
        out_specs=[HBM] * (n + p + w + 1),
        scratch_shapes=scratch,
        compiler_params=pltpu.CompilerParams(
            collective_id=1, has_side_effects=True, vmem_limit_bytes=48 * 1024 * 1024
        ),
    )(*piece_arrays, *came, *arrays, *backs, small)


def gelu_pair(v):
    size = jnp.abs(v)
    t = 1.0 / (1.0 + (0.3275911 * 0.5 ** 0.5) * size)
    bell = jnp.exp(-0.5 * (v * v))
    poly = t * (0.254829592 + t * (-0.284496736 + t * (1.421413741 + t * (-1.453152027 + t * 1.061405429))))
    tail = 0.5 * poly * bell
    cdf = jnp.where(v >= 0.0, 1.0 - tail, tail)
    return v * cdf, cdf + v * (bell * (1.0 / (2.0 * math.pi) ** 0.5))


def ffn_kernel(x_ref, up_ref, bias_ref, down_ref, active_ref, slope_ref, sum_ref):
    rows = x_ref.shape[0]
    part = rows // 2

    @pl.when(pl.program_id(0) == 0)
    def _():
        sum_ref[...] = jnp.zeros(sum_ref.shape, f32)

    for i in range(2):
        at = pl.ds(i * part, part)
        hidden = jnp.dot(x_ref[at, :], up_ref[0], preferred_element_type=f32) + bias_ref[0]
        active, slope = gelu_pair(hidden)
        active = active.astype(bf16)
        active_ref[0, at, :] = active
        slope_ref[0, at, :] = slope.astype(bf16)
        sum_ref[at, :] += jnp.dot(active, down_ref[0], preferred_element_type=f32)


def ffn_forward(normed_low, up_all, up_bias, down_all):
    zsize, width, units = up_all.shape
    rows = normed_low.shape[0]
    tile = units // 2
    like = jax.ShapeDtypeStruct
    tiles = pl.BlockSpec((1, rows, tile), lambda s: (s // 2, 0, s % 2))
    return pl.pallas_call(
        ffn_kernel,
        grid=(2 * zsize,),
        in_specs=[
            pl.BlockSpec((rows, width), lambda s: (0, 0)),
            pl.BlockSpec((1, width, tile), lambda s: (s // 2, 0, s % 2)),
            pl.BlockSpec((1, 1, tile), lambda s: (s // 2, 0, s % 2)),
            pl.BlockSpec((1, tile, width), lambda s: (s // 2, s % 2, 0)),
        ],
        out_specs=[tiles, tiles, pl.BlockSpec((rows, width), lambda s: (0, 0))],
        out_shape=[
            like((zsize, rows, units), bf16), like((zsize, rows, units), bf16), like((rows, width), f32),
        ],
        compiler_params=pltpu.CompilerParams(vmem_limit_bytes=40 * 1024 * 1024),
    )(normed_low, up_all, up_bias[:, None, :], down_all)


def ffn_back_kernel(core_ref, second_ref, normed_ref, up_ref, down_ref, active_ref, slope_ref,
                    give_up_ref, keep_up_ref, give_down_ref, keep_down_ref, back_ref, bias_ref, turned_ref):
    s = pl.program_id(0)
    half = turned_ref.shape[0] // 2
    c = core_ref[0]

    @pl.when(s == 0)
    def _():
        back_ref[...] = jnp.zeros(back_ref.shape, f32)
        turned_ref[...] = normed_ref[...].T

    second = second_ref[...]
    upstream = lax.dot_general(second, down_ref[0], (((1,), (1,)), ((), ())), preferred_element_type=f32)
    grad = (upstream * slope_ref[0].astype(f32)).astype(bf16)
    bias_ref[0] = jnp.sum(grad.astype(f32), axis=0, keepdims=True)
    down = lax.dot_general(active_ref[0], second, (((0,), (0,)), ((), ())), preferred_element_type=f32).astype(bf16)

    @pl.when(s % 2 == 0)
    def _():
        give_down_ref[0] = down

    @pl.when(s % 2 == 1)
    def _():
        keep_down_ref[0] = down

    back_ref[...] += lax.dot_general(grad, up_ref[0], (((1,), (1,)), ((), ())), preferred_element_type=f32)
    give = turned_ref[pl.ds(pl.multiple_of((1 - c) * half, half), half), :]
    give_up_ref[0] = jnp.dot(give, grad, preferred_element_type=f32).astype(bf16)
    keep = turned_ref[pl.ds(pl.multiple_of(c * half, half), half), :]
    keep_up_ref[0] = jnp.dot(keep, grad, preferred_element_type=f32).astype(bf16)


def ffn_backward(core, second_low, normed_low, up_all, down_all, active, slope):
    zsize, width, units = up_all.shape
    rows = normed_low.shape[0]
    tile = units // 2
    like = jax.ShapeDtypeStruct
    part = lambda s, c: (1 - c[0] + (2 * c[0] - 1) * (s % 2))
    whole = pl.BlockSpec((rows, width), lambda s, c: (0, 0))
    tiles = pl.BlockSpec((1, rows, tile), lambda s, c: (s // 2, 0, part(s, c)))
    up_half = pl.BlockSpec((1, width // 2, tile), lambda s, c: (s // 2, 0, part(s, c)))
    down_half = pl.BlockSpec((1, tile, width), lambda s, c: (s // 2, 0, 0))
    return pl.pallas_call(
        ffn_back_kernel,
        grid_spec=pltpu.PrefetchScalarGridSpec(
            num_scalar_prefetch=1,
            grid=(2 * zsize,),
            in_specs=[
                whole, whole,
                pl.BlockSpec((1, width, tile), lambda s, c: (s // 2, 0, part(s, c))),
                pl.BlockSpec((1, tile, width), lambda s, c: (s // 2, part(s, c), 0)),
                tiles, tiles,
            ],
            out_specs=[
                up_half, up_half, down_half, down_half, whole,
                pl.BlockSpec((1, 1, tile), lambda s, c: (s // 2, 0, part(s, c))),
            ],
            scratch_shapes=[pltpu.VMEM((width, rows), bf16)],
        ),
        out_shape=[
            like((zsize, width // 2, units), bf16), like((zsize, width // 2, units), bf16),
            like((zsize, tile, width), bf16), like((zsize, tile, width), bf16),
            like((rows, width), f32), like((zsize, 1, units), f32),
        ],
        compiler_params=pltpu.CompilerParams(vmem_limit_bytes=40 * 1024 * 1024),
    )(core, second_low, normed_low, up_all, down_all, active, slope)


PAIR = [(0, 1), (1, 0)]


def first_halving(got, keep, order):
    zsize, half, cols = keep.shape
    shape = (zsize, 2, 2, half // 4, cols)
    got, keep = got.reshape(shape), keep.reshape(shape)
    i = lax.axis_index(ORDERS[order][0])
    pick = lambda array, j: lax.dynamic_index_in_dim(array, j, 1, keepdims=False)
    return pick(keep, 1 - i) + pick(got, 1 - i), pick(keep, i) + pick(got, i)


def per_device(blocks, tokens, segments, qkv_weight, qkv_bias, out_weight, out_bias, gain_one, shift_one,
               up_weight, up_bias, down_weight, down_bias, gain_two, shift_two, proj_weight, out_grad, embed_grad):
    groups, local_rows, model_width = tokens.shape
    length = segments.shape[1]
    zsize = length // local_rows
    head_cols = qkv_weight.shape[2]
    units_here = up_weight.shape[1]
    rows = groups * local_rows
    zi = lax.axis_index("z")
    cosine, sine = rotary_tables(doc_positions(segments), HEAD_DIM)
    half = HEAD_DIM // 2
    signs = jnp.where(jnp.arange(2 * HEAD_DIM) % HEAD_DIM < half, -1.0, 1.0)
    cosine = jnp.concatenate([cosine, cosine], axis=-1)
    sine = jnp.concatenate([sine, sine], axis=-1) * signs
    firsts = segments[:, ::BLOCK]
    lasts = segments[:, BLOCK - 1::BLOCK]
    bounds = (
        jnp.sum(segments[:, None, :] < firsts[:, :, None], axis=2, dtype=jnp.int32) // BLOCK,
        (jnp.sum(segments[:, None, :] <= lasts[:, :, None], axis=2, dtype=jnp.int32) + BLOCK - 1) // BLOCK,
    )
    docs = segments[:, :, None]

    def cut(array, rows_at):
        shape = array.shape
        return array.reshape(shape[:rows_at] + (2, 2, 2, shape[rows_at] // 8) + shape[rows_at + 1:])

    token_rows = tokens.reshape(rows, model_width)
    token_blocks, bias_blocks, out_all, up_all, down_all = gather_start(
        token_rows,
        up_bias.reshape(8, units_here // 8),
        [("xy", cut(out_weight, 0)), ("xy", cut(up_weight, 0)), ("yx", cut(down_weight, 0))],
        zsize,
    )
    token_blocks = token_blocks.reshape(zsize, groups, local_rows, model_width)
    out_all = out_all.reshape(model_width, model_width)
    up_all = up_all.reshape(zsize, model_width, units_here)
    down_all = down_all.reshape(zsize, units_here, model_width)
    full_up_bias = bias_blocks.reshape(zsize, units_here)

    own_mixed, *kept = attend_forward(bounds, token_blocks, qkv_weight, qkv_bias, cosine, sine, docs)
    mixed = swap(own_mixed, zsize, True).reshape(rows, model_width)

    first_sum = tokens.reshape(rows, model_width).astype(f32) + (
        jnp.dot(mixed, out_all, preferred_element_type=f32) + out_bias
    )
    normed, scaled_one, inv_one = norm_forward(first_sum, gain_one, shift_one)
    normed_low = normed.astype(bf16)
    active, slope, ffn = ffn_forward(normed_low, up_all, full_up_bias, down_all)
    second_sum = normed + (ffn + down_bias)
    result, scaled_two, inv_two = norm_forward(second_sum, gain_two, shift_two)
    result_low = result.astype(bf16)
    embedded = jnp.dot(result_low, proj_weight, preferred_element_type=f32).astype(bf16)
    embed_rows = embed_grad.reshape(rows, -1)
    grad_result = out_grad.reshape(rows, model_width).astype(f32) + jnp.einsum(
        "np,dp->nd", embed_rows, proj_weight, preferred_element_type=f32
    )
    proj_grad = jnp.einsum("nd,np->dp", result_low, embed_rows, preferred_element_type=f32)
    grad_second, gain_two_grad, shift_two_grad = norm_backward(grad_result, scaled_two, inv_two, gain_two)
    second_low = grad_second.astype(bf16)
    down_bias_grad = jnp.sum(second_low.astype(f32), axis=0)
    core = lax.axis_index("core").reshape(1)
    give_up, keep_up, give_down, keep_down, ffn_back, up_bias_grad = ffn_backward(
        core, second_low, normed_low, up_all, down_all, active, slope
    )
    got_down = lax.ppermute(give_down, "core", PAIR)
    got_up = lax.ppermute(give_up, "core", PAIR)
    grad_normed = grad_second + ffn_back
    grad_first, gain_one_grad, shift_one_grad = norm_backward(grad_normed, scaled_one, inv_one, gain_one)
    first_low = grad_first.astype(bf16)
    out_bias_grad = jnp.sum(first_low.astype(f32), axis=0)
    out_grad_w = jnp.einsum("nh,nd->hd", mixed, first_low, preferred_element_type=f32).astype(bf16)
    grad_mixed = jnp.einsum("nd,hd->nh", first_low, out_all, preferred_element_type=f32).astype(bf16)
    grad_mixed = grad_mixed.reshape(groups, local_rows, model_width)
    upstream = swap(grad_mixed, zsize, False)
    send_down, keep_down = first_halving(got_down, keep_down, "yx")
    send_up, keep_up = first_halving(got_up, keep_up, "xy")
    upstream, send_down, send_up = lax.optimization_barrier((upstream, send_down, send_up))
    got_down = lax.ppermute(send_down, ORDERS["yx"][0], PAIR)
    got_up = lax.ppermute(send_up, ORDERS["xy"][0], PAIR)
    grad_qkv, qkv_bias_grad = attend_backward(bounds, kept, own_mixed, upstream, cosine, sine)
    grad_qkv, got_down, got_up = lax.optimization_barrier((grad_qkv, got_down, got_up))
    qkv_bias_grad = qkv_bias_grad[:3]
    by_z = grad_qkv.reshape(3, groups, zsize, local_rows, head_cols)
    qkv_weight_grad = jnp.einsum("zgld,cgzle->cde", token_blocks, by_z, preferred_element_type=f32)
    backs = [
        jnp.einsum("czle,cde->zld", by_z[:, g], qkv_weight, preferred_element_type=f32).astype(bf16)
        for g in range(groups)
    ]
    small = jnp.concatenate(
        [
            out_bias_grad, gain_one_grad, shift_one_grad, down_bias_grad, gain_two_grad, shift_two_grad,
            up_bias_grad.reshape(-1),
            lax.dynamic_update_slice(
                jnp.zeros((zsize, 3 * head_cols), f32), qkv_bias_grad.reshape(1, -1), (zi, 0)
            ).reshape(-1),
        ]
    )
    proj_cols = proj_grad.shape[1]
    proj_grad = jnp.pad(proj_grad.astype(bf16), ((0, 0), (0, -proj_cols % 128)))
    up_grad, down_grad, out_grad_w, qkv_weight_grad, proj_grad, *back, small = reduce_end(
        [("xy", keep_up, got_up), ("yx", keep_down, got_down)],
        [
            ("xy", cut(out_grad_w.reshape(zsize, head_cols, model_width), 1)),
            ("yx", cut(qkv_weight_grad.astype(bf16), 1)),
            ("xy", cut(proj_grad[None], 1)),
        ],
        backs,
        small.reshape(8, -1),
        zsize,
    )
    tokens_grad = grad_first.reshape(groups, local_rows, model_width) + jnp.stack(back).astype(f32)
    qkv_weight_grad = qkv_weight_grad.reshape(qkv_weight.shape)
    proj_grad = proj_grad.reshape(model_width, -1)[:, :proj_cols].astype(f32)
    out_grad_w = out_grad_w.reshape(out_weight.shape)
    up_grad = up_grad.reshape(up_weight.shape)
    down_grad = down_grad.reshape(down_weight.shape)
    if blocks > 1:
        down_grad, up_grad, out_grad_w, qkv_weight_grad = lax.psum(
            (down_grad, up_grad, out_grad_w, qkv_weight_grad), ("xb", "yb")
        )
        small, proj_grad = lax.psum((small, proj_grad), ("xb", "yb"))
    small = small.reshape(-1)
    base = 6 * model_width
    vec = [small[i * model_width:(i + 1) * model_width] for i in range(6)]
    up_bias_grad = lax.dynamic_slice(small, (base + zi * units_here,), (units_here,))
    qkv_bias_grad = lax.dynamic_slice(
        small, (base + zsize * units_here + zi * 3 * head_cols,), (3 * head_cols,)
    ).reshape(3, head_cols)
    shape3 = (groups, local_rows, model_width)
    return (
        result_low.reshape(shape3),
        embedded.reshape(groups, local_rows, -1),
        tokens_grad,
        qkv_weight_grad.astype(f32),
        qkv_bias_grad,
        out_grad_w.astype(f32),
        vec[0], vec[1], vec[2],
        up_grad.astype(f32),
        up_bias_grad,
        down_grad.astype(f32),
        vec[3], vec[4], vec[5],
        proj_grad,
    )


def solution(mesh):
    dp_size, zsize = mesh.shape["dp"], mesh.shape["tensor"]
    side = math.isqrt(dp_size // 2) // 2
    cut = Mesh(mesh.devices.reshape(side, 2, side, 2, 2, zsize), DP + ("z",))
    rows3 = P(DP, "z", None)
    in_specs = (
        rows3, P(DP, None), P(None, None, "z"), P(None, "z"), P("z", None), P(), P(), P(),
        P(None, "z"), P("z"), P("z", None), P(), P(), P(), P(), rows3, rows3,
    )
    out_specs = (
        rows3, rows3, rows3, P(None, None, "z"), P(None, "z"), P("z", None), P(), P(), P(),
        P(None, "z"), P("z"), P("z", None), P(), P(), P(), P(),
    )

    def run(*args):
        return per_device(side * side, *args)

    return jax.shard_map(run, mesh=cut, in_specs=in_specs, out_specs=out_specs, check_vma=False)
```

```python
import functools
import math

import jax
import jax.numpy as jnp
from jax import lax
from jax.experimental import pallas as pl
from jax.experimental.pallas import tpu as pltpu
from jax.sharding import Mesh
from jax.sharding import PartitionSpec as P

HEAD_DIM = 64
eps = 1e-05
DP = ("xb", "x", "yb", "y", "core")
CELL = ("x", "y", "core")
ALL = DP + ("z",)
f32 = jnp.float32
bf16 = jnp.bfloat16
VMEM = 60 * 1024 * 1024


def doc_positions(segment_rows):
    below = segment_rows[:, None, :] < jnp.arange(4, dtype=jnp.int32)[None, :, None]
    starts = jnp.sum(below, axis=2, dtype=jnp.int32)
    row_index = jnp.arange(segment_rows.shape[1], dtype=jnp.int32)[None]
    start = starts[:, 3:4]
    for doc in (2, 1, 0):
        start = jnp.where(segment_rows == doc, starts[:, doc:doc + 1], start)
    return row_index - start


def rotary_tables(positions):
    half_dim = HEAD_DIM // 2
    lane = jnp.arange(2 * HEAD_DIM, dtype=jnp.int32)
    exponent = (lane % half_dim).astype(f32) * (2.0 / HEAD_DIM)
    frequency = jnp.exp(-exponent * math.log(10000.0))
    sign = jnp.where(lane % HEAD_DIM < half_dim, -1.0, 1.0)
    angles = positions.astype(f32)[..., None] * frequency
    return (jnp.cos(angles), jnp.sin(angles) * sign)


def norm_forward(field, gain, shift):
    row_mean = jnp.mean(field, axis=-1, keepdims=True)
    centred = field - row_mean
    variance = jnp.mean(centred * centred, axis=-1, keepdims=True)
    inv_std = lax.rsqrt(variance + eps)
    scaled = centred * inv_std
    return (scaled * gain + shift, scaled, inv_std)


def norm_backward(upstream, scaled, inv_std, gain):
    grad_scaled = upstream * gain
    grad_input = inv_std * (
        grad_scaled
        - jnp.mean(grad_scaled, axis=-1, keepdims=True)
        - scaled * jnp.mean(grad_scaled * scaled, axis=-1, keepdims=True)
    )
    return (grad_input, jnp.sum(upstream * scaled, axis=0), jnp.sum(upstream, axis=0))


BLOCK = 256


def turn_halves(field, sign_sine):
    lane = lax.broadcasted_iota(jnp.int32, field.shape, 1)
    half = HEAD_DIM // 2
    width = field.shape[1]
    swapped = jnp.where(lane % HEAD_DIM < half, pltpu.roll(field, width - half, 1), pltpu.roll(field, half, 1))
    return swapped * sign_sine


def scores_of(keys, queries):
    return lax.dot_general(keys, queries, (((1,), (1,)), ((), ())), preferred_element_type=f32)


def attend_kernel(lo_ref, hi_ref, tok_ref, w_ref, b_ref, cos_ref, sin_ref, seg_ref, mixed_ref, q_ref, k_ref, v_ref,
                  lse_ref, vt_ref, m_ref, l_ref, acc_ref):
    group = pl.program_id(0)
    zsize, _, rows, _ = tok_ref.shape
    length = zsize * rows
    heads = q_ref.shape[1]
    pair = 2 * HEAD_DIM
    scale = HEAD_DIM ** (-0.5)

    def project(i, carry):
        at = pl.ds(pl.multiple_of(i * rows, rows), rows)
        x = tok_ref[i, 0]
        lane = lax.broadcasted_iota(jnp.int32, (rows, pair), 1)
        doc = seg_ref[0, at, :]
        same = lane - HEAD_DIM == doc
        low = lane < HEAD_DIM
        feature = lane < HEAD_DIM + 4
        extra_q = jnp.where(same, 1.0, 0.0)
        extra_k = jnp.where(jnp.logical_and(feature, jnp.logical_not(same)), -1e9, 0.0)
        cosine = cos_ref[0, at, :]
        sine = sin_ref[0, at, :]
        for c in range(3):
            field = jnp.dot(x, w_ref[c], preferred_element_type=f32) + b_ref[c:c + 1, :]
            for j in range(heads // 2):
                part = field[:, j * pair:(j + 1) * pair]
                if c < 2:
                    part = part * cosine + turn_halves(part, sine)
                if c == 0:
                    part = part * scale
                for h in range(2):
                    one = part if h == 0 else pltpu.roll(part, HEAD_DIM, 1)
                    head = 2 * j + h
                    if c == 0:
                        q_ref[0, head, at, :] = jnp.where(low, one, extra_q).astype(bf16)
                    elif c == 1:
                        k_ref[0, head, at, :] = jnp.where(low, one, extra_k).astype(bf16)
                    else:
                        one = jnp.where(low, one, 0.0)
                        v_ref[0, head, at, :] = one.astype(bf16)
                        vt_ref[head, :, at] = one.T[:HEAD_DIM].astype(bf16)
        return carry

    lax.fori_loop(0, zsize, project, 0)

    def query_block(i, carry):
        at = pl.ds(pl.multiple_of(i * BLOCK, BLOCK), BLOCK)
        m_ref[...] = jnp.full(m_ref.shape, -1e30, f32)
        l_ref[...] = jnp.zeros(l_ref.shape, f32)
        acc_ref[...] = jnp.zeros(acc_ref.shape, f32)

        def key_block(j, carry):
            keys_at = pl.ds(pl.multiple_of(j * BLOCK, BLOCK), BLOCK)
            st = [scores_of(k_ref[0, h, keys_at, :], q_ref[0, h, at, :]) for h in range(heads)]
            peak = m_ref[...]
            new = jnp.maximum(peak, jnp.concatenate([jnp.max(t, axis=0, keepdims=True) for t in st], axis=0))
            p = [jnp.exp(st[h] - new[h:h + 1, :]) for h in range(heads)]
            old = jnp.exp(peak - new)
            m_ref[...] = new
            l_ref[...] = l_ref[...] * old + jnp.concatenate([jnp.sum(t, axis=0, keepdims=True) for t in p], axis=0)
            part = [
                jnp.dot(vt_ref[h, :, keys_at], p[h].astype(bf16), preferred_element_type=f32) for h in range(heads)
            ]
            for h in range(heads):
                acc_ref[h] = acc_ref[h] * old[h:h + 1, :] + part[h]
            return carry

        lax.fori_loop(lo_ref[group, i], hi_ref[group, i], key_block, 0)
        out = [acc_ref[h] / l_ref[h:h + 1, :] for h in range(heads)]
        for j in range(heads // 2):
            both = jnp.concatenate([out[2 * j], out[2 * j + 1]], axis=0)
            mixed_ref[0, at, j * pair:(j + 1) * pair] = both.T.astype(bf16)
        lse_ref[0, :, at] = m_ref[...] + jnp.log(l_ref[...])
        return carry

    lax.fori_loop(0, length // BLOCK, query_block, 0)


def attend_forward(bounds, tokens, weight, bias, cosine, sine, docs):
    zsize, groups, rows, width = tokens.shape
    length = zsize * rows
    cols = weight.shape[2]
    heads = cols // HEAD_DIM
    pair = 2 * HEAD_DIM
    whole = lambda shape: pl.BlockSpec(shape, lambda i, *_: (0,) * len(shape))
    of_group = lambda shape: pl.BlockSpec(shape, lambda i, *_: (i,) + (0,) * (len(shape) - 1))
    like = jax.ShapeDtypeStruct
    return pl.pallas_call(
        attend_kernel,
        grid_spec=pltpu.PrefetchScalarGridSpec(
            num_scalar_prefetch=2,
            grid=(groups,),
            in_specs=[
                pl.BlockSpec((zsize, 1, rows, width), lambda i, *_: (0, i, 0, 0)),
                whole(weight.shape), whole(bias.shape),
                of_group((1, length, pair)), of_group((1, length, pair)), of_group((1, length, 1)),
            ],
            out_specs=[
                of_group((1, length, cols)),
                of_group((1, heads, length, pair)), of_group((1, heads, length, pair)), of_group((1, heads, length, pair)),
                of_group((1, heads, length)),
            ],
            scratch_shapes=[
                pltpu.VMEM((heads, HEAD_DIM, length), bf16),
                pltpu.VMEM((heads, BLOCK), f32), pltpu.VMEM((heads, BLOCK), f32),
                pltpu.VMEM((heads, HEAD_DIM, BLOCK), f32),
            ],
        ),
        out_shape=[
            like((groups, length, cols), bf16),
            like((groups, heads, length, pair), bf16), like((groups, heads, length, pair), bf16),
            like((groups, heads, length, pair), bf16), like((groups, heads, length), f32),
        ],
        compiler_params=pltpu.CompilerParams(vmem_limit_bytes=VMEM),
        cost_estimate=pl.CostEstimate(
            flops=groups * (2 * length * width * 3 * cols + 4 * length * length * cols),
            bytes_accessed=2 * length * width + 6 * width * cols + 8 * length * cols,
            transcendentals=length * length * heads,
        ),
    )(*bounds, tokens, weight, bias, cosine, sine, docs)


def attend_back_kernel(lo_ref, hi_ref, z_ref, q_ref, k_ref, v_ref, lse_ref, mixed_ref, cos_ref, sin_ref, tok_ref, w_ref, *refs):
    do_refs, refs = refs[:tok_ref.shape[0]], refs[tok_ref.shape[0]:]
    (back_ref, wgrad_ref, sum_ref, grad_ref, wsum_ref, dox_ref, kt_ref, delta_ref, dk_ref, dv_ref, dqt_ref) = refs
    group = pl.program_id(0)
    heads, length = q_ref.shape[1], q_ref.shape[2]
    pair = 2 * HEAD_DIM
    scale = HEAD_DIM ** (-0.5)
    blocks = length // BLOCK

    zsize, _, rows, _ = tok_ref.shape
    low_half = lax.broadcasted_iota(jnp.int32, (rows, pair), 1) < HEAD_DIM
    for step in range(zsize):
        at = pl.ds(pl.multiple_of(lax.rem(z_ref[0] + zsize - step, zsize) * rows, rows), rows)
        for j in range(heads // 2):
            upstream = do_refs[step][0, :, j * pair:(j + 1) * pair].astype(f32)
            product = (upstream * mixed_ref[0, at, j * pair:(j + 1) * pair].astype(f32)).T
            for h in range(2):
                head = 2 * j + h
                one = upstream if h == 0 else pltpu.roll(upstream, HEAD_DIM, 1)
                dox_ref[head, at, :] = jnp.where(low_half, one, 0.0).astype(bf16)
                delta_ref[head:head + 1, at] = jnp.sum(
                    product[h * HEAD_DIM:(h + 1) * HEAD_DIM], axis=0, keepdims=True
                )
                kt_ref[head, :, at] = k_ref[0, head, at, :].astype(f32).T[:HEAD_DIM].astype(bf16)
                dk_ref[head, at, :] = jnp.zeros((rows, pair), f32)
                dv_ref[head, at, :] = jnp.zeros((rows, pair), f32)

    @pl.when(group == 0)
    def _():
        sum_ref[...] = jnp.zeros(sum_ref.shape, f32)
        wsum_ref[...] = jnp.zeros(wsum_ref.shape, f32)

    def put(c, j, at, field):
        low = field.astype(bf16)
        grad_ref[c, at, j * pair:(j + 1) * pair] = low
        cols = pl.ds(j * pair, pair)
        sum_ref[c:c + 1, cols] = sum_ref[c:c + 1, cols] + jnp.sum(low.astype(f32), axis=0, keepdims=True)

    def back(field, at):
        return field * cos_ref[0, at, :] - turn_halves(field, sin_ref[0, at, :])

    def query_block(i, carry):
        at = pl.ds(pl.multiple_of(i * BLOCK, BLOCK), BLOCK)
        dqt_ref[...] = jnp.zeros(dqt_ref.shape, f32)

        def key_block(j, carry):
            keys_at = pl.ds(pl.multiple_of(j * BLOCK, BLOCK), BLOCK)
            every = range(heads)
            queries = [q_ref[0, h, at, :] for h in every]
            upstream = [dox_ref[h, at, :] for h in every]
            st = [scores_of(k_ref[0, h, keys_at, :], queries[h]) for h in every]
            dp = [scores_of(v_ref[0, h, keys_at, :], upstream[h]) for h in every]
            p = [jnp.exp(st[h] - lse_ref[0, h:h + 1, at]) for h in every]
            ds = [(p[h] * (dp[h] - delta_ref[h:h + 1, at])).astype(bf16) for h in every]
            dv = [jnp.dot(p[h].astype(bf16), upstream[h], preferred_element_type=f32) for h in every]
            dk = [jnp.dot(ds[h], queries[h], preferred_element_type=f32) for h in every]
            dq = [jnp.dot(kt_ref[h, :, keys_at], ds[h], preferred_element_type=f32) for h in every]
            for h in every:
                dv_ref[h, keys_at, :] = dv_ref[h, keys_at, :] + dv[h]
                dk_ref[h, keys_at, :] = dk_ref[h, keys_at, :] + dk[h]
                dqt_ref[h] = dqt_ref[h] + dq[h]
            return carry

        lax.fori_loop(lo_ref[group, i], hi_ref[group, i], key_block, 0)
        for j in range(heads // 2):
            both = jnp.concatenate([dqt_ref[2 * j], dqt_ref[2 * j + 1]], axis=0)
            put(0, j, at, back(both.T * scale, at))
        return carry

    lax.fori_loop(0, blocks, query_block, 0)

    def finish(i, carry):
        at = pl.ds(pl.multiple_of(i * BLOCK, BLOCK), BLOCK)
        low = lax.broadcasted_iota(jnp.int32, (BLOCK, pair), 1) < HEAD_DIM
        for j in range(heads // 2):
            field = jnp.where(low, dk_ref[2 * j, at, :], pltpu.roll(dk_ref[2 * j + 1, at, :], HEAD_DIM, 1))
            put(1, j, at, back(field, at))
            field = jnp.where(low, dv_ref[2 * j, at, :], pltpu.roll(dv_ref[2 * j + 1, at, :], HEAD_DIM, 1))
            put(2, j, at, field)
        return carry

    lax.fori_loop(0, blocks, finish, 0)

    def onward(i, carry):
        at = pl.ds(pl.multiple_of(i * rows, rows), rows)
        total = None
        x = tok_ref[i, 0]
        for c in range(3):
            grad = grad_ref[c, at, :]
            part = lax.dot_general(grad, w_ref[c], (((1,), (1,)), ((), ())), preferred_element_type=f32)
            total = part if total is None else total + part
            wsum_ref[c] += lax.dot_general(x, grad, (((0,), (0,)), ((), ())), preferred_element_type=f32)
        back_ref[0, i] = total.astype(bf16)
        return carry

    lax.fori_loop(0, zsize, onward, 0)

    @pl.when(group == pl.num_programs(0) - 1)
    def _():
        wgrad_ref[...] = wsum_ref[...].astype(bf16)


def attend_backward(bounds, zi, kept, mixed, upstream, cosine, sine, tokens, weight):
    queries, keys, values, lse = kept
    groups, heads, length, pair = queries.shape
    zsize, _, rows, width = tokens.shape
    cols = heads * HEAD_DIM
    whole = lambda shape: pl.BlockSpec(shape, lambda i, *_: (0,) * len(shape))
    of_group = lambda shape: pl.BlockSpec(shape, lambda i, *_: (i,) + (0,) * (len(shape) - 1))
    like = jax.ShapeDtypeStruct
    wide = (heads, length, pair)
    return pl.pallas_call(
        attend_back_kernel,
        grid_spec=pltpu.PrefetchScalarGridSpec(
            num_scalar_prefetch=3,
            grid=(groups,),
            in_specs=[of_group((1,) + wide)] * 3 + [
                of_group((1, heads, length)), of_group((1, length, cols)),
                of_group((1, length, pair)), of_group((1, length, pair)),
                pl.BlockSpec((zsize, 1, rows, width), lambda i, *_: (0, i, 0, 0)), whole(weight.shape),
            ] + [of_group((1, rows, cols))] * zsize,
            out_specs=[of_group((1, zsize, rows, width)), whole(weight.shape), whole((8, cols))],
            scratch_shapes=[
                pltpu.VMEM((3, length, cols), bf16), pltpu.VMEM(weight.shape, f32),
                pltpu.VMEM(wide, bf16), pltpu.VMEM((heads, HEAD_DIM, length), bf16), pltpu.VMEM((heads, length), f32),
                pltpu.VMEM(wide, f32), pltpu.VMEM(wide, f32), pltpu.VMEM((heads, HEAD_DIM, BLOCK), f32),
            ],
        ),
        out_shape=[
            like((groups, zsize, rows, width), bf16), like(weight.shape, bf16), like((8, cols), f32),
        ],
        compiler_params=pltpu.CompilerParams(vmem_limit_bytes=VMEM),
        cost_estimate=pl.CostEstimate(
            flops=groups * 10 * length * length * cols, bytes_accessed=24 * length * cols, transcendentals=length * length * heads
        ),
    )(*bounds, zi.reshape(1), queries, keys, values, lse, mixed, cosine, sine, tokens, weight, *upstream)


MESH_ID = pl.DeviceIdType.MESH
HBM = pl.BlockSpec(memory_space=pl.ANY)


def other(axis):
    return {axis: 1 - lax.axis_index(axis)}


def greet(zsize):
    z = lax.axis_index("z")
    barrier = pltpu.get_barrier_semaphore()
    for axis in CELL:
        pl.semaphore_signal(barrier, inc=1, device_id=other(axis), device_id_type=MESH_ID)

    @pl.when(z > 0)
    def _():
        pl.semaphore_signal(barrier, inc=1, device_id={"z": z - 1}, device_id_type=MESH_ID)

    @pl.when(z < zsize - 1)
    def _():
        pl.semaphore_signal(barrier, inc=1, device_id={"z": z + 1}, device_id_type=MESH_ID)

    peers = len(CELL) + jnp.where(z > 0, 1, 0) + jnp.where(z < zsize - 1, 1, 0)
    pl.semaphore_wait(barrier, peers)


def remote(src, dst, send_sem, recv_sem, device):
    return pltpu.make_async_remote_copy(
        src_ref=src, dst_ref=dst, send_sem=send_sem, recv_sem=recv_sem, device_id=device, device_id_type=MESH_ID
    )


def swap_kernel(zsize, to_rows, origin, target, held, local_sem, send, recv):
    groups = target.shape[0]
    rows, cols = (target.shape[1], target.shape[2] // zsize) if to_rows else (target.shape[1] // zsize, target.shape[2])
    z = lax.axis_index("z")

    def source(g, peer):
        if to_rows:
            return origin.at[g, pl.ds(pl.multiple_of(peer * rows, rows), rows), :]
        return origin.at[g, :, pl.ds(pl.multiple_of(peer * cols, cols), cols)]

    def place(g, peer):
        if to_rows:
            return target.at[g, :, pl.ds(pl.multiple_of(peer * cols, cols), cols)]
        return target.at[g, pl.ds(pl.multiple_of(peer * rows, rows), rows), :]

    def copy_to(g, step):
        peer = lax.rem(z + step, zsize)
        return remote(source(g, peer), place(g, z), send.at[step, g], recv.at[step, g], {"z": peer})

    def copy_from(g, step):
        peer = lax.rem(z + zsize - step, zsize)
        return remote(source(g, peer), place(g, peer), send.at[step, g], recv.at[step, g], {"z": peer})

    into = [pltpu.make_async_copy(source(g, z), held.at[g], local_sem.at[0, g]) for g in range(groups)]
    onward = [pltpu.make_async_copy(held.at[g], place(g, z), local_sem.at[1, g]) for g in range(groups)]
    for copy in into:
        copy.start()
    barrier = pltpu.get_barrier_semaphore()
    for step in range(1, zsize):
        peer = lax.rem(z + step, zsize)
        pl.semaphore_signal(barrier, inc=1, device_id={"z": peer}, device_id_type=MESH_ID)
    pl.semaphore_wait(barrier, zsize - 1)
    for g in range(groups):
        for step in range(1, zsize):
            copy_to(g, step).start()
    for g in range(groups):
        into[g].wait()
        onward[g].start()
    for g in range(groups):
        for step in range(1, zsize):
            copy_from(g, step).wait_recv()
        onward[g].wait()
    for g in range(groups):
        for step in range(1, zsize):
            copy_to(g, step).wait_send()


def swap(array, zsize, to_rows):
    groups, rows, cols = array.shape
    if to_rows:
        rows //= zsize
        shape = (groups, rows, zsize * cols)
    else:
        cols //= zsize
        shape = (groups, zsize * rows, cols)
    return pl.pallas_call(
        functools.partial(swap_kernel, zsize, to_rows),
        out_shape=jax.ShapeDtypeStruct(shape, bf16),
        in_specs=[HBM],
        out_specs=HBM,
        scratch_shapes=[
            pltpu.VMEM((groups, rows, cols), bf16),
            pltpu.SemaphoreType.DMA((2, groups)),
            pltpu.SemaphoreType.DMA((zsize, groups)),
            pltpu.SemaphoreType.DMA((zsize, groups)),
        ],
        compiler_params=pltpu.CompilerParams(
            collective_id=2 if to_rows else 3, has_side_effects=True, vmem_limit_bytes=VMEM
        ),
    )(array)


ORDERS = {"xy": ("x", "y"), "yx": ("y", "x")}


def gather_kernel(zsize, orders, *refs):
    n = len(orders)
    tok, bias, shards = refs[0], refs[1], refs[2:2 + n]
    tok_all, bias_all, wholes = refs[2 + n], refs[3 + n], refs[4 + n:4 + 2 * n]
    held = refs[4 + 2 * n:6 + 3 * n]
    local_sem, z_send, z_recv, p_send, p_recv = refs[6 + 3 * n:]
    z = lax.axis_index("z")
    c = lax.axis_index("core")
    place = [(lax.axis_index(o[0]), lax.axis_index(o[1])) for o in orders]

    sources = list(shards) + [tok, bias]
    targets = list(wholes) + [tok_all, bias_all]
    into = [pltpu.make_async_copy(sources[i], held[i], local_sem.at[0, i]) for i in range(n + 2)]
    local = [pltpu.make_async_copy(held[i], targets[i].at[z], local_sem.at[1, i]) for i in range(n + 2)]
    for copy in into:
        copy.start()
    greet(zsize)

    def line(item, src, step, side):
        to = z + 1 if side == 0 else z - 1
        if item < n:
            f, s = place[item]
            own = shards[item].at[c, f, s]
            dst = wholes[item].at[src, c, f, s]
        else:
            own = (tok, bias)[item - n]
            dst = (tok_all, bias_all)[item - n].at[src]
        return remote(
            own if step == 0 else dst, dst, z_send.at[side, item, step], z_recv.at[side, item, step], {"z": to}
        )

    def exchange(k, src, stage, slot):
        f, s = place[k]
        whole = wholes[k]
        ref = (whole.at[src, c, f, s], whole.at[src, c, f], whole.at[src, c])[stage]
        axis = (orders[k][1], orders[k][0], "core")[stage]
        return remote(ref, ref, p_send.at[slot, k, stage], p_recv.at[slot, k, stage], other(axis))

    def valid_from(side, step):
        return z - step - 1 >= 0 if side == 0 else z + step + 1 < zsize

    def source(side, step):
        return z - step - 1 if side == 0 else z + step + 1

    def has_next(side):
        return z < zsize - 1 if side == 0 else z > 0

    for side in range(2):

        @pl.when(has_next(side))
        def _():
            for item in range(n):
                line(item, z, 0, side).start()

    def stage_on(stage, step):
        for side in range(2):

            @pl.when(valid_from(side, step))
            def _():
                src = source(side, step)
                slot = side * (zsize - 1) + step
                for k in range(n):
                    exchange(k, src, stage - 1, slot).wait_recv()
                    if stage < 3:
                        exchange(k, src, stage, slot).start()

    def arrive(items, step):
        for side in range(2):

            @pl.when(valid_from(side, step))
            def _():
                src = source(side, step)
                for item in items:
                    line(item, src, step, side).wait_recv()
                    if step + 1 < zsize - 1:

                        @pl.when(has_next(side))
                        def _():
                            line(item, src, step + 1, side).start()

                    if item < n:
                        exchange(item, src, 0, side * (zsize - 1) + step).start()

    for copy, onward in zip(into, local):
        copy.wait()
        onward.start()
    for step in range(zsize - 1):
        arrive(range(n), step)
        if step == zsize - 2:
            for side in range(2):

                @pl.when(has_next(side))
                def _():
                    for item in range(n, n + 2):
                        line(item, z, 0, side).start()

        if step >= 1:
            stage_on(1, step - 1)
    for step in range(zsize - 1):
        if step == 0:
            stage_on(1, zsize - 2)
        stage_on(2, step)
        arrive(range(n, n + 2), step)
    for step in range(zsize - 1):
        stage_on(3, step)
    for copy in local:
        copy.wait()
    for side in range(2):

        @pl.when(has_next(side))
        def _():
            for item in range(n + 2):
                line(item, z, 0, side).wait_send()

        for step in range(zsize - 1):

            @pl.when(valid_from(side, step))
            def _():
                src = source(side, step)
                if step + 1 < zsize - 1:

                    @pl.when(has_next(side))
                    def _():
                        for item in range(n + 2):
                            line(item, src, step + 1, side).wait_send()

                for k in range(n):
                    for stage in range(3):
                        exchange(k, src, stage, side * (zsize - 1) + step).wait_send()


def gather_start(tokens, bias, weights, zsize):
    orders = [ORDERS[o] for o, _ in weights]
    shards = [w for _, w in weights]
    n = len(shards)
    stack = lambda a: jax.ShapeDtypeStruct((zsize,) + a.shape, a.dtype)
    return pl.pallas_call(
        functools.partial(gather_kernel, zsize, orders),
        out_shape=[stack(tokens), stack(bias)] + [stack(w) for w in shards],
        in_specs=[HBM] * (n + 2),
        out_specs=[HBM] * (n + 2),
        scratch_shapes=[pltpu.VMEM(a.shape, a.dtype) for a in shards + [tokens, bias]] + [
            pltpu.SemaphoreType.DMA((2, n + 2)),
            pltpu.SemaphoreType.DMA((2, n + 2, zsize - 1)),
            pltpu.SemaphoreType.DMA((2, n + 2, zsize - 1)),
            pltpu.SemaphoreType.DMA((2 * (zsize - 1), n, 3)),
            pltpu.SemaphoreType.DMA((2 * (zsize - 1), n, 3)),
        ],
        compiler_params=pltpu.CompilerParams(
            collective_id=0, has_side_effects=True, vmem_limit_bytes=VMEM
        ),
    )(tokens, bias, *shards)


def add_rows(dst, src):
    rows = dst.shape[0]
    step = min(rows, 32)

    def body(i, carry):
        at = pl.ds(pl.multiple_of(i * step, step), step)
        dst[at, :] = dst[at, :] + src[at, :]
        return carry

    lax.fori_loop(0, rows // step, body, 0)


def reduce_kernel(zsize, orders, w, *refs):
    n = 3
    p = len(orders) - n
    items = n + p
    pieces, came, refs = refs[:p], refs[p:2 * p], refs[2 * p:]
    parts, backs, small = refs[:n], refs[n], refs[n + 1]
    pos = n + 2
    piece_out, part_out, back_out = refs[pos:pos + p], refs[pos + p:pos + p + n], refs[pos + p + n]
    small_out = refs[pos + p + n + 1]
    outs = list(part_out) + list(piece_out)
    pos += p + n + 2
    mine = refs[pos:pos + items + w]
    pos += items + w
    got_c, got_1, got_2 = refs[pos:pos + n], refs[pos + n:pos + n + items], refs[pos + n + items:pos + n + 2 * items]
    pos += n + 2 * items
    lines = [0] + list(range(n, items + w))
    line_backs = list(range(items, items + w))
    got_z = dict(zip(lines, refs[pos:pos + len(lines)]))
    pos += len(lines)
    small_mine, small_got, small_line, small_total, part_line, part_total = refs[pos:pos + 6]
    (local_sem, send, recv, z_send, z_recv, s_send, s_recv, t_send, t_recv, g_send, g_recv, end_sem) = refs[pos + 6:]
    z = lax.axis_index("z")
    c = lax.axis_index("core")
    orders = orders[p:] + orders[:p]
    place = [(lax.axis_index(o[0]), lax.axis_index(o[1])) for o in orders]
    turn = []
    for i in range(zsize // 2):
        turn += [i, zsize - 1 - i]
    few = parts[1].shape[0]
    steps = [(1, b) for b in range(few)] + [(2, 0)] + [(0, b) for b in turn]

    def load(k, b):
        src = parts[k].at[b, c] if k < n else pieces[k - n].at[b] if k < items else backs.at[k - items, b]
        return pltpu.make_async_copy(src, mine[k].at[b], local_sem.at[k, b])

    def load_came(k, b):
        return pltpu.make_async_copy(came[k - n].at[b], got_1[k].at[b], local_sem.at[items + w + 1 + k - n, b])

    load_small = pltpu.make_async_copy(small, small_mine.at[0], local_sem.at[items + w, 0])

    def half(k, b, stage):
        f, s = place[k]
        if stage == 0:
            src, dst, axis = parts[k].at[b, 1 - c], got_c[k].at[b], "core"
        elif stage == 1:
            src, dst, axis = mine[k].at[b, 1 - f], got_1[k].at[b], orders[k][0]
        else:
            held = mine[k].at[b, f] if k < n else mine[k].at[b]
            src, dst, axis = held.at[1 - s], got_2[k].at[b], orders[k][1]
        return remote(src, dst, send.at[stage, k, b], recv.at[stage, k, b], other(axis))

    def own(k, b):
        if k >= items:
            return mine[k].at[b]
        f, s = place[k]
        return mine[k].at[b, s] if k >= n else mine[k].at[b, f, s]

    def hop(k, b, side):
        to = z + 1 if side == 0 else z - 1
        at = b if side == 0 else jnp.where(b == z - 1, zsize, b)
        return remote(own(k, b), got_z[k].at[at], z_send.at[k, b], z_recv.at[k, at], {"z": to})

    def take(k, b, side):
        at = b if side == 0 else jnp.where(b == z, zsize, b)
        ref = got_z[k].at[at]
        sender = z - 1 if side == 0 else z + 1
        remote(own(k, b), ref, z_send.at[k, b], z_recv.at[k, at], {"z": sender}).wait_recv()
        add_rows(own(k, b), ref)

    def line_start(ks, messages):
        for side in range(2):

            @pl.when(z == (0 if side == 0 else zsize - 1))
            def _():
                for i in messages:
                    for k in ks:
                        hop(k, zsize - 1 - i if side == 0 else i, side).start()

    def line_slot(ks, slot):
        for i in range(slot):
            for side in range(2):
                b = zsize - 1 - i if side == 0 else i

                @pl.when(z == (slot - i if side == 0 else zsize - 1 - slot + i))
                def _():
                    for k in ks:
                        take(k, b, side)

                        @pl.when(z < b if side == 0 else z > b)
                        def _():
                            hop(k, b, side).start()

    def small_swap(stage):
        return remote(
            small_mine.at[stage], small_got.at[stage], s_send.at[stage], s_recv.at[stage], other(CELL[stage])
        )

    def small_step(stage):
        small_swap(stage).wait_recv()
        small_mine[stage + 1] = small_mine[stage] + small_got[stage]
        if stage < 2:
            small_swap(stage + 1).start()

    last = len(CELL)
    last_part = own(2, 0)

    def total_copy(item, way):
        line, total = ((small_line, small_total), (part_line, part_total))[item]
        src = (small_mine.at[last], last_part)[item] if way == 0 else total
        dst = line if way == 0 else total
        to = z + 1 if way == 0 else z - 1
        return remote(src, dst, t_send.at[item, way], t_recv.at[item, way], {"z": to})

    def total_step(tick):
        if 0 <= tick < zsize:

            @pl.when(z == tick)
            def _():
                if tick > 0:
                    for item in range(2):
                        total_copy(item, 0).wait_recv()
                    small_mine[last] = small_mine[last] + small_line[...]
                    add_rows(last_part, part_line)
                if tick < zsize - 1:
                    for item in range(2):
                        total_copy(item, 0).start()
                else:
                    small_total[...] = small_mine[last]
                    part_total[...] = last_part[...]

        back_tick = tick - (zsize - 1)
        if 0 <= back_tick < zsize:

            @pl.when(z == zsize - 1 - back_tick)
            def _():
                if back_tick > 0:
                    for item in range(2):
                        total_copy(item, 1).wait_recv()
                if back_tick < zsize - 1:
                    for item in range(2):
                        total_copy(item, 1).start()

    line_pieces = list(range(n, items))
    piece_steps = [(k, b) for b in turn for k in line_pieces]
    for b in turn:
        for k in line_backs:
            load(k, b).start()
    for k, b in piece_steps:
        load(k, b).start()
        load_came(k, b).start()
    for k, b in steps:
        load(k, b).start()
    load_small.start()
    greet(zsize)
    for k, b in steps:
        half(k, b, 0).start()
    for b in turn:
        for k in line_backs:
            load(k, b).wait()
    line_start(line_backs, [0])
    load_small.wait()
    small_swap(0).start()

    def stage_1(k, b):
        f, s = place[k]
        load(k, b).wait()
        half(k, b, 0).wait_recv()
        for i in range(2):
            add_rows(mine[k].at[b, 1 - f, i], got_c[k].at[b, 1 - f, i])
        half(k, b, 1).start()
        for i in range(2):
            add_rows(mine[k].at[b, f, i], got_c[k].at[b, f, i])

    def stage_2(k, b):
        f, s = place[k]
        held = mine[k].at[b, f] if k < n else mine[k].at[b]
        if k < n:
            half(k, b, 1).wait_recv()
        else:
            load(k, b).wait()
            load_came(k, b).wait()
        add_rows(held.at[1 - s], got_1[k].at[b, 1 - s])
        half(k, b, 2).start()
        add_rows(held.at[s], got_1[k].at[b, s])

    def stage_3(k, b):
        half(k, b, 2).wait_recv()
        add_rows(own(k, b), got_2[k].at[b])

    def result(k, b):
        return part_total if k == 2 else own(k, b)

    def out_of(k, b):
        return outs[k].at[b] if k == 1 else outs[k]

    def put(k, b, slot):
        f, s = place[k]
        return pltpu.make_async_copy(result(k, b), out_of(k, b).at[c, f, s], end_sem.at[slot])

    def spread(k, b, stage, slot):
        f, s = place[k]
        out = out_of(k, b)
        dst = (out.at[c, f, s], out.at[c, f], out.at[c])[stage]
        src = result(k, b) if stage == 0 else dst
        axis = (orders[k][1], orders[k][0], "core")[stage]
        return remote(src, dst, g_send.at[slot, stage], g_recv.at[slot, stage], other(axis))

    spreads = [
        [(1, b, b) for b in range(few)],
        [(k, z, few + k - n) for k in line_pieces],
        [(0, z, few + p), (2, 0, few + p + 1)],
    ]

    def spread_step(group, stage):
        for k, b, slot in spreads[group]:
            if stage == 0:
                spread(k, b, 0, slot).start()
                put(k, b, slot).start()
                continue
            if stage == 1:
                put(k, b, slot).wait()
            spread(k, b, stage - 1, slot).wait_recv()
            if stage < 3:
                spread(k, b, stage, slot).start()

    def sent(ks):
        for b in range(zsize):

            @pl.when(z != b)
            def _():
                for k in ks:
                    hop(k, b, 0).wait_send()

    at_end = jnp.logical_or(z == 0, z == zsize - 1)
    for k, b in piece_steps:
        stage_2(k, b)
    for k, b in steps:
        stage_1(k, b)
    small_step(0)
    for k, b in piece_steps:
        stage_3(k, b)
    line_start(line_pieces, range(zsize - 1))
    for k, b in steps:
        stage_2(k, b)
    small_step(1)
    line_slot(line_backs, 1)
    for k, b in steps:
        stage_3(k, b)
    small_step(2)
    spread_step(0, 0)
    line_start([0], range(zsize - 1))
    total_step(0)

    @pl.when(at_end)
    def _():
        sent(line_pieces)

    line_start(line_backs, range(1, zsize - 1))
    ticks = list(range(1, 2 * zsize - 1))
    later = [(0, 1), (0, 2), (0, 3)]

    def fill(group_stages, count):
        for _ in range(count):
            if group_stages:
                spread_step(*group_stages.pop(0))

    for slot in range(1, zsize):
        line_slot(line_pieces, slot)
        total_step(ticks.pop(0))
        fill(later, 1)
        if slot >= 2:
            line_slot([0], slot - 1)
    fill(later, 3)
    spread_step(1, 0)
    later = [(1, 1), (1, 2), (1, 3)]
    total_step(ticks.pop(0))
    line_slot([0], zsize - 1)
    for slot in range(2, zsize - 1):
        line_slot(line_backs, slot)
        fill(later, 1)
    for tick in ticks:
        total_step(tick)
    spread_step(2, 0)
    fill(later, 1)
    spread_step(2, 1)
    fill(later, 1)
    spread_step(2, 2)
    fill(later, 3)
    line_slot(line_backs, zsize - 1)
    finish_back = [
        pltpu.make_async_copy(mine[k].at[z], back_out.at[k - items], local_sem.at[k, 0]) for k in line_backs
    ]
    for copy in finish_back:
        copy.start()
    finish_small = pltpu.make_async_copy(small_total, small_out, local_sem.at[items + w, 0])
    finish_small.start()
    spread_step(2, 3)
    for copy in finish_back:
        copy.wait()
    finish_small.wait()
    sent([0] + line_backs)

    @pl.when(jnp.logical_not(at_end))
    def _():
        sent(line_pieces)

    for way in range(2):

        @pl.when(z < zsize - 1 if way == 0 else z > 0)
        def _():
            for item in range(2):
                total_copy(item, way).wait_send()

    for k, b in steps:
        for stage in range(3):
            half(k, b, stage).wait_send()
    for k, b in piece_steps:
        half(k, b, 2).wait_send()
    for stage in range(3):
        small_swap(stage).wait_send()
    for group in spreads:
        for k, b, slot in group:
            for stage in range(3):
                spread(k, b, stage, slot).wait_send()


def reduce_end(pieces, parts, backs, small, zsize):
    orders = [ORDERS[o[0]] for o in pieces + parts]
    piece_arrays = [a for _, a, _ in pieces]
    came = [a for _, _, a in pieces]
    arrays = [a for _, a in parts]
    p, n, w = len(pieces), len(parts), backs.shape[0]
    shapes = [a.shape for a in arrays]
    like = jax.ShapeDtypeStruct
    outs = [like((2, 2, 2) + a.shape[2:], bf16) for a in piece_arrays]
    outs += [like(s if i == 1 else s[1:], bf16) for i, s in enumerate(shapes)]
    outs += [like((w,) + backs.shape[2:], bf16), like(small.shape, f32)]
    held = lambda shape: pltpu.VMEM(shape, bf16)
    scratch = [held((s[0],) + s[2:]) for s in shapes]
    scratch += [held(a.shape) for a in piece_arrays] + [held(backs.shape[1:])] * w
    scratch += [held((s[0],) + s[2:]) for s in shapes]
    scratch += [held((s[0],) + s[3:]) for s in shapes] + [held(a.shape) for a in piece_arrays]
    scratch += [held((s[0],) + s[4:]) for s in shapes] + [held(a.shape[:1] + a.shape[2:]) for a in piece_arrays]
    scratch += [held((zsize + 1,) + shapes[0][4:])]
    scratch += [held((zsize + 1,) + a.shape[2:]) for a in piece_arrays] + [held((zsize + 1,) + backs.shape[2:])] * w
    scratch += [pltpu.VMEM((4,) + small.shape, f32), pltpu.VMEM((3,) + small.shape, f32)]
    scratch += [pltpu.VMEM(small.shape, f32)] * 2 + [held(shapes[2][4:])] * 2
    dma = pltpu.SemaphoreType.DMA
    most = max(zsize, shapes[1][0])
    ends = shapes[1][0] + p + 2
    scratch += [
        dma((n + 2 * p + w + 1, most)), dma((3, n + p, most)), dma((3, n + p, most)),
        dma((n + p + w, zsize)), dma((n + p + w, zsize + 1)),
        dma((3,)), dma((3,)), dma((2, 2)), dma((2, 2)), dma((ends, 3)), dma((ends, 3)), dma((ends,)),
    ]
    return pl.pallas_call(
        functools.partial(reduce_kernel, zsize, orders, w),
        out_shape=outs,
        in_specs=[HBM] * (n + 2 * p + 2),
        out_specs=[HBM] * (n + p + 2),
        scratch_shapes=scratch,
        compiler_params=pltpu.CompilerParams(
            collective_id=1, has_side_effects=True, vmem_limit_bytes=VMEM
        ),
    )(*piece_arrays, *came, *arrays, backs, small)


def gelu_pair(v):
    size = jnp.abs(v)
    t = 1.0 / (1.0 + (0.3275911 * 0.5 ** 0.5) * size)
    bell = jnp.exp(-0.5 * (v * v))
    poly = t * (0.254829592 + t * (-0.284496736 + t * (1.421413741 + t * (-1.453152027 + t * 1.061405429))))
    tail = 0.5 * poly * bell
    cdf = jnp.where(v >= 0.0, 1.0 - tail, tail)
    return v * cdf, cdf + v * (bell * (1.0 / (2.0 * math.pi) ** 0.5))


def ffn_kernel(x_ref, up_ref, bias_ref, down_ref, active_ref, slope_ref, sum_ref):
    rows = x_ref.shape[0]
    part = rows // 2

    @pl.when(pl.program_id(0) == 0)
    def _():
        sum_ref[...] = jnp.zeros(sum_ref.shape, f32)

    for i in range(2):
        at = pl.ds(i * part, part)
        hidden = jnp.dot(x_ref[at, :], up_ref[0], preferred_element_type=f32) + bias_ref[0]
        active, slope = gelu_pair(hidden)
        active = active.astype(bf16)
        active_ref[0, at, :] = active
        slope_ref[0, at, :] = slope.astype(bf16)
        sum_ref[at, :] += jnp.dot(active, down_ref[0], preferred_element_type=f32)


def ffn_forward(normed_low, up_all, up_bias, down_all):
    zsize, width, units = up_all.shape
    rows = normed_low.shape[0]
    tile = units // 2
    like = jax.ShapeDtypeStruct
    tiles = pl.BlockSpec((1, rows, tile), lambda s: (s // 2, 0, s % 2))
    return pl.pallas_call(
        ffn_kernel,
        grid=(2 * zsize,),
        in_specs=[
            pl.BlockSpec((rows, width), lambda s: (0, 0)),
            pl.BlockSpec((1, width, tile), lambda s: (s // 2, 0, s % 2)),
            pl.BlockSpec((1, 1, tile), lambda s: (s // 2, 0, s % 2)),
            pl.BlockSpec((1, tile, width), lambda s: (s // 2, s % 2, 0)),
        ],
        out_specs=[tiles, tiles, pl.BlockSpec((rows, width), lambda s: (0, 0))],
        out_shape=[
            like((zsize, rows, units), bf16), like((zsize, rows, units), bf16), like((rows, width), f32),
        ],
        compiler_params=pltpu.CompilerParams(vmem_limit_bytes=VMEM),
    )(normed_low, up_all, up_bias[:, None, :], down_all)


def ffn_back_kernel(core_ref, second_ref, normed_ref, up_ref, down_ref, active_ref, slope_ref,
                    give_up_ref, keep_up_ref, give_down_ref, keep_down_ref, back_ref, bias_ref, turned_ref):
    s = pl.program_id(0)
    half = turned_ref.shape[0] // 2
    c = core_ref[0]

    @pl.when(s == 0)
    def _():
        back_ref[...] = jnp.zeros(back_ref.shape, f32)
        turned_ref[...] = normed_ref[...].T

    second = second_ref[...]
    upstream = lax.dot_general(second, down_ref[0], (((1,), (1,)), ((), ())), preferred_element_type=f32)
    grad = (upstream * slope_ref[0].astype(f32)).astype(bf16)
    bias_ref[0] = jnp.sum(grad.astype(f32), axis=0, keepdims=True)
    down = lax.dot_general(active_ref[0], second, (((0,), (0,)), ((), ())), preferred_element_type=f32).astype(bf16)

    @pl.when(s % 2 == 0)
    def _():
        give_down_ref[0] = down

    @pl.when(s % 2 == 1)
    def _():
        keep_down_ref[0] = down

    back_ref[...] += lax.dot_general(grad, up_ref[0], (((1,), (1,)), ((), ())), preferred_element_type=f32)
    give = turned_ref[pl.ds(pl.multiple_of((1 - c) * half, half), half), :]
    give_up_ref[0] = jnp.dot(give, grad, preferred_element_type=f32).astype(bf16)
    keep = turned_ref[pl.ds(pl.multiple_of(c * half, half), half), :]
    keep_up_ref[0] = jnp.dot(keep, grad, preferred_element_type=f32).astype(bf16)


def ffn_backward(core, second_low, normed_low, up_all, down_all, active, slope):
    zsize, width, units = up_all.shape
    rows = normed_low.shape[0]
    tile = units // 2
    like = jax.ShapeDtypeStruct
    part = lambda s, c: (1 - c[0] + (2 * c[0] - 1) * (s % 2))
    whole = pl.BlockSpec((rows, width), lambda s, c: (0, 0))
    tiles = pl.BlockSpec((1, rows, tile), lambda s, c: (s // 2, 0, part(s, c)))
    up_half = pl.BlockSpec((1, width // 2, tile), lambda s, c: (s // 2, 0, part(s, c)))
    down_half = pl.BlockSpec((1, tile, width), lambda s, c: (s // 2, 0, 0))
    return pl.pallas_call(
        ffn_back_kernel,
        grid_spec=pltpu.PrefetchScalarGridSpec(
            num_scalar_prefetch=1,
            grid=(2 * zsize,),
            in_specs=[
                whole, whole,
                pl.BlockSpec((1, width, tile), lambda s, c: (s // 2, 0, part(s, c))),
                pl.BlockSpec((1, tile, width), lambda s, c: (s // 2, part(s, c), 0)),
                tiles, tiles,
            ],
            out_specs=[
                up_half, up_half, down_half, down_half, whole,
                pl.BlockSpec((1, 1, tile), lambda s, c: (s // 2, 0, part(s, c))),
            ],
            scratch_shapes=[pltpu.VMEM((width, rows), bf16)],
        ),
        out_shape=[
            like((zsize, width // 2, units), bf16), like((zsize, width // 2, units), bf16),
            like((zsize, tile, width), bf16), like((zsize, tile, width), bf16),
            like((rows, width), f32), like((zsize, 1, units), f32),
        ],
        compiler_params=pltpu.CompilerParams(vmem_limit_bytes=VMEM),
    )(core, second_low, normed_low, up_all, down_all, active, slope)


PAIR = [(0, 1), (1, 0)]


def first_halving(got, keep, order):
    zsize, half, cols = keep.shape
    shape = (zsize, 2, 2, half // 4, cols)
    got, keep = got.reshape(shape), keep.reshape(shape)
    i = lax.axis_index(ORDERS[order][0])
    pick = lambda array, j: lax.dynamic_index_in_dim(array, j, 1, keepdims=False)
    return pick(keep, 1 - i) + pick(got, 1 - i), pick(keep, i) + pick(got, i)


def widen_kernel(up_ref, down_ref, out_ref, qkv_ref, first_ref, back_ref, up_o, down_o, out_o, qkv_o, first_o):
    for source, target in ((up_ref, up_o), (down_ref, down_o), (out_ref, out_o), (qkv_ref, qkv_o)):
        target[...] = source[...].astype(f32)
    first_o[...] = first_ref[...] + back_ref[...].astype(f32)


def widen(up, down, out, qkv, first, back):
    steps = 8

    def rows_of(array):
        return pl.BlockSpec((array.shape[0] // steps, array.shape[1]), lambda i: (i, 0))

    arrays = [up, down, out]
    specs = [rows_of(a) for a in arrays]
    specs.append(pl.BlockSpec((3, qkv.shape[1] // steps, qkv.shape[2]), lambda i: (0, i, 0)))
    specs.append(rows_of(first))
    return pl.pallas_call(
        widen_kernel,
        grid=(steps,),
        in_specs=specs + [rows_of(back)],
        out_specs=specs,
        out_shape=[jax.ShapeDtypeStruct(a.shape, f32) for a in arrays + [qkv, first]],
        compiler_params=pltpu.CompilerParams(vmem_limit_bytes=VMEM),
    )(up, down, out, qkv, first, back)


def per_device(blocks, tokens, segments, qkv_weight, qkv_bias, out_weight, out_bias, gain_one, shift_one,
               up_weight, up_bias, down_weight, down_bias, gain_two, shift_two, proj_weight, out_grad, embed_grad):
    groups, local_rows, model_width = tokens.shape
    length = segments.shape[1]
    zsize = length // local_rows
    head_cols = qkv_weight.shape[2]
    units_here = up_weight.shape[1]
    rows = groups * local_rows
    zi = lax.axis_index("z")
    cosine, sine = rotary_tables(doc_positions(segments))
    firsts = segments[:, ::BLOCK]
    lasts = segments[:, BLOCK - 1::BLOCK]
    bounds = (
        jnp.sum(segments[:, None, :] < firsts[:, :, None], axis=2, dtype=jnp.int32) // BLOCK,
        (jnp.sum(segments[:, None, :] <= lasts[:, :, None], axis=2, dtype=jnp.int32) + BLOCK - 1) // BLOCK,
    )
    docs = segments[:, :, None]

    def cut(array, rows_at):
        shape = array.shape
        return array.reshape(shape[:rows_at] + (2, 2, 2, shape[rows_at] // 8) + shape[rows_at + 1:])

    token_rows = tokens.reshape(rows, model_width)
    token_blocks, bias_blocks, out_all, up_all, down_all = gather_start(
        token_rows,
        up_bias.reshape(8, units_here // 8),
        [("xy", cut(out_weight, 0)), ("xy", cut(up_weight, 0)), ("yx", cut(down_weight, 0))],
        zsize,
    )
    token_blocks = token_blocks.reshape(zsize, groups, local_rows, model_width)
    out_all = out_all.reshape(model_width, model_width)
    up_all = up_all.reshape(zsize, model_width, units_here)
    down_all = down_all.reshape(zsize, units_here, model_width)
    full_up_bias = bias_blocks.reshape(zsize, units_here)

    own_mixed, *kept = attend_forward(bounds, token_blocks, qkv_weight, qkv_bias, cosine, sine, docs)
    mixed = swap(own_mixed, zsize, True).reshape(rows, model_width)

    first_sum = tokens.reshape(rows, model_width).astype(f32) + (
        jnp.dot(mixed, out_all, preferred_element_type=f32) + out_bias
    )
    normed, scaled_one, inv_one = norm_forward(first_sum, gain_one, shift_one)
    normed_low = normed.astype(bf16)
    active, slope, ffn = ffn_forward(normed_low, up_all, full_up_bias, down_all)
    second_sum = normed + (ffn + down_bias)
    result, scaled_two, inv_two = norm_forward(second_sum, gain_two, shift_two)
    result_low = result.astype(bf16)
    embedded = jnp.dot(result_low, proj_weight, preferred_element_type=f32).astype(bf16)
    embed_rows = embed_grad.reshape(rows, -1)
    grad_result = out_grad.reshape(rows, model_width).astype(f32) + jnp.einsum(
        "np,dp->nd", embed_rows, proj_weight, preferred_element_type=f32
    )
    proj_grad = jnp.einsum("nd,np->dp", result_low, embed_rows, preferred_element_type=f32)
    grad_second, gain_two_grad, shift_two_grad = norm_backward(grad_result, scaled_two, inv_two, gain_two)
    second_low = grad_second.astype(bf16)
    down_bias_grad = jnp.sum(second_low.astype(f32), axis=0)
    core = lax.axis_index("core").reshape(1)
    give_up, keep_up, give_down, keep_down, ffn_back, up_bias_grad = ffn_backward(
        core, second_low, normed_low, up_all, down_all, active, slope
    )
    got_down = lax.ppermute(give_down, "core", PAIR)
    got_up = lax.ppermute(give_up, "core", PAIR)
    grad_normed = grad_second + ffn_back
    grad_first, gain_one_grad, shift_one_grad = norm_backward(grad_normed, scaled_one, inv_one, gain_one)
    first_low = grad_first.astype(bf16)
    out_bias_grad = jnp.sum(first_low.astype(f32), axis=0)
    out_grad_w = jnp.einsum("nh,nd->hd", mixed, first_low, preferred_element_type=f32).astype(bf16)
    grad_mixed = jnp.einsum("nd,hd->nh", first_low, out_all, preferred_element_type=f32).astype(bf16)
    grad_mixed = grad_mixed.reshape(groups, local_rows, model_width)
    upstream = []
    for step in range(zsize):
        part = lax.dynamic_slice_in_dim(grad_mixed, lax.rem(zi + step, zsize) * head_cols, head_cols, 2)
        ring = [(i, (i + step) % zsize) for i in range(zsize)]
        upstream.append(lax.ppermute(part, "z", ring) if step else part)
    send_down, keep_down = first_halving(got_down, keep_down, "yx")
    send_up, keep_up = first_halving(got_up, keep_up, "xy")
    upstream, send_down, send_up = lax.optimization_barrier((tuple(upstream), send_down, send_up))
    got_down = lax.ppermute(send_down, ORDERS["yx"][0], PAIR)
    got_up = lax.ppermute(send_up, ORDERS["xy"][0], PAIR)
    backs, qkv_weight_grad, qkv_bias_grad = attend_backward(
        bounds, zi, kept, own_mixed, upstream, cosine, sine, token_blocks, qkv_weight
    )
    backs, got_down, got_up = lax.optimization_barrier((backs, got_down, got_up))
    qkv_bias_grad = qkv_bias_grad[:3]
    small = jnp.concatenate(
        [
            out_bias_grad, gain_one_grad, shift_one_grad, down_bias_grad, gain_two_grad, shift_two_grad,
            up_bias_grad.reshape(-1),
            lax.dynamic_update_slice(
                jnp.zeros((zsize, 3 * head_cols), f32), qkv_bias_grad.reshape(1, -1), (zi, 0)
            ).reshape(-1),
        ]
    )
    proj_cols = proj_grad.shape[1]
    proj_grad = jnp.pad(proj_grad.astype(bf16), ((0, 0), (0, -proj_cols % 128)))
    up_grad, down_grad, out_grad_w, qkv_weight_grad, proj_grad, back, small = reduce_end(
        [("xy", keep_up, got_up), ("yx", keep_down, got_down)],
        [
            ("xy", cut(out_grad_w.reshape(zsize, head_cols, model_width), 1)),
            ("yx", cut(qkv_weight_grad, 1)),
            ("xy", cut(proj_grad[None], 1)),
        ],
        backs,
        small.reshape(8, -1),
        zsize,
    )
    qkv_weight_grad = qkv_weight_grad.reshape(qkv_weight.shape)
    proj_grad = proj_grad.reshape(model_width, -1)[:, :proj_cols].astype(f32)
    out_grad_w = out_grad_w.reshape(out_weight.shape)
    up_grad = up_grad.reshape(up_weight.shape)
    down_grad = down_grad.reshape(down_weight.shape)
    if blocks > 1:
        down_grad, up_grad, out_grad_w, qkv_weight_grad = lax.psum(
            (down_grad, up_grad, out_grad_w, qkv_weight_grad), ("xb", "yb")
        )
        small, proj_grad = lax.psum((small, proj_grad), ("xb", "yb"))
    small = small.reshape(-1)
    up_grad, down_grad, out_grad_w, qkv_weight_grad, tokens_grad = widen(
        up_grad, down_grad, out_grad_w, qkv_weight_grad, grad_first, back.reshape(rows, model_width)
    )
    base = 6 * model_width
    vec = [small[i * model_width:(i + 1) * model_width] for i in range(6)]
    up_bias_grad = lax.dynamic_slice(small, (base + zi * units_here,), (units_here,))
    qkv_bias_grad = lax.dynamic_slice(
        small, (base + zsize * units_here + zi * 3 * head_cols,), (3 * head_cols,)
    ).reshape(3, head_cols)
    shape3 = (groups, local_rows, model_width)
    return (
        result_low.reshape(shape3),
        embedded.reshape(groups, local_rows, -1),
        tokens_grad.reshape(shape3),
        qkv_weight_grad,
        qkv_bias_grad,
        out_grad_w,
        vec[0], vec[1], vec[2],
        up_grad,
        up_bias_grad,
        down_grad,
        vec[3], vec[4], vec[5],
        proj_grad,
    )


def solution(mesh):
    dp_size, zsize = mesh.shape["dp"], mesh.shape["tensor"]
    side = math.isqrt(dp_size // 2) // 2
    cut = Mesh(mesh.devices.reshape(side, 2, side, 2, 2, zsize), DP + ("z",))
    rows3 = P(DP, "z", None)
    in_specs = (
        rows3, P(DP, None), P(None, None, "z"), P(None, "z"), P("z", None), P(), P(), P(),
        P(None, "z"), P("z"), P("z", None), P(), P(), P(), P(), rows3, rows3,
    )
    out_specs = (
        rows3, rows3, rows3, P(None, None, "z"), P(None, "z"), P("z", None), P(), P(), P(),
        P(None, "z"), P("z"), P("z", None), P(), P(), P(), P(),
    )

    def run(*args):
        return per_device(side * side, *args)

    return jax.shard_map(run, mesh=cut, in_specs=in_specs, out_specs=out_specs, check_vma=False)
```

```python
import functools
import math

import jax
import jax.numpy as jnp
from jax import lax
from jax.experimental import pallas as pl
from jax.experimental.pallas import tpu as pltpu
from jax.sharding import Mesh
from jax.sharding import PartitionSpec as P

HEAD_DIM = 64
eps = 1e-05
DP = ("xb", "x", "yb", "y", "core")
CELL = ("x", "y", "core")
ALL = DP + ("z",)
f32 = jnp.float32
bf16 = jnp.bfloat16
VMEM = 60 * 1024 * 1024


def doc_positions(segment_rows):
    below = segment_rows[:, None, :] < jnp.arange(4, dtype=jnp.int32)[None, :, None]
    starts = jnp.sum(below, axis=2, dtype=jnp.int32)
    row_index = jnp.arange(segment_rows.shape[1], dtype=jnp.int32)[None]
    start = starts[:, 3:4]
    for doc in (2, 1, 0):
        start = jnp.where(segment_rows == doc, starts[:, doc:doc + 1], start)
    return row_index - start


def rotary_tables(positions):
    half_dim = HEAD_DIM // 2
    lane = jnp.arange(2 * HEAD_DIM, dtype=jnp.int32)
    exponent = (lane % half_dim).astype(f32) * (2.0 / HEAD_DIM)
    frequency = jnp.exp(-exponent * math.log(10000.0))
    sign = jnp.where(lane % HEAD_DIM < half_dim, -1.0, 1.0)
    angles = positions.astype(f32)[..., None] * frequency
    return (jnp.cos(angles), jnp.sin(angles) * sign)


def norm_forward(field, gain, shift):
    row_mean = jnp.mean(field, axis=-1, keepdims=True)
    centred = field - row_mean
    variance = jnp.mean(centred * centred, axis=-1, keepdims=True)
    inv_std = lax.rsqrt(variance + eps)
    scaled = centred * inv_std
    return (scaled * gain + shift, scaled, inv_std)


def norm_backward(upstream, scaled, inv_std, gain):
    grad_scaled = upstream * gain
    grad_input = inv_std * (
        grad_scaled
        - jnp.mean(grad_scaled, axis=-1, keepdims=True)
        - scaled * jnp.mean(grad_scaled * scaled, axis=-1, keepdims=True)
    )
    return (grad_input, jnp.sum(upstream * scaled, axis=0), jnp.sum(upstream, axis=0))


BLOCK = 256


def turn_halves(field, sign_sine):
    lane = lax.broadcasted_iota(jnp.int32, field.shape, 1)
    half = HEAD_DIM // 2
    width = field.shape[1]
    swapped = jnp.where(lane % HEAD_DIM < half, pltpu.roll(field, width - half, 1), pltpu.roll(field, half, 1))
    return swapped * sign_sine


def scores_of(keys, queries):
    return lax.dot_general(keys, queries, (((1,), (1,)), ((), ())), preferred_element_type=f32)


def attend_kernel(lo_ref, hi_ref, tok_ref, w_ref, b_ref, cos_ref, sin_ref, seg_ref, mixed_ref, q_ref, k_ref, v_ref,
                  lse_ref, vt_ref, m_ref, l_ref, acc_ref):
    group = pl.program_id(0)
    zsize, _, rows, _ = tok_ref.shape
    length = zsize * rows
    heads = q_ref.shape[1]
    pair = 2 * HEAD_DIM
    scale = HEAD_DIM ** (-0.5)

    def project(i, carry):
        at = pl.ds(pl.multiple_of(i * rows, rows), rows)
        x = tok_ref[i, 0]
        lane = lax.broadcasted_iota(jnp.int32, (rows, pair), 1)
        doc = seg_ref[0, at, :]
        same = lane - HEAD_DIM == doc
        low = lane < HEAD_DIM
        feature = lane < HEAD_DIM + 4
        extra_q = jnp.where(same, 1.0, 0.0)
        extra_k = jnp.where(jnp.logical_and(feature, jnp.logical_not(same)), -1e9, 0.0)
        cosine = cos_ref[0, at, :]
        sine = sin_ref[0, at, :]
        for c in range(3):
            field = jnp.dot(x, w_ref[c], preferred_element_type=f32) + b_ref[c:c + 1, :]
            for j in range(heads // 2):
                part = field[:, j * pair:(j + 1) * pair]
                if c < 2:
                    part = part * cosine + turn_halves(part, sine)
                if c == 0:
                    part = part * scale
                for h in range(2):
                    one = part if h == 0 else pltpu.roll(part, HEAD_DIM, 1)
                    head = 2 * j + h
                    if c == 0:
                        q_ref[0, head, at, :] = jnp.where(low, one, extra_q).astype(bf16)
                    elif c == 1:
                        k_ref[0, head, at, :] = jnp.where(low, one, extra_k).astype(bf16)
                    else:
                        one = jnp.where(low, one, 0.0)
                        v_ref[0, head, at, :] = one.astype(bf16)
                        vt_ref[head, :, at] = one.T[:HEAD_DIM].astype(bf16)
        return carry

    lax.fori_loop(0, zsize, project, 0)

    def query_block(i, carry):
        at = pl.ds(pl.multiple_of(i * BLOCK, BLOCK), BLOCK)
        m_ref[...] = jnp.full(m_ref.shape, -1e30, f32)
        l_ref[...] = jnp.zeros(l_ref.shape, f32)
        acc_ref[...] = jnp.zeros(acc_ref.shape, f32)

        def key_block(j, carry):
            keys_at = pl.ds(pl.multiple_of(j * BLOCK, BLOCK), BLOCK)
            st = [scores_of(k_ref[0, h, keys_at, :], q_ref[0, h, at, :]) for h in range(heads)]
            peak = m_ref[...]
            new = jnp.maximum(peak, jnp.concatenate([jnp.max(t, axis=0, keepdims=True) for t in st], axis=0))
            p = [jnp.exp(st[h] - new[h:h + 1, :]) for h in range(heads)]
            old = jnp.exp(peak - new)
            m_ref[...] = new
            l_ref[...] = l_ref[...] * old + jnp.concatenate([jnp.sum(t, axis=0, keepdims=True) for t in p], axis=0)
            part = [
                jnp.dot(vt_ref[h, :, keys_at], p[h].astype(bf16), preferred_element_type=f32) for h in range(heads)
            ]
            for h in range(heads):
                acc_ref[h] = acc_ref[h] * old[h:h + 1, :] + part[h]
            return carry

        lax.fori_loop(lo_ref[group, i], hi_ref[group, i], key_block, 0)
        out = [acc_ref[h] / l_ref[h:h + 1, :] for h in range(heads)]
        for j in range(heads // 2):
            both = jnp.concatenate([out[2 * j], out[2 * j + 1]], axis=0)
            mixed_ref[0, at, j * pair:(j + 1) * pair] = both.T.astype(bf16)
        lse_ref[0, :, at] = m_ref[...] + jnp.log(l_ref[...])
        return carry

    lax.fori_loop(0, length // BLOCK, query_block, 0)


def attend_forward(bounds, tokens, weight, bias, cosine, sine, docs):
    zsize, groups, rows, width = tokens.shape
    length = zsize * rows
    cols = weight.shape[2]
    heads = cols // HEAD_DIM
    pair = 2 * HEAD_DIM
    whole = lambda shape: pl.BlockSpec(shape, lambda i, *_: (0,) * len(shape))
    of_group = lambda shape: pl.BlockSpec(shape, lambda i, *_: (i,) + (0,) * (len(shape) - 1))
    like = jax.ShapeDtypeStruct
    return pl.pallas_call(
        attend_kernel,
        grid_spec=pltpu.PrefetchScalarGridSpec(
            num_scalar_prefetch=2,
            grid=(groups,),
            in_specs=[
                pl.BlockSpec((zsize, 1, rows, width), lambda i, *_: (0, i, 0, 0)),
                whole(weight.shape), whole(bias.shape),
                of_group((1, length, pair)), of_group((1, length, pair)), of_group((1, length, 1)),
            ],
            out_specs=[
                of_group((1, length, cols)),
                of_group((1, heads, length, pair)), of_group((1, heads, length, pair)), of_group((1, heads, length, pair)),
                of_group((1, heads, length)),
            ],
            scratch_shapes=[
                pltpu.VMEM((heads, HEAD_DIM, length), bf16),
                pltpu.VMEM((heads, BLOCK), f32), pltpu.VMEM((heads, BLOCK), f32),
                pltpu.VMEM((heads, HEAD_DIM, BLOCK), f32),
            ],
        ),
        out_shape=[
            like((groups, length, cols), bf16),
            like((groups, heads, length, pair), bf16), like((groups, heads, length, pair), bf16),
            like((groups, heads, length, pair), bf16), like((groups, heads, length), f32),
        ],
        compiler_params=pltpu.CompilerParams(vmem_limit_bytes=VMEM),
        cost_estimate=pl.CostEstimate(
            flops=groups * (2 * length * width * 3 * cols + 4 * length * length * cols),
            bytes_accessed=2 * length * width + 6 * width * cols + 8 * length * cols,
            transcendentals=length * length * heads,
        ),
    )(*bounds, tokens, weight, bias, cosine, sine, docs)


def attend_back_kernel(group, last, lo_ref, hi_ref, z_ref, q_ref, k_ref, v_ref, lse_ref, mixed_ref, cos_ref, sin_ref, tok_ref, w_ref, *refs):
    zsize, _, rows, _ = tok_ref.shape
    do_refs, refs = refs[:zsize], refs[zsize:]
    if group:
        before_ref, refs = refs[0], refs[1:]
    back_refs, refs = refs[:1 if last else zsize], refs[1 if last else zsize:]
    wgrad_ref, sum_ref, grad_ref, wsum_ref, dox_ref, kt_ref, delta_ref, dk_ref, dv_ref, dqt_ref = refs
    heads, length = q_ref.shape[1], q_ref.shape[2]
    pair = 2 * HEAD_DIM
    scale = HEAD_DIM ** (-0.5)
    blocks = length // BLOCK

    low_half = lax.broadcasted_iota(jnp.int32, (rows, pair), 1) < HEAD_DIM
    for step in range(zsize):
        at = pl.ds(pl.multiple_of(lax.rem(z_ref[0] + zsize - step, zsize) * rows, rows), rows)
        for j in range(heads // 2):
            upstream = do_refs[step][0, :, j * pair:(j + 1) * pair].astype(f32)
            product = (upstream * mixed_ref[0, at, j * pair:(j + 1) * pair].astype(f32)).T
            for h in range(2):
                head = 2 * j + h
                one = upstream if h == 0 else pltpu.roll(upstream, HEAD_DIM, 1)
                dox_ref[head, at, :] = jnp.where(low_half, one, 0.0).astype(bf16)
                delta_ref[head:head + 1, at] = jnp.sum(
                    product[h * HEAD_DIM:(h + 1) * HEAD_DIM], axis=0, keepdims=True
                )
                kt_ref[head, :, at] = k_ref[0, head, at, :].astype(f32).T[:HEAD_DIM].astype(bf16)
                dk_ref[head, at, :] = jnp.zeros((rows, pair), f32)
                dv_ref[head, at, :] = jnp.zeros((rows, pair), f32)

    sum_ref[...] = jnp.zeros(sum_ref.shape, f32)
    wsum_ref[...] = before_ref[...] if group else jnp.zeros(wsum_ref.shape, f32)

    def put(c, j, at, field):
        low = field.astype(bf16)
        grad_ref[c, at, j * pair:(j + 1) * pair] = low
        cols = pl.ds(j * pair, pair)
        sum_ref[c:c + 1, cols] = sum_ref[c:c + 1, cols] + jnp.sum(low.astype(f32), axis=0, keepdims=True)

    def back(field, at):
        return field * cos_ref[0, at, :] - turn_halves(field, sin_ref[0, at, :])

    def query_block(i, carry):
        at = pl.ds(pl.multiple_of(i * BLOCK, BLOCK), BLOCK)
        dqt_ref[...] = jnp.zeros(dqt_ref.shape, f32)

        def key_block(j, carry):
            keys_at = pl.ds(pl.multiple_of(j * BLOCK, BLOCK), BLOCK)
            every = range(heads)
            queries = [q_ref[0, h, at, :] for h in every]
            upstream = [dox_ref[h, at, :] for h in every]
            st = [scores_of(k_ref[0, h, keys_at, :], queries[h]) for h in every]
            dp = [scores_of(v_ref[0, h, keys_at, :], upstream[h]) for h in every]
            p = [jnp.exp(st[h] - lse_ref[0, h:h + 1, at]) for h in every]
            ds = [(p[h] * (dp[h] - delta_ref[h:h + 1, at])).astype(bf16) for h in every]
            dv = [jnp.dot(p[h].astype(bf16), upstream[h], preferred_element_type=f32) for h in every]
            dk = [jnp.dot(ds[h], queries[h], preferred_element_type=f32) for h in every]
            dq = [jnp.dot(kt_ref[h, :, keys_at], ds[h], preferred_element_type=f32) for h in every]
            for h in every:
                dv_ref[h, keys_at, :] = dv_ref[h, keys_at, :] + dv[h]
                dk_ref[h, keys_at, :] = dk_ref[h, keys_at, :] + dk[h]
                dqt_ref[h] = dqt_ref[h] + dq[h]
            return carry

        lax.fori_loop(lo_ref[group, i], hi_ref[group, i], key_block, 0)
        for j in range(heads // 2):
            both = jnp.concatenate([dqt_ref[2 * j], dqt_ref[2 * j + 1]], axis=0)
            put(0, j, at, back(both.T * scale, at))
        return carry

    lax.fori_loop(0, blocks, query_block, 0)

    def finish(i, carry):
        at = pl.ds(pl.multiple_of(i * BLOCK, BLOCK), BLOCK)
        low = lax.broadcasted_iota(jnp.int32, (BLOCK, pair), 1) < HEAD_DIM
        for j in range(heads // 2):
            field = jnp.where(low, dk_ref[2 * j, at, :], pltpu.roll(dk_ref[2 * j + 1, at, :], HEAD_DIM, 1))
            put(1, j, at, back(field, at))
            field = jnp.where(low, dv_ref[2 * j, at, :], pltpu.roll(dv_ref[2 * j + 1, at, :], HEAD_DIM, 1))
            put(2, j, at, field)
        return carry

    lax.fori_loop(0, blocks, finish, 0)

    def onward(i, target):
        at = pl.ds(pl.multiple_of(i * rows, rows), rows)
        total = None
        x = tok_ref[i, 0]
        for c in range(3):
            grad = grad_ref[c, at, :]
            part = lax.dot_general(grad, w_ref[c], (((1,), (1,)), ((), ())), preferred_element_type=f32)
            total = part if total is None else total + part
            wsum_ref[c] += lax.dot_general(x, grad, (((0,), (0,)), ((), ())), preferred_element_type=f32)
        target[...] = total.astype(bf16)

    for step in range(zsize):
        if last:
            onward(step, back_refs[0].at[0, step])
        else:
            onward(lax.rem(z_ref[0] + step, zsize), back_refs[step])
    wgrad_ref[...] = wsum_ref[...].astype(wgrad_ref.dtype)


def attend_backward(group, before, bounds, zi, kept, mixed, upstream, cosine, sine, tokens, weight):
    queries, keys, values, lse = kept
    groups, heads, length, pair = queries.shape
    zsize, _, rows, width = tokens.shape
    cols = heads * HEAD_DIM
    last = group == groups - 1
    whole = lambda shape: pl.BlockSpec(shape, lambda i, *_: (0,) * len(shape))
    of_group = lambda shape: pl.BlockSpec(shape, lambda i, *_: (group,) + (0,) * (len(shape) - 1))
    like = jax.ShapeDtypeStruct
    wide = (heads, length, pair)
    return pl.pallas_call(
        functools.partial(attend_back_kernel, group, last),
        grid_spec=pltpu.PrefetchScalarGridSpec(
            num_scalar_prefetch=3,
            grid=(1,),
            in_specs=[of_group((1,) + wide)] * 3 + [
                of_group((1, heads, length)), of_group((1, length, cols)),
                of_group((1, length, pair)), of_group((1, length, pair)),
                pl.BlockSpec((zsize, 1, rows, width), lambda i, *_: (0, group, 0, 0)), whole(weight.shape),
            ] + [of_group((1, rows, cols))] * zsize + [whole(weight.shape)] * (group > 0),
            out_specs=([whole((1, zsize, rows, width))] if last else [whole((rows, width))] * zsize) + [
                whole(weight.shape), whole((8, cols)),
            ],
            scratch_shapes=[
                pltpu.VMEM((3, length, cols), bf16), pltpu.VMEM(weight.shape, f32),
                pltpu.VMEM(wide, bf16), pltpu.VMEM((heads, HEAD_DIM, length), bf16), pltpu.VMEM((heads, length), f32),
                pltpu.VMEM(wide, f32), pltpu.VMEM(wide, f32), pltpu.VMEM((heads, HEAD_DIM, BLOCK), f32),
            ],
        ),
        out_shape=([like((1, zsize, rows, width), bf16)] if last else [like((rows, width), bf16)] * zsize) + [
            like(weight.shape, bf16 if last else f32), like((8, cols), f32),
        ],
        compiler_params=pltpu.CompilerParams(vmem_limit_bytes=VMEM),
        cost_estimate=pl.CostEstimate(
            flops=0 if last else 40 * length * length * cols,
            bytes_accessed=0 if last else 48 * length * cols,
            transcendentals=0 if last else 2 * length * length * heads,
        ),
    )(*bounds, zi.reshape(1), queries, keys, values, lse, mixed, cosine, sine, tokens, weight, *upstream,
      *([before] if group else []))


MESH_ID = pl.DeviceIdType.MESH
HBM = pl.BlockSpec(memory_space=pl.ANY)


def other(axis):
    return {axis: 1 - lax.axis_index(axis)}


def greet(zsize):
    z = lax.axis_index("z")
    barrier = pltpu.get_barrier_semaphore()
    for axis in CELL:
        pl.semaphore_signal(barrier, inc=1, device_id=other(axis), device_id_type=MESH_ID)

    @pl.when(z > 0)
    def _():
        pl.semaphore_signal(barrier, inc=1, device_id={"z": z - 1}, device_id_type=MESH_ID)

    @pl.when(z < zsize - 1)
    def _():
        pl.semaphore_signal(barrier, inc=1, device_id={"z": z + 1}, device_id_type=MESH_ID)

    peers = len(CELL) + jnp.where(z > 0, 1, 0) + jnp.where(z < zsize - 1, 1, 0)
    pl.semaphore_wait(barrier, peers)


def remote(src, dst, send_sem, recv_sem, device):
    return pltpu.make_async_remote_copy(
        src_ref=src, dst_ref=dst, send_sem=send_sem, recv_sem=recv_sem, device_id=device, device_id_type=MESH_ID
    )


def swap_kernel(zsize, to_rows, origin, target, held, local_sem, send, recv):
    groups = target.shape[0]
    rows, cols = (target.shape[1], target.shape[2] // zsize) if to_rows else (target.shape[1] // zsize, target.shape[2])
    z = lax.axis_index("z")

    def source(g, peer):
        if to_rows:
            return origin.at[g, pl.ds(pl.multiple_of(peer * rows, rows), rows), :]
        return origin.at[g, :, pl.ds(pl.multiple_of(peer * cols, cols), cols)]

    def place(g, peer):
        if to_rows:
            return target.at[g, :, pl.ds(pl.multiple_of(peer * cols, cols), cols)]
        return target.at[g, pl.ds(pl.multiple_of(peer * rows, rows), rows), :]

    def copy_to(g, step):
        peer = lax.rem(z + step, zsize)
        return remote(source(g, peer), place(g, z), send.at[step, g], recv.at[step, g], {"z": peer})

    def copy_from(g, step):
        peer = lax.rem(z + zsize - step, zsize)
        return remote(source(g, peer), place(g, peer), send.at[step, g], recv.at[step, g], {"z": peer})

    into = [pltpu.make_async_copy(source(g, z), held.at[g], local_sem.at[0, g]) for g in range(groups)]
    onward = [pltpu.make_async_copy(held.at[g], place(g, z), local_sem.at[1, g]) for g in range(groups)]
    for copy in into:
        copy.start()
    barrier = pltpu.get_barrier_semaphore()
    for step in range(1, zsize):
        peer = lax.rem(z + step, zsize)
        pl.semaphore_signal(barrier, inc=1, device_id={"z": peer}, device_id_type=MESH_ID)
    pl.semaphore_wait(barrier, zsize - 1)
    for g in range(groups):
        for step in range(1, zsize):
            copy_to(g, step).start()
    for g in range(groups):
        into[g].wait()
        onward[g].start()
    for g in range(groups):
        for step in range(1, zsize):
            copy_from(g, step).wait_recv()
        onward[g].wait()
    for g in range(groups):
        for step in range(1, zsize):
            copy_to(g, step).wait_send()


def swap(array, zsize, to_rows):
    groups, rows, cols = array.shape
    if to_rows:
        rows //= zsize
        shape = (groups, rows, zsize * cols)
    else:
        cols //= zsize
        shape = (groups, zsize * rows, cols)
    return pl.pallas_call(
        functools.partial(swap_kernel, zsize, to_rows),
        out_shape=jax.ShapeDtypeStruct(shape, bf16),
        in_specs=[HBM],
        out_specs=HBM,
        scratch_shapes=[
            pltpu.VMEM((groups, rows, cols), bf16),
            pltpu.SemaphoreType.DMA((2, groups)),
            pltpu.SemaphoreType.DMA((zsize, groups)),
            pltpu.SemaphoreType.DMA((zsize, groups)),
        ],
        compiler_params=pltpu.CompilerParams(
            collective_id=2 if to_rows else 3, has_side_effects=True, vmem_limit_bytes=VMEM
        ),
    )(array)


ORDERS = {"xy": ("x", "y"), "yx": ("y", "x")}


def gather_kernel(zsize, orders, *refs):
    n = len(orders)
    tok, bias, shards = refs[0], refs[1], refs[2:2 + n]
    tok_all, bias_all, wholes = refs[2 + n], refs[3 + n], refs[4 + n:4 + 2 * n]
    held = refs[4 + 2 * n:6 + 3 * n]
    local_sem, z_send, z_recv, p_send, p_recv = refs[6 + 3 * n:]
    z = lax.axis_index("z")
    c = lax.axis_index("core")
    place = [(lax.axis_index(o[0]), lax.axis_index(o[1])) for o in orders]

    sources = list(shards) + [tok, bias]
    targets = list(wholes) + [tok_all, bias_all]
    into = [pltpu.make_async_copy(sources[i], held[i], local_sem.at[0, i]) for i in range(n + 2)]
    local = [pltpu.make_async_copy(held[i], targets[i].at[z], local_sem.at[1, i]) for i in range(n + 2)]
    for copy in into:
        copy.start()
    greet(zsize)

    def line(item, src, step, side):
        to = z + 1 if side == 0 else z - 1
        if item < n:
            f, s = place[item]
            own = shards[item].at[c, f, s]
            dst = wholes[item].at[src, c, f, s]
        else:
            own = (tok, bias)[item - n]
            dst = (tok_all, bias_all)[item - n].at[src]
        return remote(
            own if step == 0 else dst, dst, z_send.at[side, item, step], z_recv.at[side, item, step], {"z": to}
        )

    def exchange(k, src, stage, slot):
        f, s = place[k]
        whole = wholes[k]
        ref = (whole.at[src, c, f, s], whole.at[src, c, f], whole.at[src, c])[stage]
        axis = (orders[k][1], orders[k][0], "core")[stage]
        return remote(ref, ref, p_send.at[slot, k, stage], p_recv.at[slot, k, stage], other(axis))

    def valid_from(side, step):
        return z - step - 1 >= 0 if side == 0 else z + step + 1 < zsize

    def source(side, step):
        return z - step - 1 if side == 0 else z + step + 1

    def has_next(side):
        return z < zsize - 1 if side == 0 else z > 0

    for side in range(2):

        @pl.when(has_next(side))
        def _():
            for item in range(n):
                line(item, z, 0, side).start()

    def stage_on(stage, step):
        for side in range(2):

            @pl.when(valid_from(side, step))
            def _():
                src = source(side, step)
                slot = side * (zsize - 1) + step
                for k in range(n):
                    exchange(k, src, stage - 1, slot).wait_recv()
                    if stage < 3:
                        exchange(k, src, stage, slot).start()

    def arrive(items, step):
        for side in range(2):

            @pl.when(valid_from(side, step))
            def _():
                src = source(side, step)
                for item in items:
                    line(item, src, step, side).wait_recv()
                    if step + 1 < zsize - 1:

                        @pl.when(has_next(side))
                        def _():
                            line(item, src, step + 1, side).start()

                    if item < n:
                        exchange(item, src, 0, side * (zsize - 1) + step).start()

    for copy, onward in zip(into, local):
        copy.wait()
        onward.start()
    for step in range(zsize - 1):
        arrive(range(n), step)
        if step == zsize - 2:
            for side in range(2):

                @pl.when(has_next(side))
                def _():
                    for item in range(n, n + 2):
                        line(item, z, 0, side).start()

        if step >= 1:
            stage_on(1, step - 1)
    for step in range(zsize - 1):
        if step == 0:
            stage_on(1, zsize - 2)
        stage_on(2, step)
        arrive(range(n, n + 2), step)
    for step in range(zsize - 1):
        stage_on(3, step)
    for copy in local:
        copy.wait()
    for side in range(2):

        @pl.when(has_next(side))
        def _():
            for item in range(n + 2):
                line(item, z, 0, side).wait_send()

        for step in range(zsize - 1):

            @pl.when(valid_from(side, step))
            def _():
                src = source(side, step)
                if step + 1 < zsize - 1:

                    @pl.when(has_next(side))
                    def _():
                        for item in range(n + 2):
                            line(item, src, step + 1, side).wait_send()

                for k in range(n):
                    for stage in range(3):
                        exchange(k, src, stage, side * (zsize - 1) + step).wait_send()


def gather_start(tokens, bias, weights, zsize):
    orders = [ORDERS[o] for o, _ in weights]
    shards = [w for _, w in weights]
    n = len(shards)
    stack = lambda a: jax.ShapeDtypeStruct((zsize,) + a.shape, a.dtype)
    return pl.pallas_call(
        functools.partial(gather_kernel, zsize, orders),
        out_shape=[stack(tokens), stack(bias)] + [stack(w) for w in shards],
        in_specs=[HBM] * (n + 2),
        out_specs=[HBM] * (n + 2),
        scratch_shapes=[pltpu.VMEM(a.shape, a.dtype) for a in shards + [tokens, bias]] + [
            pltpu.SemaphoreType.DMA((2, n + 2)),
            pltpu.SemaphoreType.DMA((2, n + 2, zsize - 1)),
            pltpu.SemaphoreType.DMA((2, n + 2, zsize - 1)),
            pltpu.SemaphoreType.DMA((2 * (zsize - 1), n, 3)),
            pltpu.SemaphoreType.DMA((2 * (zsize - 1), n, 3)),
        ],
        compiler_params=pltpu.CompilerParams(
            collective_id=0, has_side_effects=True, vmem_limit_bytes=VMEM
        ),
    )(tokens, bias, *shards)


def add_rows(dst, src):
    rows = dst.shape[0]
    step = min(rows, 32)

    def body(i, carry):
        at = pl.ds(pl.multiple_of(i * step, step), step)
        dst[at, :] = dst[at, :] + src[at, :]
        return carry

    lax.fori_loop(0, rows // step, body, 0)


def reduce_kernel(zsize, orders, w, *refs):
    n = 3
    p = len(orders) - n
    items = n + p
    pieces, came, refs = refs[:p], refs[p:2 * p], refs[2 * p:]
    parts, backs, small = refs[:n], refs[n], refs[n + 1]
    pos = n + 2
    piece_out, part_out, back_out = refs[pos:pos + p], refs[pos + p:pos + p + n], refs[pos + p + n]
    small_out = refs[pos + p + n + 1]
    outs = list(part_out) + list(piece_out)
    pos += p + n + 2
    mine = refs[pos:pos + items + w]
    pos += items + w
    got_c, got_1, got_2 = refs[pos:pos + n], refs[pos + n:pos + n + items], refs[pos + n + items:pos + n + 2 * items]
    pos += n + 2 * items
    lines = [0] + list(range(n, items + w))
    line_backs = list(range(items, items + w))
    got_z = dict(zip(lines, refs[pos:pos + len(lines)]))
    pos += len(lines)
    small_mine, small_got, small_line, small_total, part_line, part_total = refs[pos:pos + 6]
    (local_sem, send, recv, z_send, z_recv, s_send, s_recv, t_send, t_recv, g_send, g_recv, end_sem) = refs[pos + 6:]
    z = lax.axis_index("z")
    c = lax.axis_index("core")
    orders = orders[p:] + orders[:p]
    place = [(lax.axis_index(o[0]), lax.axis_index(o[1])) for o in orders]
    turn = []
    for i in range(zsize // 2):
        turn += [i, zsize - 1 - i]
    few = parts[1].shape[0]
    steps = [(1, b) for b in range(few)] + [(2, 0)] + [(0, b) for b in turn]

    def load(k, b):
        src = parts[k].at[b, c] if k < n else pieces[k - n].at[b] if k < items else backs.at[k - items, b]
        return pltpu.make_async_copy(src, mine[k].at[b], local_sem.at[k, b])

    def load_came(k, b):
        return pltpu.make_async_copy(came[k - n].at[b], got_1[k].at[b], local_sem.at[items + w + 1 + k - n, b])

    load_small = pltpu.make_async_copy(small, small_mine.at[0], local_sem.at[items + w, 0])

    def half(k, b, stage):
        f, s = place[k]
        if stage == 0:
            src, dst, axis = parts[k].at[b, 1 - c], got_c[k].at[b], "core"
        elif stage == 1:
            src, dst, axis = mine[k].at[b, 1 - f], got_1[k].at[b], orders[k][0]
        else:
            held = mine[k].at[b, f] if k < n else mine[k].at[b]
            src, dst, axis = held.at[1 - s], got_2[k].at[b], orders[k][1]
        return remote(src, dst, send.at[stage, k, b], recv.at[stage, k, b], other(axis))

    def own(k, b):
        if k >= items:
            return mine[k].at[b]
        f, s = place[k]
        return mine[k].at[b, s] if k >= n else mine[k].at[b, f, s]

    def hop(k, b, side):
        to = z + 1 if side == 0 else z - 1
        at = b if side == 0 else jnp.where(b == z - 1, zsize, b)
        return remote(own(k, b), got_z[k].at[at], z_send.at[k, b], z_recv.at[k, at], {"z": to})

    def take(k, b, side):
        at = b if side == 0 else jnp.where(b == z, zsize, b)
        ref = got_z[k].at[at]
        sender = z - 1 if side == 0 else z + 1
        remote(own(k, b), ref, z_send.at[k, b], z_recv.at[k, at], {"z": sender}).wait_recv()
        add_rows(own(k, b), ref)

    def line_start(ks, messages):
        for side in range(2):

            @pl.when(z == (0 if side == 0 else zsize - 1))
            def _():
                for i in messages:
                    for k in ks:
                        hop(k, zsize - 1 - i if side == 0 else i, side).start()

    def line_slot(ks, slot):
        for i in range(slot):
            for side in range(2):
                b = zsize - 1 - i if side == 0 else i

                @pl.when(z == (slot - i if side == 0 else zsize - 1 - slot + i))
                def _():
                    for k in ks:
                        take(k, b, side)

                        @pl.when(z < b if side == 0 else z > b)
                        def _():
                            hop(k, b, side).start()

    def small_swap(stage):
        return remote(
            small_mine.at[stage], small_got.at[stage], s_send.at[stage], s_recv.at[stage], other(CELL[stage])
        )

    def small_step(stage):
        small_swap(stage).wait_recv()
        small_mine[stage + 1] = small_mine[stage] + small_got[stage]
        if stage < 2:
            small_swap(stage + 1).start()

    last = len(CELL)
    last_part = own(2, 0)

    def total_copy(item, way):
        line, total = ((small_line, small_total), (part_line, part_total))[item]
        src = (small_mine.at[last], last_part)[item] if way == 0 else total
        dst = line if way == 0 else total
        to = z + 1 if way == 0 else z - 1
        return remote(src, dst, t_send.at[item, way], t_recv.at[item, way], {"z": to})

    def total_step(tick):
        if 0 <= tick < zsize:

            @pl.when(z == tick)
            def _():
                if tick > 0:
                    for item in range(2):
                        total_copy(item, 0).wait_recv()
                    small_mine[last] = small_mine[last] + small_line[...]
                    add_rows(last_part, part_line)
                if tick < zsize - 1:
                    for item in range(2):
                        total_copy(item, 0).start()
                else:
                    small_total[...] = small_mine[last]
                    part_total[...] = last_part[...]

        back_tick = tick - (zsize - 1)
        if 0 <= back_tick < zsize:

            @pl.when(z == zsize - 1 - back_tick)
            def _():
                if back_tick > 0:
                    for item in range(2):
                        total_copy(item, 1).wait_recv()
                if back_tick < zsize - 1:
                    for item in range(2):
                        total_copy(item, 1).start()

    line_pieces = list(range(n, items))
    piece_steps = [(k, b) for b in turn for k in line_pieces]
    for b in turn:
        for k in line_backs:
            load(k, b).start()
    for k, b in piece_steps:
        load(k, b).start()
        load_came(k, b).start()
    for k, b in steps:
        load(k, b).start()
    load_small.start()
    greet(zsize)
    for k, b in steps:
        half(k, b, 0).start()
    for b in turn:
        for k in line_backs:
            load(k, b).wait()
    line_start(line_backs, [0])
    load_small.wait()
    small_swap(0).start()

    def stage_1(k, b):
        f, s = place[k]
        load(k, b).wait()
        half(k, b, 0).wait_recv()
        for i in range(2):
            add_rows(mine[k].at[b, 1 - f, i], got_c[k].at[b, 1 - f, i])
        half(k, b, 1).start()
        for i in range(2):
            add_rows(mine[k].at[b, f, i], got_c[k].at[b, f, i])

    def stage_2(k, b):
        f, s = place[k]
        held = mine[k].at[b, f] if k < n else mine[k].at[b]
        if k < n:
            half(k, b, 1).wait_recv()
        else:
            load(k, b).wait()
            load_came(k, b).wait()
        add_rows(held.at[1 - s], got_1[k].at[b, 1 - s])
        half(k, b, 2).start()
        add_rows(held.at[s], got_1[k].at[b, s])

    def stage_3(k, b):
        half(k, b, 2).wait_recv()
        add_rows(own(k, b), got_2[k].at[b])

    def result(k, b):
        return part_total if k == 2 else own(k, b)

    def out_of(k, b):
        return outs[k].at[b] if k == 1 else outs[k]

    def put(k, b, slot):
        f, s = place[k]
        return pltpu.make_async_copy(result(k, b), out_of(k, b).at[c, f, s], end_sem.at[slot])

    def spread(k, b, stage, slot):
        f, s = place[k]
        out = out_of(k, b)
        dst = (out.at[c, f, s], out.at[c, f], out.at[c])[stage]
        src = result(k, b) if stage == 0 else dst
        axis = (orders[k][1], orders[k][0], "core")[stage]
        return remote(src, dst, g_send.at[slot, stage], g_recv.at[slot, stage], other(axis))

    spreads = [
        [(1, b, b) for b in range(few)],
        [(k, z, few + k - n) for k in line_pieces],
        [(0, z, few + p), (2, 0, few + p + 1)],
    ]

    def spread_step(group, stage):
        for k, b, slot in spreads[group]:
            if stage == 0:
                spread(k, b, 0, slot).start()
                put(k, b, slot).start()
                continue
            if stage == 1:
                put(k, b, slot).wait()
            spread(k, b, stage - 1, slot).wait_recv()
            if stage < 3:
                spread(k, b, stage, slot).start()

    def sent(ks):
        for b in range(zsize):

            @pl.when(z != b)
            def _():
                for k in ks:
                    hop(k, b, 0).wait_send()

    at_end = jnp.logical_or(z == 0, z == zsize - 1)
    for k, b in piece_steps:
        stage_2(k, b)
    for k, b in steps:
        stage_1(k, b)
    small_step(0)
    for b in turn:
        for k in line_pieces:
            stage_3(k, b)
        for side in range(2):

            @pl.when(jnp.logical_and(z == (0 if side == 0 else zsize - 1), z != b))
            def _():
                for k in line_pieces:
                    hop(k, b, side).start()

    for k, b in steps:
        stage_2(k, b)
    small_step(1)
    line_slot(line_backs, 1)
    for k, b in steps:
        stage_3(k, b)
    small_step(2)
    spread_step(0, 0)
    line_start([0], range(zsize - 1))
    total_step(0)

    @pl.when(at_end)
    def _():
        sent(line_pieces)

    line_start(line_backs, range(1, zsize - 1))
    ticks = list(range(1, 2 * zsize - 1))
    later = [(0, 1), (0, 2), (0, 3)]

    def fill(group_stages, count):
        for _ in range(count):
            if group_stages:
                spread_step(*group_stages.pop(0))

    for slot in range(1, zsize):
        line_slot(line_pieces, slot)
        total_step(ticks.pop(0))
        fill(later, 1)
        if slot >= 2:
            line_slot([0], slot - 1)
    fill(later, 3)
    spread_step(1, 0)
    later = [(1, 1), (1, 2), (1, 3)]
    total_step(ticks.pop(0))
    line_slot([0], zsize - 1)
    for slot in range(2, zsize - 1):
        line_slot(line_backs, slot)
        fill(later, 1)
    for tick in ticks:
        total_step(tick)
    spread_step(2, 0)
    fill(later, 1)
    spread_step(2, 1)
    fill(later, 1)
    spread_step(2, 2)
    fill(later, 3)
    line_slot(line_backs, zsize - 1)
    finish_back = [
        pltpu.make_async_copy(mine[k].at[z], back_out.at[k - items], local_sem.at[k, 0]) for k in line_backs
    ]
    for copy in finish_back:
        copy.start()
    finish_small = pltpu.make_async_copy(small_total, small_out, local_sem.at[items + w, 0])
    finish_small.start()
    spread_step(2, 3)
    for copy in finish_back:
        copy.wait()
    finish_small.wait()
    sent([0] + line_backs)

    @pl.when(jnp.logical_not(at_end))
    def _():
        sent(line_pieces)

    for way in range(2):

        @pl.when(z < zsize - 1 if way == 0 else z > 0)
        def _():
            for item in range(2):
                total_copy(item, way).wait_send()

    for k, b in steps:
        for stage in range(3):
            half(k, b, stage).wait_send()
    for k, b in piece_steps:
        half(k, b, 2).wait_send()
    for stage in range(3):
        small_swap(stage).wait_send()
    for group in spreads:
        for k, b, slot in group:
            for stage in range(3):
                spread(k, b, stage, slot).wait_send()


def reduce_end(pieces, parts, backs, small, zsize):
    orders = [ORDERS[o[0]] for o in pieces + parts]
    piece_arrays = [a for _, a, _ in pieces]
    came = [a for _, _, a in pieces]
    arrays = [a for _, a in parts]
    p, n, w = len(pieces), len(parts), backs.shape[0]
    shapes = [a.shape for a in arrays]
    like = jax.ShapeDtypeStruct
    outs = [like((2, 2, 2) + a.shape[2:], bf16) for a in piece_arrays]
    outs += [like(s if i == 1 else s[1:], bf16) for i, s in enumerate(shapes)]
    outs += [like((w,) + backs.shape[2:], bf16), like(small.shape, f32)]
    held = lambda shape: pltpu.VMEM(shape, bf16)
    scratch = [held((s[0],) + s[2:]) for s in shapes]
    scratch += [held(a.shape) for a in piece_arrays] + [held(backs.shape[1:])] * w
    scratch += [held((s[0],) + s[2:]) for s in shapes]
    scratch += [held((s[0],) + s[3:]) for s in shapes] + [held(a.shape) for a in piece_arrays]
    scratch += [held((s[0],) + s[4:]) for s in shapes] + [held(a.shape[:1] + a.shape[2:]) for a in piece_arrays]
    scratch += [held((zsize + 1,) + shapes[0][4:])]
    scratch += [held((zsize + 1,) + a.shape[2:]) for a in piece_arrays] + [held((zsize + 1,) + backs.shape[2:])] * w
    scratch += [pltpu.VMEM((4,) + small.shape, f32), pltpu.VMEM((3,) + small.shape, f32)]
    scratch += [pltpu.VMEM(small.shape, f32)] * 2 + [held(shapes[2][4:])] * 2
    dma = pltpu.SemaphoreType.DMA
    most = max(zsize, shapes[1][0])
    ends = shapes[1][0] + p + 2
    scratch += [
        dma((n + 2 * p + w + 1, most)), dma((3, n + p, most)), dma((3, n + p, most)),
        dma((n + p + w, zsize)), dma((n + p + w, zsize + 1)),
        dma((3,)), dma((3,)), dma((2, 2)), dma((2, 2)), dma((ends, 3)), dma((ends, 3)), dma((ends,)),
    ]
    return pl.pallas_call(
        functools.partial(reduce_kernel, zsize, orders, w),
        out_shape=outs,
        in_specs=[HBM] * (n + 2 * p + 2),
        out_specs=[HBM] * (n + p + 2),
        scratch_shapes=scratch,
        compiler_params=pltpu.CompilerParams(
            collective_id=1, has_side_effects=True, vmem_limit_bytes=VMEM
        ),
    )(*piece_arrays, *came, *arrays, backs, small)


def gelu_pair(v):
    size = jnp.abs(v)
    t = 1.0 / (1.0 + (0.3275911 * 0.5 ** 0.5) * size)
    bell = jnp.exp(-0.5 * (v * v))
    poly = t * (0.254829592 + t * (-0.284496736 + t * (1.421413741 + t * (-1.453152027 + t * 1.061405429))))
    tail = 0.5 * poly * bell
    cdf = jnp.where(v >= 0.0, 1.0 - tail, tail)
    return v * cdf, cdf + v * (bell * (1.0 / (2.0 * math.pi) ** 0.5))


def ffn_kernel(x_ref, up_ref, bias_ref, down_ref, active_ref, slope_ref, sum_ref):
    rows = x_ref.shape[0]
    part = rows // 2

    @pl.when(pl.program_id(0) == 0)
    def _():
        sum_ref[...] = jnp.zeros(sum_ref.shape, f32)

    for i in range(2):
        at = pl.ds(i * part, part)
        hidden = jnp.dot(x_ref[at, :], up_ref[0], preferred_element_type=f32) + bias_ref[0]
        active, slope = gelu_pair(hidden)
        active = active.astype(bf16)
        active_ref[0, at, :] = active
        slope_ref[0, at, :] = slope.astype(bf16)
        sum_ref[at, :] += jnp.dot(active, down_ref[0], preferred_element_type=f32)


def ffn_forward(normed_low, up_all, up_bias, down_all):
    zsize, width, units = up_all.shape
    rows = normed_low.shape[0]
    tile = units // 2
    like = jax.ShapeDtypeStruct
    tiles = pl.BlockSpec((1, rows, tile), lambda s: (s // 2, 0, s % 2))
    return pl.pallas_call(
        ffn_kernel,
        grid=(2 * zsize,),
        in_specs=[
            pl.BlockSpec((rows, width), lambda s: (0, 0)),
            pl.BlockSpec((1, width, tile), lambda s: (s // 2, 0, s % 2)),
            pl.BlockSpec((1, 1, tile), lambda s: (s // 2, 0, s % 2)),
            pl.BlockSpec((1, tile, width), lambda s: (s // 2, s % 2, 0)),
        ],
        out_specs=[tiles, tiles, pl.BlockSpec((rows, width), lambda s: (0, 0))],
        out_shape=[
            like((zsize, rows, units), bf16), like((zsize, rows, units), bf16), like((rows, width), f32),
        ],
        compiler_params=pltpu.CompilerParams(vmem_limit_bytes=VMEM),
    )(normed_low, up_all, up_bias[:, None, :], down_all)


def ffn_back_kernel(core_ref, second_ref, normed_ref, up_ref, down_ref, active_ref, slope_ref,
                    give_up_ref, keep_up_ref, give_down_ref, keep_down_ref, back_ref, bias_ref, turned_ref):
    s = pl.program_id(0)
    half = turned_ref.shape[0] // 2
    c = core_ref[0]

    @pl.when(s == 0)
    def _():
        back_ref[...] = jnp.zeros(back_ref.shape, f32)
        turned_ref[...] = normed_ref[...].T

    second = second_ref[...]
    upstream = lax.dot_general(second, down_ref[0], (((1,), (1,)), ((), ())), preferred_element_type=f32)
    grad = (upstream * slope_ref[0].astype(f32)).astype(bf16)
    bias_ref[0] = jnp.sum(grad.astype(f32), axis=0, keepdims=True)
    down = lax.dot_general(active_ref[0], second, (((0,), (0,)), ((), ())), preferred_element_type=f32).astype(bf16)

    @pl.when(s % 2 == 0)
    def _():
        give_down_ref[0] = down

    @pl.when(s % 2 == 1)
    def _():
        keep_down_ref[0] = down

    back_ref[...] += lax.dot_general(grad, up_ref[0], (((1,), (1,)), ((), ())), preferred_element_type=f32)
    give = turned_ref[pl.ds(pl.multiple_of((1 - c) * half, half), half), :]
    give_up_ref[0] = jnp.dot(give, grad, preferred_element_type=f32).astype(bf16)
    keep = turned_ref[pl.ds(pl.multiple_of(c * half, half), half), :]
    keep_up_ref[0] = jnp.dot(keep, grad, preferred_element_type=f32).astype(bf16)


def ffn_backward(core, second_low, normed_low, up_all, down_all, active, slope):
    zsize, width, units = up_all.shape
    rows = normed_low.shape[0]
    tile = units // 2
    like = jax.ShapeDtypeStruct
    part = lambda s, c: (1 - c[0] + (2 * c[0] - 1) * (s % 2))
    whole = pl.BlockSpec((rows, width), lambda s, c: (0, 0))
    tiles = pl.BlockSpec((1, rows, tile), lambda s, c: (s // 2, 0, part(s, c)))
    up_half = pl.BlockSpec((1, width // 2, tile), lambda s, c: (s // 2, 0, part(s, c)))
    down_half = pl.BlockSpec((1, tile, width), lambda s, c: (s // 2, 0, 0))
    return pl.pallas_call(
        ffn_back_kernel,
        grid_spec=pltpu.PrefetchScalarGridSpec(
            num_scalar_prefetch=1,
            grid=(2 * zsize,),
            in_specs=[
                whole, whole,
                pl.BlockSpec((1, width, tile), lambda s, c: (s // 2, 0, part(s, c))),
                pl.BlockSpec((1, tile, width), lambda s, c: (s // 2, part(s, c), 0)),
                tiles, tiles,
            ],
            out_specs=[
                up_half, up_half, down_half, down_half, whole,
                pl.BlockSpec((1, 1, tile), lambda s, c: (s // 2, 0, part(s, c))),
            ],
            scratch_shapes=[pltpu.VMEM((width, rows), bf16)],
        ),
        out_shape=[
            like((zsize, width // 2, units), bf16), like((zsize, width // 2, units), bf16),
            like((zsize, tile, width), bf16), like((zsize, tile, width), bf16),
            like((rows, width), f32), like((zsize, 1, units), f32),
        ],
        compiler_params=pltpu.CompilerParams(vmem_limit_bytes=VMEM),
    )(core, second_low, normed_low, up_all, down_all, active, slope)


PAIR = [(0, 1), (1, 0)]


def first_halving(got, keep, order):
    zsize, half, cols = keep.shape
    shape = (zsize, 2, 2, half // 4, cols)
    got, keep = got.reshape(shape), keep.reshape(shape)
    i = lax.axis_index(ORDERS[order][0])
    pick = lambda array, j: lax.dynamic_index_in_dim(array, j, 1, keepdims=False)
    return pick(keep, 1 - i) + pick(got, 1 - i), pick(keep, i) + pick(got, i)


def widen_kernel(up_ref, down_ref, out_ref, qkv_ref, first_ref, back_ref, up_o, down_o, out_o, qkv_o, first_o):
    for source, target in ((up_ref, up_o), (down_ref, down_o), (out_ref, out_o), (qkv_ref, qkv_o)):
        target[...] = source[...].astype(f32)
    first_o[...] = first_ref[...] + back_ref[...]


def widen(up, down, out, qkv, first, back):
    steps = 8

    def rows_of(array):
        return pl.BlockSpec((array.shape[0] // steps, array.shape[1]), lambda i: (i, 0))

    arrays = [up, down, out]
    specs = [rows_of(a) for a in arrays]
    specs.append(pl.BlockSpec((3, qkv.shape[1] // steps, qkv.shape[2]), lambda i: (0, i, 0)))
    specs.append(rows_of(first))
    return pl.pallas_call(
        widen_kernel,
        grid=(steps,),
        in_specs=specs + [rows_of(back)],
        out_specs=specs,
        out_shape=[jax.ShapeDtypeStruct(a.shape, f32) for a in arrays + [qkv, first]],
        compiler_params=pltpu.CompilerParams(vmem_limit_bytes=VMEM),
    )(up, down, out, qkv, first, back)


def per_device(blocks, tokens, segments, qkv_weight, qkv_bias, out_weight, out_bias, gain_one, shift_one,
               up_weight, up_bias, down_weight, down_bias, gain_two, shift_two, proj_weight, out_grad, embed_grad):
    groups, local_rows, model_width = tokens.shape
    length = segments.shape[1]
    zsize = length // local_rows
    head_cols = qkv_weight.shape[2]
    units_here = up_weight.shape[1]
    rows = groups * local_rows
    zi = lax.axis_index("z")
    cosine, sine = rotary_tables(doc_positions(segments))
    firsts = segments[:, ::BLOCK]
    lasts = segments[:, BLOCK - 1::BLOCK]
    bounds = (
        jnp.sum(segments[:, None, :] < firsts[:, :, None], axis=2, dtype=jnp.int32) // BLOCK,
        (jnp.sum(segments[:, None, :] <= lasts[:, :, None], axis=2, dtype=jnp.int32) + BLOCK - 1) // BLOCK,
    )
    docs = segments[:, :, None]

    def cut(array, rows_at):
        shape = array.shape
        return array.reshape(shape[:rows_at] + (2, 2, 2, shape[rows_at] // 8) + shape[rows_at + 1:])

    token_rows = tokens.reshape(rows, model_width)
    token_blocks, bias_blocks, out_all, up_all, down_all = gather_start(
        token_rows,
        up_bias.reshape(8, units_here // 8),
        [("xy", cut(out_weight, 0)), ("xy", cut(up_weight, 0)), ("yx", cut(down_weight, 0))],
        zsize,
    )
    token_blocks = token_blocks.reshape(zsize, groups, local_rows, model_width)
    out_all = out_all.reshape(model_width, model_width)
    up_all = up_all.reshape(zsize, model_width, units_here)
    down_all = down_all.reshape(zsize, units_here, model_width)
    full_up_bias = bias_blocks.reshape(zsize, units_here)

    own_mixed, *kept = attend_forward(bounds, token_blocks, qkv_weight, qkv_bias, cosine, sine, docs)
    mixed = swap(own_mixed, zsize, True).reshape(rows, model_width)

    first_sum = tokens.reshape(rows, model_width).astype(f32) + (
        jnp.dot(mixed, out_all, preferred_element_type=f32) + out_bias
    )
    normed, scaled_one, inv_one = norm_forward(first_sum, gain_one, shift_one)
    normed_low = normed.astype(bf16)
    active, slope, ffn = ffn_forward(normed_low, up_all, full_up_bias, down_all)
    second_sum = normed + (ffn + down_bias)
    result, scaled_two, inv_two = norm_forward(second_sum, gain_two, shift_two)
    result_low = result.astype(bf16)
    embedded = jnp.dot(result_low, proj_weight, preferred_element_type=f32).astype(bf16)
    embed_rows = embed_grad.reshape(rows, -1)
    grad_result = out_grad.reshape(rows, model_width).astype(f32) + jnp.einsum(
        "np,dp->nd", embed_rows, proj_weight, preferred_element_type=f32
    )
    proj_grad = jnp.einsum("nd,np->dp", result_low, embed_rows, preferred_element_type=f32)
    grad_second, gain_two_grad, shift_two_grad = norm_backward(grad_result, scaled_two, inv_two, gain_two)
    second_low = grad_second.astype(bf16)
    down_bias_grad = jnp.sum(second_low.astype(f32), axis=0)
    core = lax.axis_index("core").reshape(1)
    give_up, keep_up, give_down, keep_down, ffn_back, up_bias_grad = ffn_backward(
        core, second_low, normed_low, up_all, down_all, active, slope
    )
    got_down = lax.ppermute(give_down, "core", PAIR)
    got_up = lax.ppermute(give_up, "core", PAIR)
    grad_normed = grad_second + ffn_back
    grad_first, gain_one_grad, shift_one_grad = norm_backward(grad_normed, scaled_one, inv_one, gain_one)
    first_low = grad_first.astype(bf16)
    out_bias_grad = jnp.sum(first_low.astype(f32), axis=0)
    out_grad_w = jnp.einsum("nh,nd->hd", mixed, first_low, preferred_element_type=f32).astype(bf16)
    grad_mixed = jnp.einsum("nd,hd->nh", first_low, out_all, preferred_element_type=f32).astype(bf16)
    grad_mixed = grad_mixed.reshape(groups, local_rows, model_width)
    upstream = []
    for step in range(zsize):
        part = lax.dynamic_slice_in_dim(grad_mixed, lax.rem(zi + step, zsize) * head_cols, head_cols, 2)
        ring = [(i, (i + step) % zsize) for i in range(zsize)]
        upstream.append(lax.ppermute(part, "z", ring) if step else part)
    send_down, keep_down = first_halving(got_down, keep_down, "yx")
    send_up, keep_up = first_halving(got_up, keep_up, "xy")
    got_down = lax.ppermute(send_down, ORDERS["yx"][0], PAIR)
    got_up = lax.ppermute(send_up, ORDERS["xy"][0], PAIR)
    qkv_weight_grad, qkv_bias_grad, early = None, 0.0, []
    for g in range(groups):
        *backs, qkv_weight_grad, bias_part = attend_backward(
            g, qkv_weight_grad, bounds, zi, kept, own_mixed, upstream, cosine, sine, token_blocks, qkv_weight
        )
        qkv_bias_grad = qkv_bias_grad + bias_part[:3]
        if g < groups - 1:
            early.append([
                lax.ppermute(part, "z", [(i, (i + step) % zsize) for i in range(zsize)]) if step else part
                for step, part in enumerate(backs)
            ])
    backs, got_down, got_up = lax.optimization_barrier((backs[0], got_down, got_up))

    small = jnp.concatenate(
        [
            out_bias_grad, gain_one_grad, shift_one_grad, down_bias_grad, gain_two_grad, shift_two_grad,
            up_bias_grad.reshape(-1),
            lax.dynamic_update_slice(
                jnp.zeros((zsize, 3 * head_cols), f32), qkv_bias_grad.reshape(1, -1), (zi, 0)
            ).reshape(-1),
        ]
    )
    proj_cols = proj_grad.shape[1]
    proj_grad = jnp.pad(proj_grad.astype(bf16), ((0, 0), (0, -proj_cols % 128)))
    up_grad, down_grad, out_grad_w, qkv_weight_grad, proj_grad, back, small = reduce_end(
        [("xy", keep_up, got_up), ("yx", keep_down, got_down)],
        [
            ("xy", cut(out_grad_w.reshape(zsize, head_cols, model_width), 1)),
            ("yx", cut(qkv_weight_grad, 1)),
            ("xy", cut(proj_grad[None], 1)),
        ],
        backs,
        small.reshape(8, -1),
        zsize,
    )
    back, early = lax.optimization_barrier((back, early))
    qkv_weight_grad = qkv_weight_grad.reshape(qkv_weight.shape)
    proj_grad = proj_grad.reshape(model_width, -1)[:, :proj_cols].astype(f32)
    out_grad_w = out_grad_w.reshape(out_weight.shape)
    up_grad = up_grad.reshape(up_weight.shape)
    down_grad = down_grad.reshape(down_weight.shape)
    if blocks > 1:
        down_grad, up_grad, out_grad_w, qkv_weight_grad = lax.psum(
            (down_grad, up_grad, out_grad_w, qkv_weight_grad), ("xb", "yb")
        )
        small, proj_grad = lax.psum((small, proj_grad), ("xb", "yb"))
    small = small.reshape(-1)
    up_grad, down_grad, out_grad_w, qkv_weight_grad, tokens_grad = widen(
        up_grad, down_grad, out_grad_w, qkv_weight_grad, grad_first,
        jnp.concatenate([sum(part.astype(f32) for part in parts) for parts in early] + [back[0].astype(f32)]),
    )
    base = 6 * model_width
    vec = [small[i * model_width:(i + 1) * model_width] for i in range(6)]
    up_bias_grad = lax.dynamic_slice(small, (base + zi * units_here,), (units_here,))
    qkv_bias_grad = lax.dynamic_slice(
        small, (base + zsize * units_here + zi * 3 * head_cols,), (3 * head_cols,)
    ).reshape(3, head_cols)
    shape3 = (groups, local_rows, model_width)
    return (
        result_low.reshape(shape3),
        embedded.reshape(groups, local_rows, -1),
        tokens_grad.reshape(shape3),
        qkv_weight_grad,
        qkv_bias_grad,
        out_grad_w,
        vec[0], vec[1], vec[2],
        up_grad,
        up_bias_grad,
        down_grad,
        vec[3], vec[4], vec[5],
        proj_grad,
    )


def solution(mesh):
    dp_size, zsize = mesh.shape["dp"], mesh.shape["tensor"]
    side = math.isqrt(dp_size // 2) // 2
    cut = Mesh(mesh.devices.reshape(side, 2, side, 2, 2, zsize), DP + ("z",))
    rows3 = P(DP, "z", None)
    in_specs = (
        rows3, P(DP, None), P(None, None, "z"), P(None, "z"), P("z", None), P(), P(), P(),
        P(None, "z"), P("z"), P("z", None), P(), P(), P(), P(), rows3, rows3,
    )
    out_specs = (
        rows3, rows3, rows3, P(None, None, "z"), P(None, "z"), P("z", None), P(), P(), P(),
        P(None, "z"), P("z"), P("z", None), P(), P(), P(), P(),
    )

    def run(*args):
        return per_device(side * side, *args)

    return jax.shard_map(run, mesh=cut, in_specs=in_specs, out_specs=out_specs, check_vma=False)
```

```python
import functools
import math

import jax
import jax.numpy as jnp
from jax import lax
from jax.experimental import pallas as pl
from jax.experimental.pallas import tpu as pltpu
from jax.sharding import Mesh
from jax.sharding import PartitionSpec as P

HEAD_DIM = 64
eps = 1e-05
DP = ("xb", "x", "yb", "y", "core")
CELL = ("x", "y", "core")
ALL = DP + ("z",)
f32 = jnp.float32
bf16 = jnp.bfloat16
VMEM = 60 * 1024 * 1024


def doc_positions(segment_rows):
    below = segment_rows[:, None, :] < jnp.arange(4, dtype=jnp.int32)[None, :, None]
    starts = jnp.sum(below, axis=2, dtype=jnp.int32)
    row_index = jnp.arange(segment_rows.shape[1], dtype=jnp.int32)[None]
    start = starts[:, 3:4]
    for doc in (2, 1, 0):
        start = jnp.where(segment_rows == doc, starts[:, doc:doc + 1], start)
    return row_index - start


def rotary_tables(positions):
    half_dim = HEAD_DIM // 2
    lane = jnp.arange(2 * HEAD_DIM, dtype=jnp.int32)
    exponent = (lane % half_dim).astype(f32) * (2.0 / HEAD_DIM)
    frequency = jnp.exp(-exponent * math.log(10000.0))
    sign = jnp.where(lane % HEAD_DIM < half_dim, -1.0, 1.0)
    angles = positions.astype(f32)[..., None] * frequency
    return (jnp.cos(angles), jnp.sin(angles) * sign)


def norm_forward(field, gain, shift):
    row_mean = jnp.mean(field, axis=-1, keepdims=True)
    centred = field - row_mean
    variance = jnp.mean(centred * centred, axis=-1, keepdims=True)
    inv_std = lax.rsqrt(variance + eps)
    scaled = centred * inv_std
    return (scaled * gain + shift, scaled, inv_std)


def norm_backward(upstream, scaled, inv_std, gain):
    grad_scaled = upstream * gain
    grad_input = inv_std * (
        grad_scaled
        - jnp.mean(grad_scaled, axis=-1, keepdims=True)
        - scaled * jnp.mean(grad_scaled * scaled, axis=-1, keepdims=True)
    )
    return (grad_input, jnp.sum(upstream * scaled, axis=0), jnp.sum(upstream, axis=0))


BLOCK = 256


def turn_halves(field, sign_sine):
    lane = lax.broadcasted_iota(jnp.int32, field.shape, 1)
    half = HEAD_DIM // 2
    width = field.shape[1]
    swapped = jnp.where(lane % HEAD_DIM < half, pltpu.roll(field, width - half, 1), pltpu.roll(field, half, 1))
    return swapped * sign_sine


def scores_of(keys, queries):
    return lax.dot_general(keys, queries, (((1,), (1,)), ((), ())), preferred_element_type=f32)


def attend_kernel(group, lo_ref, hi_ref, tok_ref, w_ref, b_ref, cos_ref, sin_ref, seg_ref, mixed_ref, q_ref, k_ref, v_ref,
                  lse_ref, vt_ref, m_ref, l_ref, acc_ref):
    zsize, _, rows, _ = tok_ref.shape
    length = zsize * rows
    heads = q_ref.shape[1]
    pair = 2 * HEAD_DIM
    scale = HEAD_DIM ** (-0.5)

    def project(i, carry):
        at = pl.ds(pl.multiple_of(i * rows, rows), rows)
        x = tok_ref[i, 0]
        lane = lax.broadcasted_iota(jnp.int32, (rows, pair), 1)
        doc = seg_ref[0, at, :]
        same = lane - HEAD_DIM == doc
        low = lane < HEAD_DIM
        feature = lane < HEAD_DIM + 4
        extra_q = jnp.where(same, 1.0, 0.0)
        extra_k = jnp.where(jnp.logical_and(feature, jnp.logical_not(same)), -1e9, 0.0)
        cosine = cos_ref[0, at, :]
        sine = sin_ref[0, at, :]
        for c in range(3):
            field = jnp.dot(x, w_ref[c], preferred_element_type=f32) + b_ref[c:c + 1, :]
            for j in range(heads // 2):
                part = field[:, j * pair:(j + 1) * pair]
                if c < 2:
                    part = part * cosine + turn_halves(part, sine)
                if c == 0:
                    part = part * scale
                for h in range(2):
                    one = part if h == 0 else pltpu.roll(part, HEAD_DIM, 1)
                    head = 2 * j + h
                    if c == 0:
                        q_ref[0, head, at, :] = jnp.where(low, one, extra_q).astype(bf16)
                    elif c == 1:
                        k_ref[0, head, at, :] = jnp.where(low, one, extra_k).astype(bf16)
                    else:
                        one = jnp.where(low, one, 0.0)
                        v_ref[0, head, at, :] = one.astype(bf16)
                        vt_ref[head, :, at] = one.T[:HEAD_DIM].astype(bf16)
        return carry

    lax.fori_loop(0, zsize, project, 0)

    def query_block(i, carry):
        at = pl.ds(pl.multiple_of(i * BLOCK, BLOCK), BLOCK)
        m_ref[...] = jnp.full(m_ref.shape, -1e30, f32)
        l_ref[...] = jnp.zeros(l_ref.shape, f32)
        acc_ref[...] = jnp.zeros(acc_ref.shape, f32)

        def key_block(j, carry):
            keys_at = pl.ds(pl.multiple_of(j * BLOCK, BLOCK), BLOCK)
            st = [scores_of(k_ref[0, h, keys_at, :], q_ref[0, h, at, :]) for h in range(heads)]
            peak = m_ref[...]
            new = jnp.maximum(peak, jnp.concatenate([jnp.max(t, axis=0, keepdims=True) for t in st], axis=0))
            p = [jnp.exp(st[h] - new[h:h + 1, :]) for h in range(heads)]
            old = jnp.exp(peak - new)
            m_ref[...] = new
            l_ref[...] = l_ref[...] * old + jnp.concatenate([jnp.sum(t, axis=0, keepdims=True) for t in p], axis=0)
            part = [
                jnp.dot(vt_ref[h, :, keys_at], p[h].astype(bf16), preferred_element_type=f32) for h in range(heads)
            ]
            for h in range(heads):
                acc_ref[h] = acc_ref[h] * old[h:h + 1, :] + part[h]
            return carry

        lax.fori_loop(lo_ref[group, i], hi_ref[group, i], key_block, 0)
        out = [acc_ref[h] / l_ref[h:h + 1, :] for h in range(heads)]
        for j in range(heads // 2):
            both = jnp.concatenate([out[2 * j], out[2 * j + 1]], axis=0)
            mixed_ref[0, at, j * pair:(j + 1) * pair] = both.T.astype(bf16)
        lse_ref[0, :, at] = m_ref[...] + jnp.log(l_ref[...])
        return carry

    lax.fori_loop(0, length // BLOCK, query_block, 0)


def attend_forward(group, bounds, tokens, weight, bias, cosine, sine, docs):
    zsize, _, rows, width = tokens.shape
    length = zsize * rows
    cols = weight.shape[2]
    heads = cols // HEAD_DIM
    pair = 2 * HEAD_DIM
    whole = lambda shape: pl.BlockSpec(shape, lambda i, *_: (0,) * len(shape))
    of_group = lambda shape: pl.BlockSpec(shape, lambda i, *_: (group,) + (0,) * (len(shape) - 1))
    like = jax.ShapeDtypeStruct
    return pl.pallas_call(
        functools.partial(attend_kernel, group),
        grid_spec=pltpu.PrefetchScalarGridSpec(
            num_scalar_prefetch=2,
            grid=(1,),
            in_specs=[
                pl.BlockSpec((zsize, 1, rows, width), lambda i, *_: (0, group, 0, 0)),
                whole(weight.shape), whole(bias.shape),
                of_group((1, length, pair)), of_group((1, length, pair)), of_group((1, length, 1)),
            ],
            out_specs=[
                whole((1, length, cols)),
                whole((1, heads, length, pair)), whole((1, heads, length, pair)), whole((1, heads, length, pair)),
                whole((1, heads, length)),
            ],
            scratch_shapes=[
                pltpu.VMEM((heads, HEAD_DIM, length), bf16),
                pltpu.VMEM((heads, BLOCK), f32), pltpu.VMEM((heads, BLOCK), f32),
                pltpu.VMEM((heads, HEAD_DIM, BLOCK), f32),
            ],
        ),
        out_shape=[
            like((1, length, cols), bf16),
            like((1, heads, length, pair), bf16), like((1, heads, length, pair), bf16),
            like((1, heads, length, pair), bf16), like((1, heads, length), f32),
        ],
        compiler_params=pltpu.CompilerParams(vmem_limit_bytes=VMEM),
        cost_estimate=pl.CostEstimate(
            flops=2 * length * width * 3 * cols + 4 * length * length * cols,
            bytes_accessed=2 * length * width + 6 * width * cols + 8 * length * cols,
            transcendentals=length * length * heads,
        ),
    )(*bounds, tokens, weight, bias, cosine, sine, docs)


def attend_back_kernel(group, last, lo_ref, hi_ref, z_ref, q_ref, k_ref, v_ref, lse_ref, mixed_ref, cos_ref, sin_ref, tok_ref, w_ref, *refs):
    zsize, _, rows, _ = tok_ref.shape
    do_refs, refs = refs[:zsize], refs[zsize:]
    if group:
        before_ref, refs = refs[0], refs[1:]
    back_refs, refs = refs[:1 if last else zsize], refs[1 if last else zsize:]
    wgrad_ref, sum_ref, grad_ref, wsum_ref, dox_ref, kt_ref, delta_ref, dk_ref, dv_ref, dqt_ref = refs
    heads, length = q_ref.shape[1], q_ref.shape[2]
    pair = 2 * HEAD_DIM
    scale = HEAD_DIM ** (-0.5)
    blocks = length // BLOCK

    low_half = lax.broadcasted_iota(jnp.int32, (rows, pair), 1) < HEAD_DIM
    for step in range(zsize):
        at = pl.ds(pl.multiple_of(lax.rem(z_ref[0] + zsize - step, zsize) * rows, rows), rows)
        for j in range(heads // 2):
            upstream = do_refs[step][0, :, j * pair:(j + 1) * pair].astype(f32)
            product = (upstream * mixed_ref[0, at, j * pair:(j + 1) * pair].astype(f32)).T
            for h in range(2):
                head = 2 * j + h
                one = upstream if h == 0 else pltpu.roll(upstream, HEAD_DIM, 1)
                dox_ref[head, at, :] = jnp.where(low_half, one, 0.0).astype(bf16)
                delta_ref[head:head + 1, at] = jnp.sum(
                    product[h * HEAD_DIM:(h + 1) * HEAD_DIM], axis=0, keepdims=True
                )
                kt_ref[head, :, at] = k_ref[0, head, at, :].astype(f32).T[:HEAD_DIM].astype(bf16)
                dk_ref[head, at, :] = jnp.zeros((rows, pair), f32)
                dv_ref[head, at, :] = jnp.zeros((rows, pair), f32)

    sum_ref[...] = jnp.zeros(sum_ref.shape, f32)
    wsum_ref[...] = before_ref[...] if group else jnp.zeros(wsum_ref.shape, f32)

    def put(c, j, at, field):
        low = field.astype(bf16)
        grad_ref[c, at, j * pair:(j + 1) * pair] = low
        cols = pl.ds(j * pair, pair)
        sum_ref[c:c + 1, cols] = sum_ref[c:c + 1, cols] + jnp.sum(low.astype(f32), axis=0, keepdims=True)

    def back(field, at):
        return field * cos_ref[0, at, :] - turn_halves(field, sin_ref[0, at, :])

    def query_block(i, carry):
        at = pl.ds(pl.multiple_of(i * BLOCK, BLOCK), BLOCK)
        dqt_ref[...] = jnp.zeros(dqt_ref.shape, f32)

        def key_block(j, carry):
            keys_at = pl.ds(pl.multiple_of(j * BLOCK, BLOCK), BLOCK)
            every = range(heads)
            queries = [q_ref[0, h, at, :] for h in every]
            upstream = [dox_ref[h, at, :] for h in every]
            st = [scores_of(k_ref[0, h, keys_at, :], queries[h]) for h in every]
            dp = [scores_of(v_ref[0, h, keys_at, :], upstream[h]) for h in every]
            p = [jnp.exp(st[h] - lse_ref[0, h:h + 1, at]) for h in every]
            ds = [(p[h] * (dp[h] - delta_ref[h:h + 1, at])).astype(bf16) for h in every]
            dv = [jnp.dot(p[h].astype(bf16), upstream[h], preferred_element_type=f32) for h in every]
            dk = [jnp.dot(ds[h], queries[h], preferred_element_type=f32) for h in every]
            dq = [jnp.dot(kt_ref[h, :, keys_at], ds[h], preferred_element_type=f32) for h in every]
            for h in every:
                dv_ref[h, keys_at, :] = dv_ref[h, keys_at, :] + dv[h]
                dk_ref[h, keys_at, :] = dk_ref[h, keys_at, :] + dk[h]
                dqt_ref[h] = dqt_ref[h] + dq[h]
            return carry

        lax.fori_loop(lo_ref[group, i], hi_ref[group, i], key_block, 0)
        for j in range(heads // 2):
            both = jnp.concatenate([dqt_ref[2 * j], dqt_ref[2 * j + 1]], axis=0)
            put(0, j, at, back(both.T * scale, at))
        return carry

    lax.fori_loop(0, blocks, query_block, 0)

    def finish(i, carry):
        at = pl.ds(pl.multiple_of(i * BLOCK, BLOCK), BLOCK)
        low = lax.broadcasted_iota(jnp.int32, (BLOCK, pair), 1) < HEAD_DIM
        for j in range(heads // 2):
            field = jnp.where(low, dk_ref[2 * j, at, :], pltpu.roll(dk_ref[2 * j + 1, at, :], HEAD_DIM, 1))
            put(1, j, at, back(field, at))
            field = jnp.where(low, dv_ref[2 * j, at, :], pltpu.roll(dv_ref[2 * j + 1, at, :], HEAD_DIM, 1))
            put(2, j, at, field)
        return carry

    lax.fori_loop(0, blocks, finish, 0)

    def onward(i, target):
        at = pl.ds(pl.multiple_of(i * rows, rows), rows)
        total = None
        x = tok_ref[i, 0]
        for c in range(3):
            grad = grad_ref[c, at, :]
            part = lax.dot_general(grad, w_ref[c], (((1,), (1,)), ((), ())), preferred_element_type=f32)
            total = part if total is None else total + part
            wsum_ref[c] += lax.dot_general(x, grad, (((0,), (0,)), ((), ())), preferred_element_type=f32)
        target[...] = total.astype(bf16)

    for step in range(zsize):
        if last:
            onward(step, back_refs[0].at[0, step])
        else:
            onward(lax.rem(z_ref[0] + step, zsize), back_refs[step])
    wgrad_ref[...] = wsum_ref[...].astype(wgrad_ref.dtype)


def attend_backward(group, before, bounds, zi, kept, mixed, upstream, cosine, sine, tokens, weight):
    queries, keys, values, lse = kept
    _, heads, length, pair = queries.shape
    zsize, groups, rows, width = tokens.shape
    cols = heads * HEAD_DIM
    last = group == groups - 1
    whole = lambda shape: pl.BlockSpec(shape, lambda i, *_: (0,) * len(shape))
    of_group = lambda shape: pl.BlockSpec(shape, lambda i, *_: (group,) + (0,) * (len(shape) - 1))
    like = jax.ShapeDtypeStruct
    wide = (heads, length, pair)
    return pl.pallas_call(
        functools.partial(attend_back_kernel, group, last),
        grid_spec=pltpu.PrefetchScalarGridSpec(
            num_scalar_prefetch=3,
            grid=(1,),
            in_specs=[whole((1,) + wide)] * 3 + [
                whole((1, heads, length)), whole((1, length, cols)),
                of_group((1, length, pair)), of_group((1, length, pair)),
                pl.BlockSpec((zsize, 1, rows, width), lambda i, *_: (0, group, 0, 0)), whole(weight.shape),
            ] + [whole((1, rows, cols))] * zsize + [whole(weight.shape)] * (group > 0),
            out_specs=([whole((1, zsize, rows, width))] if last else [whole((rows, width))] * zsize) + [
                whole(weight.shape), whole((8, cols)),
            ],
            scratch_shapes=[
                pltpu.VMEM((3, length, cols), bf16), pltpu.VMEM(weight.shape, f32),
                pltpu.VMEM(wide, bf16), pltpu.VMEM((heads, HEAD_DIM, length), bf16), pltpu.VMEM((heads, length), f32),
                pltpu.VMEM(wide, f32), pltpu.VMEM(wide, f32), pltpu.VMEM((heads, HEAD_DIM, BLOCK), f32),
            ],
        ),
        out_shape=([like((1, zsize, rows, width), bf16)] if last else [like((rows, width), bf16)] * zsize) + [
            like(weight.shape, bf16 if last else f32), like((8, cols), f32),
        ],
        compiler_params=pltpu.CompilerParams(vmem_limit_bytes=VMEM),
        cost_estimate=pl.CostEstimate(
            flops=0 if last else 40 * length * length * cols,
            bytes_accessed=0 if last else 48 * length * cols,
            transcendentals=0 if last else 2 * length * length * heads,
        ),
    )(*bounds, zi.reshape(1), queries, keys, values, lse, mixed, cosine, sine, tokens, weight, *upstream,
      *([before] if group else []))


MESH_ID = pl.DeviceIdType.MESH
HBM = pl.BlockSpec(memory_space=pl.ANY)


def other(axis):
    return {axis: 1 - lax.axis_index(axis)}


def greet(zsize):
    z = lax.axis_index("z")
    barrier = pltpu.get_barrier_semaphore()
    for axis in CELL:
        pl.semaphore_signal(barrier, inc=1, device_id=other(axis), device_id_type=MESH_ID)

    @pl.when(z > 0)
    def _():
        pl.semaphore_signal(barrier, inc=1, device_id={"z": z - 1}, device_id_type=MESH_ID)

    @pl.when(z < zsize - 1)
    def _():
        pl.semaphore_signal(barrier, inc=1, device_id={"z": z + 1}, device_id_type=MESH_ID)

    peers = len(CELL) + jnp.where(z > 0, 1, 0) + jnp.where(z < zsize - 1, 1, 0)
    pl.semaphore_wait(barrier, peers)


def remote(src, dst, send_sem, recv_sem, device):
    return pltpu.make_async_remote_copy(
        src_ref=src, dst_ref=dst, send_sem=send_sem, recv_sem=recv_sem, device_id=device, device_id_type=MESH_ID
    )


ORDERS = {"xy": ("x", "y"), "yx": ("y", "x")}


def gather_kernel(zsize, orders, *refs):
    n = len(orders)
    tok, bias, shards = refs[0], refs[1], refs[2:2 + n]
    tok_all, bias_all, wholes = refs[2 + n], refs[3 + n], refs[4 + n:4 + 2 * n]
    held = refs[4 + 2 * n:6 + 3 * n]
    local_sem, z_send, z_recv, p_send, p_recv = refs[6 + 3 * n:]
    z = lax.axis_index("z")
    c = lax.axis_index("core")
    place = [(lax.axis_index(o[0]), lax.axis_index(o[1])) for o in orders]

    sources = list(shards) + [tok, bias]
    targets = list(wholes) + [tok_all, bias_all]
    into = [pltpu.make_async_copy(sources[i], held[i], local_sem.at[0, i]) for i in range(n + 2)]
    local = [pltpu.make_async_copy(held[i], targets[i].at[z], local_sem.at[1, i]) for i in range(n + 2)]
    for copy in into:
        copy.start()
    greet(zsize)

    def line(item, src, step, side):
        to = z + 1 if side == 0 else z - 1
        if item < n:
            f, s = place[item]
            own = shards[item].at[c, f, s]
            dst = wholes[item].at[src, c, f, s]
        else:
            own = (tok, bias)[item - n]
            dst = (tok_all, bias_all)[item - n].at[src]
        return remote(
            own if step == 0 else dst, dst, z_send.at[side, item, step], z_recv.at[side, item, step], {"z": to}
        )

    def exchange(k, src, stage, slot):
        f, s = place[k]
        whole = wholes[k]
        ref = (whole.at[src, c, f, s], whole.at[src, c, f], whole.at[src, c])[stage]
        axis = (orders[k][1], orders[k][0], "core")[stage]
        return remote(ref, ref, p_send.at[slot, k, stage], p_recv.at[slot, k, stage], other(axis))

    def valid_from(side, step):
        return z - step - 1 >= 0 if side == 0 else z + step + 1 < zsize

    def source(side, step):
        return z - step - 1 if side == 0 else z + step + 1

    def has_next(side):
        return z < zsize - 1 if side == 0 else z > 0

    for side in range(2):

        @pl.when(has_next(side))
        def _():
            for item in range(n):
                line(item, z, 0, side).start()

    def stage_on(stage, step):
        for side in range(2):

            @pl.when(valid_from(side, step))
            def _():
                src = source(side, step)
                slot = side * (zsize - 1) + step
                for k in range(n):
                    exchange(k, src, stage - 1, slot).wait_recv()
                    if stage < 3:
                        exchange(k, src, stage, slot).start()

    def arrive(items, step):
        for side in range(2):

            @pl.when(valid_from(side, step))
            def _():
                src = source(side, step)
                for item in items:
                    line(item, src, step, side).wait_recv()
                    if step + 1 < zsize - 1:

                        @pl.when(has_next(side))
                        def _():
                            line(item, src, step + 1, side).start()

                    if item < n:
                        exchange(item, src, 0, side * (zsize - 1) + step).start()

    for copy, onward in zip(into, local):
        copy.wait()
        onward.start()
    for step in range(zsize - 1):
        arrive(range(n), step)
        if step == zsize - 2:
            for side in range(2):

                @pl.when(has_next(side))
                def _():
                    for item in range(n, n + 2):
                        line(item, z, 0, side).start()

        if step >= 1:
            stage_on(1, step - 1)
    for step in range(zsize - 1):
        if step == 0:
            stage_on(1, zsize - 2)
        stage_on(2, step)
        arrive(range(n, n + 2), step)
    for step in range(zsize - 1):
        stage_on(3, step)
    for copy in local:
        copy.wait()
    for side in range(2):

        @pl.when(has_next(side))
        def _():
            for item in range(n + 2):
                line(item, z, 0, side).wait_send()

        for step in range(zsize - 1):

            @pl.when(valid_from(side, step))
            def _():
                src = source(side, step)
                if step + 1 < zsize - 1:

                    @pl.when(has_next(side))
                    def _():
                        for item in range(n + 2):
                            line(item, src, step + 1, side).wait_send()

                for k in range(n):
                    for stage in range(3):
                        exchange(k, src, stage, side * (zsize - 1) + step).wait_send()


def gather_start(tokens, bias, weights, zsize):
    orders = [ORDERS[o] for o, _ in weights]
    shards = [w for _, w in weights]
    n = len(shards)
    stack = lambda a: jax.ShapeDtypeStruct((zsize,) + a.shape, a.dtype)
    return pl.pallas_call(
        functools.partial(gather_kernel, zsize, orders),
        out_shape=[stack(tokens), stack(bias)] + [stack(w) for w in shards],
        in_specs=[HBM] * (n + 2),
        out_specs=[HBM] * (n + 2),
        scratch_shapes=[pltpu.VMEM(a.shape, a.dtype) for a in shards + [tokens, bias]] + [
            pltpu.SemaphoreType.DMA((2, n + 2)),
            pltpu.SemaphoreType.DMA((2, n + 2, zsize - 1)),
            pltpu.SemaphoreType.DMA((2, n + 2, zsize - 1)),
            pltpu.SemaphoreType.DMA((2 * (zsize - 1), n, 3)),
            pltpu.SemaphoreType.DMA((2 * (zsize - 1), n, 3)),
        ],
        compiler_params=pltpu.CompilerParams(
            collective_id=0, has_side_effects=True, vmem_limit_bytes=VMEM
        ),
    )(tokens, bias, *shards)


def add_rows(dst, src):
    rows = dst.shape[0]
    step = math.gcd(rows, 32)

    def body(i, carry):
        at = pl.ds(pl.multiple_of(i * step, step), step)
        dst[at, :] = dst[at, :] + src[at, :]
        return carry

    lax.fori_loop(0, rows // step, body, 0)


def reduce_kernel(zsize, orders, w, *refs):
    n = 3
    p = len(orders) - n
    items = n + p
    pieces, came, refs = refs[:p], refs[p:2 * p], refs[2 * p:]
    parts, backs, small = refs[:n], refs[n], refs[n + 1]
    pos = n + 2
    piece_out, part_out, back_out = refs[pos:pos + p], refs[pos + p:pos + p + n], refs[pos + p + n]
    small_out = refs[pos + p + n + 1]
    outs = list(part_out) + list(piece_out)
    pos += p + n + 2
    mine = refs[pos:pos + items + w]
    pos += items + w
    got_c, got_1, got_2 = refs[pos:pos + n], refs[pos + n:pos + n + items], refs[pos + n + items:pos + n + 2 * items]
    pos += n + 2 * items
    lines = [0] + list(range(n, items + w))
    line_backs = list(range(items, items + w))
    got_z = dict(zip(lines, refs[pos:pos + len(lines)]))
    pos += len(lines)
    small_mine, small_got, small_line, small_total, part_line, part_total = refs[pos:pos + 6]
    (local_sem, send, recv, z_send, z_recv, s_send, s_recv, t_send, t_recv, g_send, g_recv, end_sem) = refs[pos + 6:]
    z = lax.axis_index("z")
    c = lax.axis_index("core")
    orders = orders[p:] + orders[:p]
    place = [(lax.axis_index(o[0]), lax.axis_index(o[1])) for o in orders]
    turn = []
    for i in range(zsize // 2):
        turn += [i, zsize - 1 - i]
    few = parts[1].shape[0]
    steps = [(1, b) for b in range(few)] + [(2, 0)] + [(0, b) for b in turn]

    def load(k, b):
        src = parts[k].at[b, c] if k < n else pieces[k - n].at[b] if k < items else backs.at[k - items, b]
        return pltpu.make_async_copy(src, mine[k].at[b], local_sem.at[k, b])

    def load_came(k, b):
        return pltpu.make_async_copy(came[k - n].at[b], got_1[k].at[b], local_sem.at[items + w + 1 + k - n, b])

    load_small = pltpu.make_async_copy(small, small_mine.at[0], local_sem.at[items + w, 0])

    def half(k, b, stage):
        f, s = place[k]
        if stage == 0:
            src, dst, axis = parts[k].at[b, 1 - c], got_c[k].at[b], "core"
        elif stage == 1:
            src, dst, axis = mine[k].at[b, 1 - f], got_1[k].at[b], orders[k][0]
        else:
            held = mine[k].at[b, f] if k < n else mine[k].at[b]
            src, dst, axis = held.at[1 - s], got_2[k].at[b], orders[k][1]
        return remote(src, dst, send.at[stage, k, b], recv.at[stage, k, b], other(axis))

    def own(k, b):
        if k >= items:
            return mine[k].at[b]
        f, s = place[k]
        return mine[k].at[b, s] if k >= n else mine[k].at[b, f, s]

    def hop(k, b, side):
        to = z + 1 if side == 0 else z - 1
        at = b if side == 0 else jnp.where(b == z - 1, zsize, b)
        return remote(own(k, b), got_z[k].at[at], z_send.at[k, b], z_recv.at[k, at], {"z": to})

    def take(k, b, side):
        at = b if side == 0 else jnp.where(b == z, zsize, b)
        ref = got_z[k].at[at]
        sender = z - 1 if side == 0 else z + 1
        remote(own(k, b), ref, z_send.at[k, b], z_recv.at[k, at], {"z": sender}).wait_recv()
        add_rows(own(k, b), ref)

    def line_start(ks, messages):
        for side in range(2):

            @pl.when(z == (0 if side == 0 else zsize - 1))
            def _():
                for i in messages:
                    for k in ks:
                        hop(k, zsize - 1 - i if side == 0 else i, side).start()

    def line_slot(ks, slot):
        for i in range(slot):
            for side in range(2):
                b = zsize - 1 - i if side == 0 else i

                @pl.when(z == (slot - i if side == 0 else zsize - 1 - slot + i))
                def _():
                    for k in ks:
                        take(k, b, side)

                        @pl.when(z < b if side == 0 else z > b)
                        def _():
                            hop(k, b, side).start()

    def small_swap(stage):
        return remote(
            small_mine.at[stage], small_got.at[stage], s_send.at[stage], s_recv.at[stage], other(CELL[stage])
        )

    def small_step(stage):
        small_swap(stage).wait_recv()
        small_mine[stage + 1] = small_mine[stage] + small_got[stage]
        if stage < 2:
            small_swap(stage + 1).start()

    last = len(CELL)
    last_part = own(2, 0)

    def total_copy(item, way):
        line, total = ((small_line, small_total), (part_line, part_total))[item]
        src = (small_mine.at[last], last_part)[item] if way == 0 else total
        dst = line if way == 0 else total
        to = z + 1 if way == 0 else z - 1
        return remote(src, dst, t_send.at[item, way], t_recv.at[item, way], {"z": to})

    def total_step(tick):
        if 0 <= tick < zsize:

            @pl.when(z == tick)
            def _():
                if tick > 0:
                    for item in range(2):
                        total_copy(item, 0).wait_recv()
                    small_mine[last] = small_mine[last] + small_line[...]
                    add_rows(last_part, part_line)
                if tick < zsize - 1:
                    for item in range(2):
                        total_copy(item, 0).start()
                else:
                    small_total[...] = small_mine[last]
                    part_total[...] = last_part[...]

        back_tick = tick - (zsize - 1)
        if 0 <= back_tick < zsize:

            @pl.when(z == zsize - 1 - back_tick)
            def _():
                if back_tick > 0:
                    for item in range(2):
                        total_copy(item, 1).wait_recv()
                if back_tick < zsize - 1:
                    for item in range(2):
                        total_copy(item, 1).start()

    line_pieces = list(range(n, items))
    piece_steps = [(k, b) for b in turn for k in line_pieces]
    for b in turn:
        for k in line_backs:
            load(k, b).start()
    for k, b in piece_steps:
        load(k, b).start()
        load_came(k, b).start()
    for k, b in steps:
        load(k, b).start()
    load_small.start()
    greet(zsize)
    for k, b in steps:
        half(k, b, 0).start()
    for b in turn:
        for k in line_backs:
            load(k, b).wait()
    line_start(line_backs, [0])
    load_small.wait()
    small_swap(0).start()

    def stage_1(k, b):
        f, s = place[k]
        load(k, b).wait()
        half(k, b, 0).wait_recv()
        for i in range(2):
            add_rows(mine[k].at[b, 1 - f, i], got_c[k].at[b, 1 - f, i])
        half(k, b, 1).start()
        for i in range(2):
            add_rows(mine[k].at[b, f, i], got_c[k].at[b, f, i])

    def stage_2(k, b):
        f, s = place[k]
        held = mine[k].at[b, f] if k < n else mine[k].at[b]
        if k < n:
            half(k, b, 1).wait_recv()
        else:
            load(k, b).wait()
            load_came(k, b).wait()
        add_rows(held.at[1 - s], got_1[k].at[b, 1 - s])
        half(k, b, 2).start()
        add_rows(held.at[s], got_1[k].at[b, s])

    def stage_3(k, b):
        half(k, b, 2).wait_recv()
        add_rows(own(k, b), got_2[k].at[b])

    def result(k, b):
        return part_total if k == 2 else own(k, b)

    def out_of(k, b):
        return outs[k].at[b] if k == 1 else outs[k]

    def put(k, b, slot):
        f, s = place[k]
        return pltpu.make_async_copy(result(k, b), out_of(k, b).at[c, f, s], end_sem.at[slot])

    def spread(k, b, stage, slot):
        f, s = place[k]
        out = out_of(k, b)
        dst = (out.at[c, f, s], out.at[c, f], out.at[c])[stage]
        src = result(k, b) if stage == 0 else dst
        axis = (orders[k][1], orders[k][0], "core")[stage]
        return remote(src, dst, g_send.at[slot, stage], g_recv.at[slot, stage], other(axis))

    spreads = [
        [(1, b, b) for b in range(few)],
        [(k, z, few + k - n) for k in line_pieces],
        [(0, z, few + p), (2, 0, few + p + 1)],
    ]

    def spread_step(group, stage):
        for k, b, slot in spreads[group]:
            if stage == 0:
                spread(k, b, 0, slot).start()
                put(k, b, slot).start()
                continue
            if stage == 1:
                put(k, b, slot).wait()
            spread(k, b, stage - 1, slot).wait_recv()
            if stage < 3:
                spread(k, b, stage, slot).start()

    def sent(ks):
        for b in range(zsize):

            @pl.when(z != b)
            def _():
                for k in ks:
                    hop(k, b, 0).wait_send()

    at_end = jnp.logical_or(z == 0, z == zsize - 1)
    for k, b in piece_steps:
        stage_2(k, b)
    for k, b in steps:
        stage_1(k, b)
    small_step(0)
    for b in turn:
        for k in line_pieces:
            stage_3(k, b)
        for side in range(2):

            @pl.when(jnp.logical_and(z == (0 if side == 0 else zsize - 1), z != b))
            def _():
                for k in line_pieces:
                    hop(k, b, side).start()

    for k, b in steps:
        stage_2(k, b)
    small_step(1)
    line_slot(line_backs, 1)
    for k, b in steps:
        stage_3(k, b)
    small_step(2)
    spread_step(0, 0)
    line_start([0], range(zsize - 1))
    total_step(0)

    @pl.when(at_end)
    def _():
        sent(line_pieces)

    line_start(line_backs, range(1, zsize - 1))
    ticks = list(range(1, 2 * zsize - 1))
    later = [(0, 1), (0, 2), (0, 3)]

    def fill(group_stages, count):
        for _ in range(count):
            if group_stages:
                spread_step(*group_stages.pop(0))

    for slot in range(1, zsize):
        line_slot(line_pieces, slot)
        total_step(ticks.pop(0))
        fill(later, 1)
        if slot >= 2:
            line_slot([0], slot - 1)
    fill(later, 3)
    spread_step(1, 0)
    later = [(1, 1), (1, 2), (1, 3)]
    total_step(ticks.pop(0))
    line_slot([0], zsize - 1)
    for slot in range(2, zsize - 1):
        line_slot(line_backs, slot)
        fill(later, 1)
    for tick in ticks:
        total_step(tick)
    spread_step(2, 0)
    fill(later, 1)
    spread_step(2, 1)
    fill(later, 1)
    spread_step(2, 2)
    fill(later, 3)
    line_slot(line_backs, zsize - 1)
    finish_back = [
        pltpu.make_async_copy(mine[k].at[z], back_out.at[k - items], local_sem.at[k, 0]) for k in line_backs
    ]
    for copy in finish_back:
        copy.start()
    finish_small = pltpu.make_async_copy(small_total, small_out, local_sem.at[items + w, 0])
    finish_small.start()
    spread_step(2, 3)
    for copy in finish_back:
        copy.wait()
    finish_small.wait()
    sent([0] + line_backs)

    @pl.when(jnp.logical_not(at_end))
    def _():
        sent(line_pieces)

    for way in range(2):

        @pl.when(z < zsize - 1 if way == 0 else z > 0)
        def _():
            for item in range(2):
                total_copy(item, way).wait_send()

    for k, b in steps:
        for stage in range(3):
            half(k, b, stage).wait_send()
    for k, b in piece_steps:
        half(k, b, 2).wait_send()
    for stage in range(3):
        small_swap(stage).wait_send()
    for group in spreads:
        for k, b, slot in group:
            for stage in range(3):
                spread(k, b, stage, slot).wait_send()


def reduce_end(pieces, parts, backs, small, zsize):
    orders = [ORDERS[o[0]] for o in pieces + parts]
    piece_arrays = [a for _, a, _ in pieces]
    came = [a for _, _, a in pieces]
    arrays = [a for _, a in parts]
    p, n, w = len(pieces), len(parts), backs.shape[0]
    shapes = [a.shape for a in arrays]
    like = jax.ShapeDtypeStruct
    outs = [like((2, 2, 2) + a.shape[2:], bf16) for a in piece_arrays]
    outs += [like(s if i == 1 else s[1:], bf16) for i, s in enumerate(shapes)]
    outs += [like((w,) + backs.shape[2:], bf16), like(small.shape, f32)]
    held = lambda shape: pltpu.VMEM(shape, bf16)
    scratch = [held((s[0],) + s[2:]) for s in shapes]
    scratch += [held(a.shape) for a in piece_arrays] + [held(backs.shape[1:])] * w
    scratch += [held((s[0],) + s[2:]) for s in shapes]
    scratch += [held((s[0],) + s[3:]) for s in shapes] + [held(a.shape) for a in piece_arrays]
    scratch += [held((s[0],) + s[4:]) for s in shapes] + [held(a.shape[:1] + a.shape[2:]) for a in piece_arrays]
    scratch += [held((zsize + 1,) + shapes[0][4:])]
    scratch += [held((zsize + 1,) + a.shape[2:]) for a in piece_arrays] + [held((zsize + 1,) + backs.shape[2:])] * w
    scratch += [pltpu.VMEM((4,) + small.shape, f32), pltpu.VMEM((3,) + small.shape, f32)]
    scratch += [pltpu.VMEM(small.shape, f32)] * 2 + [held(shapes[2][4:])] * 2
    dma = pltpu.SemaphoreType.DMA
    most = max(zsize, shapes[1][0])
    ends = shapes[1][0] + p + 2
    scratch += [
        dma((n + 2 * p + w + 1, most)), dma((3, n + p, most)), dma((3, n + p, most)),
        dma((n + p + w, zsize)), dma((n + p + w, zsize + 1)),
        dma((3,)), dma((3,)), dma((2, 2)), dma((2, 2)), dma((ends, 3)), dma((ends, 3)), dma((ends,)),
    ]
    return pl.pallas_call(
        functools.partial(reduce_kernel, zsize, orders, w),
        out_shape=outs,
        in_specs=[HBM] * (n + 2 * p + 2),
        out_specs=[HBM] * (n + p + 2),
        scratch_shapes=scratch,
        compiler_params=pltpu.CompilerParams(
            collective_id=1, has_side_effects=True, vmem_limit_bytes=VMEM
        ),
    )(*piece_arrays, *came, *arrays, backs, small)


def gelu_pair(v):
    size = jnp.abs(v)
    t = 1.0 / (1.0 + (0.3275911 * 0.5 ** 0.5) * size)
    bell = jnp.exp(-0.5 * (v * v))
    poly = t * (0.254829592 + t * (-0.284496736 + t * (1.421413741 + t * (-1.453152027 + t * 1.061405429))))
    tail = 0.5 * poly * bell
    cdf = jnp.where(v >= 0.0, 1.0 - tail, tail)
    return v * cdf, cdf + v * (bell * (1.0 / (2.0 * math.pi) ** 0.5))


def norm_rows(field):
    mean = jnp.mean(field, axis=-1, keepdims=True)
    centred = field - mean
    inv_std = lax.rsqrt(jnp.mean(centred * centred, axis=-1, keepdims=True) + eps)
    return centred * inv_std, inv_std


def ffn_kernel(zsize, groups, z_ref, tok_ref, out_ref, out_bias_ref, gain_one_ref, shift_one_ref, up_ref, bias_ref, down_ref,
               down_bias_ref, gain_two_ref, shift_two_ref, proj_ref, dy_ref, de_ref, *refs):
    pieces = refs[:zsize * groups]
    (active_ref, slope_ref, mixed_ref, x_ref, scaled_ref, inv_ref, result_ref, embed_ref, grad_ref, low_ref, proj_grad_ref,
     vec_ref, normed_ref, sum_ref) = refs[zsize * groups:]
    rows, width = x_ref.shape
    local = rows // groups
    cols = width // zsize
    chunk = 128
    heads = proj_ref.shape[0]

    @pl.when(pl.program_id(0) == 0)
    def _():
        for g in range(groups):
            for step in range(zsize):
                at = lax.rem(z_ref[0] + zsize - step, zsize) * cols
                mixed_ref[pl.ds(g * local, local), pl.ds(pl.multiple_of(at, cols), cols)] = pieces[g * zsize + step][0]
        for i in range(rows // chunk):
            at = pl.ds(i * chunk, chunk)
            attended = jnp.dot(mixed_ref[at, :], out_ref[...], preferred_element_type=f32) + out_bias_ref[...]
            scaled, inv_std = norm_rows(tok_ref[at, :].astype(f32) + attended)
            normed = scaled * gain_one_ref[...] + shift_one_ref[...]
            scaled_ref[at, :] = scaled
            inv_ref[at, :] = inv_std
            normed_ref[at, :] = normed
            x_ref[at, :] = normed.astype(bf16)
        sum_ref[...] = jnp.zeros(sum_ref.shape, f32)

    for i in range(2):
        at = pl.ds(i * (rows // 2), rows // 2)
        hidden = jnp.dot(x_ref[at, :], up_ref[0], preferred_element_type=f32) + bias_ref[0]
        active, slope = gelu_pair(hidden)
        active = active.astype(bf16)
        active_ref[0, at, :] = active
        slope_ref[0, at, :] = slope.astype(bf16)
        sum_ref[at, :] += jnp.dot(active, down_ref[0], preferred_element_type=f32)

    @pl.when(pl.program_id(0) == pl.num_programs(0) - 1)
    def _():
        total = [jnp.zeros((1, width), f32)] * 3
        for i in range(rows // chunk):
            at = pl.ds(i * chunk, chunk)
            scaled, inv_std = norm_rows(normed_ref[at, :] + (sum_ref[at, :] + down_bias_ref[...]))
            result_ref[at, :] = (scaled * gain_two_ref[...] + shift_two_ref[...]).astype(bf16)
            g, inner = i * chunk // local, i * chunk % local
            upstream = dy_ref[at, :].astype(f32) + lax.dot_general(
                de_ref[g, :, inner:inner + chunk], proj_ref[...], (((0,), (0,)), ((), ())), preferred_element_type=f32
            )
            grad_scaled = upstream * gain_two_ref[...]
            grad = inv_std * (
                grad_scaled
                - jnp.mean(grad_scaled, axis=-1, keepdims=True)
                - scaled * jnp.mean(grad_scaled * scaled, axis=-1, keepdims=True)
            )
            grad_ref[at, :] = grad
            low = grad.astype(bf16)
            low_ref[at, :] = low
            for n, field in enumerate((low.astype(f32), upstream * scaled, upstream)):
                total[n] = total[n] + jnp.sum(field, axis=0, keepdims=True)
        vec_ref[...] = jnp.zeros(vec_ref.shape, f32)
        for n in range(3):
            vec_ref[n:n + 1, :] = total[n]
        proj_grad = jnp.zeros((heads, width), f32)
        for g in range(groups):
            result = result_ref[pl.ds(g * local, local), :]
            embed_ref[g] = lax.dot_general(
                proj_ref[...], result, (((1,), (1,)), ((), ())), preferred_element_type=f32
            ).astype(bf16)
            proj_grad = proj_grad + jnp.dot(de_ref[g], result, preferred_element_type=f32)
        proj_grad_ref[...] = jnp.zeros(proj_grad_ref.shape, bf16)
        proj_grad_ref[pl.ds(0, heads), :] = proj_grad.astype(bf16)


def ffn_forward(zi, tokens, pieces, out_all, one, up_all, up_bias, down_all, two, proj, dy, de):
    zsize, width, units = up_all.shape
    rows = tokens.shape[0]
    groups, heads, local = de.shape
    tile = units // 2
    like = jax.ShapeDtypeStruct
    whole = lambda shape: pl.BlockSpec(shape, lambda s, z: (0,) * len(shape))
    tiles = pl.BlockSpec((1, rows, tile), lambda s, z: (s // 2, 0, s % 2))
    field, row = whole((rows, width)), whole((1, width))
    padded = heads + -heads % 128
    return pl.pallas_call(
        functools.partial(ffn_kernel, zsize, groups),
        grid_spec=pltpu.PrefetchScalarGridSpec(
            num_scalar_prefetch=1,
            grid=(2 * zsize,),
            in_specs=[
                field, whole((width, width)), row, row, row,
                pl.BlockSpec((1, width, tile), lambda s, z: (s // 2, 0, s % 2)),
                pl.BlockSpec((1, 1, tile), lambda s, z: (s // 2, 0, s % 2)),
                pl.BlockSpec((1, tile, width), lambda s, z: (s // 2, s % 2, 0)),
                row, row, row, whole(proj.shape), field, whole(de.shape),
            ] + [whole(p.shape) for p in pieces],
            out_specs=[
                tiles, tiles, field, field, field, whole((rows, 1)), field, whole(de.shape), field, field,
                whole((padded, width)), whole((8, width)),
            ],
            scratch_shapes=[pltpu.VMEM((rows, width), f32), pltpu.VMEM((rows, width), f32)],
        ),
        out_shape=[
            like((zsize, rows, units), bf16), like((zsize, rows, units), bf16), like((rows, width), bf16),
            like((rows, width), bf16), like((rows, width), f32), like((rows, 1), f32), like((rows, width), bf16),
            like(de.shape, bf16), like((rows, width), f32), like((rows, width), bf16), like((padded, width), bf16),
            like((8, width), f32),
        ],
        compiler_params=pltpu.CompilerParams(vmem_limit_bytes=VMEM),
    )(zi.reshape(1), tokens, out_all, *one, up_all, up_bias[:, None, :], down_all, *two, proj, dy, de, *pieces)


def ffn_back_kernel(core_ref, second_ref, normed_ref, up_ref, down_ref, active_ref, slope_ref,
                    give_up_ref, keep_up_ref, give_down_ref, keep_down_ref, back_ref, bias_ref, turned_ref):
    s = pl.program_id(0)
    half = turned_ref.shape[0] // 2
    c = core_ref[0]

    @pl.when(s == 0)
    def _():
        back_ref[...] = jnp.zeros(back_ref.shape, f32)
        turned_ref[...] = normed_ref[...].T

    second = second_ref[...]
    upstream = lax.dot_general(second, down_ref[0], (((1,), (1,)), ((), ())), preferred_element_type=f32)
    grad = (upstream * slope_ref[0].astype(f32)).astype(bf16)
    bias_ref[0] = jnp.sum(grad.astype(f32), axis=0, keepdims=True)
    down = lax.dot_general(active_ref[0], second, (((0,), (0,)), ((), ())), preferred_element_type=f32).astype(bf16)

    @pl.when(s % 2 == 0)
    def _():
        give_down_ref[0] = down

    @pl.when(s % 2 == 1)
    def _():
        keep_down_ref[0] = down

    back_ref[...] += lax.dot_general(grad, up_ref[0], (((1,), (1,)), ((), ())), preferred_element_type=f32)
    give = turned_ref[pl.ds(pl.multiple_of((1 - c) * half, half), half), :]
    give_up_ref[0] = jnp.dot(give, grad, preferred_element_type=f32).astype(bf16)
    keep = turned_ref[pl.ds(pl.multiple_of(c * half, half), half), :]
    keep_up_ref[0] = jnp.dot(keep, grad, preferred_element_type=f32).astype(bf16)


def ffn_backward(core, second_low, normed_low, up_all, down_all, active, slope):
    zsize, width, units = up_all.shape
    rows = normed_low.shape[0]
    tile = units // 2
    like = jax.ShapeDtypeStruct
    part = lambda s, c: (1 - c[0] + (2 * c[0] - 1) * (s % 2))
    whole = pl.BlockSpec((rows, width), lambda s, c: (0, 0))
    tiles = pl.BlockSpec((1, rows, tile), lambda s, c: (s // 2, 0, part(s, c)))
    up_half = pl.BlockSpec((1, width // 2, tile), lambda s, c: (s // 2, 0, part(s, c)))
    down_half = pl.BlockSpec((1, tile, width), lambda s, c: (s // 2, 0, 0))
    return pl.pallas_call(
        ffn_back_kernel,
        grid_spec=pltpu.PrefetchScalarGridSpec(
            num_scalar_prefetch=1,
            grid=(2 * zsize,),
            in_specs=[
                whole, whole,
                pl.BlockSpec((1, width, tile), lambda s, c: (s // 2, 0, part(s, c))),
                pl.BlockSpec((1, tile, width), lambda s, c: (s // 2, part(s, c), 0)),
                tiles, tiles,
            ],
            out_specs=[
                up_half, up_half, down_half, down_half, whole,
                pl.BlockSpec((1, 1, tile), lambda s, c: (s // 2, 0, part(s, c))),
            ],
            scratch_shapes=[pltpu.VMEM((width, rows), bf16)],
        ),
        out_shape=[
            like((zsize, width // 2, units), bf16), like((zsize, width // 2, units), bf16),
            like((zsize, tile, width), bf16), like((zsize, tile, width), bf16),
            like((rows, width), f32), like((zsize, 1, units), f32),
        ],
        compiler_params=pltpu.CompilerParams(vmem_limit_bytes=VMEM),
    )(core, second_low, normed_low, up_all, down_all, active, slope)


PAIR = [(0, 1), (1, 0)]


def first_halving(got, keep, order):
    zsize, half, cols = keep.shape
    shape = (zsize, 2, 2, half // 4, cols)
    got, keep = got.reshape(shape), keep.reshape(shape)
    i = lax.axis_index(ORDERS[order][0])
    pick = lambda array, j: lax.dynamic_index_in_dim(array, j, 1, keepdims=False)
    return pick(keep, 1 - i) + pick(got, 1 - i), pick(keep, i) + pick(got, i)


def widen_kernel(counts, up_ref, down_ref, out_ref, qkv_ref, first_ref, *refs):
    parts, (up_o, down_o, out_o, qkv_o, first_o) = refs[:-5], refs[-5:]
    for source, target in ((up_ref, up_o), (down_ref, down_o), (out_ref, out_o), (qkv_ref, qkv_o)):
        target[...] = source[...].astype(f32)
    per_group = pl.num_programs(0) // len(counts)
    for g, count in enumerate(counts):
        own, parts = parts[:count], parts[count:]

        @pl.when(pl.program_id(0) // per_group == g)
        def _():
            total = first_ref[...]
            for part in own:
                total = total + part[...].astype(f32)
            first_o[...] = total


def widen(up, down, out, qkv, first, parts):
    steps = 8
    per_group = steps // len(parts)

    def rows_of(array):
        return pl.BlockSpec((array.shape[0] // steps, array.shape[1]), lambda i: (i, 0))

    def of_group(g):
        block = first.shape[0] // steps
        return pl.BlockSpec((block, first.shape[1]), lambda i: (jnp.clip(i - g * per_group, 0, per_group - 1), 0))

    arrays = [up, down, out]
    specs = [rows_of(a) for a in arrays]
    specs.append(pl.BlockSpec((3, qkv.shape[1] // steps, qkv.shape[2]), lambda i: (0, i, 0)))
    specs.append(rows_of(first))
    return pl.pallas_call(
        functools.partial(widen_kernel, [len(p) for p in parts]),
        grid=(steps,),
        in_specs=specs + [of_group(g) for g, own in enumerate(parts) for _ in own],
        out_specs=specs,
        out_shape=[jax.ShapeDtypeStruct(a.shape, f32) for a in arrays + [qkv, first]],
        compiler_params=pltpu.CompilerParams(vmem_limit_bytes=VMEM),
    )(up, down, out, qkv, first, *[part for own in parts for part in own])


def per_device(blocks, tokens, segments, qkv_weight, qkv_bias, out_weight, out_bias, gain_one, shift_one,
               up_weight, up_bias, down_weight, down_bias, gain_two, shift_two, proj_weight, out_grad, embed_grad):
    groups, local_rows, model_width = tokens.shape
    length = segments.shape[1]
    zsize = length // local_rows
    head_cols = qkv_weight.shape[2]
    units_here = up_weight.shape[1]
    rows = groups * local_rows
    zi = lax.axis_index("z")
    cosine, sine = rotary_tables(doc_positions(segments))
    firsts = segments[:, ::BLOCK]
    lasts = segments[:, BLOCK - 1::BLOCK]
    bounds = (
        jnp.sum(segments[:, None, :] < firsts[:, :, None], axis=2, dtype=jnp.int32) // BLOCK,
        (jnp.sum(segments[:, None, :] <= lasts[:, :, None], axis=2, dtype=jnp.int32) + BLOCK - 1) // BLOCK,
    )
    docs = segments[:, :, None]

    def cut(array, rows_at):
        shape = array.shape
        return array.reshape(shape[:rows_at] + (2, 2, 2, shape[rows_at] // 8) + shape[rows_at + 1:])

    token_rows = tokens.reshape(rows, model_width)
    token_blocks, bias_blocks, out_all, up_all, down_all = gather_start(
        token_rows,
        up_bias.reshape(8, units_here // 8),
        [("xy", cut(out_weight, 0)), ("xy", cut(up_weight, 0)), ("yx", cut(down_weight, 0))],
        zsize,
    )
    token_blocks = token_blocks.reshape(zsize, groups, local_rows, model_width)
    out_all = out_all.reshape(model_width, model_width)
    up_all = up_all.reshape(zsize, model_width, units_here)
    down_all = down_all.reshape(zsize, units_here, model_width)
    full_up_bias = bias_blocks.reshape(zsize, units_here)

    def ring(step):
        return [(i, (i + step) % zsize) for i in range(zsize)]

    def exchange(array, size, axis):
        parts = []
        for step in range(zsize):
            part = lax.dynamic_slice_in_dim(array, lax.rem(zi + step, zsize) * size, size, axis)
            parts.append(lax.ppermute(part, "z", ring(step)) if step else part)
        return parts

    kept, pieces = [], []
    for g in range(groups):
        kept.append(attend_forward(g, bounds, token_blocks, qkv_weight, qkv_bias, cosine, sine, docs))
        pieces += exchange(kept[g][0], local_rows, 1)
    flat = lambda vector: vector.reshape(1, model_width)
    (active, slope, mixed, normed_low, scaled_one, inv_one, result_low, embedded, grad_second, second_low, proj_grad,
     vec_two) = ffn_forward(
        zi, token_rows, pieces, out_all, [flat(v) for v in (out_bias, gain_one, shift_one)], up_all, full_up_bias,
        down_all, [flat(v) for v in (down_bias, gain_two, shift_two)], proj_weight.T,
        out_grad.reshape(rows, model_width), embed_grad.transpose(0, 2, 1),
    )
    core = lax.axis_index("core").reshape(1)
    give_up, keep_up, give_down, keep_down, ffn_back, up_bias_grad = ffn_backward(
        core, second_low, normed_low, up_all, down_all, active, slope
    )
    got_down = lax.ppermute(give_down, "core", PAIR)
    got_up = lax.ppermute(give_up, "core", PAIR)
    grad_normed = grad_second + ffn_back
    grad_first, gain_one_grad, shift_one_grad = norm_backward(grad_normed, scaled_one, inv_one, gain_one)
    first_low = grad_first.astype(bf16)
    out_bias_grad = jnp.sum(first_low.astype(f32), axis=0)
    out_grad_w = jnp.einsum("nh,nd->hd", mixed, first_low, preferred_element_type=f32).astype(bf16)
    grad_mixed = jnp.einsum("nd,hd->nh", first_low, out_all, preferred_element_type=f32).astype(bf16)
    grad_mixed = grad_mixed.reshape(groups, local_rows, model_width)
    upstream = [exchange(grad_mixed[g:g + 1], head_cols, 2) for g in range(groups)]
    send_down, keep_down = first_halving(got_down, keep_down, "yx")
    send_up, keep_up = first_halving(got_up, keep_up, "xy")
    upstream[0], send_down, send_up = lax.optimization_barrier((upstream[0], send_down, send_up))
    got_down = lax.ppermute(send_down, ORDERS["yx"][0], PAIR)
    got_up = lax.ppermute(send_up, ORDERS["xy"][0], PAIR)
    qkv_weight_grad, qkv_bias_grad, early = None, 0.0, []
    for g in range(groups):
        *backs, qkv_weight_grad, bias_part = attend_backward(
            g, qkv_weight_grad, bounds, zi, kept[g][1:], kept[g][0], upstream[g], cosine, sine, token_blocks, qkv_weight
        )
        qkv_bias_grad = qkv_bias_grad + bias_part[:3]
        if g < groups - 1:
            early.append([
                lax.ppermute(part, "z", ring(step)) if step else part
                for step, part in enumerate(backs)
            ])
    backs, got_down, got_up, qkv_bias_grad = lax.optimization_barrier((backs[0], got_down, got_up, qkv_bias_grad))

    vec_one = jnp.pad(jnp.stack([out_bias_grad, gain_one_grad, shift_one_grad]), ((0, 5), (0, 0)))
    placed = lax.dynamic_update_slice(
        jnp.zeros((zsize, 3 * head_cols), f32), qkv_bias_grad.reshape(1, -1), (zi, 0)
    )
    small = jnp.concatenate([vec_one, vec_two, up_bias_grad.reshape(8, -1), placed.reshape(8, -1)], axis=1)
    up_grad, down_grad, out_grad_w, qkv_weight_grad, proj_grad, back, small = reduce_end(
        [("xy", keep_up, got_up), ("yx", keep_down, got_down)],
        [
            ("xy", cut(out_grad_w.reshape(zsize, head_cols, model_width), 1)),
            ("yx", cut(qkv_weight_grad, 1)),
            ("xy", cut(proj_grad[None], 1)),
        ],
        backs,
        small,
        zsize,
    )
    qkv_weight_grad = qkv_weight_grad.reshape(qkv_weight.shape)
    proj_grad = proj_grad.reshape(-1, model_width)[:proj_weight.shape[1]].astype(f32).T
    out_grad_w = out_grad_w.reshape(out_weight.shape)
    up_grad = up_grad.reshape(up_weight.shape)
    down_grad = down_grad.reshape(down_weight.shape)
    if blocks > 1:
        down_grad, up_grad, out_grad_w, qkv_weight_grad = lax.psum(
            (down_grad, up_grad, out_grad_w, qkv_weight_grad), ("xb", "yb")
        )
        small, proj_grad = lax.psum((small, proj_grad), ("xb", "yb"))
    up_grad, down_grad, out_grad_w, qkv_weight_grad, tokens_grad = widen(
        up_grad, down_grad, out_grad_w, qkv_weight_grad, grad_first, early + [[back[0]]]
    )
    base = 2 * model_width
    vec = list(small[:3, :model_width]) + list(small[:3, model_width:base])
    split = base + zsize * units_here // 8
    up_bias_grad = lax.dynamic_slice(small[:, base:split].reshape(-1), (zi * units_here,), (units_here,))
    qkv_bias_grad = lax.dynamic_slice(small[:, split:].reshape(-1), (zi * 3 * head_cols,), (3 * head_cols,))
    qkv_bias_grad = qkv_bias_grad.reshape(3, head_cols)
    shape3 = (groups, local_rows, model_width)
    return (
        result_low.reshape(shape3),
        embedded.transpose(0, 2, 1),
        tokens_grad.reshape(shape3),
        qkv_weight_grad,
        qkv_bias_grad,
        out_grad_w,
        vec[0], vec[1], vec[2],
        up_grad,
        up_bias_grad,
        down_grad,
        vec[3], vec[4], vec[5],
        proj_grad,
    )


def solution(mesh):
    dp_size, zsize = mesh.shape["dp"], mesh.shape["tensor"]
    side = math.isqrt(dp_size // 2) // 2
    cut = Mesh(mesh.devices.reshape(side, 2, side, 2, 2, zsize), DP + ("z",))
    rows3 = P(DP, "z", None)
    in_specs = (
        rows3, P(DP, None), P(None, None, "z"), P(None, "z"), P("z", None), P(), P(), P(),
        P(None, "z"), P("z"), P("z", None), P(), P(), P(), P(), rows3, rows3,
    )
    out_specs = (
        rows3, rows3, rows3, P(None, None, "z"), P(None, "z"), P("z", None), P(), P(), P(),
        P(None, "z"), P("z"), P("z", None), P(), P(), P(), P(),
    )

    def run(*args):
        return per_device(side * side, *args)

    return jax.shard_map(run, mesh=cut, in_specs=in_specs, out_specs=out_specs, check_vma=False)
```

```python
import functools
import math

import jax
import jax.numpy as jnp
from jax import lax
from jax.experimental import pallas as pl
from jax.experimental.pallas import tpu as pltpu
from jax.sharding import Mesh
from jax.sharding import PartitionSpec as P

HEAD_DIM = 64
eps = 1e-05
DP = ("xb", "x", "yb", "y", "core")
CELL = ("x", "y", "core")
ALL = DP + ("z",)
f32 = jnp.float32
bf16 = jnp.bfloat16
VMEM = 60 * 1024 * 1024


def doc_positions(segment_rows):
    below = segment_rows[:, None, :] < jnp.arange(4, dtype=jnp.int32)[None, :, None]
    starts = jnp.sum(below, axis=2, dtype=jnp.int32)
    row_index = jnp.arange(segment_rows.shape[1], dtype=jnp.int32)[None]
    start = starts[:, 3:4]
    for doc in (2, 1, 0):
        start = jnp.where(segment_rows == doc, starts[:, doc:doc + 1], start)
    return row_index - start


def rotary_tables(positions):
    half_dim = HEAD_DIM // 2
    lane = jnp.arange(2 * HEAD_DIM, dtype=jnp.int32)
    exponent = (lane % half_dim).astype(f32) * (2.0 / HEAD_DIM)
    frequency = jnp.exp(-exponent * math.log(10000.0))
    sign = jnp.where(lane % HEAD_DIM < half_dim, -1.0, 1.0)
    angles = positions.astype(f32)[..., None] * frequency
    return (jnp.cos(angles), jnp.sin(angles) * sign)


def norm_forward(field, gain, shift):
    row_mean = jnp.mean(field, axis=-1, keepdims=True)
    centred = field - row_mean
    variance = jnp.mean(centred * centred, axis=-1, keepdims=True)
    inv_std = lax.rsqrt(variance + eps)
    scaled = centred * inv_std
    return (scaled * gain + shift, scaled, inv_std)


def norm_backward(upstream, scaled, inv_std, gain):
    grad_scaled = upstream * gain
    grad_input = inv_std * (
        grad_scaled
        - jnp.mean(grad_scaled, axis=-1, keepdims=True)
        - scaled * jnp.mean(grad_scaled * scaled, axis=-1, keepdims=True)
    )
    return (grad_input, jnp.sum(upstream * scaled, axis=0), jnp.sum(upstream, axis=0))


BLOCK = 256


def turn_halves(field, sign_sine):
    lane = lax.broadcasted_iota(jnp.int32, field.shape, 1)
    half = HEAD_DIM // 2
    width = field.shape[1]
    swapped = jnp.where(lane % HEAD_DIM < half, pltpu.roll(field, width - half, 1), pltpu.roll(field, half, 1))
    return swapped * sign_sine


def scores_of(keys, queries):
    return lax.dot_general(keys, queries, (((1,), (1,)), ((), ())), preferred_element_type=f32)


def attend_kernel(group, lo_ref, hi_ref, tok_ref, w_ref, b_ref, cos_ref, sin_ref, seg_ref, mixed_ref, q_ref, k_ref, v_ref,
                  lse_ref, vt_ref, m_ref, l_ref, acc_ref):
    zsize, _, rows, _ = tok_ref.shape
    length = zsize * rows
    heads = q_ref.shape[1]
    pair = 2 * HEAD_DIM
    scale = HEAD_DIM ** (-0.5)

    def project(i, carry):
        at = pl.ds(pl.multiple_of(i * rows, rows), rows)
        x = tok_ref[i, 0]
        lane = lax.broadcasted_iota(jnp.int32, (rows, pair), 1)
        low = lane < HEAD_DIM
        doc = lax.broadcasted_iota(jnp.int32, (pair, rows), 0) - HEAD_DIM
        extra_q = jnp.where(doc == seg_ref[group:group + 1, at], 1.0, 0.0).T
        extra_k = jnp.where(lane < HEAD_DIM + 4, (extra_q - 1.0) * 1e9, 0.0)
        cosine = cos_ref[0, at, :]
        sine = sin_ref[0, at, :]
        for c in range(3):
            field = jnp.dot(x, w_ref[c], preferred_element_type=f32) + b_ref[c:c + 1, :]
            for j in range(heads // 2):
                part = field[:, j * pair:(j + 1) * pair]
                if c < 2:
                    part = part * cosine + turn_halves(part, sine)
                if c == 0:
                    part = part * scale
                for h in range(2):
                    one = part if h == 0 else pltpu.roll(part, HEAD_DIM, 1)
                    head = 2 * j + h
                    if c == 0:
                        q_ref[0, head, at, :] = jnp.where(low, one, extra_q).astype(bf16)
                    elif c == 1:
                        k_ref[0, head, at, :] = jnp.where(low, one, extra_k).astype(bf16)
                    else:
                        one = jnp.where(low, one, 0.0)
                        v_ref[0, head, at, :] = one.astype(bf16)
                        vt_ref[head, :, at] = one.T[:HEAD_DIM].astype(bf16)
        return carry

    lax.fori_loop(0, zsize, project, 0)

    def query_block(i, carry):
        at = pl.ds(pl.multiple_of(i * BLOCK, BLOCK), BLOCK)
        m_ref[...] = jnp.full(m_ref.shape, -1e30, f32)
        l_ref[...] = jnp.zeros(l_ref.shape, f32)
        acc_ref[...] = jnp.zeros(acc_ref.shape, f32)

        def key_block(j, carry):
            keys_at = pl.ds(pl.multiple_of(j * BLOCK, BLOCK), BLOCK)
            st = [scores_of(k_ref[0, h, keys_at, :], q_ref[0, h, at, :]) for h in range(heads)]
            peak = m_ref[...]
            new = jnp.maximum(peak, jnp.concatenate([jnp.max(t, axis=0, keepdims=True) for t in st], axis=0))
            p = [jnp.exp(st[h] - new[h:h + 1, :]) for h in range(heads)]
            old = jnp.exp(peak - new)
            m_ref[...] = new
            l_ref[...] = l_ref[...] * old + jnp.concatenate([jnp.sum(t, axis=0, keepdims=True) for t in p], axis=0)
            part = [
                jnp.dot(vt_ref[h, :, keys_at], p[h].astype(bf16), preferred_element_type=f32) for h in range(heads)
            ]
            for h in range(heads):
                acc_ref[h] = acc_ref[h] * old[h:h + 1, :] + part[h]
            return carry

        lax.fori_loop(lo_ref[group, i], hi_ref[group, i], key_block, 0)
        out = [acc_ref[h] / l_ref[h:h + 1, :] for h in range(heads)]
        for j in range(heads // 2):
            both = jnp.concatenate([out[2 * j], out[2 * j + 1]], axis=0)
            mixed_ref[0, at, j * pair:(j + 1) * pair] = both.T.astype(bf16)
        lse_ref[0, :, at] = m_ref[...] + jnp.log(l_ref[...])
        return carry

    lax.fori_loop(0, length // BLOCK, query_block, 0)


def attend_forward(group, bounds, tokens, weight, bias, cosine, sine, docs):
    zsize, _, rows, width = tokens.shape
    length = zsize * rows
    cols = weight.shape[2]
    heads = cols // HEAD_DIM
    pair = 2 * HEAD_DIM
    whole = lambda shape: pl.BlockSpec(shape, lambda i, *_: (0,) * len(shape))
    of_group = lambda shape: pl.BlockSpec(shape, lambda i, *_: (group,) + (0,) * (len(shape) - 1))
    like = jax.ShapeDtypeStruct
    return pl.pallas_call(
        functools.partial(attend_kernel, group),
        grid_spec=pltpu.PrefetchScalarGridSpec(
            num_scalar_prefetch=2,
            grid=(1,),
            in_specs=[
                pl.BlockSpec((zsize, 1, rows, width), lambda i, *_: (0, group, 0, 0)),
                whole(weight.shape), whole(bias.shape),
                of_group((1, length, pair)), of_group((1, length, pair)), whole(docs.shape),
            ],
            out_specs=[
                whole((1, length, cols)),
                whole((1, heads, length, pair)), whole((1, heads, length, pair)), whole((1, heads, length, pair)),
                whole((1, heads, length)),
            ],
            scratch_shapes=[
                pltpu.VMEM((heads, HEAD_DIM, length), bf16),
                pltpu.VMEM((heads, BLOCK), f32), pltpu.VMEM((heads, BLOCK), f32),
                pltpu.VMEM((heads, HEAD_DIM, BLOCK), f32),
            ],
        ),
        out_shape=[
            like((1, length, cols), bf16),
            like((1, heads, length, pair), bf16), like((1, heads, length, pair), bf16),
            like((1, heads, length, pair), bf16), like((1, heads, length), f32),
        ],
        compiler_params=pltpu.CompilerParams(vmem_limit_bytes=VMEM),
        cost_estimate=pl.CostEstimate(
            flops=2 * length * width * 3 * cols + 4 * length * length * cols,
            bytes_accessed=2 * length * width + 6 * width * cols + 8 * length * cols,
            transcendentals=length * length * heads,
        ),
    )(*bounds, tokens, weight, bias, cosine, sine, docs)


def attend_back_kernel(group, last, lo_ref, hi_ref, z_ref, q_ref, k_ref, v_ref, lse_ref, mixed_ref, cos_ref, sin_ref, tok_ref, w_ref, *refs):
    zsize, _, rows, _ = tok_ref.shape
    do_refs, refs = refs[:zsize], refs[zsize:]
    if group:
        before_ref, refs = refs[0], refs[1:]
    back_ref, wgrad_ref, sum_ref, grad_ref, wsum_ref, dox_ref, kt_ref, delta_ref, dk_ref, dv_ref, dqt_ref = refs
    heads, length = q_ref.shape[1], q_ref.shape[2]
    pair = 2 * HEAD_DIM
    scale = HEAD_DIM ** (-0.5)
    blocks = length // BLOCK

    low_half = lax.broadcasted_iota(jnp.int32, (rows, pair), 1) < HEAD_DIM
    for step in range(zsize):
        at = pl.ds(pl.multiple_of(lax.rem(z_ref[0] + zsize - step, zsize) * rows, rows), rows)
        for j in range(heads // 2):
            upstream = do_refs[step][0, :, j * pair:(j + 1) * pair].astype(f32)
            product = (upstream * mixed_ref[0, at, j * pair:(j + 1) * pair].astype(f32)).T
            for h in range(2):
                head = 2 * j + h
                one = upstream if h == 0 else pltpu.roll(upstream, HEAD_DIM, 1)
                dox_ref[head, at, :] = jnp.where(low_half, one, 0.0).astype(bf16)
                delta_ref[head:head + 1, at] = jnp.sum(
                    product[h * HEAD_DIM:(h + 1) * HEAD_DIM], axis=0, keepdims=True
                )
                kt_ref[head, :, at] = k_ref[0, head, at, :].astype(f32).T[:HEAD_DIM].astype(bf16)
                dk_ref[head, at, :] = jnp.zeros((rows, pair), f32)
                dv_ref[head, at, :] = jnp.zeros((rows, pair), f32)

    sum_ref[...] = jnp.zeros(sum_ref.shape, f32)
    wsum_ref[...] = before_ref[...] if group else jnp.zeros(wsum_ref.shape, f32)

    def put(c, j, at, field):
        low = field.astype(bf16)
        grad_ref[c, at, j * pair:(j + 1) * pair] = low
        cols = pl.ds(j * pair, pair)
        sum_ref[c:c + 1, cols] = sum_ref[c:c + 1, cols] + jnp.sum(low.astype(f32), axis=0, keepdims=True)

    def back(field, at):
        return field * cos_ref[0, at, :] - turn_halves(field, sin_ref[0, at, :])

    def query_block(i, carry):
        at = pl.ds(pl.multiple_of(i * BLOCK, BLOCK), BLOCK)
        dqt_ref[...] = jnp.zeros(dqt_ref.shape, f32)

        def key_block(j, carry):
            keys_at = pl.ds(pl.multiple_of(j * BLOCK, BLOCK), BLOCK)
            every = range(heads)
            queries = [q_ref[0, h, at, :] for h in every]
            upstream = [dox_ref[h, at, :] for h in every]
            st = [scores_of(k_ref[0, h, keys_at, :], queries[h]) for h in every]
            dp = [scores_of(v_ref[0, h, keys_at, :], upstream[h]) for h in every]
            p = [jnp.exp(st[h] - lse_ref[0, h:h + 1, at]) for h in every]
            ds = [(p[h] * (dp[h] - delta_ref[h:h + 1, at])).astype(bf16) for h in every]
            dv = [jnp.dot(p[h].astype(bf16), upstream[h], preferred_element_type=f32) for h in every]
            dk = [jnp.dot(ds[h], queries[h], preferred_element_type=f32) for h in every]
            dq = [jnp.dot(kt_ref[h, :, keys_at], ds[h], preferred_element_type=f32) for h in every]
            for h in every:
                dv_ref[h, keys_at, :] = dv_ref[h, keys_at, :] + dv[h]
                dk_ref[h, keys_at, :] = dk_ref[h, keys_at, :] + dk[h]
                dqt_ref[h] = dqt_ref[h] + dq[h]
            return carry

        lax.fori_loop(lo_ref[group, i], hi_ref[group, i], key_block, 0)
        for j in range(heads // 2):
            both = jnp.concatenate([dqt_ref[2 * j], dqt_ref[2 * j + 1]], axis=0)
            put(0, j, at, back(both.T * scale, at))
        return carry

    lax.fori_loop(0, blocks, query_block, 0)

    def finish(i, carry):
        at = pl.ds(pl.multiple_of(i * BLOCK, BLOCK), BLOCK)
        low = lax.broadcasted_iota(jnp.int32, (BLOCK, pair), 1) < HEAD_DIM
        for j in range(heads // 2):
            field = jnp.where(low, dk_ref[2 * j, at, :], pltpu.roll(dk_ref[2 * j + 1, at, :], HEAD_DIM, 1))
            put(1, j, at, back(field, at))
            field = jnp.where(low, dv_ref[2 * j, at, :], pltpu.roll(dv_ref[2 * j + 1, at, :], HEAD_DIM, 1))
            put(2, j, at, field)
        return carry

    lax.fori_loop(0, blocks, finish, 0)

    def onward(slot, carry):
        i = slot if last else lax.rem(z_ref[0] + slot, zsize)
        at = pl.ds(pl.multiple_of(i * rows, rows), rows)
        total = None
        x = tok_ref[i, 0]
        for c in range(3):
            grad = grad_ref[c, at, :]
            part = lax.dot_general(grad, w_ref[c], (((1,), (1,)), ((), ())), preferred_element_type=f32)
            total = part if total is None else total + part
            wsum_ref[c] += lax.dot_general(x, grad, (((0,), (0,)), ((), ())), preferred_element_type=f32)
        back_ref[0, slot] = total.astype(bf16)
        return carry

    lax.fori_loop(0, zsize, onward, 0)
    wgrad_ref[...] = wsum_ref[...].astype(wgrad_ref.dtype)


def attend_backward(group, before, bounds, zi, kept, mixed, upstream, cosine, sine, tokens, weight):
    queries, keys, values, lse = kept
    _, heads, length, pair = queries.shape
    zsize, groups, rows, width = tokens.shape
    cols = heads * HEAD_DIM
    last = group == groups - 1
    whole = lambda shape: pl.BlockSpec(shape, lambda i, *_: (0,) * len(shape))
    of_group = lambda shape: pl.BlockSpec(shape, lambda i, *_: (group,) + (0,) * (len(shape) - 1))
    like = jax.ShapeDtypeStruct
    wide = (heads, length, pair)
    return pl.pallas_call(
        functools.partial(attend_back_kernel, group, last),
        grid_spec=pltpu.PrefetchScalarGridSpec(
            num_scalar_prefetch=3,
            grid=(1,),
            in_specs=[whole((1,) + wide)] * 3 + [
                whole((1, heads, length)), whole((1, length, cols)),
                of_group((1, length, pair)), of_group((1, length, pair)),
                pl.BlockSpec((zsize, 1, rows, width), lambda i, *_: (0, group, 0, 0)), whole(weight.shape),
            ] + [whole((1, rows, cols))] * zsize + [whole(weight.shape)] * (group > 0),
            out_specs=[whole((1, zsize, rows, width)), whole(weight.shape), whole((8, cols))],
            scratch_shapes=[
                pltpu.VMEM((3, length, cols), bf16), pltpu.VMEM(weight.shape, f32),
                pltpu.VMEM(wide, bf16), pltpu.VMEM((heads, HEAD_DIM, length), bf16), pltpu.VMEM((heads, length), f32),
                pltpu.VMEM(wide, f32), pltpu.VMEM(wide, f32), pltpu.VMEM((heads, HEAD_DIM, BLOCK), f32),
            ],
        ),
        out_shape=[
            like((1, zsize, rows, width), bf16), like(weight.shape, bf16 if last else f32), like((8, cols), f32),
        ],
        compiler_params=pltpu.CompilerParams(vmem_limit_bytes=VMEM),
        cost_estimate=pl.CostEstimate(
            flops=0 if last else 40 * length * length * cols,
            bytes_accessed=0 if last else 48 * length * cols,
            transcendentals=0 if last else 2 * length * length * heads,
        ),
    )(*bounds, zi.reshape(1), queries, keys, values, lse, mixed, cosine, sine, tokens, weight, *upstream,
      *([before] if group else []))


MESH_ID = pl.DeviceIdType.MESH
HBM = pl.BlockSpec(memory_space=pl.ANY)


def other(axis):
    return {axis: 1 - lax.axis_index(axis)}


def greet(zsize):
    z = lax.axis_index("z")
    barrier = pltpu.get_barrier_semaphore()
    for axis in CELL:
        pl.semaphore_signal(barrier, inc=1, device_id=other(axis), device_id_type=MESH_ID)

    @pl.when(z > 0)
    def _():
        pl.semaphore_signal(barrier, inc=1, device_id={"z": z - 1}, device_id_type=MESH_ID)

    @pl.when(z < zsize - 1)
    def _():
        pl.semaphore_signal(barrier, inc=1, device_id={"z": z + 1}, device_id_type=MESH_ID)

    peers = len(CELL) + jnp.where(z > 0, 1, 0) + jnp.where(z < zsize - 1, 1, 0)
    pl.semaphore_wait(barrier, peers)


def remote(src, dst, send_sem, recv_sem, device):
    return pltpu.make_async_remote_copy(
        src_ref=src, dst_ref=dst, send_sem=send_sem, recv_sem=recv_sem, device_id=device, device_id_type=MESH_ID
    )


ORDERS = {"xy": ("x", "y"), "yx": ("y", "x")}


def gather_kernel(zsize, orders, *refs):
    n = len(orders)
    tok, bias, shards = refs[0], refs[1], refs[2:2 + n]
    tok_all, bias_all, wholes = refs[2 + n], refs[3 + n], refs[4 + n:4 + 2 * n]
    held = refs[4 + 2 * n:6 + 3 * n]
    local_sem, z_send, z_recv, p_send, p_recv = refs[6 + 3 * n:]
    z = lax.axis_index("z")
    c = lax.axis_index("core")
    place = [(lax.axis_index(o[0]), lax.axis_index(o[1])) for o in orders]

    sources = list(shards) + [tok, bias]
    targets = list(wholes) + [tok_all, bias_all]
    into = [pltpu.make_async_copy(sources[i], held[i], local_sem.at[0, i]) for i in range(n + 2)]
    local = [pltpu.make_async_copy(held[i], targets[i].at[z], local_sem.at[1, i]) for i in range(n + 2)]
    for copy in into:
        copy.start()
    greet(zsize)

    def line(item, src, step, side):
        to = z + 1 if side == 0 else z - 1
        if item < n:
            f, s = place[item]
            own = shards[item].at[c, f, s]
            dst = wholes[item].at[src, c, f, s]
        else:
            own = (tok, bias)[item - n]
            dst = (tok_all, bias_all)[item - n].at[src]
        return remote(
            own if step == 0 else dst, dst, z_send.at[side, item, step], z_recv.at[side, item, step], {"z": to}
        )

    def exchange(k, src, stage, slot):
        f, s = place[k]
        whole = wholes[k]
        ref = (whole.at[src, c, f, s], whole.at[src, c, f], whole.at[src, c])[stage]
        axis = (orders[k][1], orders[k][0], "core")[stage]
        return remote(ref, ref, p_send.at[slot, k, stage], p_recv.at[slot, k, stage], other(axis))

    def valid_from(side, step):
        return z - step - 1 >= 0 if side == 0 else z + step + 1 < zsize

    def source(side, step):
        return z - step - 1 if side == 0 else z + step + 1

    def has_next(side):
        return z < zsize - 1 if side == 0 else z > 0

    for side in range(2):

        @pl.when(has_next(side))
        def _():
            for item in range(n):
                line(item, z, 0, side).start()

    def stage_on(stage, step):
        for side in range(2):

            @pl.when(valid_from(side, step))
            def _():
                src = source(side, step)
                slot = side * (zsize - 1) + step
                for k in range(n):
                    exchange(k, src, stage - 1, slot).wait_recv()
                    if stage < 3:
                        exchange(k, src, stage, slot).start()

    def arrive(items, step):
        for side in range(2):

            @pl.when(valid_from(side, step))
            def _():
                src = source(side, step)
                for item in items:
                    line(item, src, step, side).wait_recv()
                    if step + 1 < zsize - 1:

                        @pl.when(has_next(side))
                        def _():
                            line(item, src, step + 1, side).start()

                    if item < n:
                        exchange(item, src, 0, side * (zsize - 1) + step).start()

    for copy, onward in zip(into, local):
        copy.wait()
        onward.start()
    for step in range(zsize - 1):
        arrive(range(n), step)
        if step == zsize - 2:
            for side in range(2):

                @pl.when(has_next(side))
                def _():
                    for item in range(n, n + 2):
                        line(item, z, 0, side).start()

        if step >= 1:
            stage_on(1, step - 1)
    for step in range(zsize - 1):
        if step == 0:
            stage_on(1, zsize - 2)
        stage_on(2, step)
        arrive(range(n, n + 2), step)
    for step in range(zsize - 1):
        stage_on(3, step)
    for copy in local:
        copy.wait()
    for side in range(2):

        @pl.when(has_next(side))
        def _():
            for item in range(n + 2):
                line(item, z, 0, side).wait_send()

        for step in range(zsize - 1):

            @pl.when(valid_from(side, step))
            def _():
                src = source(side, step)
                if step + 1 < zsize - 1:

                    @pl.when(has_next(side))
                    def _():
                        for item in range(n + 2):
                            line(item, src, step + 1, side).wait_send()

                for k in range(n):
                    for stage in range(3):
                        exchange(k, src, stage, side * (zsize - 1) + step).wait_send()


def gather_start(tokens, bias, weights, zsize):
    orders = [ORDERS[o] for o, _ in weights]
    shards = [w for _, w in weights]
    n = len(shards)
    stack = lambda a: jax.ShapeDtypeStruct((zsize,) + a.shape, a.dtype)
    return pl.pallas_call(
        functools.partial(gather_kernel, zsize, orders),
        out_shape=[stack(tokens), stack(bias)] + [stack(w) for w in shards],
        in_specs=[HBM] * (n + 2),
        out_specs=[HBM] * (n + 2),
        scratch_shapes=[pltpu.VMEM(a.shape, a.dtype) for a in shards + [tokens, bias]] + [
            pltpu.SemaphoreType.DMA((2, n + 2)),
            pltpu.SemaphoreType.DMA((2, n + 2, zsize - 1)),
            pltpu.SemaphoreType.DMA((2, n + 2, zsize - 1)),
            pltpu.SemaphoreType.DMA((2 * (zsize - 1), n, 3)),
            pltpu.SemaphoreType.DMA((2 * (zsize - 1), n, 3)),
        ],
        compiler_params=pltpu.CompilerParams(
            collective_id=0, has_side_effects=True, vmem_limit_bytes=VMEM
        ),
    )(tokens, bias, *shards)


def add_rows(dst, src):
    rows = dst.shape[0]
    step = math.gcd(rows, 32)

    def body(i, carry):
        at = pl.ds(pl.multiple_of(i * step, step), step)
        dst[at, :] = dst[at, :] + src[at, :]
        return carry

    lax.fori_loop(0, rows // step, body, 0)


def reduce_kernel(zsize, orders, w, *refs):
    n = 3
    p = len(orders) - n
    items = n + p
    pieces, came, refs = refs[:p], refs[p:2 * p], refs[2 * p:]
    parts, backs, small = refs[:n], refs[n], refs[n + 1]
    pos = n + 2
    piece_out, part_out, back_out = refs[pos:pos + p], refs[pos + p:pos + p + n], refs[pos + p + n]
    small_out = refs[pos + p + n + 1]
    outs = list(part_out) + list(piece_out)
    pos += p + n + 2
    mine = refs[pos:pos + items + w]
    pos += items + w
    got_c, got_1, got_2 = refs[pos:pos + n], refs[pos + n:pos + n + items], refs[pos + n + items:pos + n + 2 * items]
    pos += n + 2 * items
    lines = [0] + list(range(n, items + w))
    line_backs = list(range(items, items + w))
    got_z = dict(zip(lines, refs[pos:pos + len(lines)]))
    pos += len(lines)
    small_mine, small_got, small_line, small_total, part_line, part_total = refs[pos:pos + 6]
    (local_sem, send, recv, z_send, z_recv, s_send, s_recv, t_send, t_recv, g_send, g_recv, end_sem) = refs[pos + 6:]
    z = lax.axis_index("z")
    c = lax.axis_index("core")
    orders = orders[p:] + orders[:p]
    place = [(lax.axis_index(o[0]), lax.axis_index(o[1])) for o in orders]
    turn = []
    for i in range(zsize // 2):
        turn += [i, zsize - 1 - i]
    few = parts[1].shape[0]
    steps = [(1, b) for b in range(few)] + [(2, 0)] + [(0, b) for b in turn]

    def load(k, b):
        src = parts[k].at[b, c] if k < n else pieces[k - n].at[b] if k < items else backs.at[k - items, b]
        return pltpu.make_async_copy(src, mine[k].at[b], local_sem.at[k, b])

    def load_came(k, b):
        return pltpu.make_async_copy(came[k - n].at[b], got_1[k].at[b], local_sem.at[items + w + 1 + k - n, b])

    load_small = pltpu.make_async_copy(small, small_mine.at[0], local_sem.at[items + w, 0])

    def half(k, b, stage):
        f, s = place[k]
        if stage == 0:
            src, dst, axis = parts[k].at[b, 1 - c], got_c[k].at[b], "core"
        elif stage == 1:
            src, dst, axis = mine[k].at[b, 1 - f], got_1[k].at[b], orders[k][0]
        else:
            held = mine[k].at[b, f] if k < n else mine[k].at[b]
            src, dst, axis = held.at[1 - s], got_2[k].at[b], orders[k][1]
        return remote(src, dst, send.at[stage, k, b], recv.at[stage, k, b], other(axis))

    def own(k, b):
        if k >= items:
            return mine[k].at[b]
        f, s = place[k]
        return mine[k].at[b, s] if k >= n else mine[k].at[b, f, s]

    def hop(k, b, side):
        to = z + 1 if side == 0 else z - 1
        at = b if side == 0 else jnp.where(b == z - 1, zsize, b)
        return remote(own(k, b), got_z[k].at[at], z_send.at[k, b], z_recv.at[k, at], {"z": to})

    def take(k, b, side):
        at = b if side == 0 else jnp.where(b == z, zsize, b)
        ref = got_z[k].at[at]
        sender = z - 1 if side == 0 else z + 1
        remote(own(k, b), ref, z_send.at[k, b], z_recv.at[k, at], {"z": sender}).wait_recv()
        add_rows(own(k, b), ref)

    def line_start(ks, messages):
        for side in range(2):

            @pl.when(z == (0 if side == 0 else zsize - 1))
            def _():
                for i in messages:
                    for k in ks:
                        hop(k, zsize - 1 - i if side == 0 else i, side).start()

    def line_slot(ks, slot):
        for i in range(slot):
            for side in range(2):
                b = zsize - 1 - i if side == 0 else i

                @pl.when(z == (slot - i if side == 0 else zsize - 1 - slot + i))
                def _():
                    for k in ks:
                        take(k, b, side)

                        @pl.when(z < b if side == 0 else z > b)
                        def _():
                            hop(k, b, side).start()

    def small_swap(stage):
        return remote(
            small_mine.at[stage], small_got.at[stage], s_send.at[stage], s_recv.at[stage], other(CELL[stage])
        )

    def small_step(stage):
        small_swap(stage).wait_recv()
        small_mine[stage + 1] = small_mine[stage] + small_got[stage]
        if stage < 2:
            small_swap(stage + 1).start()

    last = len(CELL)
    last_part = own(2, 0)

    def total_copy(item, way):
        line, total = ((small_line, small_total), (part_line, part_total))[item]
        src = (small_mine.at[last], last_part)[item] if way == 0 else total
        dst = line if way == 0 else total
        to = z + 1 if way == 0 else z - 1
        return remote(src, dst, t_send.at[item, way], t_recv.at[item, way], {"z": to})

    def total_step(tick):
        if 0 <= tick < zsize:

            @pl.when(z == tick)
            def _():
                if tick > 0:
                    for item in range(2):
                        total_copy(item, 0).wait_recv()
                    small_mine[last] = small_mine[last] + small_line[...]
                    add_rows(last_part, part_line)
                if tick < zsize - 1:
                    for item in range(2):
                        total_copy(item, 0).start()
                else:
                    small_total[...] = small_mine[last]
                    part_total[...] = last_part[...]

        back_tick = tick - (zsize - 1)
        if 0 <= back_tick < zsize:

            @pl.when(z == zsize - 1 - back_tick)
            def _():
                if back_tick > 0:
                    for item in range(2):
                        total_copy(item, 1).wait_recv()
                if back_tick < zsize - 1:
                    for item in range(2):
                        total_copy(item, 1).start()

    line_pieces = list(range(n, items))
    piece_steps = [(k, b) for b in turn for k in line_pieces]
    for b in turn:
        for k in line_backs:
            load(k, b).start()
    for k, b in piece_steps:
        load(k, b).start()
        load_came(k, b).start()
    for k, b in steps:
        load(k, b).start()
    load_small.start()
    greet(zsize)
    for k, b in steps:
        half(k, b, 0).start()
    for b in turn:
        for k in line_backs:
            load(k, b).wait()
    line_start(line_backs, [0])
    load_small.wait()
    small_swap(0).start()

    def stage_1(k, b):
        f, s = place[k]
        load(k, b).wait()
        half(k, b, 0).wait_recv()
        for i in range(2):
            add_rows(mine[k].at[b, 1 - f, i], got_c[k].at[b, 1 - f, i])
        half(k, b, 1).start()
        for i in range(2):
            add_rows(mine[k].at[b, f, i], got_c[k].at[b, f, i])

    def stage_2(k, b):
        f, s = place[k]
        held = mine[k].at[b, f] if k < n else mine[k].at[b]
        if k < n:
            half(k, b, 1).wait_recv()
        else:
            load(k, b).wait()
            load_came(k, b).wait()
        add_rows(held.at[1 - s], got_1[k].at[b, 1 - s])
        half(k, b, 2).start()
        add_rows(held.at[s], got_1[k].at[b, s])

    def stage_3(k, b):
        half(k, b, 2).wait_recv()
        add_rows(own(k, b), got_2[k].at[b])

    def result(k, b):
        return part_total if k == 2 else own(k, b)

    def out_of(k, b):
        return outs[k].at[b] if k == 1 else outs[k]

    def put(k, b, slot):
        f, s = place[k]
        return pltpu.make_async_copy(result(k, b), out_of(k, b).at[c, f, s], end_sem.at[slot])

    def spread(k, b, stage, slot):
        f, s = place[k]
        out = out_of(k, b)
        dst = (out.at[c, f, s], out.at[c, f], out.at[c])[stage]
        src = result(k, b) if stage == 0 else dst
        axis = (orders[k][1], orders[k][0], "core")[stage]
        return remote(src, dst, g_send.at[slot, stage], g_recv.at[slot, stage], other(axis))

    spreads = [
        [(1, b, b) for b in range(few)],
        [(k, z, few + k - n) for k in line_pieces],
        [(0, z, few + p), (2, 0, few + p + 1)],
    ]

    def spread_step(group, stage):
        for k, b, slot in spreads[group]:
            if stage == 0:
                spread(k, b, 0, slot).start()
                put(k, b, slot).start()
                continue
            if stage == 1:
                put(k, b, slot).wait()
            spread(k, b, stage - 1, slot).wait_recv()
            if stage < 3:
                spread(k, b, stage, slot).start()

    def sent(ks):
        for b in range(zsize):

            @pl.when(z != b)
            def _():
                for k in ks:
                    hop(k, b, 0).wait_send()

    at_end = jnp.logical_or(z == 0, z == zsize - 1)
    for k, b in piece_steps:
        stage_2(k, b)
    for k, b in steps:
        stage_1(k, b)
    small_step(0)
    for b in turn:
        for k in line_pieces:
            stage_3(k, b)
        for side in range(2):

            @pl.when(jnp.logical_and(z == (0 if side == 0 else zsize - 1), z != b))
            def _():
                for k in line_pieces:
                    hop(k, b, side).start()

    for k, b in steps:
        stage_2(k, b)
    small_step(1)
    line_slot(line_backs, 1)
    for k, b in steps:
        stage_3(k, b)
    small_step(2)
    spread_step(0, 0)
    line_start([0], range(zsize - 1))
    total_step(0)

    @pl.when(at_end)
    def _():
        sent(line_pieces)

    line_start(line_backs, range(1, zsize - 1))
    ticks = list(range(1, 2 * zsize - 1))
    later = [(0, 1), (0, 2), (0, 3)]

    def fill(group_stages, count):
        for _ in range(count):
            if group_stages:
                spread_step(*group_stages.pop(0))

    for slot in range(1, zsize):
        line_slot(line_pieces, slot)
        total_step(ticks.pop(0))
        fill(later, 1)
        if slot >= 2:
            line_slot([0], slot - 1)
    fill(later, 3)
    spread_step(1, 0)
    later = [(1, 1), (1, 2), (1, 3)]
    total_step(ticks.pop(0))
    line_slot([0], zsize - 1)
    for slot in range(2, zsize - 1):
        line_slot(line_backs, slot)
        fill(later, 1)
    for tick in ticks:
        total_step(tick)
    spread_step(2, 0)
    fill(later, 1)
    spread_step(2, 1)
    fill(later, 1)
    spread_step(2, 2)
    fill(later, 3)
    line_slot(line_backs, zsize - 1)
    finish_back = [
        pltpu.make_async_copy(mine[k].at[z], back_out.at[k - items], local_sem.at[k, 0]) for k in line_backs
    ]
    for copy in finish_back:
        copy.start()
    finish_small = pltpu.make_async_copy(small_total, small_out, local_sem.at[items + w, 0])
    finish_small.start()
    spread_step(2, 3)
    for copy in finish_back:
        copy.wait()
    finish_small.wait()
    sent([0] + line_backs)

    @pl.when(jnp.logical_not(at_end))
    def _():
        sent(line_pieces)

    for way in range(2):

        @pl.when(z < zsize - 1 if way == 0 else z > 0)
        def _():
            for item in range(2):
                total_copy(item, way).wait_send()

    for k, b in steps:
        for stage in range(3):
            half(k, b, stage).wait_send()
    for k, b in piece_steps:
        half(k, b, 2).wait_send()
    for stage in range(3):
        small_swap(stage).wait_send()
    for group in spreads:
        for k, b, slot in group:
            for stage in range(3):
                spread(k, b, stage, slot).wait_send()


def reduce_end(pieces, parts, backs, small, zsize):
    orders = [ORDERS[o[0]] for o in pieces + parts]
    piece_arrays = [a for _, a, _ in pieces]
    came = [a for _, _, a in pieces]
    arrays = [a for _, a in parts]
    p, n, w = len(pieces), len(parts), backs.shape[0]
    shapes = [a.shape for a in arrays]
    like = jax.ShapeDtypeStruct
    outs = [like((2, 2, 2) + a.shape[2:], bf16) for a in piece_arrays]
    outs += [like(s if i == 1 else s[1:], bf16) for i, s in enumerate(shapes)]
    outs += [like((w,) + backs.shape[2:], bf16), like(small.shape, f32)]
    held = lambda shape: pltpu.VMEM(shape, bf16)
    scratch = [held((s[0],) + s[2:]) for s in shapes]
    scratch += [held(a.shape) for a in piece_arrays] + [held(backs.shape[1:])] * w
    scratch += [held((s[0],) + s[2:]) for s in shapes]
    scratch += [held((s[0],) + s[3:]) for s in shapes] + [held(a.shape) for a in piece_arrays]
    scratch += [held((s[0],) + s[4:]) for s in shapes] + [held(a.shape[:1] + a.shape[2:]) for a in piece_arrays]
    scratch += [held((zsize + 1,) + shapes[0][4:])]
    scratch += [held((zsize + 1,) + a.shape[2:]) for a in piece_arrays] + [held((zsize + 1,) + backs.shape[2:])] * w
    scratch += [pltpu.VMEM((4,) + small.shape, f32), pltpu.VMEM((3,) + small.shape, f32)]
    scratch += [pltpu.VMEM(small.shape, f32)] * 2 + [held(shapes[2][4:])] * 2
    dma = pltpu.SemaphoreType.DMA
    most = max(zsize, shapes[1][0])
    ends = shapes[1][0] + p + 2
    scratch += [
        dma((n + 2 * p + w + 1, most)), dma((3, n + p, most)), dma((3, n + p, most)),
        dma((n + p + w, zsize)), dma((n + p + w, zsize + 1)),
        dma((3,)), dma((3,)), dma((2, 2)), dma((2, 2)), dma((ends, 3)), dma((ends, 3)), dma((ends,)),
    ]
    return pl.pallas_call(
        functools.partial(reduce_kernel, zsize, orders, w),
        out_shape=outs,
        in_specs=[HBM] * (n + 2 * p + 2),
        out_specs=[HBM] * (n + p + 2),
        scratch_shapes=scratch,
        compiler_params=pltpu.CompilerParams(
            collective_id=1, has_side_effects=True, vmem_limit_bytes=VMEM
        ),
    )(*piece_arrays, *came, *arrays, backs, small)


def gelu_pair(v):
    size = jnp.abs(v)
    t = 1.0 / (1.0 + (0.3275911 * 0.5 ** 0.5) * size)
    bell = jnp.exp(-0.5 * (v * v))
    poly = t * (0.254829592 + t * (-0.284496736 + t * (1.421413741 + t * (-1.453152027 + t * 1.061405429))))
    tail = 0.5 * poly * bell
    cdf = jnp.where(v >= 0.0, 1.0 - tail, tail)
    return v * cdf, cdf + v * (bell * (1.0 / (2.0 * math.pi) ** 0.5))


def norm_rows(field):
    mean = jnp.mean(field, axis=-1, keepdims=True)
    centred = field - mean
    inv_std = lax.rsqrt(jnp.mean(centred * centred, axis=-1, keepdims=True) + eps)
    return centred * inv_std, inv_std


def ffn_kernel(zsize, groups, z_ref, tok_ref, out_ref, out_bias_ref, gain_one_ref, shift_one_ref, up_ref, bias_ref, down_ref,
               down_bias_ref, gain_two_ref, shift_two_ref, proj_ref, dy_ref, de_ref, *refs):
    pieces = refs[:zsize * groups]
    (active_ref, slope_ref, mixed_ref, x_ref, scaled_ref, inv_ref, result_ref, embed_ref, grad_ref, low_ref, proj_grad_ref,
     vec_ref, normed_ref, sum_ref) = refs[zsize * groups:]
    rows, width = x_ref.shape
    local = rows // groups
    cols = width // zsize
    chunk = 128
    heads = proj_ref.shape[0]

    @pl.when(pl.program_id(0) == 0)
    def _():
        for g in range(groups):
            for step in range(zsize):
                at = lax.rem(z_ref[0] + zsize - step, zsize) * cols
                mixed_ref[pl.ds(g * local, local), pl.ds(pl.multiple_of(at, cols), cols)] = pieces[g * zsize + step][0]
        def first(i, carry):
            at = pl.ds(pl.multiple_of(i * chunk, chunk), chunk)
            attended = jnp.dot(mixed_ref[at, :], out_ref[...], preferred_element_type=f32) + out_bias_ref[...]
            scaled, inv_std = norm_rows(tok_ref[at, :].astype(f32) + attended)
            normed = scaled * gain_one_ref[...] + shift_one_ref[...]
            scaled_ref[at, :] = scaled
            inv_ref[at, :] = inv_std
            normed_ref[at, :] = normed
            x_ref[at, :] = normed.astype(bf16)
            return carry

        lax.fori_loop(0, rows // chunk, first, 0)
        sum_ref[...] = jnp.zeros(sum_ref.shape, f32)

    parts = [pl.ds(i * chunk, chunk) for i in range(rows // chunk)]
    hidden = [jnp.dot(x_ref[at, :], up_ref[0], preferred_element_type=f32) + bias_ref[0] for at in parts]
    for at, field in zip(parts, hidden):
        active, slope = gelu_pair(field)
        slope_ref[0, at, :] = slope.astype(bf16)
        active_ref[0, :, at] = active.T.astype(bf16)
        sum_ref[at, :] += jnp.dot(active.astype(bf16), down_ref[0], preferred_element_type=f32)

    @pl.when(pl.program_id(0) == pl.num_programs(0) - 1)
    def _():
        vec_ref[...] = jnp.zeros(vec_ref.shape, f32)

        def second(i, carry):
            at = pl.ds(pl.multiple_of(i * chunk, chunk), chunk)
            scaled, inv_std = norm_rows(normed_ref[at, :] + (sum_ref[at, :] + down_bias_ref[...]))
            result_ref[at, :] = (scaled * gain_two_ref[...] + shift_two_ref[...]).astype(bf16)
            g, inner = i // (local // chunk), lax.rem(i, local // chunk)
            upstream = dy_ref[at, :].astype(f32) + lax.dot_general(
                de_ref[g, :, pl.ds(pl.multiple_of(inner * chunk, chunk), chunk)], proj_ref[...], (((0,), (0,)), ((), ())), preferred_element_type=f32
            )
            grad_scaled = upstream * gain_two_ref[...]
            grad = inv_std * (
                grad_scaled
                - jnp.mean(grad_scaled, axis=-1, keepdims=True)
                - scaled * jnp.mean(grad_scaled * scaled, axis=-1, keepdims=True)
            )
            grad_ref[at, :] = grad
            low = grad.astype(bf16)
            low_ref[at, :] = low
            for n, field in enumerate((low.astype(f32), upstream * scaled, upstream)):
                vec_ref[n:n + 1, :] = vec_ref[n:n + 1, :] + jnp.sum(field, axis=0, keepdims=True)
            return carry

        lax.fori_loop(0, rows // chunk, second, 0)
        proj_grad = jnp.zeros((heads, width), f32)
        for g in range(groups):
            result = result_ref[pl.ds(g * local, local), :]
            embed_ref[g] = lax.dot_general(
                proj_ref[...], result, (((1,), (1,)), ((), ())), preferred_element_type=f32
            ).astype(bf16)
            proj_grad = proj_grad + jnp.dot(de_ref[g], result, preferred_element_type=f32)
        proj_grad_ref[...] = jnp.zeros(proj_grad_ref.shape, bf16)
        proj_grad_ref[pl.ds(0, heads), :] = proj_grad.astype(bf16)


def ffn_forward(zi, tokens, pieces, out_all, one, up_all, up_bias, down_all, two, proj, dy, de):
    zsize, width, units = up_all.shape
    rows = tokens.shape[0]
    groups, heads, local = de.shape
    tile = units
    like = jax.ShapeDtypeStruct
    whole = lambda shape: pl.BlockSpec(shape, lambda s, z: (0,) * len(shape))
    tiles = pl.BlockSpec((1, rows, tile), lambda s, z: (s, 0, 0))
    field, row = whole((rows, width)), whole((1, width))
    padded = heads + -heads % 128
    return pl.pallas_call(
        functools.partial(ffn_kernel, zsize, groups),
        grid_spec=pltpu.PrefetchScalarGridSpec(
            num_scalar_prefetch=1,
            grid=(zsize,),
            in_specs=[
                field, whole((width, width)), row, row, row,
                pl.BlockSpec((1, width, tile), lambda s, z: (s, 0, 0)),
                pl.BlockSpec((1, 1, tile), lambda s, z: (s, 0, 0)),
                pl.BlockSpec((1, tile, width), lambda s, z: (s, 0, 0)),
                row, row, row, whole(proj.shape), field, whole(de.shape),
            ] + [whole(p.shape) for p in pieces],
            out_specs=[
                pl.BlockSpec((1, tile, rows), lambda s, z: (s, 0, 0)), tiles,
                field, field, field, whole((rows, 1)), field, whole(de.shape), field, field,
                whole((padded, width)), whole((8, width)),
            ],
            scratch_shapes=[pltpu.VMEM((rows, width), f32), pltpu.VMEM((rows, width), f32)],
        ),
        out_shape=[
            like((zsize, units, rows), bf16), like((zsize, rows, units), bf16), like((rows, width), bf16),
            like((rows, width), bf16), like((rows, width), f32), like((rows, 1), f32), like((rows, width), bf16),
            like(de.shape, bf16), like((rows, width), f32), like((rows, width), bf16), like((padded, width), bf16),
            like((8, width), f32),
        ],
        compiler_params=pltpu.CompilerParams(vmem_limit_bytes=VMEM),
    )(zi.reshape(1), tokens, out_all, *one, up_all, up_bias[:, None, :], down_all, *two, proj, dy, de, *pieces)


def ffn_back_kernel(core_ref, second_ref, normed_ref, up_ref, down_ref, active_ref, slope_ref,
                    give_up_ref, keep_up_ref, give_down_ref, keep_down_ref, back_ref, bias_ref, turned_ref):
    s = pl.program_id(0)
    half = turned_ref.shape[0] // 2
    c = core_ref[0]

    @pl.when(s == 0)
    def _():
        back_ref[...] = jnp.zeros(back_ref.shape, f32)
        turned_ref[...] = normed_ref[...].T

    second = second_ref[...]
    upstream = lax.dot_general(second, down_ref[0], (((1,), (1,)), ((), ())), preferred_element_type=f32)
    grad = (upstream * slope_ref[0].astype(f32)).astype(bf16)
    bias_ref[0] = jnp.sum(grad.astype(f32), axis=0, keepdims=True)
    units = active_ref.shape[1] // 2
    back_ref[...] += lax.dot_general(grad, up_ref[0], (((1,), (1,)), ((), ())), preferred_element_type=f32)
    for who, down_to, up_to in ((1 - c, give_down_ref, give_up_ref), (c, keep_down_ref, keep_up_ref)):
        active = active_ref[0, pl.ds(pl.multiple_of(who * units, units), units), :]
        down_to[0] = jnp.dot(active, second, preferred_element_type=f32).astype(bf16)
        turned = turned_ref[pl.ds(pl.multiple_of(who * half, half), half), :]
        up_to[0] = jnp.dot(turned, grad, preferred_element_type=f32).astype(bf16)


def ffn_backward(core, second_low, normed_low, up_all, down_all, active, slope):
    zsize, width, units = up_all.shape
    rows = normed_low.shape[0]
    like = jax.ShapeDtypeStruct
    whole = pl.BlockSpec((rows, width), lambda s, c: (0, 0))
    tiles = pl.BlockSpec((1, rows, units), lambda s, c: (s, 0, 0))
    up_half = pl.BlockSpec((1, width // 2, units), lambda s, c: (s, 0, 0))
    down_half = pl.BlockSpec((1, units // 2, width), lambda s, c: (s, 0, 0))
    return pl.pallas_call(
        ffn_back_kernel,
        grid_spec=pltpu.PrefetchScalarGridSpec(
            num_scalar_prefetch=1,
            grid=(zsize,),
            in_specs=[
                whole, whole,
                pl.BlockSpec((1, width, units), lambda s, c: (s, 0, 0)),
                pl.BlockSpec((1, units, width), lambda s, c: (s, 0, 0)),
                pl.BlockSpec((1, units, rows), lambda s, c: (s, 0, 0)), tiles,
            ],
            out_specs=[
                up_half, up_half, down_half, down_half, whole,
                pl.BlockSpec((1, 1, units), lambda s, c: (s, 0, 0)),
            ],
            scratch_shapes=[pltpu.VMEM((width, rows), bf16)],
        ),
        out_shape=[
            like((zsize, width // 2, units), bf16), like((zsize, width // 2, units), bf16),
            like((zsize, units // 2, width), bf16), like((zsize, units // 2, width), bf16),
            like((rows, width), f32), like((zsize, 1, units), f32),
        ],
        compiler_params=pltpu.CompilerParams(vmem_limit_bytes=VMEM),
    )(core, second_low, normed_low, up_all, down_all, active, slope)


PAIR = [(0, 1), (1, 0)]


def first_halving(got, keep, order):
    zsize, half, cols = keep.shape
    shape = (zsize, 2, 2, half // 4, cols)
    got, keep = got.reshape(shape), keep.reshape(shape)
    i = lax.axis_index(ORDERS[order][0])
    pick = lambda array, j: lax.dynamic_index_in_dim(array, j, 1, keepdims=False)
    return pick(keep, 1 - i) + pick(got, 1 - i), pick(keep, i) + pick(got, i)


def widen_kernel(counts, up_ref, down_ref, out_ref, qkv_ref, first_ref, *refs):
    parts, (up_o, down_o, out_o, qkv_o, first_o) = refs[:-5], refs[-5:]
    for source, target in ((up_ref, up_o), (down_ref, down_o), (out_ref, out_o), (qkv_ref, qkv_o)):
        target[...] = source[...].astype(f32)
    per_group = pl.num_programs(0) // len(counts)
    for g, count in enumerate(counts):
        own, parts = parts[:count], parts[count:]

        @pl.when(pl.program_id(0) // per_group == g)
        def _():
            total = first_ref[...]
            for part in own:
                total = total + part[...].astype(f32)
            first_o[...] = total


def widen(up, down, out, qkv, first, parts):
    steps = 8
    per_group = steps // len(parts)

    def rows_of(array):
        return pl.BlockSpec((array.shape[0] // steps, array.shape[1]), lambda i: (i, 0))

    def of_group(g):
        block = first.shape[0] // steps
        return pl.BlockSpec((block, first.shape[1]), lambda i: (jnp.clip(i - g * per_group, 0, per_group - 1), 0))

    arrays = [up, down, out]
    specs = [rows_of(a) for a in arrays]
    specs.append(pl.BlockSpec((3, qkv.shape[1] // steps, qkv.shape[2]), lambda i: (0, i, 0)))
    specs.append(rows_of(first))
    return pl.pallas_call(
        functools.partial(widen_kernel, [len(p) for p in parts]),
        grid=(steps,),
        in_specs=specs + [of_group(g) for g, own in enumerate(parts) for _ in own],
        out_specs=specs,
        out_shape=[jax.ShapeDtypeStruct(a.shape, f32) for a in arrays + [qkv, first]],
        compiler_params=pltpu.CompilerParams(vmem_limit_bytes=VMEM),
    )(up, down, out, qkv, first, *[part for own in parts for part in own])


def per_device(blocks, tokens, segments, qkv_weight, qkv_bias, out_weight, out_bias, gain_one, shift_one,
               up_weight, up_bias, down_weight, down_bias, gain_two, shift_two, proj_weight, out_grad, embed_grad):
    groups, local_rows, model_width = tokens.shape
    length = segments.shape[1]
    zsize = length // local_rows
    head_cols = qkv_weight.shape[2]
    units_here = up_weight.shape[1]
    rows = groups * local_rows
    zi = lax.axis_index("z")
    cosine, sine = rotary_tables(doc_positions(segments))
    starts = jnp.sum(segments[:, None, :] < jnp.arange(4, dtype=jnp.int32)[None, :, None], axis=2, dtype=jnp.int32)
    edges = jnp.arange(length // BLOCK, dtype=jnp.int32)[None, :, None] * BLOCK
    bounds = (
        jnp.max(jnp.where(starts[:, None, :] <= edges, starts[:, None, :], 0), axis=2) // BLOCK,
        (jnp.min(jnp.where(starts[:, None, :] >= edges + BLOCK, starts[:, None, :], length), axis=2) + BLOCK - 1) // BLOCK,
    )

    def cut(array, rows_at):
        shape = array.shape
        return array.reshape(shape[:rows_at] + (2, 2, 2, shape[rows_at] // 8) + shape[rows_at + 1:])

    token_rows = tokens.reshape(rows, model_width)
    token_blocks, bias_blocks, out_all, up_all, down_all = gather_start(
        token_rows,
        up_bias.reshape(8, units_here // 8),
        [("xy", cut(out_weight, 0)), ("xy", cut(up_weight, 0)), ("yx", cut(down_weight, 0))],
        zsize,
    )
    token_blocks = token_blocks.reshape(zsize, groups, local_rows, model_width)
    out_all = out_all.reshape(model_width, model_width)
    up_all = up_all.reshape(zsize, model_width, units_here)
    down_all = down_all.reshape(zsize, units_here, model_width)
    full_up_bias = bias_blocks.reshape(zsize, units_here)

    def ring(step):
        return [(i, (i + step) % zsize) for i in range(zsize)]

    def exchange(array, size, axis):
        parts = []
        for step in range(zsize):
            part = lax.dynamic_slice_in_dim(array, lax.rem(zi + step, zsize) * size, size, axis)
            parts.append(lax.ppermute(part, "z", ring(step)) if step else part)
        return parts

    kept, pieces = [], []
    for g in range(groups):
        kept.append(attend_forward(g, bounds, token_blocks, qkv_weight, qkv_bias, cosine, sine, segments))
        pieces += exchange(kept[g][0], local_rows, 1)
    flat = lambda vector: vector.reshape(1, model_width)
    (active, slope, mixed, normed_low, scaled_one, inv_one, result_low, embedded, grad_second, second_low, proj_grad,
     vec_two) = ffn_forward(
        zi, token_rows, pieces, out_all, [flat(v) for v in (out_bias, gain_one, shift_one)], up_all, full_up_bias,
        down_all, [flat(v) for v in (down_bias, gain_two, shift_two)], proj_weight.T,
        out_grad.reshape(rows, model_width), embed_grad.transpose(0, 2, 1),
    )
    core = lax.axis_index("core").reshape(1)
    give_up, keep_up, give_down, keep_down, ffn_back, up_bias_grad = ffn_backward(
        core, second_low, normed_low, up_all, down_all, active, slope
    )
    got_down = lax.ppermute(give_down, "core", PAIR)
    got_up = lax.ppermute(give_up, "core", PAIR)
    grad_normed = grad_second + ffn_back
    grad_first, gain_one_grad, shift_one_grad = norm_backward(grad_normed, scaled_one, inv_one, gain_one)
    first_low = grad_first.astype(bf16)
    out_bias_grad = jnp.sum(first_low.astype(f32), axis=0)
    out_grad_w = jnp.einsum("nh,nd->hd", mixed, first_low, preferred_element_type=f32).astype(bf16)
    grad_mixed = jnp.einsum("nd,hd->nh", first_low, out_all, preferred_element_type=f32).astype(bf16)
    grad_mixed = grad_mixed.reshape(groups, local_rows, model_width)
    upstream = [exchange(grad_mixed[g:g + 1], head_cols, 2) for g in range(groups)]
    send_down, keep_down = first_halving(got_down, keep_down, "yx")
    send_up, keep_up = first_halving(got_up, keep_up, "xy")
    upstream[0], send_down, send_up = lax.optimization_barrier((upstream[0], send_down, send_up))
    got_down = lax.ppermute(send_down, ORDERS["yx"][0], PAIR)
    got_up = lax.ppermute(send_up, ORDERS["xy"][0], PAIR)
    qkv_weight_grad, qkv_bias_grad, early = None, 0.0, []
    for g in range(groups):
        backs, qkv_weight_grad, bias_part = attend_backward(
            g, qkv_weight_grad, bounds, zi, kept[g][1:], kept[g][0], upstream[g], cosine, sine, token_blocks, qkv_weight
        )
        qkv_bias_grad = qkv_bias_grad + bias_part[:3]
        if g < groups - 1:
            early.append([
                lax.ppermute(backs[0, step], "z", ring(step)) if step else backs[0, step] for step in range(zsize)
            ])
    backs, got_down, got_up, qkv_bias_grad = lax.optimization_barrier((backs, got_down, got_up, qkv_bias_grad))

    vec_one = jnp.pad(jnp.stack([out_bias_grad, gain_one_grad, shift_one_grad]), ((0, 5), (0, 0)))
    placed = lax.dynamic_update_slice(
        jnp.zeros((zsize, 3 * head_cols), f32), qkv_bias_grad.reshape(1, -1), (zi, 0)
    )
    small = jnp.concatenate([vec_one, vec_two, up_bias_grad.reshape(8, -1), placed.reshape(8, -1)], axis=1)
    up_grad, down_grad, out_grad_w, qkv_weight_grad, proj_grad, back, small = reduce_end(
        [("xy", keep_up, got_up), ("yx", keep_down, got_down)],
        [
            ("xy", cut(out_grad_w.reshape(zsize, head_cols, model_width), 1)),
            ("yx", cut(qkv_weight_grad, 1)),
            ("xy", cut(proj_grad[None], 1)),
        ],
        backs,
        small,
        zsize,
    )
    qkv_weight_grad = qkv_weight_grad.reshape(qkv_weight.shape)
    proj_grad = proj_grad.reshape(-1, model_width)[:proj_weight.shape[1]].astype(f32).T
    out_grad_w = out_grad_w.reshape(out_weight.shape)
    up_grad = up_grad.reshape(up_weight.shape)
    down_grad = down_grad.reshape(down_weight.shape)
    if blocks > 1:
        down_grad, up_grad, out_grad_w, qkv_weight_grad = lax.psum(
            (down_grad, up_grad, out_grad_w, qkv_weight_grad), ("xb", "yb")
        )
        small, proj_grad = lax.psum((small, proj_grad), ("xb", "yb"))
    up_grad, down_grad, out_grad_w, qkv_weight_grad, tokens_grad = widen(
        up_grad, down_grad, out_grad_w, qkv_weight_grad, grad_first, early + [[back[0]]]
    )
    base = 2 * model_width
    vec = list(small[:3, :model_width]) + list(small[:3, model_width:base])
    split = base + zsize * units_here // 8
    up_bias_grad = lax.dynamic_slice(small[:, base:split].reshape(-1), (zi * units_here,), (units_here,))
    qkv_bias_grad = lax.dynamic_slice(small[:, split:].reshape(-1), (zi * 3 * head_cols,), (3 * head_cols,))
    qkv_bias_grad = qkv_bias_grad.reshape(3, head_cols)
    shape3 = (groups, local_rows, model_width)
    return (
        result_low.reshape(shape3),
        embedded.transpose(0, 2, 1),
        tokens_grad.reshape(shape3),
        qkv_weight_grad,
        qkv_bias_grad,
        out_grad_w,
        vec[0], vec[1], vec[2],
        up_grad,
        up_bias_grad,
        down_grad,
        vec[3], vec[4], vec[5],
        proj_grad,
    )


def solution(mesh):
    dp_size, zsize = mesh.shape["dp"], mesh.shape["tensor"]
    side = math.isqrt(dp_size // 2) // 2
    cut = Mesh(mesh.devices.reshape(side, 2, side, 2, 2, zsize), DP + ("z",))
    rows3 = P(DP, "z", None)
    in_specs = (
        rows3, P(DP, None), P(None, None, "z"), P(None, "z"), P("z", None), P(), P(), P(),
        P(None, "z"), P("z"), P("z", None), P(), P(), P(), P(), rows3, rows3,
    )
    out_specs = (
        rows3, rows3, rows3, P(None, None, "z"), P(None, "z"), P("z", None), P(), P(), P(),
        P(None, "z"), P("z"), P("z", None), P(), P(), P(), P(),
    )

    def run(*args):
        return per_device(side * side, *args)

    return jax.shard_map(run, mesh=cut, in_specs=in_specs, out_specs=out_specs, check_vma=False)
```

```python
import functools
import math

import jax
import jax.numpy as jnp
from jax import lax
from jax.experimental import pallas as pl
from jax.experimental.pallas import tpu as pltpu
from jax.sharding import Mesh
from jax.sharding import PartitionSpec as P

HEAD_DIM = 64
eps = 1e-05
DP = ("xb", "x", "yb", "y", "core")
CELL = ("x", "y", "core")
ALL = DP + ("z",)
f32 = jnp.float32
bf16 = jnp.bfloat16
VMEM = 60 * 1024 * 1024


def doc_positions(segment_rows):
    below = segment_rows[:, None, :] < jnp.arange(4, dtype=jnp.int32)[None, :, None]
    starts = jnp.sum(below, axis=2, dtype=jnp.int32)
    row_index = jnp.arange(segment_rows.shape[1], dtype=jnp.int32)[None]
    start = starts[:, 3:4]
    for doc in (2, 1, 0):
        start = jnp.where(segment_rows == doc, starts[:, doc:doc + 1], start)
    return row_index - start


def rotary_tables(positions):
    half_dim = HEAD_DIM // 2
    lane = jnp.arange(2 * HEAD_DIM, dtype=jnp.int32)
    exponent = (lane % half_dim).astype(f32) * (2.0 / HEAD_DIM)
    frequency = jnp.exp(-exponent * math.log(10000.0))
    sign = jnp.where(lane % HEAD_DIM < half_dim, -1.0, 1.0)
    angles = positions.astype(f32)[..., None] * frequency
    return (jnp.cos(angles), jnp.sin(angles) * sign)


def norm_forward(field, gain, shift):
    row_mean = jnp.mean(field, axis=-1, keepdims=True)
    centred = field - row_mean
    variance = jnp.mean(centred * centred, axis=-1, keepdims=True)
    inv_std = lax.rsqrt(variance + eps)
    scaled = centred * inv_std
    return (scaled * gain + shift, scaled, inv_std)


def norm_backward(upstream, scaled, inv_std, gain):
    grad_scaled = upstream * gain
    grad_input = inv_std * (
        grad_scaled
        - jnp.mean(grad_scaled, axis=-1, keepdims=True)
        - scaled * jnp.mean(grad_scaled * scaled, axis=-1, keepdims=True)
    )
    return (grad_input, jnp.sum(upstream * scaled, axis=0), jnp.sum(upstream, axis=0))


BLOCK = 256


def turn_halves(field, sign_sine):
    lane = lax.broadcasted_iota(jnp.int32, field.shape, 1)
    half = HEAD_DIM // 2
    width = field.shape[1]
    swapped = jnp.where(lane % HEAD_DIM < half, pltpu.roll(field, width - half, 1), pltpu.roll(field, half, 1))
    return swapped * sign_sine


def scores_of(keys, queries):
    return lax.dot_general(keys, queries, (((1,), (1,)), ((), ())), preferred_element_type=f32)


def attend_kernel(group, lo_ref, hi_ref, tok_ref, w_ref, b_ref, cos_ref, sin_ref, seg_ref, mixed_ref, q_ref, k_ref, v_ref,
                  lse_ref, vt_ref, m_ref, l_ref, acc_ref):
    zsize, _, rows, _ = tok_ref.shape
    length = zsize * rows
    heads = q_ref.shape[1]
    pair = 2 * HEAD_DIM
    scale = HEAD_DIM ** (-0.5)

    def project(i, carry):
        at = pl.ds(pl.multiple_of(i * rows, rows), rows)
        x = tok_ref[i, 0]
        lane = lax.broadcasted_iota(jnp.int32, (rows, pair), 1)
        low = lane < HEAD_DIM
        doc = lax.broadcasted_iota(jnp.int32, (pair, rows), 0) - HEAD_DIM
        extra_q = jnp.where(doc == seg_ref[group:group + 1, at], 1.0, 0.0).T
        extra_k = jnp.where(lane < HEAD_DIM + 4, (extra_q - 1.0) * 1e9, 0.0)
        cosine = cos_ref[0, at, :]
        sine = sin_ref[0, at, :]
        for c in range(3):
            field = jnp.dot(x, w_ref[c], preferred_element_type=f32) + b_ref[c:c + 1, :]
            for j in range(heads // 2):
                part = field[:, j * pair:(j + 1) * pair]
                if c < 2:
                    part = part * cosine + turn_halves(part, sine)
                if c == 0:
                    part = part * scale
                for h in range(2):
                    one = part if h == 0 else pltpu.roll(part, HEAD_DIM, 1)
                    head = 2 * j + h
                    if c == 0:
                        q_ref[0, head, at, :] = jnp.where(low, one, extra_q).astype(bf16)
                    elif c == 1:
                        k_ref[0, head, at, :] = jnp.where(low, one, extra_k).astype(bf16)
                    else:
                        one = jnp.where(low, one, 0.0)
                        v_ref[0, head, at, :] = one.astype(bf16)
                        vt_ref[head, :, at] = one.T[:HEAD_DIM].astype(bf16)
        return carry

    lax.fori_loop(0, zsize, project, 0)

    def query_block(i, carry):
        at = pl.ds(pl.multiple_of(i * BLOCK, BLOCK), BLOCK)
        m_ref[...] = jnp.full(m_ref.shape, -1e30, f32)
        l_ref[...] = jnp.zeros(l_ref.shape, f32)
        acc_ref[...] = jnp.zeros(acc_ref.shape, f32)

        def key_block(j, carry):
            keys_at = pl.ds(pl.multiple_of(j * BLOCK, BLOCK), BLOCK)
            st = [scores_of(k_ref[0, h, keys_at, :], q_ref[0, h, at, :]) for h in range(heads)]
            peak = m_ref[...]
            new = jnp.maximum(peak, jnp.concatenate([jnp.max(t, axis=0, keepdims=True) for t in st], axis=0))
            p = [jnp.exp(st[h] - new[h:h + 1, :]) for h in range(heads)]
            old = jnp.exp(peak - new)
            m_ref[...] = new
            l_ref[...] = l_ref[...] * old + jnp.concatenate([jnp.sum(t, axis=0, keepdims=True) for t in p], axis=0)
            part = [
                jnp.dot(vt_ref[h, :, keys_at], p[h].astype(bf16), preferred_element_type=f32) for h in range(heads)
            ]
            for h in range(heads):
                acc_ref[h] = acc_ref[h] * old[h:h + 1, :] + part[h]
            return carry

        lax.fori_loop(lo_ref[group, i], hi_ref[group, i], key_block, 0)
        out = [acc_ref[h] / l_ref[h:h + 1, :] for h in range(heads)]
        for j in range(heads // 2):
            both = jnp.concatenate([out[2 * j], out[2 * j + 1]], axis=0)
            mixed_ref[0, at, j * pair:(j + 1) * pair] = both.T.astype(bf16)
        lse_ref[0, :, at] = m_ref[...] + jnp.log(l_ref[...])
        return carry

    lax.fori_loop(0, length // BLOCK, query_block, 0)


def attend_forward(group, bounds, tokens, weight, bias, cosine, sine, docs):
    zsize, _, rows, width = tokens.shape
    length = zsize * rows
    cols = weight.shape[2]
    heads = cols // HEAD_DIM
    pair = 2 * HEAD_DIM
    whole = lambda shape: pl.BlockSpec(shape, lambda i, *_: (0,) * len(shape))
    of_group = lambda shape: pl.BlockSpec(shape, lambda i, *_: (group,) + (0,) * (len(shape) - 1))
    like = jax.ShapeDtypeStruct
    return pl.pallas_call(
        functools.partial(attend_kernel, group),
        grid_spec=pltpu.PrefetchScalarGridSpec(
            num_scalar_prefetch=2,
            grid=(1,),
            in_specs=[
                pl.BlockSpec((zsize, 1, rows, width), lambda i, *_: (0, group, 0, 0)),
                whole(weight.shape), whole(bias.shape),
                of_group((1, length, pair)), of_group((1, length, pair)), whole(docs.shape),
            ],
            out_specs=[
                whole((1, length, cols)),
                whole((1, heads, length, pair)), whole((1, heads, length, pair)), whole((1, heads, length, pair)),
                whole((1, heads, length)),
            ],
            scratch_shapes=[
                pltpu.VMEM((heads, HEAD_DIM, length), bf16),
                pltpu.VMEM((heads, BLOCK), f32), pltpu.VMEM((heads, BLOCK), f32),
                pltpu.VMEM((heads, HEAD_DIM, BLOCK), f32),
            ],
        ),
        out_shape=[
            like((1, length, cols), bf16),
            like((1, heads, length, pair), bf16), like((1, heads, length, pair), bf16),
            like((1, heads, length, pair), bf16), like((1, heads, length), f32),
        ],
        compiler_params=pltpu.CompilerParams(vmem_limit_bytes=VMEM),
        cost_estimate=pl.CostEstimate(
            flops=2 * length * width * 3 * cols + 4 * length * length * cols,
            bytes_accessed=2 * length * width + 6 * width * cols + 8 * length * cols,
            transcendentals=length * length * heads,
        ),
    )(*bounds, tokens, weight, bias, cosine, sine, docs)


def attend_back_kernel(group, last, lo_ref, hi_ref, z_ref, q_ref, k_ref, v_ref, lse_ref, mixed_ref, cos_ref, sin_ref, tok_hbm, w_hbm, *refs):
    zsize, _, rows, _ = tok_hbm.shape
    do_refs, refs = refs[:zsize], refs[zsize:]
    if group:
        before_hbm, refs = refs[0], refs[1:]
    back_ref, wgrad_ref, sum_ref, grad_ref, wsum_ref, dox_ref, kt_ref, delta_ref, dk_ref, dv_ref, dqt_ref, tok_ref, w_ref, sem = refs
    late = [
        pltpu.make_async_copy(tok_hbm.at[:, group], tok_ref, sem.at[0]), pltpu.make_async_copy(w_hbm, w_ref, sem.at[1]),
    ]
    if group:
        late.append(pltpu.make_async_copy(before_hbm, wsum_ref, sem.at[2]))
    for copy in late:
        copy.start()
    heads, length = q_ref.shape[1], q_ref.shape[2]
    pair = 2 * HEAD_DIM
    scale = HEAD_DIM ** (-0.5)
    blocks = length // BLOCK

    low_half = lax.broadcasted_iota(jnp.int32, (rows, pair), 1) < HEAD_DIM
    for step in range(zsize):
        at = pl.ds(pl.multiple_of(lax.rem(z_ref[0] + zsize - step, zsize) * rows, rows), rows)
        for j in range(heads // 2):
            upstream = do_refs[step][0, :, j * pair:(j + 1) * pair].astype(f32)
            product = (upstream * mixed_ref[0, at, j * pair:(j + 1) * pair].astype(f32)).T
            for h in range(2):
                head = 2 * j + h
                one = upstream if h == 0 else pltpu.roll(upstream, HEAD_DIM, 1)
                dox_ref[head, at, :] = jnp.where(low_half, one, 0.0).astype(bf16)
                delta_ref[head:head + 1, at] = jnp.sum(
                    product[h * HEAD_DIM:(h + 1) * HEAD_DIM], axis=0, keepdims=True
                )
                kt_ref[head, :, at] = k_ref[0, head, at, :].astype(f32).T[:HEAD_DIM].astype(bf16)
                dk_ref[head, at, :] = jnp.zeros((rows, pair), f32)
                dv_ref[head, at, :] = jnp.zeros((rows, pair), f32)

    sum_ref[...] = jnp.zeros(sum_ref.shape, f32)
    if not group:
        wsum_ref[...] = jnp.zeros(wsum_ref.shape, f32)

    def put(c, j, at, field):
        low = field.astype(bf16)
        grad_ref[c, at, j * pair:(j + 1) * pair] = low
        cols = pl.ds(j * pair, pair)
        sum_ref[c:c + 1, cols] = sum_ref[c:c + 1, cols] + jnp.sum(low.astype(f32), axis=0, keepdims=True)

    def back(field, at):
        return field * cos_ref[0, at, :] - turn_halves(field, sin_ref[0, at, :])

    def query_block(i, carry):
        at = pl.ds(pl.multiple_of(i * BLOCK, BLOCK), BLOCK)
        dqt_ref[...] = jnp.zeros(dqt_ref.shape, f32)

        def key_block(j, carry):
            keys_at = pl.ds(pl.multiple_of(j * BLOCK, BLOCK), BLOCK)
            every = range(heads)
            queries = [q_ref[0, h, at, :] for h in every]
            upstream = [dox_ref[h, at, :] for h in every]
            st = [scores_of(k_ref[0, h, keys_at, :], queries[h]) for h in every]
            dp = [scores_of(v_ref[0, h, keys_at, :], upstream[h]) for h in every]
            p = [jnp.exp(st[h] - lse_ref[0, h:h + 1, at]) for h in every]
            ds = [(p[h] * (dp[h] - delta_ref[h:h + 1, at])).astype(bf16) for h in every]
            dv = [jnp.dot(p[h].astype(bf16), upstream[h], preferred_element_type=f32) for h in every]
            dk = [jnp.dot(ds[h], queries[h], preferred_element_type=f32) for h in every]
            dq = [jnp.dot(kt_ref[h, :, keys_at], ds[h], preferred_element_type=f32) for h in every]
            for h in every:
                dv_ref[h, keys_at, :] = dv_ref[h, keys_at, :] + dv[h]
                dk_ref[h, keys_at, :] = dk_ref[h, keys_at, :] + dk[h]
                dqt_ref[h] = dqt_ref[h] + dq[h]
            return carry

        lax.fori_loop(lo_ref[group, i], hi_ref[group, i], key_block, 0)
        for j in range(heads // 2):
            both = jnp.concatenate([dqt_ref[2 * j], dqt_ref[2 * j + 1]], axis=0)
            put(0, j, at, back(both.T * scale, at))
        return carry

    lax.fori_loop(0, blocks, query_block, 0)

    def finish(i, carry):
        at = pl.ds(pl.multiple_of(i * BLOCK, BLOCK), BLOCK)
        low = lax.broadcasted_iota(jnp.int32, (BLOCK, pair), 1) < HEAD_DIM
        for j in range(heads // 2):
            field = jnp.where(low, dk_ref[2 * j, at, :], pltpu.roll(dk_ref[2 * j + 1, at, :], HEAD_DIM, 1))
            put(1, j, at, back(field, at))
            field = jnp.where(low, dv_ref[2 * j, at, :], pltpu.roll(dv_ref[2 * j + 1, at, :], HEAD_DIM, 1))
            put(2, j, at, field)
        return carry

    lax.fori_loop(0, blocks, finish, 0)

    def onward(slot, carry):
        i = slot if last else lax.rem(z_ref[0] + slot, zsize)
        at = pl.ds(pl.multiple_of(i * rows, rows), rows)
        total = None
        x = tok_ref[i]
        for c in range(3):
            grad = grad_ref[c, at, :]
            part = lax.dot_general(grad, w_ref[c], (((1,), (1,)), ((), ())), preferred_element_type=f32)
            total = part if total is None else total + part
            wsum_ref[c] += lax.dot_general(x, grad, (((0,), (0,)), ((), ())), preferred_element_type=f32)
        back_ref[0, slot] = total.astype(bf16)
        return carry

    for copy in late:
        copy.wait()
    lax.fori_loop(0, zsize, onward, 0)
    wgrad_ref[...] = wsum_ref[...].astype(wgrad_ref.dtype)


def attend_backward(group, before, bounds, zi, kept, mixed, upstream, cosine, sine, tokens, weight):
    queries, keys, values, lse = kept
    _, heads, length, pair = queries.shape
    zsize, groups, rows, width = tokens.shape
    cols = heads * HEAD_DIM
    last = group == groups - 1
    whole = lambda shape: pl.BlockSpec(shape, lambda i, *_: (0,) * len(shape))
    of_group = lambda shape: pl.BlockSpec(shape, lambda i, *_: (group,) + (0,) * (len(shape) - 1))
    like = jax.ShapeDtypeStruct
    wide = (heads, length, pair)
    return pl.pallas_call(
        functools.partial(attend_back_kernel, group, last),
        grid_spec=pltpu.PrefetchScalarGridSpec(
            num_scalar_prefetch=3,
            grid=(1,),
            in_specs=[whole((1,) + wide)] * 3 + [
                whole((1, heads, length)), whole((1, length, cols)),
                of_group((1, length, pair)), of_group((1, length, pair)),
                HBM, HBM,
            ] + [whole((1, rows, cols))] * zsize + [HBM] * (group > 0),
            out_specs=[whole((1, zsize, rows, width)), whole(weight.shape), whole((8, cols))],
            scratch_shapes=[
                pltpu.VMEM((3, length, cols), bf16), pltpu.VMEM(weight.shape, f32),
                pltpu.VMEM(wide, bf16), pltpu.VMEM((heads, HEAD_DIM, length), bf16), pltpu.VMEM((heads, length), f32),
                pltpu.VMEM(wide, f32), pltpu.VMEM(wide, f32), pltpu.VMEM((heads, HEAD_DIM, BLOCK), f32),
                pltpu.VMEM((zsize, rows, width), bf16), pltpu.VMEM(weight.shape, bf16), pltpu.SemaphoreType.DMA((3,)),
            ],
        ),
        out_shape=[
            like((1, zsize, rows, width), bf16), like(weight.shape, bf16 if last else f32), like((8, cols), f32),
        ],
        compiler_params=pltpu.CompilerParams(vmem_limit_bytes=VMEM),
        cost_estimate=pl.CostEstimate(
            flops=0 if last else 40 * length * length * cols,
            bytes_accessed=0 if last else 48 * length * cols,
            transcendentals=0 if last else 2 * length * length * heads,
        ),
    )(*bounds, zi.reshape(1), queries, keys, values, lse, mixed, cosine, sine, tokens, weight, *upstream,
      *([before] if group else []))


MESH_ID = pl.DeviceIdType.MESH
HBM = pl.BlockSpec(memory_space=pl.ANY)


def other(axis):
    return {axis: 1 - lax.axis_index(axis)}


def greet(zsize):
    z = lax.axis_index("z")
    barrier = pltpu.get_barrier_semaphore()
    for axis in CELL:
        pl.semaphore_signal(barrier, inc=1, device_id=other(axis), device_id_type=MESH_ID)

    @pl.when(z > 0)
    def _():
        pl.semaphore_signal(barrier, inc=1, device_id={"z": z - 1}, device_id_type=MESH_ID)

    @pl.when(z < zsize - 1)
    def _():
        pl.semaphore_signal(barrier, inc=1, device_id={"z": z + 1}, device_id_type=MESH_ID)

    peers = len(CELL) + jnp.where(z > 0, 1, 0) + jnp.where(z < zsize - 1, 1, 0)
    pl.semaphore_wait(barrier, peers)


def remote(src, dst, send_sem, recv_sem, device):
    return pltpu.make_async_remote_copy(
        src_ref=src, dst_ref=dst, send_sem=send_sem, recv_sem=recv_sem, device_id=device, device_id_type=MESH_ID
    )


ORDERS = {"xy": ("x", "y"), "yx": ("y", "x")}


def gather_kernel(zsize, orders, *refs):
    n = len(orders)
    tok, bias, shards = refs[0], refs[1], refs[2:2 + n]
    tok_all, bias_all, wholes = refs[2 + n], refs[3 + n], refs[4 + n:4 + 2 * n]
    held = refs[4 + 2 * n:6 + 3 * n]
    local_sem, z_send, z_recv, p_send, p_recv = refs[6 + 3 * n:]
    z = lax.axis_index("z")
    c = lax.axis_index("core")
    place = [(lax.axis_index(o[0]), lax.axis_index(o[1])) for o in orders]

    sources = list(shards) + [tok, bias]
    targets = list(wholes) + [tok_all, bias_all]
    into = [pltpu.make_async_copy(sources[i], held[i], local_sem.at[0, i]) for i in range(n + 2)]
    local = [pltpu.make_async_copy(held[i], targets[i].at[z], local_sem.at[1, i]) for i in range(n + 2)]
    for copy in into:
        copy.start()
    greet(zsize)

    def line(item, src, step, side):
        to = z + 1 if side == 0 else z - 1
        if item < n:
            f, s = place[item]
            own = shards[item].at[c, f, s]
            dst = wholes[item].at[src, c, f, s]
        else:
            own = (tok, bias)[item - n]
            dst = (tok_all, bias_all)[item - n].at[src]
        return remote(
            own if step == 0 else dst, dst, z_send.at[side, item, step], z_recv.at[side, item, step], {"z": to}
        )

    def exchange(k, src, stage, slot):
        f, s = place[k]
        whole = wholes[k]
        ref = (whole.at[src, c, f, s], whole.at[src, c, f], whole.at[src, c])[stage]
        axis = (orders[k][1], orders[k][0], "core")[stage]
        return remote(ref, ref, p_send.at[slot, k, stage], p_recv.at[slot, k, stage], other(axis))

    def valid_from(side, step):
        return z - step - 1 >= 0 if side == 0 else z + step + 1 < zsize

    def source(side, step):
        return z - step - 1 if side == 0 else z + step + 1

    def has_next(side):
        return z < zsize - 1 if side == 0 else z > 0

    for side in range(2):

        @pl.when(has_next(side))
        def _():
            for item in range(n):
                line(item, z, 0, side).start()

    def stage_on(stage, step):
        for side in range(2):

            @pl.when(valid_from(side, step))
            def _():
                src = source(side, step)
                slot = side * (zsize - 1) + step
                for k in range(n):
                    exchange(k, src, stage - 1, slot).wait_recv()
                    if stage < 3:
                        exchange(k, src, stage, slot).start()

    def arrive(items, step):
        for side in range(2):

            @pl.when(valid_from(side, step))
            def _():
                src = source(side, step)
                for item in items:
                    line(item, src, step, side).wait_recv()
                    if step + 1 < zsize - 1:

                        @pl.when(has_next(side))
                        def _():
                            line(item, src, step + 1, side).start()

                    if item < n:
                        exchange(item, src, 0, side * (zsize - 1) + step).start()

    for copy, onward in zip(into, local):
        copy.wait()
        onward.start()
    for step in range(zsize - 1):
        arrive(range(n), step)
        if step == zsize - 2:
            for side in range(2):

                @pl.when(has_next(side))
                def _():
                    for item in range(n, n + 2):
                        line(item, z, 0, side).start()

        if step >= 1:
            stage_on(1, step - 1)
    for step in range(zsize - 1):
        if step == 0:
            stage_on(1, zsize - 2)
        stage_on(2, step)
        arrive(range(n, n + 2), step)
    for step in range(zsize - 1):
        stage_on(3, step)
    for copy in local:
        copy.wait()
    for side in range(2):

        @pl.when(has_next(side))
        def _():
            for item in range(n + 2):
                line(item, z, 0, side).wait_send()

        for step in range(zsize - 1):

            @pl.when(valid_from(side, step))
            def _():
                src = source(side, step)
                if step + 1 < zsize - 1:

                    @pl.when(has_next(side))
                    def _():
                        for item in range(n + 2):
                            line(item, src, step + 1, side).wait_send()

                for k in range(n):
                    for stage in range(3):
                        exchange(k, src, stage, side * (zsize - 1) + step).wait_send()


def gather_start(tokens, bias, weights, zsize):
    orders = [ORDERS[o] for o, _ in weights]
    shards = [w for _, w in weights]
    n = len(shards)
    stack = lambda a: jax.ShapeDtypeStruct((zsize,) + a.shape, a.dtype)
    return pl.pallas_call(
        functools.partial(gather_kernel, zsize, orders),
        out_shape=[stack(tokens), stack(bias)] + [stack(w) for w in shards],
        in_specs=[HBM] * (n + 2),
        out_specs=[HBM] * (n + 2),
        scratch_shapes=[pltpu.VMEM(a.shape, a.dtype) for a in shards + [tokens, bias]] + [
            pltpu.SemaphoreType.DMA((2, n + 2)),
            pltpu.SemaphoreType.DMA((2, n + 2, zsize - 1)),
            pltpu.SemaphoreType.DMA((2, n + 2, zsize - 1)),
            pltpu.SemaphoreType.DMA((2 * (zsize - 1), n, 3)),
            pltpu.SemaphoreType.DMA((2 * (zsize - 1), n, 3)),
        ],
        compiler_params=pltpu.CompilerParams(
            collective_id=0, has_side_effects=True, vmem_limit_bytes=VMEM
        ),
    )(tokens, bias, *shards)


def add_rows(dst, src):
    rows = dst.shape[0]
    step = math.gcd(rows, 32)

    def body(i, carry):
        at = pl.ds(pl.multiple_of(i * step, step), step)
        dst[at, :] = dst[at, :] + src[at, :]
        return carry

    lax.fori_loop(0, rows // step, body, 0)


def reduce_kernel(zsize, orders, w, *refs):
    n = 3
    p = len(orders) - n
    items = n + p
    pieces, came, refs = refs[:p], refs[p:2 * p], refs[2 * p:]
    parts, backs, small = refs[:n], refs[n], refs[n + 1]
    pos = n + 2
    piece_out, part_out, back_out = refs[pos:pos + p], refs[pos + p:pos + p + n], refs[pos + p + n]
    small_out = refs[pos + p + n + 1]
    outs = list(part_out) + list(piece_out)
    pos += p + n + 2
    mine = refs[pos:pos + items + w]
    pos += items + w
    got_c, got_1, got_2 = refs[pos:pos + n], refs[pos + n:pos + n + items], refs[pos + n + items:pos + n + 2 * items]
    pos += n + 2 * items
    lines = [0] + list(range(n, items + w))
    line_backs = list(range(items, items + w))
    got_z = dict(zip(lines, refs[pos:pos + len(lines)]))
    pos += len(lines)
    small_mine, small_got, small_line, small_total, part_line, part_total = refs[pos:pos + 6]
    (local_sem, send, recv, z_send, z_recv, s_send, s_recv, t_send, t_recv, g_send, g_recv, end_sem) = refs[pos + 6:]
    z = lax.axis_index("z")
    c = lax.axis_index("core")
    orders = orders[p:] + orders[:p]
    place = [(lax.axis_index(o[0]), lax.axis_index(o[1])) for o in orders]
    turn = []
    for i in range(zsize // 2):
        turn += [i, zsize - 1 - i]
    few = parts[1].shape[0]
    steps = [(1, b) for b in range(few)] + [(2, 0)] + [(0, b) for b in turn]

    def load(k, b):
        src = parts[k].at[b, c] if k < n else pieces[k - n].at[b] if k < items else backs.at[k - items, b]
        return pltpu.make_async_copy(src, mine[k].at[b], local_sem.at[k, b])

    def load_came(k, b):
        return pltpu.make_async_copy(came[k - n].at[b], got_1[k].at[b], local_sem.at[items + w + 1 + k - n, b])

    load_small = pltpu.make_async_copy(small, small_mine.at[0], local_sem.at[items + w, 0])

    def half(k, b, stage):
        f, s = place[k]
        if stage == 0:
            src, dst, axis = parts[k].at[b, 1 - c], got_c[k].at[b], "core"
        elif stage == 1:
            src, dst, axis = mine[k].at[b, 1 - f], got_1[k].at[b], orders[k][0]
        else:
            held = mine[k].at[b, f] if k < n else mine[k].at[b]
            src, dst, axis = held.at[1 - s], got_2[k].at[b], orders[k][1]
        return remote(src, dst, send.at[stage, k, b], recv.at[stage, k, b], other(axis))

    def own(k, b):
        if k >= items:
            return mine[k].at[b]
        f, s = place[k]
        return mine[k].at[b, s] if k >= n else mine[k].at[b, f, s]

    def hop(k, b, side):
        to = z + 1 if side == 0 else z - 1
        at = b if side == 0 else jnp.where(b == z - 1, zsize, b)
        return remote(own(k, b), got_z[k].at[at], z_send.at[k, b], z_recv.at[k, at], {"z": to})

    def take(k, b, side):
        at = b if side == 0 else jnp.where(b == z, zsize, b)
        ref = got_z[k].at[at]
        sender = z - 1 if side == 0 else z + 1
        remote(own(k, b), ref, z_send.at[k, b], z_recv.at[k, at], {"z": sender}).wait_recv()
        add_rows(own(k, b), ref)

    def line_start(ks, messages):
        for side in range(2):

            @pl.when(z == (0 if side == 0 else zsize - 1))
            def _():
                for i in messages:
                    for k in ks:
                        hop(k, zsize - 1 - i if side == 0 else i, side).start()

    def line_slot(ks, slot):
        for i in range(slot):
            for side in range(2):
                b = zsize - 1 - i if side == 0 else i

                @pl.when(z == (slot - i if side == 0 else zsize - 1 - slot + i))
                def _():
                    for k in ks:
                        take(k, b, side)

                        @pl.when(z < b if side == 0 else z > b)
                        def _():
                            hop(k, b, side).start()

    def small_swap(stage):
        return remote(
            small_mine.at[stage], small_got.at[stage], s_send.at[stage], s_recv.at[stage], other(CELL[stage])
        )

    def small_step(stage):
        small_swap(stage).wait_recv()
        small_mine[stage + 1] = small_mine[stage] + small_got[stage]
        if stage < 2:
            small_swap(stage + 1).start()

    last = len(CELL)
    last_part = own(2, 0)

    def total_copy(item, way):
        line, total = ((small_line, small_total), (part_line, part_total))[item]
        src = (small_mine.at[last], last_part)[item] if way == 0 else total
        dst = line if way == 0 else total
        to = z + 1 if way == 0 else z - 1
        return remote(src, dst, t_send.at[item, way], t_recv.at[item, way], {"z": to})

    def total_step(tick):
        if 0 <= tick < zsize:

            @pl.when(z == tick)
            def _():
                if tick > 0:
                    for item in range(2):
                        total_copy(item, 0).wait_recv()
                    small_mine[last] = small_mine[last] + small_line[...]
                    add_rows(last_part, part_line)
                if tick < zsize - 1:
                    for item in range(2):
                        total_copy(item, 0).start()
                else:
                    small_total[...] = small_mine[last]
                    part_total[...] = last_part[...]

        back_tick = tick - (zsize - 1)
        if 0 <= back_tick < zsize:

            @pl.when(z == zsize - 1 - back_tick)
            def _():
                if back_tick > 0:
                    for item in range(2):
                        total_copy(item, 1).wait_recv()
                if back_tick < zsize - 1:
                    for item in range(2):
                        total_copy(item, 1).start()

    line_pieces = list(range(n, items))
    piece_steps = [(k, b) for b in turn for k in line_pieces]
    for b in turn:
        for k in line_backs:
            load(k, b).start()
    for k, b in piece_steps:
        load(k, b).start()
        load_came(k, b).start()
    for k, b in steps:
        load(k, b).start()
    load_small.start()
    greet(zsize)
    for k, b in steps:
        half(k, b, 0).start()
    for b in turn:
        for k in line_backs:
            load(k, b).wait()
    line_start(line_backs, [0])
    load_small.wait()
    small_swap(0).start()

    def stage_1(k, b):
        f, s = place[k]
        load(k, b).wait()
        half(k, b, 0).wait_recv()
        for i in range(2):
            add_rows(mine[k].at[b, 1 - f, i], got_c[k].at[b, 1 - f, i])
        half(k, b, 1).start()
        for i in range(2):
            add_rows(mine[k].at[b, f, i], got_c[k].at[b, f, i])

    def stage_2(k, b):
        f, s = place[k]
        held = mine[k].at[b, f] if k < n else mine[k].at[b]
        if k < n:
            half(k, b, 1).wait_recv()
        else:
            load(k, b).wait()
            load_came(k, b).wait()
        add_rows(held.at[1 - s], got_1[k].at[b, 1 - s])
        half(k, b, 2).start()
        add_rows(held.at[s], got_1[k].at[b, s])

    def stage_3(k, b):
        half(k, b, 2).wait_recv()
        add_rows(own(k, b), got_2[k].at[b])

    def result(k, b):
        return part_total if k == 2 else own(k, b)

    def out_of(k, b):
        return outs[k].at[b] if k == 1 else outs[k]

    def put(k, b, slot):
        f, s = place[k]
        return pltpu.make_async_copy(result(k, b), out_of(k, b).at[c, f, s], end_sem.at[slot])

    def spread(k, b, stage, slot):
        f, s = place[k]
        out = out_of(k, b)
        dst = (out.at[c, f, s], out.at[c, f], out.at[c])[stage]
        src = result(k, b) if stage == 0 else dst
        axis = (orders[k][1], orders[k][0], "core")[stage]
        return remote(src, dst, g_send.at[slot, stage], g_recv.at[slot, stage], other(axis))

    spreads = [
        [(1, b, b) for b in range(few)],
        [(k, z, few + k - n) for k in line_pieces],
        [(0, z, few + p), (2, 0, few + p + 1)],
    ]

    def spread_step(group, stage):
        for k, b, slot in spreads[group]:
            if stage == 0:
                spread(k, b, 0, slot).start()
                put(k, b, slot).start()
                continue
            if stage == 1:
                put(k, b, slot).wait()
            spread(k, b, stage - 1, slot).wait_recv()
            if stage < 3:
                spread(k, b, stage, slot).start()

    def sent(ks):
        for b in range(zsize):

            @pl.when(z != b)
            def _():
                for k in ks:
                    hop(k, b, 0).wait_send()

    at_end = jnp.logical_or(z == 0, z == zsize - 1)
    for k, b in piece_steps:
        stage_2(k, b)
    for k, b in steps:
        stage_1(k, b)
    small_step(0)
    for b in turn:
        for k in line_pieces:
            stage_3(k, b)
        for side in range(2):

            @pl.when(jnp.logical_and(z == (0 if side == 0 else zsize - 1), z != b))
            def _():
                for k in line_pieces:
                    hop(k, b, side).start()

    for k, b in steps:
        stage_2(k, b)
    small_step(1)
    line_slot(line_backs, 1)
    for k, b in steps:
        stage_3(k, b)
    small_step(2)
    spread_step(0, 0)
    line_start([0], range(zsize - 1))
    total_step(0)

    @pl.when(at_end)
    def _():
        sent(line_pieces)

    line_start(line_backs, range(1, zsize - 1))
    ticks = list(range(1, 2 * zsize - 1))
    later = [(0, 1), (0, 2), (0, 3)]

    def fill(group_stages, count):
        for _ in range(count):
            if group_stages:
                spread_step(*group_stages.pop(0))

    for slot in range(1, zsize):
        line_slot(line_pieces, slot)
        total_step(ticks.pop(0))
        fill(later, 1)
        if slot >= 2:
            line_slot([0], slot - 1)
    fill(later, 3)
    spread_step(1, 0)
    later = [(1, 1), (1, 2), (1, 3)]
    total_step(ticks.pop(0))
    line_slot([0], zsize - 1)
    for slot in range(2, zsize - 1):
        line_slot(line_backs, slot)
        fill(later, 1)
    for tick in ticks:
        total_step(tick)
    spread_step(2, 0)
    fill(later, 1)
    spread_step(2, 1)
    fill(later, 1)
    spread_step(2, 2)
    fill(later, 3)
    line_slot(line_backs, zsize - 1)
    finish_back = [
        pltpu.make_async_copy(mine[k].at[z], back_out.at[k - items], local_sem.at[k, 0]) for k in line_backs
    ]
    for copy in finish_back:
        copy.start()
    finish_small = pltpu.make_async_copy(small_total, small_out, local_sem.at[items + w, 0])
    finish_small.start()
    spread_step(2, 3)
    for copy in finish_back:
        copy.wait()
    finish_small.wait()
    sent([0] + line_backs)

    @pl.when(jnp.logical_not(at_end))
    def _():
        sent(line_pieces)

    for way in range(2):

        @pl.when(z < zsize - 1 if way == 0 else z > 0)
        def _():
            for item in range(2):
                total_copy(item, way).wait_send()

    for k, b in steps:
        for stage in range(3):
            half(k, b, stage).wait_send()
    for k, b in piece_steps:
        half(k, b, 2).wait_send()
    for stage in range(3):
        small_swap(stage).wait_send()
    for group in spreads:
        for k, b, slot in group:
            for stage in range(3):
                spread(k, b, stage, slot).wait_send()


def reduce_end(pieces, parts, backs, small, zsize):
    orders = [ORDERS[o[0]] for o in pieces + parts]
    piece_arrays = [a for _, a, _ in pieces]
    came = [a for _, _, a in pieces]
    arrays = [a for _, a in parts]
    p, n, w = len(pieces), len(parts), backs.shape[0]
    shapes = [a.shape for a in arrays]
    like = jax.ShapeDtypeStruct
    outs = [like((2, 2, 2) + a.shape[2:], bf16) for a in piece_arrays]
    outs += [like(s if i == 1 else s[1:], bf16) for i, s in enumerate(shapes)]
    outs += [like((w,) + backs.shape[2:], bf16), like(small.shape, f32)]
    held = lambda shape: pltpu.VMEM(shape, bf16)
    scratch = [held((s[0],) + s[2:]) for s in shapes]
    scratch += [held(a.shape) for a in piece_arrays] + [held(backs.shape[1:])] * w
    scratch += [held((s[0],) + s[2:]) for s in shapes]
    scratch += [held((s[0],) + s[3:]) for s in shapes] + [held(a.shape) for a in piece_arrays]
    scratch += [held((s[0],) + s[4:]) for s in shapes] + [held(a.shape[:1] + a.shape[2:]) for a in piece_arrays]
    scratch += [held((zsize + 1,) + shapes[0][4:])]
    scratch += [held((zsize + 1,) + a.shape[2:]) for a in piece_arrays] + [held((zsize + 1,) + backs.shape[2:])] * w
    scratch += [pltpu.VMEM((4,) + small.shape, f32), pltpu.VMEM((3,) + small.shape, f32)]
    scratch += [pltpu.VMEM(small.shape, f32)] * 2 + [held(shapes[2][4:])] * 2
    dma = pltpu.SemaphoreType.DMA
    most = max(zsize, shapes[1][0])
    ends = shapes[1][0] + p + 2
    scratch += [
        dma((n + 2 * p + w + 1, most)), dma((3, n + p, most)), dma((3, n + p, most)),
        dma((n + p + w, zsize)), dma((n + p + w, zsize + 1)),
        dma((3,)), dma((3,)), dma((2, 2)), dma((2, 2)), dma((ends, 3)), dma((ends, 3)), dma((ends,)),
    ]
    return pl.pallas_call(
        functools.partial(reduce_kernel, zsize, orders, w),
        out_shape=outs,
        in_specs=[HBM] * (n + 2 * p + 2),
        out_specs=[HBM] * (n + p + 2),
        scratch_shapes=scratch,
        compiler_params=pltpu.CompilerParams(
            collective_id=1, has_side_effects=True, vmem_limit_bytes=VMEM
        ),
    )(*piece_arrays, *came, *arrays, backs, small)


def gelu_pair(v):
    size = jnp.abs(v)
    t = 1.0 / (1.0 + (0.3275911 * 0.5 ** 0.5) * size)
    bell = jnp.exp(-0.5 * (v * v))
    poly = t * (0.254829592 + t * (-0.284496736 + t * (1.421413741 + t * (-1.453152027 + t * 1.061405429))))
    tail = 0.5 * poly * bell
    cdf = jnp.where(v >= 0.0, 1.0 - tail, tail)
    return v * cdf, cdf + v * (bell * (1.0 / (2.0 * math.pi) ** 0.5))


def norm_rows(field):
    mean = jnp.mean(field, axis=-1, keepdims=True)
    centred = field - mean
    inv_std = lax.rsqrt(jnp.mean(centred * centred, axis=-1, keepdims=True) + eps)
    return centred * inv_std, inv_std


def ffn_kernel(zsize, groups, z_ref, tok_ref, out_ref, out_bias_ref, gain_one_ref, shift_one_ref, up_ref, bias_ref, down_ref,
               down_bias_ref, gain_two_ref, shift_two_ref, proj_ref, dy_ref, de_ref, *refs):
    pieces = refs[:zsize * groups]
    (active_ref, slope_ref, mixed_ref, x_ref, scaled_ref, inv_ref, result_ref, embed_ref, grad_ref, low_ref, proj_grad_ref,
     vec_ref, normed_ref, sum_ref) = refs[zsize * groups:]
    rows, width = x_ref.shape
    local = rows // groups
    cols = width // zsize
    chunk = 128
    heads = proj_ref.shape[0]

    @pl.when(pl.program_id(0) == 0)
    def _():
        for g in range(groups):
            for step in range(zsize):
                at = lax.rem(z_ref[0] + zsize - step, zsize) * cols
                mixed_ref[pl.ds(g * local, local), pl.ds(pl.multiple_of(at, cols), cols)] = pieces[g * zsize + step][0]
        def first(i, carry):
            at = pl.ds(pl.multiple_of(i * chunk, chunk), chunk)
            attended = jnp.dot(mixed_ref[at, :], out_ref[...], preferred_element_type=f32) + out_bias_ref[...]
            scaled, inv_std = norm_rows(tok_ref[at, :].astype(f32) + attended)
            normed = scaled * gain_one_ref[...] + shift_one_ref[...]
            scaled_ref[at, :] = scaled
            inv_ref[at, :] = inv_std
            normed_ref[at, :] = normed
            x_ref[at, :] = normed.astype(bf16)
            return carry

        lax.fori_loop(0, rows // chunk, first, 0)
        sum_ref[...] = jnp.zeros(sum_ref.shape, f32)

    parts = [pl.ds(i * chunk, chunk) for i in range(rows // chunk)]
    hidden = [jnp.dot(x_ref[at, :], up_ref[0], preferred_element_type=f32) + bias_ref[0] for at in parts]
    for at, field in zip(parts, hidden):
        active, slope = gelu_pair(field)
        slope_ref[0, at, :] = slope.astype(bf16)
        active_ref[0, :, at] = active.T.astype(bf16)
        sum_ref[at, :] += jnp.dot(active.astype(bf16), down_ref[0], preferred_element_type=f32)

    @pl.when(pl.program_id(0) == pl.num_programs(0) - 1)
    def _():
        vec_ref[...] = jnp.zeros(vec_ref.shape, f32)

        def second(i, carry):
            at = pl.ds(pl.multiple_of(i * chunk, chunk), chunk)
            scaled, inv_std = norm_rows(normed_ref[at, :] + (sum_ref[at, :] + down_bias_ref[...]))
            result_ref[at, :] = (scaled * gain_two_ref[...] + shift_two_ref[...]).astype(bf16)
            g, inner = i // (local // chunk), lax.rem(i, local // chunk)
            upstream = dy_ref[at, :].astype(f32) + lax.dot_general(
                de_ref[g, :, pl.ds(pl.multiple_of(inner * chunk, chunk), chunk)], proj_ref[...], (((0,), (0,)), ((), ())), preferred_element_type=f32
            )
            grad_scaled = upstream * gain_two_ref[...]
            grad = inv_std * (
                grad_scaled
                - jnp.mean(grad_scaled, axis=-1, keepdims=True)
                - scaled * jnp.mean(grad_scaled * scaled, axis=-1, keepdims=True)
            )
            grad_ref[at, :] = grad
            low = grad.astype(bf16)
            low_ref[at, :] = low
            for n, field in enumerate((low.astype(f32), upstream * scaled, upstream)):
                vec_ref[n:n + 1, :] = vec_ref[n:n + 1, :] + jnp.sum(field, axis=0, keepdims=True)
            return carry

        lax.fori_loop(0, rows // chunk, second, 0)
        proj_grad = jnp.zeros((heads, width), f32)
        for g in range(groups):
            result = result_ref[pl.ds(g * local, local), :]
            embed_ref[g] = lax.dot_general(
                proj_ref[...], result, (((1,), (1,)), ((), ())), preferred_element_type=f32
            ).astype(bf16)
            proj_grad = proj_grad + jnp.dot(de_ref[g], result, preferred_element_type=f32)
        proj_grad_ref[...] = jnp.zeros(proj_grad_ref.shape, bf16)
        proj_grad_ref[pl.ds(0, heads), :] = proj_grad.astype(bf16)


def ffn_forward(zi, tokens, pieces, out_all, one, up_all, up_bias, down_all, two, proj, dy, de):
    zsize, width, units = up_all.shape
    rows = tokens.shape[0]
    groups, heads, local = de.shape
    tile = units
    like = jax.ShapeDtypeStruct
    whole = lambda shape: pl.BlockSpec(shape, lambda s, z: (0,) * len(shape))
    tiles = pl.BlockSpec((1, rows, tile), lambda s, z: (s, 0, 0))
    field, row = whole((rows, width)), whole((1, width))
    padded = heads + -heads % 128
    return pl.pallas_call(
        functools.partial(ffn_kernel, zsize, groups),
        grid_spec=pltpu.PrefetchScalarGridSpec(
            num_scalar_prefetch=1,
            grid=(zsize,),
            in_specs=[
                field, whole((width, width)), row, row, row,
                pl.BlockSpec((1, width, tile), lambda s, z: (s, 0, 0)),
                pl.BlockSpec((1, 1, tile), lambda s, z: (s, 0, 0)),
                pl.BlockSpec((1, tile, width), lambda s, z: (s, 0, 0)),
                row, row, row, whole(proj.shape), field, whole(de.shape),
            ] + [whole(p.shape) for p in pieces],
            out_specs=[
                pl.BlockSpec((1, tile, rows), lambda s, z: (s, 0, 0)), tiles,
                field, field, field, whole((rows, 1)), field, whole(de.shape), field, field,
                whole((padded, width)), whole((8, width)),
            ],
            scratch_shapes=[pltpu.VMEM((rows, width), f32), pltpu.VMEM((rows, width), f32)],
        ),
        out_shape=[
            like((zsize, units, rows), bf16), like((zsize, rows, units), bf16), like((rows, width), bf16),
            like((rows, width), bf16), like((rows, width), f32), like((rows, 1), f32), like((rows, width), bf16),
            like(de.shape, bf16), like((rows, width), f32), like((rows, width), bf16), like((padded, width), bf16),
            like((8, width), f32),
        ],
        compiler_params=pltpu.CompilerParams(vmem_limit_bytes=VMEM),
    )(zi.reshape(1), tokens, out_all, *one, up_all, up_bias[:, None, :], down_all, *two, proj, dy, de, *pieces)


def ffn_back_kernel(core_ref, second_ref, normed_ref, up_ref, down_ref, active_ref, slope_ref,
                    give_up_ref, keep_up_ref, give_down_ref, keep_down_ref, back_ref, bias_ref, turned_ref):
    s = pl.program_id(0)
    half = turned_ref.shape[0] // 2
    c = core_ref[0]

    @pl.when(s == 0)
    def _():
        back_ref[...] = jnp.zeros(back_ref.shape, f32)
        turned_ref[...] = normed_ref[...].T

    second = second_ref[...]
    upstream = lax.dot_general(second, down_ref[0], (((1,), (1,)), ((), ())), preferred_element_type=f32)
    grad = (upstream * slope_ref[0].astype(f32)).astype(bf16)
    bias_ref[0] = jnp.sum(grad.astype(f32), axis=0, keepdims=True)
    units = active_ref.shape[1] // 2
    back_ref[...] += lax.dot_general(grad, up_ref[0], (((1,), (1,)), ((), ())), preferred_element_type=f32)
    for who, down_to, up_to in ((1 - c, give_down_ref, give_up_ref), (c, keep_down_ref, keep_up_ref)):
        active = active_ref[0, pl.ds(pl.multiple_of(who * units, units), units), :]
        down_to[0] = jnp.dot(active, second, preferred_element_type=f32).astype(bf16)
        turned = turned_ref[pl.ds(pl.multiple_of(who * half, half), half), :]
        up_to[0] = jnp.dot(turned, grad, preferred_element_type=f32).astype(bf16)


def ffn_backward(core, second_low, normed_low, up_all, down_all, active, slope):
    zsize, width, units = up_all.shape
    rows = normed_low.shape[0]
    like = jax.ShapeDtypeStruct
    whole = pl.BlockSpec((rows, width), lambda s, c: (0, 0))
    tiles = pl.BlockSpec((1, rows, units), lambda s, c: (s, 0, 0))
    up_half = pl.BlockSpec((1, width // 2, units), lambda s, c: (s, 0, 0))
    down_half = pl.BlockSpec((1, units // 2, width), lambda s, c: (s, 0, 0))
    return pl.pallas_call(
        ffn_back_kernel,
        grid_spec=pltpu.PrefetchScalarGridSpec(
            num_scalar_prefetch=1,
            grid=(zsize,),
            in_specs=[
                whole, whole,
                pl.BlockSpec((1, width, units), lambda s, c: (s, 0, 0)),
                pl.BlockSpec((1, units, width), lambda s, c: (s, 0, 0)),
                pl.BlockSpec((1, units, rows), lambda s, c: (s, 0, 0)), tiles,
            ],
            out_specs=[
                up_half, up_half, down_half, down_half, whole,
                pl.BlockSpec((1, 1, units), lambda s, c: (s, 0, 0)),
            ],
            scratch_shapes=[pltpu.VMEM((width, rows), bf16)],
        ),
        out_shape=[
            like((zsize, width // 2, units), bf16), like((zsize, width // 2, units), bf16),
            like((zsize, units // 2, width), bf16), like((zsize, units // 2, width), bf16),
            like((rows, width), f32), like((zsize, 1, units), f32),
        ],
        compiler_params=pltpu.CompilerParams(vmem_limit_bytes=VMEM),
    )(core, second_low, normed_low, up_all, down_all, active, slope)


PAIR = [(0, 1), (1, 0)]


def first_halving(got, keep, order):
    zsize, half, cols = keep.shape
    shape = (zsize, 2, 2, half // 4, cols)
    got, keep = got.reshape(shape), keep.reshape(shape)
    i = lax.axis_index(ORDERS[order][0])
    pick = lambda array, j: lax.dynamic_index_in_dim(array, j, 1, keepdims=False)
    return pick(keep, 1 - i) + pick(got, 1 - i), pick(keep, i) + pick(got, i)


def widen_kernel(counts, up_ref, down_ref, out_ref, qkv_ref, first_ref, *refs):
    parts, (up_o, down_o, out_o, qkv_o, first_o) = refs[:-5], refs[-5:]
    for source, target in ((up_ref, up_o), (down_ref, down_o), (out_ref, out_o), (qkv_ref, qkv_o)):
        target[...] = source[...].astype(f32)
    per_group = pl.num_programs(0) // len(counts)
    for g, count in enumerate(counts):
        own, parts = parts[:count], parts[count:]

        @pl.when(pl.program_id(0) // per_group == g)
        def _():
            total = first_ref[...]
            for part in own:
                total = total + part[...].astype(f32)
            first_o[...] = total


def widen(up, down, out, qkv, first, parts):
    steps = 4
    per_group = steps // len(parts)

    def rows_of(array):
        return pl.BlockSpec((array.shape[0] // steps, array.shape[1]), lambda i: (i, 0))

    def of_group(g):
        block = first.shape[0] // steps
        return pl.BlockSpec((block, first.shape[1]), lambda i: (jnp.clip(i - g * per_group, 0, per_group - 1), 0))

    arrays = [up, down, out]
    specs = [rows_of(a) for a in arrays]
    specs.append(pl.BlockSpec((3, qkv.shape[1] // steps, qkv.shape[2]), lambda i: (0, i, 0)))
    specs.append(rows_of(first))
    return pl.pallas_call(
        functools.partial(widen_kernel, [len(p) for p in parts]),
        grid=(steps,),
        in_specs=specs + [of_group(g) for g, own in enumerate(parts) for _ in own],
        out_specs=specs,
        out_shape=[jax.ShapeDtypeStruct(a.shape, f32) for a in arrays + [qkv, first]],
        compiler_params=pltpu.CompilerParams(vmem_limit_bytes=VMEM),
    )(up, down, out, qkv, first, *[part for own in parts for part in own])


def per_device(blocks, tokens, segments, qkv_weight, qkv_bias, out_weight, out_bias, gain_one, shift_one,
               up_weight, up_bias, down_weight, down_bias, gain_two, shift_two, proj_weight, out_grad, embed_grad):
    groups, local_rows, model_width = tokens.shape
    length = segments.shape[1]
    zsize = length // local_rows
    head_cols = qkv_weight.shape[2]
    units_here = up_weight.shape[1]
    rows = groups * local_rows
    zi = lax.axis_index("z")
    cosine, sine = rotary_tables(doc_positions(segments))
    starts = jnp.sum(segments[:, None, :] < jnp.arange(4, dtype=jnp.int32)[None, :, None], axis=2, dtype=jnp.int32)
    edges = jnp.arange(length // BLOCK, dtype=jnp.int32)[None, :, None] * BLOCK
    bounds = (
        jnp.max(jnp.where(starts[:, None, :] <= edges, starts[:, None, :], 0), axis=2) // BLOCK,
        (jnp.min(jnp.where(starts[:, None, :] >= edges + BLOCK, starts[:, None, :], length), axis=2) + BLOCK - 1) // BLOCK,
    )

    def cut(array, rows_at):
        shape = array.shape
        return array.reshape(shape[:rows_at] + (2, 2, 2, shape[rows_at] // 8) + shape[rows_at + 1:])

    token_rows = tokens.reshape(rows, model_width)
    token_blocks, bias_blocks, out_all, up_all, down_all = gather_start(
        token_rows,
        up_bias.reshape(8, units_here // 8),
        [("xy", cut(out_weight, 0)), ("xy", cut(up_weight, 0)), ("yx", cut(down_weight, 0))],
        zsize,
    )
    token_blocks = token_blocks.reshape(zsize, groups, local_rows, model_width)
    out_all = out_all.reshape(model_width, model_width)
    up_all = up_all.reshape(zsize, model_width, units_here)
    down_all = down_all.reshape(zsize, units_here, model_width)
    full_up_bias = bias_blocks.reshape(zsize, units_here)

    def ring(step):
        return [(i, (i + step) % zsize) for i in range(zsize)]

    def exchange(array, size, axis):
        parts = []
        for step in range(zsize):
            part = lax.dynamic_slice_in_dim(array, lax.rem(zi + step, zsize) * size, size, axis)
            parts.append(lax.ppermute(part, "z", ring(step)) if step else part)
        return parts

    kept, pieces = [], []
    for g in range(groups):
        kept.append(attend_forward(g, bounds, token_blocks, qkv_weight, qkv_bias, cosine, sine, segments))
        pieces += exchange(kept[g][0], local_rows, 1)
    flat = lambda vector: vector.reshape(1, model_width)
    (active, slope, mixed, normed_low, scaled_one, inv_one, result_low, embedded, grad_second, second_low, proj_grad,
     vec_two) = ffn_forward(
        zi, token_rows, pieces, out_all, [flat(v) for v in (out_bias, gain_one, shift_one)], up_all, full_up_bias,
        down_all, [flat(v) for v in (down_bias, gain_two, shift_two)], proj_weight.T,
        out_grad.reshape(rows, model_width), embed_grad.transpose(0, 2, 1),
    )
    core = lax.axis_index("core").reshape(1)
    give_up, keep_up, give_down, keep_down, ffn_back, up_bias_grad = ffn_backward(
        core, second_low, normed_low, up_all, down_all, active, slope
    )
    got_down = lax.ppermute(give_down, "core", PAIR)
    got_up = lax.ppermute(give_up, "core", PAIR)
    grad_normed = grad_second + ffn_back
    grad_first, gain_one_grad, shift_one_grad = norm_backward(grad_normed, scaled_one, inv_one, gain_one)
    first_low = grad_first.astype(bf16)
    out_bias_grad = jnp.sum(first_low.astype(f32), axis=0)
    out_grad_w = jnp.einsum("nh,nd->hd", mixed, first_low, preferred_element_type=f32).astype(bf16)
    grad_mixed = jnp.einsum("nd,hd->nh", first_low, out_all, preferred_element_type=f32).astype(bf16)
    grad_mixed = grad_mixed.reshape(groups, local_rows, model_width)
    upstream = [exchange(grad_mixed[g:g + 1], head_cols, 2) for g in range(groups)]
    send_down, keep_down = first_halving(got_down, keep_down, "yx")
    send_up, keep_up = first_halving(got_up, keep_up, "xy")
    upstream[0], send_down, send_up = lax.optimization_barrier((upstream[0], send_down, send_up))
    got_down = lax.ppermute(send_down, ORDERS["yx"][0], PAIR)
    got_up = lax.ppermute(send_up, ORDERS["xy"][0], PAIR)
    qkv_weight_grad, qkv_bias_grad, early = None, 0.0, []
    for g in range(groups):
        backs, qkv_weight_grad, bias_part = attend_backward(
            g, qkv_weight_grad, bounds, zi, kept[g][1:], kept[g][0], upstream[g], cosine, sine, token_blocks, qkv_weight
        )
        qkv_bias_grad = qkv_bias_grad + bias_part[:3]
        if g < groups - 1:
            early.append([
                lax.ppermute(backs[0, step], "z", ring(step)) if step else backs[0, step] for step in range(zsize)
            ])
    backs, got_down, got_up, qkv_bias_grad = lax.optimization_barrier((backs, got_down, got_up, qkv_bias_grad))

    vec_one = jnp.pad(jnp.stack([out_bias_grad, gain_one_grad, shift_one_grad]), ((0, 5), (0, 0)))
    placed = lax.dynamic_update_slice(
        jnp.zeros((zsize, 3 * head_cols), f32), qkv_bias_grad.reshape(1, -1), (zi, 0)
    )
    small = jnp.concatenate([vec_one, vec_two, up_bias_grad.reshape(8, -1), placed.reshape(8, -1)], axis=1)
    up_grad, down_grad, out_grad_w, qkv_weight_grad, proj_grad, back, small = reduce_end(
        [("xy", keep_up, got_up), ("yx", keep_down, got_down)],
        [
            ("xy", cut(out_grad_w.reshape(zsize, head_cols, model_width), 1)),
            ("yx", cut(qkv_weight_grad, 1)),
            ("xy", cut(proj_grad[None], 1)),
        ],
        backs,
        small,
        zsize,
    )
    qkv_weight_grad = qkv_weight_grad.reshape(qkv_weight.shape)
    proj_grad = proj_grad.reshape(-1, model_width)[:proj_weight.shape[1]].astype(f32).T
    out_grad_w = out_grad_w.reshape(out_weight.shape)
    up_grad = up_grad.reshape(up_weight.shape)
    down_grad = down_grad.reshape(down_weight.shape)
    if blocks > 1:
        down_grad, up_grad, out_grad_w, qkv_weight_grad = lax.psum(
            (down_grad, up_grad, out_grad_w, qkv_weight_grad), ("xb", "yb")
        )
        small, proj_grad = lax.psum((small, proj_grad), ("xb", "yb"))
    up_grad, down_grad, out_grad_w, qkv_weight_grad, tokens_grad = widen(
        up_grad, down_grad, out_grad_w, qkv_weight_grad, grad_first, early + [[back[0]]]
    )
    base = 2 * model_width
    vec = list(small[:3, :model_width]) + list(small[:3, model_width:base])
    split = base + zsize * units_here // 8
    up_bias_grad = lax.dynamic_slice(small[:, base:split].reshape(-1), (zi * units_here,), (units_here,))
    qkv_bias_grad = lax.dynamic_slice(small[:, split:].reshape(-1), (zi * 3 * head_cols,), (3 * head_cols,))
    qkv_bias_grad = qkv_bias_grad.reshape(3, head_cols)
    shape3 = (groups, local_rows, model_width)
    return (
        result_low.reshape(shape3),
        embedded.transpose(0, 2, 1),
        tokens_grad.reshape(shape3),
        qkv_weight_grad,
        qkv_bias_grad,
        out_grad_w,
        vec[0], vec[1], vec[2],
        up_grad,
        up_bias_grad,
        down_grad,
        vec[3], vec[4], vec[5],
        proj_grad,
    )


def solution(mesh):
    dp_size, zsize = mesh.shape["dp"], mesh.shape["tensor"]
    side = math.isqrt(dp_size // 2) // 2
    cut = Mesh(mesh.devices.reshape(side, 2, side, 2, 2, zsize), DP + ("z",))
    rows3 = P(DP, "z", None)
    in_specs = (
        rows3, P(DP, None), P(None, None, "z"), P(None, "z"), P("z", None), P(), P(), P(),
        P(None, "z"), P("z"), P("z", None), P(), P(), P(), P(), rows3, rows3,
    )
    out_specs = (
        rows3, rows3, rows3, P(None, None, "z"), P(None, "z"), P("z", None), P(), P(), P(),
        P(None, "z"), P("z"), P("z", None), P(), P(), P(), P(),
    )

    def run(*args):
        return per_device(side * side, *args)

    return jax.shard_map(run, mesh=cut, in_specs=in_specs, out_specs=out_specs, check_vma=False)
```

```python
import functools
import math

import jax
import jax.numpy as jnp
from jax import lax
from jax.experimental import pallas as pl
from jax.experimental.pallas import tpu as pltpu
from jax.sharding import Mesh
from jax.sharding import PartitionSpec as P

HEAD_DIM = 64
eps = 1e-05
DP = ("xb", "x", "yb", "y", "core")
CELL = ("x", "y", "core")
ALL = DP + ("z",)
f32 = jnp.float32
bf16 = jnp.bfloat16
VMEM = 60 * 1024 * 1024


def doc_positions(segment_rows):
    below = segment_rows[:, None, :] < jnp.arange(4, dtype=jnp.int32)[None, :, None]
    starts = jnp.sum(below, axis=2, dtype=jnp.int32)
    row_index = jnp.arange(segment_rows.shape[1], dtype=jnp.int32)[None]
    start = starts[:, 3:4]
    for doc in (2, 1, 0):
        start = jnp.where(segment_rows == doc, starts[:, doc:doc + 1], start)
    return row_index - start


def rotary_tables(positions):
    half_dim = HEAD_DIM // 2
    lane = jnp.arange(2 * HEAD_DIM, dtype=jnp.int32)
    exponent = (lane % half_dim).astype(f32) * (2.0 / HEAD_DIM)
    frequency = jnp.exp(-exponent * math.log(10000.0))
    sign = jnp.where(lane % HEAD_DIM < half_dim, -1.0, 1.0)
    angles = positions.astype(f32)[..., None] * frequency
    return (jnp.cos(angles), jnp.sin(angles) * sign)


def norm_forward(field, gain, shift):
    row_mean = jnp.mean(field, axis=-1, keepdims=True)
    centred = field - row_mean
    variance = jnp.mean(centred * centred, axis=-1, keepdims=True)
    inv_std = lax.rsqrt(variance + eps)
    scaled = centred * inv_std
    return (scaled * gain + shift, scaled, inv_std)


def norm_backward(upstream, scaled, inv_std, gain):
    grad_scaled = upstream * gain
    grad_input = inv_std * (
        grad_scaled
        - jnp.mean(grad_scaled, axis=-1, keepdims=True)
        - scaled * jnp.mean(grad_scaled * scaled, axis=-1, keepdims=True)
    )
    return (grad_input, jnp.sum(upstream * scaled, axis=0), jnp.sum(upstream, axis=0))


BLOCK = 256


def turn_halves(field, sign_sine):
    lane = lax.broadcasted_iota(jnp.int32, field.shape, 1)
    half = HEAD_DIM // 2
    width = field.shape[1]
    swapped = jnp.where(lane % HEAD_DIM < half, pltpu.roll(field, width - half, 1), pltpu.roll(field, half, 1))
    return swapped * sign_sine


def scores_of(keys, queries):
    return lax.dot_general(keys, queries, (((1,), (1,)), ((), ())), preferred_element_type=f32)


def attend_kernel(group, lo_ref, hi_ref, tok_ref, w_ref, b_ref, cos_ref, sin_ref, seg_ref, mixed_ref, q_ref, k_ref, v_ref,
                  lse_ref, vt_ref, m_ref, l_ref, acc_ref):
    zsize, _, rows, _ = tok_ref.shape
    length = zsize * rows
    heads = q_ref.shape[1]
    pair = 2 * HEAD_DIM
    scale = HEAD_DIM ** (-0.5)

    def project(i, carry):
        at = pl.ds(pl.multiple_of(i * rows, rows), rows)
        x = tok_ref[i, 0]
        lane = lax.broadcasted_iota(jnp.int32, (rows, pair), 1)
        low = lane < HEAD_DIM
        doc = lax.broadcasted_iota(jnp.int32, (pair, rows), 0) - HEAD_DIM
        extra_q = jnp.where(doc == seg_ref[group:group + 1, at], 1.0, 0.0).T
        extra_k = jnp.where(lane < HEAD_DIM + 4, (extra_q - 1.0) * 1e9, 0.0)
        cosine = cos_ref[0, at, :]
        sine = sin_ref[0, at, :]
        for c in range(3):
            field = jnp.dot(x, w_ref[c], preferred_element_type=f32) + b_ref[c:c + 1, :]
            for j in range(heads // 2):
                part = field[:, j * pair:(j + 1) * pair]
                if c < 2:
                    part = part * cosine + turn_halves(part, sine)
                if c == 0:
                    part = part * scale
                for h in range(2):
                    one = part if h == 0 else pltpu.roll(part, HEAD_DIM, 1)
                    head = 2 * j + h
                    if c == 0:
                        q_ref[0, head, at, :] = jnp.where(low, one, extra_q).astype(bf16)
                    elif c == 1:
                        k_ref[0, head, at, :] = jnp.where(low, one, extra_k).astype(bf16)
                    else:
                        one = jnp.where(low, one, 0.0)
                        v_ref[0, head, at, :] = one.astype(bf16)
                        vt_ref[head, :, at] = one.T[:HEAD_DIM].astype(bf16)
        return carry

    lax.fori_loop(0, zsize, project, 0)

    def query_block(i, carry):
        at = pl.ds(pl.multiple_of(i * BLOCK, BLOCK), BLOCK)
        m_ref[...] = jnp.full(m_ref.shape, -1e30, f32)
        l_ref[...] = jnp.zeros(l_ref.shape, f32)
        acc_ref[...] = jnp.zeros(acc_ref.shape, f32)

        def key_block(j, carry):
            keys_at = pl.ds(pl.multiple_of(j * BLOCK, BLOCK), BLOCK)
            st = [scores_of(k_ref[0, h, keys_at, :], q_ref[0, h, at, :]) for h in range(heads)]
            peak = m_ref[...]
            new = jnp.maximum(peak, jnp.concatenate([jnp.max(t, axis=0, keepdims=True) for t in st], axis=0))
            p = [jnp.exp(st[h] - new[h:h + 1, :]) for h in range(heads)]
            old = jnp.exp(peak - new)
            m_ref[...] = new
            l_ref[...] = l_ref[...] * old + jnp.concatenate([jnp.sum(t, axis=0, keepdims=True) for t in p], axis=0)
            part = [
                jnp.dot(vt_ref[h, :, keys_at], p[h].astype(bf16), preferred_element_type=f32) for h in range(heads)
            ]
            for h in range(heads):
                acc_ref[h] = acc_ref[h] * old[h:h + 1, :] + part[h]
            return carry

        lax.fori_loop(lo_ref[group, i], hi_ref[group, i], key_block, 0)
        out = [acc_ref[h] / l_ref[h:h + 1, :] for h in range(heads)]
        for j in range(heads // 2):
            both = jnp.concatenate([out[2 * j], out[2 * j + 1]], axis=0)
            mixed_ref[0, at, j * pair:(j + 1) * pair] = both.T.astype(bf16)
        lse_ref[0, :, at] = m_ref[...] + jnp.log(l_ref[...])
        return carry

    lax.fori_loop(0, length // BLOCK, query_block, 0)


def attend_forward(group, bounds, tokens, weight, bias, cosine, sine, docs):
    zsize, _, rows, width = tokens.shape
    length = zsize * rows
    cols = weight.shape[2]
    heads = cols // HEAD_DIM
    pair = 2 * HEAD_DIM
    whole = lambda shape: pl.BlockSpec(shape, lambda i, *_: (0,) * len(shape))
    of_group = lambda shape: pl.BlockSpec(shape, lambda i, *_: (group,) + (0,) * (len(shape) - 1))
    like = jax.ShapeDtypeStruct
    return pl.pallas_call(
        functools.partial(attend_kernel, group),
        grid_spec=pltpu.PrefetchScalarGridSpec(
            num_scalar_prefetch=2,
            grid=(1,),
            in_specs=[
                pl.BlockSpec((zsize, 1, rows, width), lambda i, *_: (0, group, 0, 0)),
                whole(weight.shape), whole(bias.shape),
                of_group((1, length, pair)), of_group((1, length, pair)), whole(docs.shape),
            ],
            out_specs=[
                whole((1, length, cols)),
                whole((1, heads, length, pair)), whole((1, heads, length, pair)), whole((1, heads, length, pair)),
                whole((1, heads, length)),
            ],
            scratch_shapes=[
                pltpu.VMEM((heads, HEAD_DIM, length), bf16),
                pltpu.VMEM((heads, BLOCK), f32), pltpu.VMEM((heads, BLOCK), f32),
                pltpu.VMEM((heads, HEAD_DIM, BLOCK), f32),
            ],
        ),
        out_shape=[
            like((1, length, cols), bf16),
            like((1, heads, length, pair), bf16), like((1, heads, length, pair), bf16),
            like((1, heads, length, pair), bf16), like((1, heads, length), f32),
        ],
        compiler_params=pltpu.CompilerParams(vmem_limit_bytes=VMEM),
        cost_estimate=pl.CostEstimate(
            flops=2 * length * width * 3 * cols + 4 * length * length * cols,
            bytes_accessed=2 * length * width + 6 * width * cols + 8 * length * cols,
            transcendentals=length * length * heads,
        ),
    )(*bounds, tokens, weight, bias, cosine, sine, docs)


def attend_back_kernel(group, last, lo_ref, hi_ref, z_ref, q_ref, k_ref, v_ref, lse_ref, mixed_ref, cos_ref, sin_ref, tok_hbm, w_hbm, *refs):
    zsize, _, rows, _ = tok_hbm.shape
    do_refs, refs = refs[:zsize], refs[zsize:]
    if group:
        before_hbm, refs = refs[0], refs[1:]
    back_ref, wgrad_ref, sum_ref, grad_ref, wsum_ref, dox_ref, kt_ref, delta_ref, dk_ref, dv_ref, dqt_ref, tok_ref, w_ref, sem = refs
    late = [
        pltpu.make_async_copy(tok_hbm.at[:, group], tok_ref, sem.at[0]), pltpu.make_async_copy(w_hbm, w_ref, sem.at[1]),
    ]
    if group:
        late.append(pltpu.make_async_copy(before_hbm, wsum_ref, sem.at[2]))
    for copy in late:
        copy.start()
    heads, length = q_ref.shape[1], q_ref.shape[2]
    pair = 2 * HEAD_DIM
    scale = HEAD_DIM ** (-0.5)
    blocks = length // BLOCK

    low_half = lax.broadcasted_iota(jnp.int32, (rows, pair), 1) < HEAD_DIM
    for step in range(zsize):
        at = pl.ds(pl.multiple_of(lax.rem(z_ref[0] + zsize - step, zsize) * rows, rows), rows)
        for j in range(heads // 2):
            upstream = do_refs[step][0, :, j * pair:(j + 1) * pair].astype(f32)
            product = (upstream * mixed_ref[0, at, j * pair:(j + 1) * pair].astype(f32)).T
            for h in range(2):
                head = 2 * j + h
                one = upstream if h == 0 else pltpu.roll(upstream, HEAD_DIM, 1)
                dox_ref[head, at, :] = jnp.where(low_half, one, 0.0).astype(bf16)
                delta_ref[head:head + 1, at] = jnp.sum(
                    product[h * HEAD_DIM:(h + 1) * HEAD_DIM], axis=0, keepdims=True
                )
                kt_ref[head, :, at] = k_ref[0, head, at, :].astype(f32).T[:HEAD_DIM].astype(bf16)
                dk_ref[head, at, :] = jnp.zeros((rows, pair), f32)
                dv_ref[head, at, :] = jnp.zeros((rows, pair), f32)

    sum_ref[...] = jnp.zeros(sum_ref.shape, f32)
    if not group:
        wsum_ref[...] = jnp.zeros(wsum_ref.shape, f32)

    def put(c, j, at, field):
        low = field.astype(bf16)
        grad_ref[c, at, j * pair:(j + 1) * pair] = low
        cols = pl.ds(j * pair, pair)
        sum_ref[c:c + 1, cols] = sum_ref[c:c + 1, cols] + jnp.sum(low.astype(f32), axis=0, keepdims=True)

    def back(field, at):
        return field * cos_ref[0, at, :] - turn_halves(field, sin_ref[0, at, :])

    def query_block(i, carry):
        at = pl.ds(pl.multiple_of(i * BLOCK, BLOCK), BLOCK)
        dqt_ref[...] = jnp.zeros(dqt_ref.shape, f32)

        def key_block(j, carry):
            keys_at = pl.ds(pl.multiple_of(j * BLOCK, BLOCK), BLOCK)
            every = range(heads)
            queries = [q_ref[0, h, at, :] for h in every]
            upstream = [dox_ref[h, at, :] for h in every]
            st = [scores_of(k_ref[0, h, keys_at, :], queries[h]) for h in every]
            dp = [scores_of(v_ref[0, h, keys_at, :], upstream[h]) for h in every]
            p = [jnp.exp(st[h] - lse_ref[0, h:h + 1, at]) for h in every]
            ds = [(p[h] * (dp[h] - delta_ref[h:h + 1, at])).astype(bf16) for h in every]
            dv = [jnp.dot(p[h].astype(bf16), upstream[h], preferred_element_type=f32) for h in every]
            dk = [jnp.dot(ds[h], queries[h], preferred_element_type=f32) for h in every]
            dq = [jnp.dot(kt_ref[h, :, keys_at], ds[h], preferred_element_type=f32) for h in every]
            for h in every:
                dv_ref[h, keys_at, :] = dv_ref[h, keys_at, :] + dv[h]
                dk_ref[h, keys_at, :] = dk_ref[h, keys_at, :] + dk[h]
                dqt_ref[h] = dqt_ref[h] + dq[h]
            return carry

        lax.fori_loop(lo_ref[group, i], hi_ref[group, i], key_block, 0)
        for j in range(heads // 2):
            both = jnp.concatenate([dqt_ref[2 * j], dqt_ref[2 * j + 1]], axis=0)
            put(0, j, at, back(both.T * scale, at))
        return carry

    lax.fori_loop(0, blocks, query_block, 0)

    def finish(i, carry):
        at = pl.ds(pl.multiple_of(i * BLOCK, BLOCK), BLOCK)
        low = lax.broadcasted_iota(jnp.int32, (BLOCK, pair), 1) < HEAD_DIM
        for j in range(heads // 2):
            field = jnp.where(low, dk_ref[2 * j, at, :], pltpu.roll(dk_ref[2 * j + 1, at, :], HEAD_DIM, 1))
            put(1, j, at, back(field, at))
            field = jnp.where(low, dv_ref[2 * j, at, :], pltpu.roll(dv_ref[2 * j + 1, at, :], HEAD_DIM, 1))
            put(2, j, at, field)
        return carry

    lax.fori_loop(0, blocks, finish, 0)

    def onward(slot, carry):
        i = slot if last else lax.rem(z_ref[0] + slot, zsize)
        at = pl.ds(pl.multiple_of(i * rows, rows), rows)
        total = None
        x = tok_ref[i]
        for c in range(3):
            grad = grad_ref[c, at, :]
            part = lax.dot_general(grad, w_ref[c], (((1,), (1,)), ((), ())), preferred_element_type=f32)
            total = part if total is None else total + part
            wsum_ref[c] += lax.dot_general(x, grad, (((0,), (0,)), ((), ())), preferred_element_type=f32)
        back_ref[0, slot] = total.astype(bf16)
        return carry

    for copy in late:
        copy.wait()
    lax.fori_loop(0, zsize, onward, 0)
    wgrad_ref[...] = wsum_ref[...].astype(wgrad_ref.dtype)


def attend_backward(group, before, bounds, zi, kept, mixed, upstream, cosine, sine, tokens, weight):
    queries, keys, values, lse = kept
    _, heads, length, pair = queries.shape
    zsize, groups, rows, width = tokens.shape
    cols = heads * HEAD_DIM
    last = group == groups - 1
    whole = lambda shape: pl.BlockSpec(shape, lambda i, *_: (0,) * len(shape))
    of_group = lambda shape: pl.BlockSpec(shape, lambda i, *_: (group,) + (0,) * (len(shape) - 1))
    like = jax.ShapeDtypeStruct
    wide = (heads, length, pair)
    return pl.pallas_call(
        functools.partial(attend_back_kernel, group, last),
        grid_spec=pltpu.PrefetchScalarGridSpec(
            num_scalar_prefetch=3,
            grid=(1,),
            in_specs=[whole((1,) + wide)] * 3 + [
                whole((1, heads, length)), whole((1, length, cols)),
                of_group((1, length, pair)), of_group((1, length, pair)),
                HBM, HBM,
            ] + [whole((1, rows, cols))] * zsize + [HBM] * (group > 0),
            out_specs=[whole((1, zsize, rows, width)), whole(weight.shape), whole((8, cols))],
            scratch_shapes=[
                pltpu.VMEM((3, length, cols), bf16), pltpu.VMEM(weight.shape, f32),
                pltpu.VMEM(wide, bf16), pltpu.VMEM((heads, HEAD_DIM, length), bf16), pltpu.VMEM((heads, length), f32),
                pltpu.VMEM(wide, f32), pltpu.VMEM(wide, f32), pltpu.VMEM((heads, HEAD_DIM, BLOCK), f32),
                pltpu.VMEM((zsize, rows, width), bf16), pltpu.VMEM(weight.shape, bf16), pltpu.SemaphoreType.DMA((3,)),
            ],
        ),
        out_shape=[
            like((1, zsize, rows, width), bf16), like(weight.shape, bf16 if last else f32), like((8, cols), f32),
        ],
        compiler_params=pltpu.CompilerParams(vmem_limit_bytes=VMEM),
        cost_estimate=pl.CostEstimate(
            flops=0 if last else 40 * length * length * cols,
            bytes_accessed=0 if last else 48 * length * cols,
            transcendentals=0 if last else 2 * length * length * heads,
        ),
    )(*bounds, zi.reshape(1), queries, keys, values, lse, mixed, cosine, sine, tokens, weight, *upstream,
      *([before] if group else []))


MESH_ID = pl.DeviceIdType.MESH
HBM = pl.BlockSpec(memory_space=pl.ANY)


def other(axis):
    return {axis: 1 - lax.axis_index(axis)}


def greet(zsize):
    z = lax.axis_index("z")
    barrier = pltpu.get_barrier_semaphore()
    for axis in CELL:
        pl.semaphore_signal(barrier, inc=1, device_id=other(axis), device_id_type=MESH_ID)

    @pl.when(z > 0)
    def _():
        pl.semaphore_signal(barrier, inc=1, device_id={"z": z - 1}, device_id_type=MESH_ID)

    @pl.when(z < zsize - 1)
    def _():
        pl.semaphore_signal(barrier, inc=1, device_id={"z": z + 1}, device_id_type=MESH_ID)

    peers = len(CELL) + jnp.where(z > 0, 1, 0) + jnp.where(z < zsize - 1, 1, 0)
    pl.semaphore_wait(barrier, peers)


def remote(src, dst, send_sem, recv_sem, device):
    return pltpu.make_async_remote_copy(
        src_ref=src, dst_ref=dst, send_sem=send_sem, recv_sem=recv_sem, device_id=device, device_id_type=MESH_ID
    )


ORDERS = {"xy": ("x", "y"), "yx": ("y", "x")}


def gather_kernel(zsize, orders, *refs):
    n = len(orders)
    tok, bias, shards = refs[0], refs[1], refs[2:2 + n]
    tok_all, bias_all, wholes = refs[2 + n], refs[3 + n], refs[4 + n:4 + 2 * n]
    held = refs[4 + 2 * n:6 + 3 * n]
    local_sem, z_send, z_recv, p_send, p_recv = refs[6 + 3 * n:]
    z = lax.axis_index("z")
    c = lax.axis_index("core")
    place = [(lax.axis_index(o[0]), lax.axis_index(o[1])) for o in orders]

    sources = list(shards) + [tok, bias]
    targets = list(wholes) + [tok_all, bias_all]
    into = [pltpu.make_async_copy(sources[i], held[i], local_sem.at[0, i]) for i in range(n + 2)]
    local = [pltpu.make_async_copy(held[i], targets[i].at[z], local_sem.at[1, i]) for i in range(n + 2)]
    for copy in into:
        copy.start()
    greet(zsize)

    def line(item, src, step, side):
        to = z + 1 if side == 0 else z - 1
        if item < n:
            f, s = place[item]
            own = shards[item].at[c, f, s]
            dst = wholes[item].at[src, c, f, s]
        else:
            own = (tok, bias)[item - n]
            dst = (tok_all, bias_all)[item - n].at[src]
        return remote(
            own if step == 0 else dst, dst, z_send.at[side, item, step], z_recv.at[side, item, step], {"z": to}
        )

    def exchange(k, src, stage, slot):
        f, s = place[k]
        whole = wholes[k]
        ref = (whole.at[src, c, f, s], whole.at[src, c, f], whole.at[src, c])[stage]
        axis = (orders[k][1], orders[k][0], "core")[stage]
        return remote(ref, ref, p_send.at[slot, k, stage], p_recv.at[slot, k, stage], other(axis))

    def valid_from(side, step):
        return z - step - 1 >= 0 if side == 0 else z + step + 1 < zsize

    def source(side, step):
        return z - step - 1 if side == 0 else z + step + 1

    def has_next(side):
        return z < zsize - 1 if side == 0 else z > 0

    for side in range(2):

        @pl.when(has_next(side))
        def _():
            for item in range(n):
                line(item, z, 0, side).start()

    def stage_on(stage, step):
        for side in range(2):

            @pl.when(valid_from(side, step))
            def _():
                src = source(side, step)
                slot = side * (zsize - 1) + step
                for k in range(n):
                    exchange(k, src, stage - 1, slot).wait_recv()
                    if stage < 3:
                        exchange(k, src, stage, slot).start()

    def arrive(items, step):
        for side in range(2):

            @pl.when(valid_from(side, step))
            def _():
                src = source(side, step)
                for item in items:
                    line(item, src, step, side).wait_recv()
                    if step + 1 < zsize - 1:

                        @pl.when(has_next(side))
                        def _():
                            line(item, src, step + 1, side).start()

                    if item < n:
                        exchange(item, src, 0, side * (zsize - 1) + step).start()

    for copy, onward in zip(into, local):
        copy.wait()
        onward.start()
    for step in range(zsize - 1):
        arrive(range(n), step)
        if step == zsize - 2:
            for side in range(2):

                @pl.when(has_next(side))
                def _():
                    for item in range(n, n + 2):
                        line(item, z, 0, side).start()

        if step >= 1:
            stage_on(1, step - 1)
    for step in range(zsize - 1):
        if step == 0:
            stage_on(1, zsize - 2)
        stage_on(2, step)
        arrive(range(n, n + 2), step)
    for step in range(zsize - 1):
        stage_on(3, step)
    for copy in local:
        copy.wait()
    for side in range(2):

        @pl.when(has_next(side))
        def _():
            for item in range(n + 2):
                line(item, z, 0, side).wait_send()

        for step in range(zsize - 1):

            @pl.when(valid_from(side, step))
            def _():
                src = source(side, step)
                if step + 1 < zsize - 1:

                    @pl.when(has_next(side))
                    def _():
                        for item in range(n + 2):
                            line(item, src, step + 1, side).wait_send()

                for k in range(n):
                    for stage in range(3):
                        exchange(k, src, stage, side * (zsize - 1) + step).wait_send()


def gather_start(tokens, bias, weights, zsize):
    orders = [ORDERS[o] for o, _ in weights]
    shards = [w for _, w in weights]
    n = len(shards)
    stack = lambda a: jax.ShapeDtypeStruct((zsize,) + a.shape, a.dtype)
    return pl.pallas_call(
        functools.partial(gather_kernel, zsize, orders),
        out_shape=[stack(tokens), stack(bias)] + [stack(w) for w in shards],
        in_specs=[HBM] * (n + 2),
        out_specs=[HBM] * (n + 2),
        scratch_shapes=[pltpu.VMEM(a.shape, a.dtype) for a in shards + [tokens, bias]] + [
            pltpu.SemaphoreType.DMA((2, n + 2)),
            pltpu.SemaphoreType.DMA((2, n + 2, zsize - 1)),
            pltpu.SemaphoreType.DMA((2, n + 2, zsize - 1)),
            pltpu.SemaphoreType.DMA((2 * (zsize - 1), n, 3)),
            pltpu.SemaphoreType.DMA((2 * (zsize - 1), n, 3)),
        ],
        compiler_params=pltpu.CompilerParams(
            collective_id=0, has_side_effects=True, vmem_limit_bytes=VMEM
        ),
    )(tokens, bias, *shards)


def add_rows(dst, src):
    rows = dst.shape[0]
    step = math.gcd(rows, 64)

    def body(i, carry):
        at = pl.ds(pl.multiple_of(i * step, step), step)
        dst[at, :] = dst[at, :] + src[at, :]
        return carry

    lax.fori_loop(0, rows // step, body, 0)


def reduce_kernel(zsize, orders, w, *refs):
    n = 3
    p = len(orders) - n
    items = n + p
    pieces, came, refs = refs[:p], refs[p:2 * p], refs[2 * p:]
    parts, backs, small = refs[:n], refs[n], refs[n + 1]
    pos = n + 2
    piece_out, part_out, back_out = refs[pos:pos + p], refs[pos + p:pos + p + n], refs[pos + p + n]
    small_out = refs[pos + p + n + 1]
    outs = list(part_out) + list(piece_out)
    pos += p + n + 2
    mine = refs[pos:pos + items + w]
    pos += items + w
    got_c, got_1, got_2 = refs[pos:pos + n], refs[pos + n:pos + n + items], refs[pos + n + items:pos + n + 2 * items]
    pos += n + 2 * items
    lines = [0] + list(range(n, items + w))
    line_backs = list(range(items, items + w))
    got_z = dict(zip(lines, refs[pos:pos + len(lines)]))
    pos += len(lines)
    small_mine, small_got, small_line, small_total, part_line, part_total = refs[pos:pos + 6]
    (local_sem, send, recv, z_send, z_recv, s_send, s_recv, t_send, t_recv, g_send, g_recv, end_sem) = refs[pos + 6:]
    z = lax.axis_index("z")
    c = lax.axis_index("core")
    orders = orders[p:] + orders[:p]
    place = [(lax.axis_index(o[0]), lax.axis_index(o[1])) for o in orders]
    turn = []
    for i in range(zsize // 2):
        turn += [i, zsize - 1 - i]
    few = parts[1].shape[0]
    steps = [(1, b) for b in range(few)] + [(2, 0)] + [(0, b) for b in turn]

    def load(k, b):
        src = parts[k].at[b, c] if k < n else pieces[k - n].at[b] if k < items else backs.at[k - items, b]
        return pltpu.make_async_copy(src, mine[k].at[b], local_sem.at[k, b])

    def load_came(k, b):
        return pltpu.make_async_copy(came[k - n].at[b], got_1[k].at[b], local_sem.at[items + w + 1 + k - n, b])

    load_small = pltpu.make_async_copy(small, small_mine.at[0], local_sem.at[items + w, 0])

    def half(k, b, stage):
        f, s = place[k]
        if stage == 0:
            src, dst, axis = parts[k].at[b, 1 - c], got_c[k].at[b], "core"
        elif stage == 1:
            src, dst, axis = mine[k].at[b, 1 - f], got_1[k].at[b], orders[k][0]
        else:
            held = mine[k].at[b, f] if k < n else mine[k].at[b]
            src, dst, axis = held.at[1 - s], got_2[k].at[b], orders[k][1]
        return remote(src, dst, send.at[stage, k, b], recv.at[stage, k, b], other(axis))

    def own(k, b):
        if k >= items:
            return mine[k].at[b]
        f, s = place[k]
        return mine[k].at[b, s] if k >= n else mine[k].at[b, f, s]

    def hop(k, b, side):
        to = z + 1 if side == 0 else z - 1
        at = b if side == 0 else jnp.where(b == z - 1, zsize, b)
        return remote(own(k, b), got_z[k].at[at], z_send.at[k, b], z_recv.at[k, at], {"z": to})

    def take(k, b, side):
        at = b if side == 0 else jnp.where(b == z, zsize, b)
        ref = got_z[k].at[at]
        sender = z - 1 if side == 0 else z + 1
        remote(own(k, b), ref, z_send.at[k, b], z_recv.at[k, at], {"z": sender}).wait_recv()
        add_rows(own(k, b), ref)

    def line_start(ks, messages):
        for side in range(2):

            @pl.when(z == (0 if side == 0 else zsize - 1))
            def _():
                for i in messages:
                    for k in ks:
                        hop(k, zsize - 1 - i if side == 0 else i, side).start()

    def line_slot(ks, slot):
        for i in range(slot):
            for side in range(2):
                b = zsize - 1 - i if side == 0 else i

                @pl.when(z == (slot - i if side == 0 else zsize - 1 - slot + i))
                def _():
                    for k in ks:
                        take(k, b, side)

                        @pl.when(z < b if side == 0 else z > b)
                        def _():
                            hop(k, b, side).start()

    def small_swap(stage):
        return remote(
            small_mine.at[stage], small_got.at[stage], s_send.at[stage], s_recv.at[stage], other(CELL[stage])
        )

    def small_step(stage):
        small_swap(stage).wait_recv()
        small_mine[stage + 1] = small_mine[stage] + small_got[stage]
        if stage < 2:
            small_swap(stage + 1).start()

    last = len(CELL)
    last_part = own(2, 0)

    def total_copy(item, way):
        line, total = ((small_line, small_total), (part_line, part_total))[item]
        src = (small_mine.at[last], last_part)[item] if way == 0 else total
        dst = line if way == 0 else total
        to = z + 1 if way == 0 else z - 1
        return remote(src, dst, t_send.at[item, way], t_recv.at[item, way], {"z": to})

    def total_step(tick):
        if 0 <= tick < zsize:

            @pl.when(z == tick)
            def _():
                if tick > 0:
                    for item in range(2):
                        total_copy(item, 0).wait_recv()
                    small_mine[last] = small_mine[last] + small_line[...]
                    add_rows(last_part, part_line)
                if tick < zsize - 1:
                    for item in range(2):
                        total_copy(item, 0).start()
                else:
                    small_total[...] = small_mine[last]
                    part_total[...] = last_part[...]

        back_tick = tick - (zsize - 1)
        if 0 <= back_tick < zsize:

            @pl.when(z == zsize - 1 - back_tick)
            def _():
                if back_tick > 0:
                    for item in range(2):
                        total_copy(item, 1).wait_recv()
                if back_tick < zsize - 1:
                    for item in range(2):
                        total_copy(item, 1).start()

    line_pieces = list(range(n, items))
    piece_steps = [(k, b) for b in turn for k in line_pieces]
    for b in turn:
        for k in line_backs:
            load(k, b).start()
    for k, b in piece_steps:
        load(k, b).start()
        load_came(k, b).start()
    for k, b in steps:
        load(k, b).start()
    load_small.start()
    greet(zsize)
    for k, b in steps:
        half(k, b, 0).start()
    for b in turn:
        for k in line_backs:
            load(k, b).wait()
    line_start(line_backs, [0])
    load_small.wait()
    small_swap(0).start()

    def stage_1(k, b):
        f, s = place[k]
        load(k, b).wait()
        half(k, b, 0).wait_recv()
        for i in range(2):
            add_rows(mine[k].at[b, 1 - f, i], got_c[k].at[b, 1 - f, i])
        half(k, b, 1).start()
        for i in range(2):
            add_rows(mine[k].at[b, f, i], got_c[k].at[b, f, i])

    def stage_2(k, b):
        f, s = place[k]
        held = mine[k].at[b, f] if k < n else mine[k].at[b]
        if k < n:
            half(k, b, 1).wait_recv()
        else:
            load(k, b).wait()
            load_came(k, b).wait()
        add_rows(held.at[1 - s], got_1[k].at[b, 1 - s])
        half(k, b, 2).start()
        add_rows(held.at[s], got_1[k].at[b, s])

    def stage_3(k, b):
        half(k, b, 2).wait_recv()
        add_rows(own(k, b), got_2[k].at[b])

    def result(k, b):
        return part_total if k == 2 else own(k, b)

    def out_of(k, b):
        return outs[k].at[b] if k == 1 else outs[k]

    def put(k, b, slot):
        f, s = place[k]
        return pltpu.make_async_copy(result(k, b), out_of(k, b).at[c, f, s], end_sem.at[slot])

    def spread(k, b, stage, slot):
        f, s = place[k]
        out = out_of(k, b)
        dst = (out.at[c, f, s], out.at[c, f], out.at[c])[stage]
        src = result(k, b) if stage == 0 else dst
        axis = (orders[k][1], orders[k][0], "core")[stage]
        return remote(src, dst, g_send.at[slot, stage], g_recv.at[slot, stage], other(axis))

    spreads = [
        [(1, b, b) for b in range(few)],
        [(k, z, few + k - n) for k in line_pieces],
        [(0, z, few + p), (2, 0, few + p + 1)],
    ]

    def spread_step(group, stage):
        for k, b, slot in spreads[group]:
            if stage == 0:
                spread(k, b, 0, slot).start()
                put(k, b, slot).start()
                continue
            if stage == 1:
                put(k, b, slot).wait()
            spread(k, b, stage - 1, slot).wait_recv()
            if stage < 3:
                spread(k, b, stage, slot).start()

    def sent(ks):
        for b in range(zsize):

            @pl.when(z != b)
            def _():
                for k in ks:
                    hop(k, b, 0).wait_send()

    at_end = jnp.logical_or(z == 0, z == zsize - 1)
    for k, b in piece_steps:
        stage_2(k, b)
    for k, b in steps:
        stage_1(k, b)
    small_step(0)
    for b in turn:
        for k in line_pieces:
            stage_3(k, b)
        for side in range(2):

            @pl.when(jnp.logical_and(z == (0 if side == 0 else zsize - 1), z != b))
            def _():
                for k in line_pieces:
                    hop(k, b, side).start()

    for k, b in steps:
        stage_2(k, b)
    small_step(1)
    line_slot(line_backs, 1)
    for k, b in steps:
        stage_3(k, b)
    small_step(2)
    spread_step(0, 0)
    line_start([0], range(zsize - 1))
    total_step(0)

    @pl.when(at_end)
    def _():
        sent(line_pieces)

    line_start(line_backs, range(1, zsize - 1))
    ticks = list(range(1, 2 * zsize - 1))
    later = [(0, 1), (0, 2), (0, 3)]

    def fill(group_stages, count):
        for _ in range(count):
            if group_stages:
                spread_step(*group_stages.pop(0))

    for slot in range(1, zsize):
        line_slot(line_pieces, slot)
        total_step(ticks.pop(0))
        fill(later, 1)
        if slot >= 2:
            line_slot([0], slot - 1)
    fill(later, 3)
    spread_step(1, 0)
    later = [(1, 1), (1, 2), (1, 3)]
    total_step(ticks.pop(0))
    line_slot([0], zsize - 1)
    for slot in range(2, zsize - 1):
        line_slot(line_backs, slot)
        fill(later, 1)
    for tick in ticks:
        total_step(tick)
    spread_step(2, 0)
    fill(later, 1)
    spread_step(2, 1)
    fill(later, 1)
    spread_step(2, 2)
    fill(later, 3)
    line_slot(line_backs, zsize - 1)
    finish_back = [
        pltpu.make_async_copy(mine[k].at[z], back_out.at[k - items], local_sem.at[k, 0]) for k in line_backs
    ]
    for copy in finish_back:
        copy.start()
    finish_small = pltpu.make_async_copy(small_total, small_out, local_sem.at[items + w, 0])
    finish_small.start()
    spread_step(2, 3)
    for copy in finish_back:
        copy.wait()
    finish_small.wait()
    sent([0] + line_backs)

    @pl.when(jnp.logical_not(at_end))
    def _():
        sent(line_pieces)

    for way in range(2):

        @pl.when(z < zsize - 1 if way == 0 else z > 0)
        def _():
            for item in range(2):
                total_copy(item, way).wait_send()

    for k, b in steps:
        for stage in range(3):
            half(k, b, stage).wait_send()
    for k, b in piece_steps:
        half(k, b, 2).wait_send()
    for stage in range(3):
        small_swap(stage).wait_send()
    for group in spreads:
        for k, b, slot in group:
            for stage in range(3):
                spread(k, b, stage, slot).wait_send()


def reduce_end(pieces, parts, backs, small, zsize):
    orders = [ORDERS[o[0]] for o in pieces + parts]
    piece_arrays = [a for _, a, _ in pieces]
    came = [a for _, _, a in pieces]
    arrays = [a for _, a in parts]
    p, n, w = len(pieces), len(parts), backs.shape[0]
    shapes = [a.shape for a in arrays]
    like = jax.ShapeDtypeStruct
    outs = [like((2, 2, 2) + a.shape[2:], bf16) for a in piece_arrays]
    outs += [like(s if i == 1 else s[1:], bf16) for i, s in enumerate(shapes)]
    outs += [like((w,) + backs.shape[2:], bf16), like(small.shape, f32)]
    held = lambda shape: pltpu.VMEM(shape, bf16)
    scratch = [held((s[0],) + s[2:]) for s in shapes]
    scratch += [held(a.shape) for a in piece_arrays] + [held(backs.shape[1:])] * w
    scratch += [held((s[0],) + s[2:]) for s in shapes]
    scratch += [held((s[0],) + s[3:]) for s in shapes] + [held(a.shape) for a in piece_arrays]
    scratch += [held((s[0],) + s[4:]) for s in shapes] + [held(a.shape[:1] + a.shape[2:]) for a in piece_arrays]
    scratch += [held((zsize + 1,) + shapes[0][4:])]
    scratch += [held((zsize + 1,) + a.shape[2:]) for a in piece_arrays] + [held((zsize + 1,) + backs.shape[2:])] * w
    scratch += [pltpu.VMEM((4,) + small.shape, f32), pltpu.VMEM((3,) + small.shape, f32)]
    scratch += [pltpu.VMEM(small.shape, f32)] * 2 + [held(shapes[2][4:])] * 2
    dma = pltpu.SemaphoreType.DMA
    most = max(zsize, shapes[1][0])
    ends = shapes[1][0] + p + 2
    scratch += [
        dma((n + 2 * p + w + 1, most)), dma((3, n + p, most)), dma((3, n + p, most)),
        dma((n + p + w, zsize)), dma((n + p + w, zsize + 1)),
        dma((3,)), dma((3,)), dma((2, 2)), dma((2, 2)), dma((ends, 3)), dma((ends, 3)), dma((ends,)),
    ]
    return pl.pallas_call(
        functools.partial(reduce_kernel, zsize, orders, w),
        out_shape=outs,
        in_specs=[HBM] * (n + 2 * p + 2),
        out_specs=[HBM] * (n + p + 2),
        scratch_shapes=scratch,
        compiler_params=pltpu.CompilerParams(
            collective_id=1, has_side_effects=True, vmem_limit_bytes=VMEM
        ),
    )(*piece_arrays, *came, *arrays, backs, small)


def gelu_pair(v):
    size = jnp.abs(v)
    t = 1.0 / (1.0 + (0.3275911 * 0.5 ** 0.5) * size)
    bell = jnp.exp(-0.5 * (v * v))
    poly = t * (0.254829592 + t * (-0.284496736 + t * (1.421413741 + t * (-1.453152027 + t * 1.061405429))))
    tail = 0.5 * poly * bell
    cdf = jnp.where(v >= 0.0, 1.0 - tail, tail)
    return v * cdf, cdf + v * (bell * (1.0 / (2.0 * math.pi) ** 0.5))


def norm_rows(field):
    mean = jnp.mean(field, axis=-1, keepdims=True)
    centred = field - mean
    inv_std = lax.rsqrt(jnp.mean(centred * centred, axis=-1, keepdims=True) + eps)
    return centred * inv_std, inv_std


def ffn_kernel(zsize, groups, z_ref, tok_ref, out_ref, out_bias_ref, gain_one_ref, shift_one_ref, up_ref, bias_ref, down_ref,
               down_bias_ref, gain_two_ref, shift_two_ref, proj_ref, dy_ref, de_ref, *refs):
    pieces = refs[:zsize * groups]
    (active_ref, slope_ref, mixed_ref, x_ref, scaled_ref, inv_ref, result_ref, embed_ref, grad_ref, low_ref, proj_grad_ref,
     vec_ref, normed_ref, sum_ref) = refs[zsize * groups:]
    rows, width = x_ref.shape
    local = rows // groups
    cols = width // zsize
    chunk = 128
    heads = proj_ref.shape[0]

    @pl.when(pl.program_id(0) == 0)
    def _():
        for g in range(groups):
            for step in range(zsize):
                at = lax.rem(z_ref[0] + zsize - step, zsize) * cols
                mixed_ref[pl.ds(g * local, local), pl.ds(pl.multiple_of(at, cols), cols)] = pieces[g * zsize + step][0]
        def first(i, carry):
            at = pl.ds(pl.multiple_of(i * chunk, chunk), chunk)
            attended = jnp.dot(mixed_ref[at, :], out_ref[...], preferred_element_type=f32) + out_bias_ref[...]
            scaled, inv_std = norm_rows(tok_ref[at, :].astype(f32) + attended)
            normed = scaled * gain_one_ref[...] + shift_one_ref[...]
            scaled_ref[at, :] = scaled
            inv_ref[at, :] = inv_std
            normed_ref[at, :] = normed
            x_ref[at, :] = normed.astype(bf16)
            return carry

        lax.fori_loop(0, rows // chunk, first, 0)
        sum_ref[...] = jnp.zeros(sum_ref.shape, f32)

    parts = [pl.ds(i * chunk, chunk) for i in range(rows // chunk)]
    hidden = [jnp.dot(x_ref[at, :], up_ref[0], preferred_element_type=f32) + bias_ref[0] for at in parts]
    for at, field in zip(parts, hidden):
        active, slope = gelu_pair(field)
        slope_ref[0, at, :] = slope.astype(bf16)
        active_ref[0, :, at] = active.T.astype(bf16)
        sum_ref[at, :] += jnp.dot(active.astype(bf16), down_ref[0], preferred_element_type=f32)

    @pl.when(pl.program_id(0) == pl.num_programs(0) - 1)
    def _():
        vec_ref[...] = jnp.zeros(vec_ref.shape, f32)

        def second(i, carry):
            at = pl.ds(pl.multiple_of(i * chunk, chunk), chunk)
            scaled, inv_std = norm_rows(normed_ref[at, :] + (sum_ref[at, :] + down_bias_ref[...]))
            result_ref[at, :] = (scaled * gain_two_ref[...] + shift_two_ref[...]).astype(bf16)
            g, inner = i // (local // chunk), lax.rem(i, local // chunk)
            upstream = dy_ref[at, :].astype(f32) + lax.dot_general(
                de_ref[g, :, pl.ds(pl.multiple_of(inner * chunk, chunk), chunk)], proj_ref[...], (((0,), (0,)), ((), ())), preferred_element_type=f32
            )
            grad_scaled = upstream * gain_two_ref[...]
            grad = inv_std * (
                grad_scaled
                - jnp.mean(grad_scaled, axis=-1, keepdims=True)
                - scaled * jnp.mean(grad_scaled * scaled, axis=-1, keepdims=True)
            )
            grad_ref[at, :] = grad
            low = grad.astype(bf16)
            low_ref[at, :] = low
            for n, field in enumerate((low.astype(f32), upstream * scaled, upstream)):
                vec_ref[n:n + 1, :] = vec_ref[n:n + 1, :] + jnp.sum(field, axis=0, keepdims=True)
            return carry

        lax.fori_loop(0, rows // chunk, second, 0)
        proj_grad = jnp.zeros((heads, width), f32)
        for g in range(groups):
            result = result_ref[pl.ds(g * local, local), :]
            embed_ref[g] = lax.dot_general(
                proj_ref[...], result, (((1,), (1,)), ((), ())), preferred_element_type=f32
            ).astype(bf16)
            proj_grad = proj_grad + jnp.dot(de_ref[g], result, preferred_element_type=f32)
        proj_grad_ref[...] = jnp.zeros(proj_grad_ref.shape, bf16)
        proj_grad_ref[pl.ds(0, heads), :] = proj_grad.astype(bf16)


def ffn_forward(zi, tokens, pieces, out_all, one, up_all, up_bias, down_all, two, proj, dy, de):
    zsize, width, units = up_all.shape
    rows = tokens.shape[0]
    groups, heads, local = de.shape
    tile = units
    like = jax.ShapeDtypeStruct
    whole = lambda shape: pl.BlockSpec(shape, lambda s, z: (0,) * len(shape))
    tiles = pl.BlockSpec((1, rows, tile), lambda s, z: (s, 0, 0))
    field, row = whole((rows, width)), whole((1, width))
    padded = heads + -heads % 128
    return pl.pallas_call(
        functools.partial(ffn_kernel, zsize, groups),
        grid_spec=pltpu.PrefetchScalarGridSpec(
            num_scalar_prefetch=1,
            grid=(zsize,),
            in_specs=[
                field, whole((width, width)), row, row, row,
                pl.BlockSpec((1, width, tile), lambda s, z: (s, 0, 0)),
                pl.BlockSpec((1, 1, tile), lambda s, z: (s, 0, 0)),
                pl.BlockSpec((1, tile, width), lambda s, z: (s, 0, 0)),
                row, row, row, whole(proj.shape), field, whole(de.shape),
            ] + [whole(p.shape) for p in pieces],
            out_specs=[
                pl.BlockSpec((1, tile, rows), lambda s, z: (s, 0, 0)), tiles,
                field, field, field, whole((rows, 1)), field, whole(de.shape), field, field,
                whole((padded, width)), whole((8, width)),
            ],
            scratch_shapes=[pltpu.VMEM((rows, width), f32), pltpu.VMEM((rows, width), f32)],
        ),
        out_shape=[
            like((zsize, units, rows), bf16), like((zsize, rows, units), bf16), like((rows, width), bf16),
            like((rows, width), bf16), like((rows, width), f32), like((rows, 1), f32), like((rows, width), bf16),
            like(de.shape, bf16), like((rows, width), f32), like((rows, width), bf16), like((padded, width), bf16),
            like((8, width), f32),
        ],
        compiler_params=pltpu.CompilerParams(vmem_limit_bytes=VMEM),
    )(zi.reshape(1), tokens, out_all, *one, up_all, up_bias[:, None, :], down_all, *two, proj, dy, de, *pieces)


def ffn_back_kernel(core_ref, second_ref, normed_ref, up_ref, down_ref, active_ref, slope_ref,
                    give_up_ref, keep_up_ref, give_down_ref, keep_down_ref, back_ref, bias_ref, turned_ref):
    s = pl.program_id(0)
    half = turned_ref.shape[0] // 2
    c = core_ref[0]

    @pl.when(s == 0)
    def _():
        back_ref[...] = jnp.zeros(back_ref.shape, f32)
        turned_ref[...] = normed_ref[...].T

    second = second_ref[...]
    upstream = lax.dot_general(second, down_ref[0], (((1,), (1,)), ((), ())), preferred_element_type=f32)
    grad = (upstream * slope_ref[0].astype(f32)).astype(bf16)
    bias_ref[0] = jnp.sum(grad.astype(f32), axis=0, keepdims=True)
    units = active_ref.shape[1] // 2
    back_ref[...] += lax.dot_general(grad, up_ref[0], (((1,), (1,)), ((), ())), preferred_element_type=f32)
    for who, down_to, up_to in ((1 - c, give_down_ref, give_up_ref), (c, keep_down_ref, keep_up_ref)):
        active = active_ref[0, pl.ds(pl.multiple_of(who * units, units), units), :]
        down_to[0] = jnp.dot(active, second, preferred_element_type=f32).astype(bf16)
        turned = turned_ref[pl.ds(pl.multiple_of(who * half, half), half), :]
        up_to[0] = jnp.dot(turned, grad, preferred_element_type=f32).astype(bf16)


def ffn_backward(core, second_low, normed_low, up_all, down_all, active, slope):
    zsize, width, units = up_all.shape
    rows = normed_low.shape[0]
    like = jax.ShapeDtypeStruct
    whole = pl.BlockSpec((rows, width), lambda s, c: (0, 0))
    tiles = pl.BlockSpec((1, rows, units), lambda s, c: (s, 0, 0))
    up_half = pl.BlockSpec((1, width // 2, units), lambda s, c: (s, 0, 0))
    down_half = pl.BlockSpec((1, units // 2, width), lambda s, c: (s, 0, 0))
    return pl.pallas_call(
        ffn_back_kernel,
        grid_spec=pltpu.PrefetchScalarGridSpec(
            num_scalar_prefetch=1,
            grid=(zsize,),
            in_specs=[
                whole, whole,
                pl.BlockSpec((1, width, units), lambda s, c: (s, 0, 0)),
                pl.BlockSpec((1, units, width), lambda s, c: (s, 0, 0)),
                pl.BlockSpec((1, units, rows), lambda s, c: (s, 0, 0)), tiles,
            ],
            out_specs=[
                up_half, up_half, down_half, down_half, whole,
                pl.BlockSpec((1, 1, units), lambda s, c: (s, 0, 0)),
            ],
            scratch_shapes=[pltpu.VMEM((width, rows), bf16)],
        ),
        out_shape=[
            like((zsize, width // 2, units), bf16), like((zsize, width // 2, units), bf16),
            like((zsize, units // 2, width), bf16), like((zsize, units // 2, width), bf16),
            like((rows, width), f32), like((zsize, 1, units), f32),
        ],
        compiler_params=pltpu.CompilerParams(vmem_limit_bytes=VMEM),
    )(core, second_low, normed_low, up_all, down_all, active, slope)


PAIR = [(0, 1), (1, 0)]


def first_halving(got, keep, order):
    zsize, half, cols = keep.shape
    shape = (zsize, 2, 2, half // 4, cols)
    got, keep = got.reshape(shape), keep.reshape(shape)
    i = lax.axis_index(ORDERS[order][0])
    pick = lambda array, j: lax.dynamic_index_in_dim(array, j, 1, keepdims=False)
    return pick(keep, 1 - i) + pick(got, 1 - i), pick(keep, i) + pick(got, i)


def widen_kernel(counts, up_ref, down_ref, out_ref, qkv_ref, first_ref, *refs):
    parts, (up_o, down_o, out_o, qkv_o, first_o) = refs[:-5], refs[-5:]
    for source, target in ((up_ref, up_o), (down_ref, down_o), (out_ref, out_o), (qkv_ref, qkv_o)):
        target[...] = source[...].astype(f32)
    per_group = pl.num_programs(0) // len(counts)
    for g, count in enumerate(counts):
        own, parts = parts[:count], parts[count:]

        @pl.when(pl.program_id(0) // per_group == g)
        def _():
            total = first_ref[...]
            for part in own:
                total = total + part[...].astype(f32)
            first_o[...] = total


def widen(up, down, out, qkv, first, parts):
    steps = 4
    per_group = steps // len(parts)

    def rows_of(array):
        return pl.BlockSpec((array.shape[0] // steps, array.shape[1]), lambda i: (i, 0))

    def of_group(g):
        block = first.shape[0] // steps
        return pl.BlockSpec((block, first.shape[1]), lambda i: (jnp.clip(i - g * per_group, 0, per_group - 1), 0))

    arrays = [up, down, out]
    specs = [rows_of(a) for a in arrays]
    specs.append(pl.BlockSpec((3, qkv.shape[1] // steps, qkv.shape[2]), lambda i: (0, i, 0)))
    specs.append(rows_of(first))
    return pl.pallas_call(
        functools.partial(widen_kernel, [len(p) for p in parts]),
        grid=(steps,),
        in_specs=specs + [of_group(g) for g, own in enumerate(parts) for _ in own],
        out_specs=specs,
        out_shape=[jax.ShapeDtypeStruct(a.shape, f32) for a in arrays + [qkv, first]],
        compiler_params=pltpu.CompilerParams(vmem_limit_bytes=VMEM),
    )(up, down, out, qkv, first, *[part for own in parts for part in own])


def per_device(blocks, tokens, segments, qkv_weight, qkv_bias, out_weight, out_bias, gain_one, shift_one,
               up_weight, up_bias, down_weight, down_bias, gain_two, shift_two, proj_weight, out_grad, embed_grad):
    groups, local_rows, model_width = tokens.shape
    length = segments.shape[1]
    zsize = length // local_rows
    head_cols = qkv_weight.shape[2]
    units_here = up_weight.shape[1]
    rows = groups * local_rows
    zi = lax.axis_index("z")
    cosine, sine = rotary_tables(doc_positions(segments))
    starts = jnp.sum(segments[:, None, :] < jnp.arange(4, dtype=jnp.int32)[None, :, None], axis=2, dtype=jnp.int32)
    edges = jnp.arange(length // BLOCK, dtype=jnp.int32)[None, :, None] * BLOCK
    bounds = (
        jnp.max(jnp.where(starts[:, None, :] <= edges, starts[:, None, :], 0), axis=2) // BLOCK,
        (jnp.min(jnp.where(starts[:, None, :] >= edges + BLOCK, starts[:, None, :], length), axis=2) + BLOCK - 1) // BLOCK,
    )

    def cut(array, rows_at):
        shape = array.shape
        return array.reshape(shape[:rows_at] + (2, 2, 2, shape[rows_at] // 8) + shape[rows_at + 1:])

    token_rows = tokens.reshape(rows, model_width)
    token_blocks, bias_blocks, out_all, up_all, down_all = gather_start(
        token_rows,
        up_bias.reshape(8, units_here // 8),
        [("xy", cut(out_weight, 0)), ("xy", cut(up_weight, 0)), ("yx", cut(down_weight, 0))],
        zsize,
    )
    token_blocks = token_blocks.reshape(zsize, groups, local_rows, model_width)
    out_all = out_all.reshape(model_width, model_width)
    up_all = up_all.reshape(zsize, model_width, units_here)
    down_all = down_all.reshape(zsize, units_here, model_width)
    full_up_bias = bias_blocks.reshape(zsize, units_here)

    def ring(step):
        return [(i, (i + step) % zsize) for i in range(zsize)]

    def exchange(array, size, axis):
        parts = []
        for step in range(zsize):
            part = lax.dynamic_slice_in_dim(array, lax.rem(zi + step, zsize) * size, size, axis)
            parts.append(lax.ppermute(part, "z", ring(step)) if step else part)
        return parts

    kept, pieces = [], []
    for g in range(groups):
        kept.append(attend_forward(g, bounds, token_blocks, qkv_weight, qkv_bias, cosine, sine, segments))
        pieces += exchange(kept[g][0], local_rows, 1)
    flat = lambda vector: vector.reshape(1, model_width)
    (active, slope, mixed, normed_low, scaled_one, inv_one, result_low, embedded, grad_second, second_low, proj_grad,
     vec_two) = ffn_forward(
        zi, token_rows, pieces, out_all, [flat(v) for v in (out_bias, gain_one, shift_one)], up_all, full_up_bias,
        down_all, [flat(v) for v in (down_bias, gain_two, shift_two)], proj_weight.T,
        out_grad.reshape(rows, model_width), embed_grad.transpose(0, 2, 1),
    )
    core = lax.axis_index("core").reshape(1)
    give_up, keep_up, give_down, keep_down, ffn_back, up_bias_grad = ffn_backward(
        core, second_low, normed_low, up_all, down_all, active, slope
    )
    got_down = lax.ppermute(give_down, "core", PAIR)
    got_up = lax.ppermute(give_up, "core", PAIR)
    grad_normed = grad_second + ffn_back
    grad_first, gain_one_grad, shift_one_grad = norm_backward(grad_normed, scaled_one, inv_one, gain_one)
    first_low = grad_first.astype(bf16)
    out_bias_grad = jnp.sum(first_low.astype(f32), axis=0)
    out_grad_w = jnp.einsum("nh,nd->hd", mixed, first_low, preferred_element_type=f32).astype(bf16)
    grad_mixed = jnp.einsum("nd,hd->nh", first_low, out_all, preferred_element_type=f32).astype(bf16)
    grad_mixed = grad_mixed.reshape(groups, local_rows, model_width)
    upstream = [exchange(grad_mixed[g:g + 1], head_cols, 2) for g in range(groups)]
    send_down, keep_down = first_halving(got_down, keep_down, "yx")
    send_up, keep_up = first_halving(got_up, keep_up, "xy")
    upstream[0], send_down, send_up = lax.optimization_barrier((upstream[0], send_down, send_up))
    got_down = lax.ppermute(send_down, ORDERS["yx"][0], PAIR)
    got_up = lax.ppermute(send_up, ORDERS["xy"][0], PAIR)
    qkv_weight_grad, qkv_bias_grad, early = None, 0.0, []
    for g in range(groups):
        backs, qkv_weight_grad, bias_part = attend_backward(
            g, qkv_weight_grad, bounds, zi, kept[g][1:], kept[g][0], upstream[g], cosine, sine, token_blocks, qkv_weight
        )
        qkv_bias_grad = qkv_bias_grad + bias_part[:3]
        if g < groups - 1:
            early.append([
                lax.ppermute(backs[0, step], "z", ring(step)) if step else backs[0, step] for step in range(zsize)
            ])
    backs, got_down, got_up, qkv_bias_grad = lax.optimization_barrier((backs, got_down, got_up, qkv_bias_grad))

    vec_one = jnp.pad(jnp.stack([out_bias_grad, gain_one_grad, shift_one_grad]), ((0, 5), (0, 0)))
    placed = lax.dynamic_update_slice(
        jnp.zeros((zsize, 3 * head_cols), f32), qkv_bias_grad.reshape(1, -1), (zi, 0)
    )
    small = jnp.concatenate([vec_one, vec_two, up_bias_grad.reshape(8, -1), placed.reshape(8, -1)], axis=1)
    up_grad, down_grad, out_grad_w, qkv_weight_grad, proj_grad, back, small = reduce_end(
        [("xy", keep_up, got_up), ("yx", keep_down, got_down)],
        [
            ("xy", cut(out_grad_w.reshape(zsize, head_cols, model_width), 1)),
            ("yx", cut(qkv_weight_grad, 1)),
            ("xy", cut(proj_grad[None], 1)),
        ],
        backs,
        small,
        zsize,
    )
    qkv_weight_grad = qkv_weight_grad.reshape(qkv_weight.shape)
    proj_grad = proj_grad.reshape(-1, model_width)[:proj_weight.shape[1]].astype(f32).T
    out_grad_w = out_grad_w.reshape(out_weight.shape)
    up_grad = up_grad.reshape(up_weight.shape)
    down_grad = down_grad.reshape(down_weight.shape)
    if blocks > 1:
        down_grad, up_grad, out_grad_w, qkv_weight_grad = lax.psum(
            (down_grad, up_grad, out_grad_w, qkv_weight_grad), ("xb", "yb")
        )
        small, proj_grad = lax.psum((small, proj_grad), ("xb", "yb"))
    up_grad, down_grad, out_grad_w, qkv_weight_grad, tokens_grad = widen(
        up_grad, down_grad, out_grad_w, qkv_weight_grad, grad_first, early + [[back[0]]]
    )
    base = 2 * model_width
    vec = list(small[:3, :model_width]) + list(small[:3, model_width:base])
    split = base + zsize * units_here // 8
    up_bias_grad = lax.dynamic_slice(small[:, base:split].reshape(-1), (zi * units_here,), (units_here,))
    qkv_bias_grad = lax.dynamic_slice(small[:, split:].reshape(-1), (zi * 3 * head_cols,), (3 * head_cols,))
    qkv_bias_grad = qkv_bias_grad.reshape(3, head_cols)
    shape3 = (groups, local_rows, model_width)
    return (
        result_low.reshape(shape3),
        embedded.transpose(0, 2, 1),
        tokens_grad.reshape(shape3),
        qkv_weight_grad,
        qkv_bias_grad,
        out_grad_w,
        vec[0], vec[1], vec[2],
        up_grad,
        up_bias_grad,
        down_grad,
        vec[3], vec[4], vec[5],
        proj_grad,
    )


def solution(mesh):
    dp_size, zsize = mesh.shape["dp"], mesh.shape["tensor"]
    side = math.isqrt(dp_size // 2) // 2
    cut = Mesh(mesh.devices.reshape(side, 2, side, 2, 2, zsize), DP + ("z",))
    rows3 = P(DP, "z", None)
    in_specs = (
        rows3, P(DP, None), P(None, None, "z"), P(None, "z"), P("z", None), P(), P(), P(),
        P(None, "z"), P("z"), P("z", None), P(), P(), P(), P(), rows3, rows3,
    )
    out_specs = (
        rows3, rows3, rows3, P(None, None, "z"), P(None, "z"), P("z", None), P(), P(), P(),
        P(None, "z"), P("z"), P("z", None), P(), P(), P(), P(),
    )

    def run(*args):
        return per_device(side * side, *args)

    return jax.shard_map(run, mesh=cut, in_specs=in_specs, out_specs=out_specs, check_vma=False)
```
